32 devices in a mesh: branch: 2 (over x), rows: 16 (over z, y, core).
Axes of the slice: x: 2, y: 2, z: 4, core: 2. Of those that a mesh axis runs over, the one named last changes fastest.
Arguments:
- inputs: bfloat16 [16, 1024, 1024], P('rows', 'branch'), may hold values from -6 to 6
- lengths: int32 [16, 8], P('rows'), may hold values from 1 to 512, as said below
- norm_gain: float32 [1024], replicated, may hold values from 0.5 to 1.5
- query_weight: bfloat16 [1024, 512], P(None, 'branch'), may hold values from -0.1875 to 0.1875
- keyval_weight: bfloat16 [1024, 2, 128], P(None, None, 'branch'), may hold values from -0.1875 to 0.1875
- mixer_weight: bfloat16 [1024, 2, 1536], P(None, None, 'branch'), may hold values from -0.1875 to 0.1875
- state_weight: bfloat16 [1024, 2, 128], replicated, may hold values from -0.1875 to 0.1875
- step_weight: bfloat16 [1024, 24], P(None, 'branch'), may hold values from -0.1875 to 0.1875
- conv_mixer: float32 [4, 1536], P(None, 'branch'), may hold values from -3 to 3
- conv_state: float32 [4, 2, 128], replicated, may hold values from -3 to 3
- bias_mixer: float32 [1536], P('branch'), may hold values from -3 to 3
- bias_state: float32 [2, 128], replicated, may hold values from -3 to 3
- step_bias: float32 [24], P('branch'), may hold values from -6.9 to -2.3
- decay_log: float32 [24], P('branch'), may hold values from 0 to 2.77
- skip_gain: float32 [24], P('branch'), may hold values from 0.5 to 1.5
- ssd_gain: float32 [1536], P('branch'), may hold values from 0.5 to 1.5
- attn_output: bfloat16 [512, 1024], P('branch'), may hold values from -2 to 2
- ssd_output: bfloat16 [1536, 1024], P('branch'), may hold values from -0.15625 to 0.15625
- ffn_gain: float32 [1024], replicated, may hold values from 0.5 to 1.5
- gate_weight: bfloat16 [1024, 2048], replicated, may hold values from -0.1875 to 0.1875
- up_weight: bfloat16 [1024, 2048], replicated, may hold values from -0.1875 to 0.1875
- down_weight: bfloat16 [2048, 1024], replicated, may hold values from -0.125 to 0.125
- cotangent: bfloat16 [16, 1024, 1024], P('rows', 'branch'), may hold values from -6 to 6
Outputs:
- block_out: bfloat16 [16, 1024, 1024], P('rows', 'branch')
- input_grad: bfloat16 [16, 1024, 1024], P('rows', 'branch')
- norm_gain_grad: float32 [1024], replicated
- query_weight_grad: float32 [1024, 512], P('rows', 'branch')
- keyval_weight_grad: float32 [1024, 2, 128], P('rows', None, 'branch')
- mixer_weight_grad: float32 [1024, 2, 1536], P('rows', None, 'branch')
- state_weight_grad: float32 [1024, 2, 128], replicated
- step_weight_grad: float32 [1024, 24], P('rows', 'branch')
- conv_mixer_grad: float32 [4, 1536], P(None, ('branch', 'rows'))
- conv_state_grad: float32 [4, 2, 128], replicated
- bias_mixer_grad: float32 [1536], P(('branch', 'rows'))
- bias_state_grad: float32 [2, 128], replicated
- step_bias_grad: float32 [24], replicated
- decay_log_grad: float32 [24], replicated
- skip_gain_grad: float32 [24], replicated
- ssd_gain_grad: float32 [1536], P(('branch', 'rows'))
- attn_output_grad: float32 [512, 1024], P('branch', 'rows')
- ssd_output_grad: float32 [1536, 1024], P('branch', 'rows')
- ffn_gain_grad: float32 [1024], replicated
- gate_weight_grad: float32 [1024, 2048], P(None, ('branch', 'rows'))
- up_weight_grad: float32 [1024, 2048], P(None, ('branch', 'rows'))
- down_weight_grad: float32 [2048, 1024], P(('branch', 'rows'))
The draws below stay inside these ranges and needn't reach their ends.
Inputs may be any that keep to these rules, and one draw needn't show every extreme that they name: Each row holds the 8 lengths of one pack's documents in order; they sum to 896, so the last 128 positions of every pack are padding.
All inputs are finite; a program needn't handle non-finite values.
Results may differ from the reference program's by a relative error of at most 0.017.
Values may be sent and summed in bfloat16 or wider, within the bound.
A program may use at most 192 MiB of HBM per device.

```python
import jax
import jax.numpy as jnp
from jax import lax

D = 1024
QH = 8
KVH = 2
HD = 64
SH = 24
SP = 64
STATE = 128
CONV = 4
FF = 2048
SEQ = 1024
DOCS = 8
ABLK = 512
SBLK = 256
USED = 896
PACKS = 16


def draw_lengths(key, part):
    longest = SEQ // 2
    rest = USED - longest

    def one_pack(pack_key):
        cut_key, place_key = jax.random.split(pack_key)
        picks = jax.random.permutation(cut_key, rest - 1)[:DOCS - 2].astype(jnp.int32) + 1
        cuts = jnp.sort(picks)
        bounds = jnp.concatenate([jnp.zeros((1,), jnp.int32), cuts, jnp.full((1,), rest, jnp.int32)])
        others = (bounds[1:] - bounds[:-1]).astype(jnp.int32)
        place = jax.random.randint(place_key, (), 0, DOCS).astype(jnp.int32)
        slots = jnp.arange(DOCS, dtype=jnp.int32)
        before = jnp.concatenate([others, jnp.zeros((1,), jnp.int32)])
        after = jnp.concatenate([jnp.zeros((1,), jnp.int32), others])
        result = jnp.where(slots < place, before, jnp.where(slots == place, longest, after))
        return result.astype(jnp.int32)
    pack_keys = jax.random.split(key, PACKS)
    return jax.vmap(one_pack)(pack_keys)


def steps_of(stream_key, extent, shards, low, high):
    level = 1.0
    for position, shards_of in shards:
        heights = jax.random.uniform(jax.random.fold_in(jax.random.fold_in(stream_key, 6), position), (shards_of,), jnp.float32, low / len(shards), high / len(shards))
        level = level * jnp.repeat(jnp.exp(heights), extent[position] // shards_of).reshape((-1,) + (1,) * (len(extent) - 1 - position))
    return level


def centred(own_key, shape, spread, limit, cuts=(), held_as=jnp.bfloat16):
    values = spread * jax.random.normal(own_key, shape, jnp.float32)
    if cuts:
        values = values * steps_of(own_key, shape, cuts, -0.22, 0.18)
    return jnp.clip(values, -limit, limit).astype(held_as)


def setup_inputs(seed: int = 0) -> dict:
    key_list = jax.random.split(jax.random.key(seed), 24)
    inputs = centred(key_list[0], (PACKS, SEQ, D), 1.0, 6.0, ((0, 16), (1, 2)))
    lengths = draw_lengths(jax.random.fold_in(key_list[23], 71), 0)
    norm_gain = jnp.clip(1.0 + 0.1 * jax.random.normal(key_list[2], (D,), jnp.float32), 0.5, 1.5)
    query_weight = centred(key_list[3], (D, QH * HD), D ** -0.5, 0.1875, ((1, 2),))
    keyval_weight = centred(key_list[4], (D, 2, KVH * HD), D ** -0.5, 0.1875, ((2, 2),))
    mixer_weight = centred(key_list[5], (D, 2, SH * SP), D ** -0.5, 0.1875, ((2, 2),))
    state_weight = centred(key_list[6], (D, 2, STATE), D ** -0.5, 0.1875)
    step_weight = centred(key_list[7], (D, SH), D ** -0.5, 0.1875, ((1, 2),))
    conv_mixer = centred(key_list[8], (CONV, SH * SP), CONV ** -0.5, 3.0, ((1, 2),), jnp.float32)
    conv_state = centred(key_list[9], (CONV, 2, STATE), CONV ** -0.5, 3.0, (), jnp.float32)
    bias_mixer = centred(key_list[10], (SH * SP,), 0.5, 3.0, ((0, 2),), jnp.float32)
    bias_state = centred(key_list[11], (2, STATE), 0.5, 3.0, (), jnp.float32)
    step_bias = jnp.clip(-6.9 + 4.6000001430511475 * jax.random.uniform(key_list[12], (SH,), jnp.float32) ** steps_of(key_list[12], (SH,), ((0, 2),), -0.2, 0.2), -6.9, -2.3)
    decay_log = jnp.clip(2.77 * jax.random.uniform(key_list[13], (SH,), jnp.float32) ** steps_of(key_list[13], (SH,), ((0, 2),), -0.2, 0.2), 0.0, 2.77)
    skip_gain = jnp.clip(0.5 + 1.0 * jax.random.uniform(key_list[14], (SH,), jnp.float32) ** steps_of(key_list[14], (SH,), ((0, 2),), -0.2, 0.2), 0.5, 1.5)
    ssd_gain = jnp.clip(1.0 + 0.1 * jax.random.normal(key_list[15], (SH * SP,), jnp.float32), 0.5, 1.5)
    attn_output = centred(key_list[16], (QH * HD, D), (QH * HD // 64) ** -0.5, 2.0, ((0, 2),))
    ssd_output = centred(key_list[17], (SH * SP, D), (SH * SP) ** -0.5, 0.15625, ((0, 2),))
    ffn_gain = jnp.clip(1.0 + 0.1 * jax.random.normal(key_list[18], (D,), jnp.float32), 0.5, 1.5)
    gate_weight = centred(key_list[19], (D, FF), D ** -0.5, 0.1875)
    up_weight = centred(key_list[20], (D, FF), D ** -0.5, 0.1875)
    down_weight = centred(key_list[21], (FF, D), FF ** -0.5, 0.125)
    cotangent = centred(key_list[22], (PACKS, SEQ, D), 1.0, 6.0, ((0, 16), (1, 2)))
    return {"inputs": inputs, "lengths": lengths, "norm_gain": norm_gain, "query_weight": query_weight, "keyval_weight": keyval_weight, "mixer_weight": mixer_weight, "state_weight": state_weight, "step_weight": step_weight, "conv_mixer": conv_mixer, "conv_state": conv_state, "bias_mixer": bias_mixer, "bias_state": bias_state, "step_bias": step_bias, "decay_log": decay_log, "skip_gain": skip_gain, "ssd_gain": ssd_gain, "attn_output": attn_output, "ssd_output": ssd_output, "ffn_gain": ffn_gain, "gate_weight": gate_weight, "up_weight": up_weight, "down_weight": down_weight, "cotangent": cotangent}


EPSILON = 1e-05
ROPE_BASE = 100000000000.0
PRECISE = lax.Precision.HIGHEST

@jax.custom_vjp
def low(v):
    return lax.optimization_barrier(v.astype(jnp.bfloat16)).astype(jnp.float32)

@jax.custom_vjp
def low_back(v):
    return v

def low_keep(v):
    return (low(v), None)

def low_pass(kept, grad):
    return (grad,)

def back_keep(v):
    return (v, None)

def back_low(kept, grad):
    return (low(grad),)
low.defvjp(low_keep, low_pass)
low_back.defvjp(back_keep, back_low)

def matmul_hi(left_side, right_side):
    return jnp.dot(left_side, right_side, precision=PRECISE)

def rms_scale(values):
    return lax.rsqrt(lax.optimization_barrier(jnp.mean(values * values, axis=-1, keepdims=True)) + EPSILON)

def rms_norm(values, gain):
    return values * rms_scale(values) * gain

def doc_tables(length_row, seq_len, doc_count):
    doc_ends = jnp.cumsum(length_row).astype(jnp.int32)
    starts = (doc_ends - length_row).astype(jnp.int32)
    places = jnp.arange(seq_len, dtype=jnp.int32)
    segment = lax.optimization_barrier(jnp.sum((places[:, None] >= doc_ends[None, :]).astype(jnp.int32), axis=1)).astype(jnp.int32)
    matches = segment[:, None] == jnp.arange(doc_count, dtype=jnp.int32)[None, :]
    offsets = lax.optimization_barrier(jnp.sum(jnp.where(matches, starts[None, :], 0), axis=1)).astype(jnp.int32)
    return (segment, places - offsets, (segment < doc_count).astype(jnp.float32))

def rotate(head_rows, within, direction):
    head_dim = head_rows.shape[-1]
    half_dim = head_dim // 2
    frequency = ROPE_BASE ** (-(jnp.arange(half_dim, dtype=jnp.float32) * 2.0) / head_dim)
    angles = within.astype(jnp.float32)[:, None] * frequency[None, :]
    cosine = jnp.cos(angles)[:, None, :]
    sine_part = direction * jnp.sin(angles)[:, None, :]
    first_half = head_rows[..., :half_dim]
    second_half = head_rows[..., half_dim:]
    return jnp.concatenate([first_half * cosine - second_half * sine_part, second_half * cosine + first_half * sine_part], axis=-1)

def causal_conv(conv_input, conv_weight, conv_bias, segment):
    tap_count = conv_weight.shape[0]
    result = conv_bias[None, :] + conv_weight[tap_count - 1][None, :] * conv_input
    for offset in range(1, tap_count):
        shifted = jnp.concatenate([jnp.zeros((offset, conv_input.shape[1]), jnp.float32), conv_input[:-offset]], axis=0)
        shifted_seg = jnp.concatenate([jnp.full((offset,), -1, jnp.int32), segment[:-offset]])
        same_doc = (shifted_seg == segment).astype(jnp.float32)
        result = result + conv_weight[tap_count - 1 - offset][None, :] * shifted * same_doc[:, None]
    return result

def ssd_scan(head_inputs, step_sizes, decay_rate, state_in, state_out, segment, block_len):
    seq_len, head_count, head_dim = head_inputs.shape
    state_dim = state_in.shape[1]
    blocks = seq_len // block_len
    seg_blocks = segment.reshape(blocks, block_len)
    previous = jnp.concatenate([jnp.full((1,), -1, jnp.int32), seg_blocks[:-1, -1]])
    lower_mask = jnp.arange(block_len)[:, None] >= jnp.arange(block_len)[None, :]

    def advance(carry_state, pieces):
        input_block, step_block, in_block, out_block, seg_block, prev_seg = pieces
        log_rates = step_block * decay_rate[None, :]
        cumulative = jnp.cumsum(log_rates, axis=0)
        allowed = ((seg_block[:, None] == seg_block[None, :]) & lower_mask)[:, :, None]
        log_gaps = jnp.where(allowed, cumulative[:, None, :] - cumulative[None, :, :], 0.0)
        decays = jnp.where(allowed, jnp.exp(log_gaps), 0.0)
        intersection = jnp.dot(out_block, in_block.T, precision=PRECISE)
        weights = intersection[:, :, None] * decays * step_block[None, :, :]
        inside_part = jnp.einsum('tsh,shp->thp', weights, input_block, precision=PRECISE)
        carried = (seg_block == prev_seg).astype(jnp.float32)
        entry_decay = jnp.exp(cumulative) * carried[:, None]
        outside_part = jnp.einsum('tn,hpn->thp', out_block, carry_state, precision=PRECISE) * entry_decay[:, :, None]
        tail_mask = (seg_block == seg_block[-1]).astype(jnp.float32)
        to_end = jnp.exp(cumulative[-1][None, :] - cumulative) * tail_mask[:, None] * step_block
        kept_state = carry_state * (jnp.exp(cumulative[-1]) * carried[-1])[:, None, None]
        new_state = kept_state + jnp.einsum('sh,shp,sn->hpn', to_end, input_block, in_block, precision=PRECISE)
        return (new_state, inside_part + outside_part)
    pieces = (head_inputs.reshape(blocks, block_len, head_count, head_dim), step_sizes.reshape(blocks, block_len, head_count), state_in.reshape(blocks, block_len, state_dim), state_out.reshape(blocks, block_len, state_dim), seg_blocks, previous)
    starting = jnp.zeros((head_count, head_dim, state_dim), jnp.float32)
    final_state, outputs = lax.scan(jax.checkpoint(advance), starting, pieces)
    return outputs.reshape(seq_len, head_count, head_dim)

def mixer_local(mixer_proj, state_proj, step_proj, conv_mixer, conv_state, bias_mixer, bias_state, step_bias, decay_log, skip_gain, segment, block_len, head_dim):
    inner_dim = mixer_proj.shape[1] // 2
    state_dim = state_proj.shape[1] // 2
    gate_part = mixer_proj[:, :inner_dim]
    conv_input = jnp.concatenate([mixer_proj[:, inner_dim:], state_proj], axis=1)
    conv_weight = jnp.concatenate([conv_mixer, conv_state.reshape(conv_state.shape[0], -1)], axis=1)
    conv_bias = jnp.concatenate([bias_mixer, bias_state.reshape(-1)])
    activated = jax.nn.silu(causal_conv(conv_input, conv_weight, conv_bias, segment))
    head_count = inner_dim // head_dim
    head_inputs = activated[:, :inner_dim].reshape(-1, head_count, head_dim)
    state_in = activated[:, inner_dim:inner_dim + state_dim]
    state_out = activated[:, inner_dim + state_dim:]
    step_sizes = jax.nn.softplus(step_proj + step_bias[None, :])
    decay_rate = -jnp.exp(decay_log)
    scanned = ssd_scan(head_inputs, step_sizes, decay_rate, state_in, state_out, segment, block_len)
    combined = scanned + skip_gain[None, :, None] * head_inputs
    return combined.reshape(-1, inner_dim) * jax.nn.silu(gate_part)

def attend(queries, key_rows, value_rows, segment):
    seq_len = queries.shape[0]
    places = jnp.arange(seq_len, dtype=jnp.int32)
    scale_factor = HD ** (-0.5)

    def one_block(row_start):
        block_q = lax.dynamic_slice_in_dim(queries, row_start, ABLK, 0)
        block_seg = lax.dynamic_slice_in_dim(segment, row_start, ABLK, 0)
        block_pos = row_start + jnp.arange(ABLK, dtype=jnp.int32)
        scores = low_back(jnp.einsum('qkgd,skd->kgqs', block_q, key_rows, precision=PRECISE))
        allowed = (block_seg[:, None] == segment[None, :]) & (block_pos[:, None] >= places[None, :])
        logits = jnp.where(allowed, scores * scale_factor, -jnp.inf)
        row_peak = lax.optimization_barrier(jnp.max(logits, axis=-1, keepdims=True))
        powered = jnp.exp(logits - row_peak)
        softmax_rows = powered / lax.optimization_barrier(jnp.sum(powered, axis=-1, keepdims=True))
        return low_back(jnp.einsum('kgqs,skd->qkgd', low(softmax_rows), value_rows, precision=PRECISE))
    starts = jnp.arange(seq_len // ABLK, dtype=jnp.int32) * ABLK
    return lax.map(jax.checkpoint(one_block), starts).reshape(queries.shape)

def pack_forward(rows_in, segment, within, valid_rows, params):
    norm_gain, query_weight, keyval_weight, mixer_weight, state_weight, step_weight, conv_mixer, conv_state, bias_mixer, bias_state, step_bias, decay_log, skip_gain, ssd_gain, attn_output, ssd_output, ffn_gain, gate_weight, up_weight, down_weight = params
    seq_len, model_dim = rows_in.shape
    normed = low(rms_norm(rows_in, norm_gain))
    query_proj = low_back(matmul_hi(normed, query_weight))
    keyval_proj = low_back(matmul_hi(normed, keyval_weight.reshape(model_dim, -1)))
    mixer_proj = low_back(matmul_hi(normed, mixer_weight.reshape(model_dim, -1)))
    state_proj = low_back(matmul_hi(normed, state_weight.reshape(model_dim, -1)))
    step_proj = low_back(matmul_hi(normed, step_weight))
    queries = low(rotate(query_proj.reshape(seq_len, QH, HD), within, 1.0)).reshape(seq_len, KVH, QH // KVH, HD)
    keyval_rows = keyval_proj.reshape(seq_len, 2, KVH, HD)
    key_rows = low(rotate(keyval_rows[:, 0], within, 1.0))
    value_rows = low(keyval_rows[:, 1])
    attn_low = low(attend(queries, key_rows, value_rows, segment).reshape(seq_len, QH * HD))
    gated_rows = mixer_local(mixer_proj, state_proj, step_proj, conv_mixer, conv_state, bias_mixer, bias_state, step_bias, decay_log, skip_gain, segment, SBLK, SP)
    ssd_low = low(rms_norm(gated_rows, ssd_gain))
    mixer_sum = low_back(matmul_hi(attn_low, attn_output) + matmul_hi(ssd_low, ssd_output))
    hidden = rows_in + valid_rows[:, None] * mixer_sum
    normed_ffn = low(rms_norm(hidden, ffn_gain))
    gate_vals = low_back(matmul_hi(normed_ffn, gate_weight))
    up_vals = low_back(matmul_hi(normed_ffn, up_weight))
    act_low = low(jax.nn.silu(gate_vals) * up_vals)
    return hidden + low_back(matmul_hi(act_low, down_weight))

def reference(inputs, lengths, norm_gain, query_weight, keyval_weight, mixer_weight, state_weight, step_weight, conv_mixer, conv_state, bias_mixer, bias_state, step_bias, decay_log, skip_gain, ssd_gain, attn_output, ssd_output, ffn_gain, gate_weight, up_weight, down_weight, cotangent):
    params = tuple((weight_item.astype(jnp.float32) for weight_item in (norm_gain, query_weight, keyval_weight, mixer_weight, state_weight, step_weight, conv_mixer, conv_state, bias_mixer, bias_state, step_bias, decay_log, skip_gain, ssd_gain, attn_output, ssd_output, ffn_gain, gate_weight, up_weight, down_weight)))

    def one_pack(totals, pieces):
        pack_rows, length_row, upstream = pieces
        segment, within, valid_rows = doc_tables(length_row, SEQ, DOCS)

        def forward(rows_in, *weights):
            return pack_forward(rows_in, segment, within, valid_rows, weights)
        pack_out, pullback = jax.vjp(forward, pack_rows.astype(jnp.float32), *params)
        grads = pullback(upstream.astype(jnp.float32))
        new_totals = tuple((running + piece_grad for running, piece_grad in zip(totals, grads[1:])))
        return (new_totals, (pack_out.astype(jnp.bfloat16), grads[0].astype(jnp.bfloat16)))
    starting = tuple((jnp.zeros(param_item.shape, jnp.float32) for param_item in params))
    totals, (block_out, input_grad) = lax.scan(one_pack, starting, (inputs, lengths, cotangent))
    return (block_out, input_grad, totals[0], totals[1], totals[2], totals[3], totals[4], totals[5], totals[6], totals[7], totals[8], totals[9], totals[10], totals[11], totals[12], totals[13], totals[14], totals[15], totals[16], totals[17], totals[18], totals[19])
```

```python
import jax
import jax.numpy as jnp
from jax import lax
from jax.sharding import PartitionSpec as P

HD = 64
SH = 24
SP = 64
ABLK = 512
SBLK = 256


EPSILON = 1e-05
ROPE_BASE = 100000000000.0
PRECISE = lax.Precision.HIGHEST


def rms_scale(values):
    return lax.rsqrt(jnp.mean(values * values, axis=-1, keepdims=True) + EPSILON)


def rms_back(upstream, values, scales, gain):
    weighted = upstream * gain
    return scales * weighted - values * scales**3 * jnp.mean(
        weighted * values, axis=-1, keepdims=True
    )


def doc_tables(length_row, seq_len, doc_count):
    order = jnp.arange(doc_count, dtype=jnp.int32)
    doc_ends = jnp.sum(jnp.where(order[:, None] >= order[None, :], length_row[None, :], 0), axis=1)
    starts = doc_ends - length_row
    places = jnp.arange(seq_len, dtype=jnp.int32)
    segment = jnp.sum((places[:, None] >= doc_ends[None, :]).astype(jnp.int32), axis=1)
    matches = segment[:, None] == jnp.arange(doc_count, dtype=jnp.int32)[None, :]
    offsets = jnp.sum(jnp.where(matches, starts[None, :], 0), axis=1)
    return (segment, places - offsets, (segment < doc_count).astype(jnp.float32))


def rotate(head_rows, within, direction):
    head_dim = head_rows.shape[-1]
    half_dim = head_dim // 2
    frequency = ROPE_BASE ** (-(jnp.arange(half_dim, dtype=jnp.float32) * 2.0) / head_dim)
    angles = within.astype(jnp.float32)[:, None] * frequency[None, :]
    cosine = jnp.cos(angles)[:, None, :]
    sine_part = direction * jnp.sin(angles)[:, None, :]
    first_half = head_rows[..., :half_dim]
    second_half = head_rows[..., half_dim:]
    return jnp.concatenate(
        [
            first_half * cosine - second_half * sine_part,
            second_half * cosine + first_half * sine_part,
        ],
        axis=-1,
    )


def causal_conv(conv_input, conv_weight, conv_bias, segment):
    tap_count = conv_weight.shape[0]
    result = conv_bias[None, :] + conv_weight[tap_count - 1][None, :] * conv_input
    for offset in range(1, tap_count):
        shifted = jnp.concatenate(
            [jnp.zeros((offset, conv_input.shape[1]), jnp.float32), conv_input[:-offset]], axis=0
        )
        shifted_seg = jnp.concatenate([jnp.full((offset,), -1, jnp.int32), segment[:-offset]])
        same_doc = (shifted_seg == segment).astype(jnp.float32)
        result = result + conv_weight[tap_count - 1 - offset][None, :] * shifted * same_doc[:, None]
    return result


def ssd_scan(head_inputs, step_sizes, decay_rate, state_in, state_out, segment, block_len):
    seq_len, head_count, head_dim = head_inputs.shape
    state_dim = state_in.shape[1]
    blocks = seq_len // block_len
    seg_blocks = segment.reshape(blocks, block_len)
    previous = jnp.concatenate([jnp.full((1,), -1, jnp.int32), seg_blocks[:-1, -1]])
    lower_mask = jnp.arange(block_len)[:, None] >= jnp.arange(block_len)[None, :]

    def advance(carry_state, pieces):
        input_block, step_block, in_block, out_block, seg_block, prev_seg = pieces
        log_rates = step_block * decay_rate[None, :]
        cumulative = jnp.dot(lower_mask.astype(jnp.float32), log_rates, precision=PRECISE)
        allowed = ((seg_block[:, None] == seg_block[None, :]) & lower_mask)[:, :, None]
        log_gaps = jnp.where(allowed, cumulative[:, None, :] - cumulative[None, :, :], 0.0)
        decays = jnp.where(allowed, jnp.exp(log_gaps), 0.0)
        intersection = jnp.dot(out_block, in_block.T, precision=PRECISE)
        weights = intersection[:, :, None] * decays * step_block[None, :, :]
        inside_part = jnp.einsum("tsh,shp->thp", weights, input_block, precision=PRECISE)
        carried = (seg_block == prev_seg).astype(jnp.float32)
        entry_decay = jnp.exp(cumulative) * carried[:, None]
        outside_part = (
            jnp.einsum("tn,hpn->thp", out_block, carry_state, precision=PRECISE)
            * entry_decay[:, :, None]
        )
        tail_mask = (seg_block == seg_block[-1]).astype(jnp.float32)
        to_end = jnp.exp(cumulative[-1][None, :] - cumulative) * tail_mask[:, None] * step_block
        kept_state = carry_state * (jnp.exp(cumulative[-1]) * carried[-1])[:, None, None]
        new_state = kept_state + jnp.einsum(
            "sh,shp,sn->hpn", to_end, input_block, in_block, precision=PRECISE
        )
        return (new_state, inside_part + outside_part)

    pieces = (
        head_inputs.reshape(blocks, block_len, head_count, head_dim),
        step_sizes.reshape(blocks, block_len, head_count),
        state_in.reshape(blocks, block_len, state_dim),
        state_out.reshape(blocks, block_len, state_dim),
        seg_blocks,
        previous,
    )
    starting = jnp.zeros((head_count, head_dim, state_dim), jnp.float32)
    final_state, outputs = lax.scan(jax.checkpoint(advance), starting, pieces)
    return outputs.reshape(seq_len, head_count, head_dim)


def mixer_local(
    mixer_proj,
    state_proj,
    step_proj,
    conv_mixer,
    conv_state,
    bias_mixer,
    bias_state,
    step_bias,
    decay_log,
    skip_gain,
    segment,
    block_len,
    head_dim,
):
    inner_dim = mixer_proj.shape[1] // 2
    state_dim = state_proj.shape[1] // 2
    gate_part = mixer_proj[:, :inner_dim]
    conv_input = jnp.concatenate([mixer_proj[:, inner_dim:], state_proj], axis=1)
    conv_weight = jnp.concatenate([conv_mixer, conv_state.reshape(conv_state.shape[0], -1)], axis=1)
    conv_bias = jnp.concatenate([bias_mixer, bias_state.reshape(-1)])
    activated = jax.nn.silu(causal_conv(conv_input, conv_weight, conv_bias, segment))
    head_count = inner_dim // head_dim
    head_inputs = activated[:, :inner_dim].reshape(-1, head_count, head_dim)
    state_in = activated[:, inner_dim : inner_dim + state_dim]
    state_out = activated[:, inner_dim + state_dim :]
    step_sizes = jax.nn.softplus(step_proj + step_bias[None, :])
    decay_rate = -jnp.exp(decay_log)
    scanned = ssd_scan(head_inputs, step_sizes, decay_rate, state_in, state_out, segment, block_len)
    combined = scanned + skip_gain[None, :, None] * head_inputs
    return combined.reshape(-1, inner_dim) * jax.nn.silu(gate_part)


def block_mask(segment, row_start, block_rows):
    places = jnp.arange(segment.shape[0], dtype=jnp.int32)
    block_seg = lax.dynamic_slice_in_dim(segment, row_start, block_rows, 0)
    block_pos = row_start + jnp.arange(block_rows, dtype=jnp.int32)
    return (block_seg[:, None] == segment[None, :]) & (block_pos[:, None] >= places[None, :])


def attend_forward(queries, key_rows, value_rows, segment, block_rows):
    scale_factor = queries.shape[-1] ** (-0.5)

    def one_block(row_start):
        block_q = lax.dynamic_slice_in_dim(queries, row_start, block_rows, 0)
        allowed = block_mask(segment, row_start, block_rows)
        raw_scores = jnp.einsum(
            "qkgd,skd->kgqs", block_q, key_rows, preferred_element_type=jnp.float32
        )
        logits = jnp.where(allowed, raw_scores * scale_factor, -jnp.inf)
        row_peak = jnp.max(logits, axis=-1, keepdims=True)
        powered = jnp.exp(logits - row_peak)
        row_total = jnp.sum(powered, axis=-1, keepdims=True)
        probs_low = (powered / row_total).astype(jnp.bfloat16)
        output = jnp.einsum(
            "kgqs,skd->qkgd", probs_low, value_rows, preferred_element_type=jnp.float32
        )
        return (output, row_peak + jnp.log(row_total))

    starts = jnp.arange(queries.shape[0] // block_rows, dtype=jnp.int32) * block_rows
    outputs, log_sums = lax.map(one_block, starts)
    return (outputs.reshape(queries.shape), log_sums)


def attend_backward(queries, key_rows, value_rows, grad_out, log_sums, segment, block_rows):
    scale_factor = queries.shape[-1] ** (-0.5)

    def one_block(carry, pieces):
        grad_keys, grad_values = carry
        row_start, block_lse = pieces
        block_q = lax.dynamic_slice_in_dim(queries, row_start, block_rows, 0)
        block_grad = lax.dynamic_slice_in_dim(grad_out, row_start, block_rows, 0)
        allowed = block_mask(segment, row_start, block_rows)
        raw_scores = jnp.einsum(
            "qkgd,skd->kgqs", block_q, key_rows, preferred_element_type=jnp.float32
        )
        logits = jnp.where(allowed, raw_scores * scale_factor, -jnp.inf)
        softmax_rows = jnp.exp(logits - block_lse)
        grad_probs = jnp.einsum(
            "qkgd,skd->kgqs", block_grad, value_rows, preferred_element_type=jnp.float32
        )
        centre = jnp.sum(softmax_rows * grad_probs, axis=-1, keepdims=True)
        grad_scores = (softmax_rows * (grad_probs - centre) * scale_factor).astype(jnp.bfloat16)
        grad_query = jnp.einsum(
            "kgqs,skd->qkgd", grad_scores, key_rows, preferred_element_type=jnp.float32
        )
        grad_keys = grad_keys + jnp.einsum(
            "kgqs,qkgd->skd", grad_scores, block_q, preferred_element_type=jnp.float32
        )
        grad_values = grad_values + jnp.einsum(
            "kgqs,qkgd->skd",
            softmax_rows.astype(jnp.bfloat16),
            block_grad,
            preferred_element_type=jnp.float32,
        )
        return ((grad_keys, grad_values), grad_query)

    starts = jnp.arange(queries.shape[0] // block_rows, dtype=jnp.int32) * block_rows
    zero_rows = jnp.zeros(key_rows.shape, jnp.float32)
    (grad_keys, grad_values), grad_queries = lax.scan(
        one_block, (zero_rows, zero_rows), (starts, log_sums)
    )
    return (grad_queries.reshape(queries.shape), grad_keys, grad_values)


def bits_of(count):
    return count.bit_length() - 1


def swap_halves(values, axis_name, bit, size):
    pairs = [(item, item ^ (1 << bit)) for item in range(size)]
    return lax.ppermute(values, axis_name, pairs)


def halve(values, place, my_bit, axis_name, bit, size):
    owners = values.shape[0]
    high = 1 << place
    parts = values.reshape((high, 2, owners // (2 * high)) + values.shape[1:])
    sent = lax.dynamic_index_in_dim(parts, 1 - my_bit, 1, keepdims=False)
    kept = lax.dynamic_index_in_dim(parts, my_bit, 1, keepdims=False)
    got = swap_halves(sent, axis_name, bit, size)
    total = (kept.astype(jnp.float32) + got.astype(jnp.float32)).astype(values.dtype)
    return total.reshape((owners // 2,) + values.shape[1:])


def scatter_sum(values, digits, order):
    left = list(digits)
    for digit in order:
        axis_name, bit, size = digit
        my_bit = (lax.axis_index(axis_name) >> bit) & 1
        values = halve(values, left.index(digit), my_bit, axis_name, bit, size)
        left.remove(digit)
    return values[0]


def gather_all(values, digits, order):
    values = values[None]
    left = []
    for digit in order:
        axis_name, bit, size = digit
        my_bit = (lax.axis_index(axis_name) >> bit) & 1
        got = swap_halves(values, axis_name, bit, size)
        place = sum(1 for item in left if digits.index(item) < digits.index(digit))
        high = 1 << place
        owners = values.shape[0]
        mine = values.reshape((high, 1, owners // high) + values.shape[1:])
        other = got.reshape(mine.shape)
        first = jnp.where(my_bit == 0, mine, other)
        second = jnp.where(my_bit == 0, other, mine)
        values = jnp.concatenate([first, second], axis=1).reshape((owners * 2,) + values.shape[1:])
        left.append(digit)
    return values


def other_branch(values):
    return lax.ppermute(values, "branch", [(0, 1), (1, 0)])


def both_halves(values, branch_pos):
    got = other_branch(values)
    return jnp.concatenate(
        [jnp.where(branch_pos == 0, values, got), jnp.where(branch_pos == 0, got, values)], axis=0
    )


def own_half_sum(values, branch_pos):
    half = values.shape[0] // 2
    sent = lax.dynamic_slice_in_dim(values, (1 - branch_pos) * half, half, 0)
    kept = lax.dynamic_slice_in_dim(values, branch_pos * half, half, 0)
    return kept.astype(jnp.float32) + other_branch(sent).astype(jnp.float32)


def per_device(
    inputs,
    lengths,
    norm_gain,
    query_weight,
    keyval_weight,
    mixer_weight,
    state_weight,
    step_weight,
    conv_mixer,
    conv_state,
    bias_mixer,
    bias_state,
    step_bias,
    decay_log,
    skip_gain,
    ssd_gain,
    attn_output,
    ssd_output,
    ffn_gain,
    gate_weight,
    up_weight,
    down_weight,
    cotangent,
):
    branch_pos = lax.axis_index("branch")
    row_count = lax.axis_size("rows")
    row_bits = bits_of(row_count)
    row_digits = [("rows", bit, row_count) for bit in range(row_bits - 1, -1, -1)]
    all_digits = [("branch", 0, 2)] + row_digits
    upward = row_digits[::-1]
    full_order = [upward[0]] + [all_digits[0]] + upward[1:]
    own_rows = inputs[0].astype(jnp.float32)
    half_len = own_rows.shape[0]
    seq_len = 2 * half_len
    model_dim = own_rows.shape[1]
    segment, within, valid_rows = doc_tables(lengths[0], seq_len, lengths.shape[1])
    own_valid = lax.dynamic_slice_in_dim(valid_rows, branch_pos * half_len, half_len, 0)
    own_scale = rms_scale(own_rows)
    own_hat = own_rows * own_scale
    normed = (own_hat * norm_gain).astype(jnp.bfloat16)
    full_normed = both_halves(normed, branch_pos)
    local_query = query_weight.shape[1] // HD
    local_keyval = keyval_weight.shape[2] // HD
    group_size = local_query // local_keyval
    keyval_flat = keyval_weight.reshape(model_dim, -1)
    mixer_flat = mixer_weight.reshape(model_dim, -1)
    state_flat = state_weight.reshape(model_dim, -1)
    query_proj = jnp.dot(full_normed, query_weight, preferred_element_type=jnp.float32)
    keyval_proj = jnp.dot(full_normed, keyval_flat, preferred_element_type=jnp.float32)
    mixer_proj = jnp.dot(full_normed, mixer_flat, preferred_element_type=jnp.float32)
    state_proj = jnp.dot(full_normed, state_flat, preferred_element_type=jnp.float32)
    step_proj = jnp.dot(full_normed, step_weight, preferred_element_type=jnp.float32)
    queries = rotate(query_proj.reshape(seq_len, local_query, HD), within, 1.0).astype(jnp.bfloat16)
    queries = queries.reshape(seq_len, local_keyval, group_size, HD)
    keyval_rows = keyval_proj.reshape(seq_len, 2, local_keyval, HD)
    key_rows = rotate(keyval_rows[:, 0], within, 1.0).astype(jnp.bfloat16)
    value_rows = keyval_rows[:, 1].astype(jnp.bfloat16)
    block_rows = min(ABLK, seq_len)
    attn_out, log_sums = attend_forward(queries, key_rows, value_rows, segment, block_rows)
    attn_low = attn_out.reshape(seq_len, -1).astype(jnp.bfloat16)

    def local_piece(
        mixer_in,
        state_in,
        step_in,
        conv_mixer_in,
        conv_state_in,
        bias_mixer_in,
        bias_state_in,
        step_bias_in,
        decay_in,
        skip_in,
    ):
        return mixer_local(
            mixer_in,
            state_in,
            step_in,
            conv_mixer_in,
            conv_state_in,
            bias_mixer_in,
            bias_state_in,
            step_bias_in,
            decay_in,
            skip_in,
            segment,
            min(SBLK, seq_len),
            SP,
        )

    gated_rows, pullback = jax.vjp(
        local_piece,
        mixer_proj,
        state_proj,
        step_proj,
        conv_mixer,
        conv_state,
        bias_mixer,
        bias_state,
        step_bias,
        decay_log,
        skip_gain,
    )
    square_sum = lax.psum(jnp.sum(gated_rows * gated_rows, axis=-1), "branch")
    gated_scale = lax.rsqrt(square_sum / (SH * SP) + EPSILON)[:, None]
    ssd_low = (gated_rows * gated_scale * ssd_gain).astype(jnp.bfloat16)
    mixer_sum = own_half_sum(
        (
            jnp.dot(attn_low, attn_output, preferred_element_type=jnp.float32)
            + jnp.dot(ssd_low, ssd_output, preferred_element_type=jnp.float32)
        ).astype(jnp.bfloat16),
        branch_pos,
    )
    hidden = own_rows + own_valid[:, None] * mixer_sum
    hidden_scale = rms_scale(hidden)
    hidden_hat = hidden * hidden_scale
    normed_ffn = (hidden_hat * ffn_gain).astype(jnp.bfloat16)
    upstream = cotangent[0]
    gate_vals = jnp.dot(normed_ffn, gate_weight, preferred_element_type=jnp.float32)
    up_vals = jnp.dot(normed_ffn, up_weight, preferred_element_type=jnp.float32)
    gate_sigmoid = jax.nn.sigmoid(gate_vals)
    act_low = (gate_vals * gate_sigmoid * up_vals).astype(jnp.bfloat16)
    ffn_out = jnp.dot(act_low, down_weight, preferred_element_type=jnp.float32)
    grad_act = jnp.einsum("rd,fd->rf", upstream, down_weight, preferred_element_type=jnp.float32)
    down_wgrad = jnp.einsum("rf,rd->fd", act_low, upstream, preferred_element_type=jnp.float32).astype(jnp.bfloat16)
    grad_gate = (
        grad_act * up_vals * gate_sigmoid * (1.0 + gate_vals * (1.0 - gate_sigmoid))
    ).astype(jnp.bfloat16)
    grad_up = (grad_act * gate_vals * gate_sigmoid).astype(jnp.bfloat16)
    gate_wgrad = jnp.einsum("rf,rd->fd", grad_gate, normed_ffn, preferred_element_type=jnp.float32).astype(jnp.bfloat16)
    up_wgrad = jnp.einsum("rf,rd->fd", grad_up, normed_ffn, preferred_element_type=jnp.float32).astype(jnp.bfloat16)
    grad_normed_ffn = jnp.einsum(
        "rf,df->rd", grad_gate, gate_weight, preferred_element_type=jnp.float32
    ) + jnp.einsum("rf,df->rd", grad_up, up_weight, preferred_element_type=jnp.float32)

    def owner_rows(partial):
        return partial.reshape((2 * row_count, -1) + partial.shape[1:])

    ffn_sums = [
        scatter_sum(owner_rows(item), all_digits, full_order)
        for item in (gate_wgrad, up_wgrad, down_wgrad)
    ]
    ffn_grads = (
        ffn_sums[0].astype(jnp.float32).T,
        ffn_sums[1].astype(jnp.float32).T,
        ffn_sums[2].astype(jnp.float32),
    )
    block_out = (hidden + ffn_out).astype(jnp.bfloat16)[None]
    grad_hidden = upstream.astype(jnp.float32) + rms_back(
        grad_normed_ffn, hidden, hidden_scale, ffn_gain
    )
    ffn_gain_grad = jnp.sum(grad_normed_ffn * hidden_hat, axis=0)
    grad_mixer = (own_valid[:, None] * grad_hidden).astype(jnp.bfloat16)
    full_grad_mixer = both_halves(grad_mixer, branch_pos)
    grad_attn = jnp.einsum(
        "sd,cd->sc", full_grad_mixer, attn_output, preferred_element_type=jnp.float32
    )
    grad_ssd = jnp.einsum(
        "sd,cd->sc", full_grad_mixer, ssd_output, preferred_element_type=jnp.float32
    )
    attn_out_wgrad = jnp.einsum(
        "sd,sc->dc", full_grad_mixer, attn_low, preferred_element_type=jnp.float32
    ).astype(jnp.bfloat16)
    ssd_out_wgrad = jnp.einsum(
        "sd,sc->dc", full_grad_mixer, ssd_low, preferred_element_type=jnp.float32
    ).astype(jnp.bfloat16)
    ssd_gain_wgrad = jnp.sum(grad_ssd * gated_rows * gated_scale, axis=0)
    weighted = grad_ssd * ssd_gain
    row_inner = lax.psum(jnp.sum(weighted * gated_rows, axis=-1), "branch")
    grad_gated = (
        gated_scale * weighted - gated_rows * gated_scale**3 * (row_inner / (SH * SP))[:, None]
    )
    (
        grad_mixer_proj,
        grad_state_proj,
        grad_step_proj,
        conv_mixer_wgrad,
        conv_state_wgrad,
        bias_mixer_wgrad,
        bias_state_wgrad,
        step_bias_wgrad,
        decay_log_wgrad,
        skip_gain_wgrad,
    ) = pullback(grad_gated)
    grad_attn_low = grad_attn.reshape(seq_len, local_keyval, group_size, HD).astype(jnp.bfloat16)
    grad_queries, grad_keys, grad_values = attend_backward(
        queries, key_rows, value_rows, grad_attn_low, log_sums, segment, block_rows
    )
    query_grad = (
        rotate(grad_queries.reshape(seq_len, local_query, HD), within, -1.0)
        .reshape(seq_len, -1)
        .astype(jnp.bfloat16)
    )
    keyval_grad = jnp.concatenate(
        [rotate(grad_keys, within, -1.0).reshape(seq_len, -1), grad_values.reshape(seq_len, -1)],
        axis=1,
    ).astype(jnp.bfloat16)
    mixer_grad = grad_mixer_proj.astype(jnp.bfloat16)
    step_grad = grad_step_proj.astype(jnp.bfloat16)
    partial_normed = (
        jnp.einsum("sc,dc->sd", query_grad, query_weight, preferred_element_type=jnp.float32)
        + jnp.einsum("sc,dc->sd", keyval_grad, keyval_flat, preferred_element_type=jnp.float32)
        + jnp.einsum("sc,dc->sd", mixer_grad, mixer_flat, preferred_element_type=jnp.float32)
        + jnp.einsum("sc,dc->sd", step_grad, step_weight, preferred_element_type=jnp.float32)
    )
    query_wgrad = jnp.einsum(
        "sd,sc->dc", full_normed, query_grad, preferred_element_type=jnp.float32
    )
    keyval_wgrad = jnp.einsum(
        "sd,sc->dc", full_normed, keyval_grad, preferred_element_type=jnp.float32
    ).reshape(keyval_weight.shape)
    mixer_wgrad = jnp.einsum(
        "sd,sc->dc", full_normed, mixer_grad, preferred_element_type=jnp.float32
    ).reshape(mixer_weight.shape)
    step_wgrad = jnp.einsum("sd,sc->dc", full_normed, step_grad, preferred_element_type=jnp.float32)
    state_low = grad_state_proj.astype(jnp.bfloat16)
    partial_normed = partial_normed + jnp.einsum(
        "sc,dc->sd", state_low, state_flat, preferred_element_type=jnp.float32
    )
    own_grad_normed = own_half_sum(partial_normed.astype(jnp.bfloat16), branch_pos)
    state_wgrad = jnp.einsum(
        "sd,sc->dc", full_normed, state_low, preferred_element_type=jnp.float32
    )
    input_grad = (grad_hidden + rms_back(own_grad_normed, own_rows, own_scale, norm_gain)).astype(
        jnp.bfloat16
    )[None]
    norm_gain_wgrad = jnp.sum(own_grad_normed * own_hat, axis=0)
    def row_sum(partial):
        low = partial.astype(jnp.bfloat16)
        return scatter_sum(
            low.reshape((row_count, -1) + low.shape[1:]), row_digits, upward
        ).astype(jnp.float32)

    query_sum = row_sum(query_wgrad)
    keyval_sum = row_sum(keyval_wgrad.reshape(model_dim, -1))
    mixer_wsum = row_sum(mixer_wgrad.reshape(model_dim, -1))
    step_sum = row_sum(step_wgrad)
    attn_out_sum = row_sum(attn_out_wgrad).T
    ssd_out_sum = row_sum(ssd_out_wgrad).T
    state_part = scatter_sum(
        owner_rows(state_wgrad.astype(jnp.bfloat16)), all_digits, full_order
    )
    state_sum = gather_all(state_part, all_digits, full_order[::-1]).astype(jnp.float32)
    local_heads = step_bias.shape[0]
    local_inner = bias_mixer.shape[0]

    def widen(head_values):
        full = jnp.zeros(head_values.shape[:-1] + (2 * head_values.shape[-1],), jnp.float32)
        return lax.dynamic_update_slice_in_dim(
            full, head_values, branch_pos * head_values.shape[-1], head_values.ndim - 1
        )

    small = [
        norm_gain_wgrad,
        ffn_gain_grad,
        conv_state_wgrad,
        bias_state_wgrad,
        widen(step_bias_wgrad),
        widen(decay_log_wgrad),
        widen(skip_gain_wgrad),
        widen(conv_mixer_wgrad),
        widen(bias_mixer_wgrad),
        widen(ssd_gain_wgrad),
    ]
    sizes = [item.size for item in small]
    flat = jnp.concatenate([item.reshape(-1) for item in small])
    unit = 2 * row_count * 128
    padded = -(-flat.shape[0] // unit) * unit
    flat = jnp.pad(flat, (0, padded - flat.shape[0]))
    flat_part = scatter_sum(flat.reshape(2 * row_count, -1, 128), all_digits, full_order)
    flat_sum = gather_all(flat_part, all_digits, full_order[::-1]).reshape(-1)
    sums = []
    begin = 0
    for item, size in zip(small, sizes):
        sums.append(flat_sum[begin : begin + size].reshape(item.shape))
        begin += size
    row_pos = lax.axis_index("rows")

    def own_columns(total):
        width = local_inner // row_count
        return lax.dynamic_slice_in_dim(
            total, branch_pos * local_inner + row_pos * width, width, total.ndim - 1
        )

    small_results = (
        sums[0],
        sums[1],
        state_sum.reshape(state_weight.shape),
        sums[2],
        sums[3],
        sums[4],
        sums[5],
        sums[6],
    )
    head_results = (
        query_sum,
        keyval_sum.reshape((-1,) + keyval_weight.shape[1:]),
        mixer_wsum.reshape((-1,) + mixer_weight.shape[1:]),
        step_sum,
        own_columns(sums[7]),
        own_columns(sums[8]),
        own_columns(sums[9]),
        attn_out_sum,
        ssd_out_sum,
    )
    return (
        block_out,
        input_grad,
        small_results[0],
        head_results[0],
        head_results[1],
        head_results[2],
        small_results[2],
        head_results[3],
        head_results[4],
        small_results[3],
        head_results[5],
        small_results[4],
        small_results[5],
        small_results[6],
        small_results[7],
        head_results[6],
        head_results[7],
        head_results[8],
        small_results[1],
        ffn_grads[0],
        ffn_grads[1],
        ffn_grads[2],
    )


def solution(mesh):
    in_specs = (
        P("rows", "branch", None),
        P("rows", None),
        P(),
        P(None, "branch"),
        P(None, None, "branch"),
        P(None, None, "branch"),
        P(),
        P(None, "branch"),
        P(None, "branch"),
        P(),
        P("branch"),
        P(),
        P("branch"),
        P("branch"),
        P("branch"),
        P("branch"),
        P("branch", None),
        P("branch", None),
        P(),
        P(),
        P(),
        P(),
        P("rows", "branch", None),
    )
    out_specs = (
        P("rows", "branch", None),
        P("rows", "branch", None),
        P(),
        P("rows", "branch"),
        P("rows", None, "branch"),
        P("rows", None, "branch"),
        P(),
        P("rows", "branch"),
        P(None, ("branch", "rows")),
        P(),
        P(("branch", "rows")),
        P(),
        P(),
        P(),
        P(),
        P(("branch", "rows")),
        P("branch", "rows"),
        P("branch", "rows"),
        P(),
        P(None, ("branch", "rows")),
        P(None, ("branch", "rows")),
        P(("branch", "rows"), None),
    )
    return jax.shard_map(
        per_device, mesh=mesh, in_specs=in_specs, out_specs=out_specs, check_vma=False
    )
```

```python
import functools

import jax
import jax.numpy as jnp
from jax import lax
from jax.experimental import pallas as pl
from jax.experimental.pallas import tpu as pltpu
from jax.sharding import PartitionSpec as P

HD = 64
SH = 24
SP = 64
BLOCK = 256
REACH = 512
EPSILON = 1e-05
ROPE_BASE = 100000000000.0
F32 = jnp.float32
BF16 = jnp.bfloat16
PRECISE = lax.Precision.HIGHEST


def mm(left, right, left_dim, right_dim):
    return lax.dot_general(
        left, right, (((left_dim,), (right_dim,)), ((), ())), preferred_element_type=F32
    )


def mm_exact(left, right):
    return jnp.dot(left, right, preferred_element_type=F32, precision=PRECISE)


def shift_right(prev, cur, amount):
    joined = jnp.concatenate([prev, cur], axis=1)
    return pltpu.roll(joined, amount, 1)[:, prev.shape[1] :]


def shift_left(cur, after, amount):
    joined = jnp.concatenate([cur, after], axis=1)
    total = joined.shape[1]
    return pltpu.roll(joined, total - amount, 1)[:, : cur.shape[1]]


def conv_rows(prev_ref, cur_ref, tap_ref, run_row, is_first):
    cur = cur_ref[...].astype(F32)
    prev = jnp.where(is_first, 0.0, prev_ref[...].astype(F32))
    taps = tap_ref[...]
    result = taps[:, 4:5] + taps[:, 3:4] * cur
    for offset in range(1, 4):
        keep = (run_row >= float(offset)).astype(F32)
        moved = shift_right(prev, cur, offset) * keep
        result = result + taps[:, 3 - offset : 4 - offset] * moved
    return result


def step_rows(step_ref, head_ref):
    raw = step_ref[...] + head_ref[:, 0:1]
    return raw, jax.nn.softplus(raw)


def masks_of(run_col, block):
    rows = lax.broadcasted_iota(jnp.int32, (block, block), 0)
    cols = lax.broadcasted_iota(jnp.int32, (block, block), 1)
    gap = (rows - cols).astype(F32)
    return (gap >= 0.0) & (gap <= run_col)


def upper_ones(block):
    rows = lax.broadcasted_iota(jnp.int32, (block, block), 0)
    cols = lax.broadcasted_iota(jnp.int32, (block, block), 1)
    return (rows <= cols).astype(F32)


def ssd_forward_kernel(
    block, heads, head_dim,
    z_ref, x_ref, xp_ref, b_ref, bp_ref, step_ref, run_ref, runc_ref, tapx_ref, tapb_ref, head_ref, skip_ref,
    gated_ref, entry_ref,
    state, xdt, yrow,
):
    index = pl.program_id(0)
    is_first = index == 0

    @pl.when(is_first)
    def _():
        state[...] = jnp.zeros_like(state)

    run_row = run_ref[0:1, :]
    act = conv_rows(xp_ref, x_ref, tapx_ref, run_row, is_first)
    act = act * jax.nn.sigmoid(act)
    vec = conv_rows(bp_ref, b_ref, tapb_ref, run_row, is_first)
    vec = vec * jax.nn.sigmoid(vec)
    size = vec.shape[0] // 2
    in_low = vec[:size].astype(BF16)
    out_low = vec[size:].astype(BF16)
    raw, step = step_rows(step_ref, head_ref)
    rate = head_ref[:, 1:2]
    cum = mm_exact(step * rate, upper_ones(block))
    cum_col = jnp.transpose(cum)
    place = lax.broadcasted_iota(jnp.int32, (1, block), 1).astype(F32)
    carried = (run_row >= place + 1.0).astype(F32)
    last_run = run_row[:, block - 1 :]
    tail = (float(block - 1) - place <= last_run).astype(F32)
    last = cum[:, block - 1 :]
    entry = jnp.exp(cum) * carried
    to_end = jnp.exp(last - cum) * tail
    keep = jnp.exp(last) * carried[:, block - 1 :]
    allowed = masks_of(runc_ref[:, 0:1], block)
    cross = jnp.where(allowed, mm(out_low, in_low, 0, 0), 0.0)
    old = state[...]
    old_low = old.astype(BF16)
    entry_ref[0] = old_low
    y_off = mm(old_low, out_low, 1, 0)
    for h in range(heads):
        rows = slice(h * head_dim, (h + 1) * head_dim)
        part = act[rows] * step[h : h + 1]
        part_low = part.astype(BF16)
        decay = jnp.exp(jnp.minimum(cum_col[:, h : h + 1] - cum[h : h + 1], 0.0))
        weight = (cross * decay).astype(BF16)
        y_in = mm(part_low, weight, 1, 1)
        yrow[rows] = y_in + y_off[rows] * entry[h : h + 1] + skip_ref[rows, 0:1] * act[rows]
        xdt[rows] = (part * to_end[h : h + 1]).astype(BF16)
        state[rows] = old[rows] * keep[h : h + 1]
    state[...] += mm(xdt[...], in_low, 1, 1)
    gate = z_ref[...].astype(F32)
    gated_ref[...] = (yrow[...] * gate * jax.nn.sigmoid(gate)).astype(gated_ref.dtype)


def ssd_backward_kernel(
    block, heads, head_dim,
    z_ref, x_ref, xp_ref, b_ref, bp_ref, step_ref, run_ref, runc_ref, tapx_ref, tapb_ref, head_ref, skip_ref,
    entry_ref, grad_ref, runn_ref,
    dm_ref, db_ref, dstep_ref, drate_ref, dtapx_ref, dtapb_ref, dskip_ref,
    dstate, nextx, nextb, accx, accb, accs, yrow, dact, xdt, dye, rowterm, colin, colst, direct, ystat,
):
    index = pl.program_id(0)
    count = pl.num_programs(0)
    is_first = index == count - 1

    @pl.when(index == 0)
    def _():
        dstate[...] = jnp.zeros_like(dstate)
        nextx[...] = jnp.zeros_like(nextx)
        nextb[...] = jnp.zeros_like(nextb)
        accx[...] = jnp.zeros_like(accx)
        accb[...] = jnp.zeros_like(accb)
        accs[...] = jnp.zeros_like(accs)
        rowterm[...] = jnp.zeros_like(rowterm)
        colin[...] = jnp.zeros_like(colin)
        colst[...] = jnp.zeros_like(colst)
        direct[...] = jnp.zeros_like(direct)
        ystat[...] = jnp.zeros_like(ystat)

    run_row = run_ref[0:1, :]
    convx = conv_rows(xp_ref, x_ref, tapx_ref, run_row, is_first)
    sigx = jax.nn.sigmoid(convx)
    act = convx * sigx
    convb = conv_rows(bp_ref, b_ref, tapb_ref, run_row, is_first)
    sigb = jax.nn.sigmoid(convb)
    vec = convb * sigb
    size = vec.shape[0] // 2
    in_low = vec[:size].astype(BF16)
    out_low = vec[size:].astype(BF16)
    raw, step = step_rows(step_ref, head_ref)
    rate = head_ref[:, 1:2]
    upper = upper_ones(block)
    cum = mm_exact(step * rate, upper)
    cum_col = jnp.transpose(cum)
    place = lax.broadcasted_iota(jnp.int32, (1, block), 1).astype(F32)
    carried = (run_row >= place + 1.0).astype(F32)
    last_run = run_row[:, block - 1 :]
    tail = (float(block - 1) - place <= last_run).astype(F32)
    last = cum[:, block - 1 :]
    entry = jnp.exp(cum) * carried
    to_end = jnp.exp(last - cum) * tail
    keep = jnp.exp(last) * carried[:, block - 1 :]
    allowed = masks_of(runc_ref[:, 0:1], block)
    cross = jnp.where(allowed, mm(out_low, in_low, 0, 0), 0.0)
    old_low = entry_ref[0]
    old = old_low.astype(F32)
    dnew = dstate[...]
    dnew_low = dnew.astype(BF16)
    y_off = mm(old_low, out_low, 1, 0)
    u_off = mm(dnew_low, in_low, 1, 0)
    gate = z_ref[...].astype(F32)
    sig = jax.nn.sigmoid(gate)
    upstream = grad_ref[...].astype(F32)
    dy = upstream * gate * sig
    dcross = jnp.zeros((block, block), F32)
    for h in range(heads):
        rows = slice(h * head_dim, (h + 1) * head_dim)
        one = slice(h, h + 1)
        xh = act[rows]
        part = xh * step[one]
        part_low = part.astype(BF16)
        dyh = dy[rows]
        dy_low = dyh.astype(BF16)
        decay = jnp.exp(jnp.minimum(cum_col[:, one] - cum[one], 0.0))
        weight = (cross * decay).astype(BF16)
        y_in = mm(part_low, weight, 1, 1)
        y_scan = y_in + y_off[rows] * entry[one]
        u_in = mm(dy_low, weight, 1, 0)
        u_st = u_off[rows] * to_end[one]
        dcross = dcross + mm(dy_low, part_low, 0, 0) * decay
        part_f = part_low.astype(F32)
        u_all = u_in + u_st
        rowterm[one] = jnp.sum(dy_low.astype(F32) * y_scan, axis=0, keepdims=True)
        colin[one] = jnp.sum(part_f * u_in, axis=0, keepdims=True)
        colst[one] = jnp.sum(part_f * u_st, axis=0, keepdims=True)
        direct[one] = jnp.sum(xh * u_all, axis=0, keepdims=True)
        skip = skip_ref[rows, 0:1]
        yrow[rows] = y_scan + skip * xh
        dact[rows] = step[one] * u_all + skip * dyh
        xdt[rows] = (part * to_end[one]).astype(BF16)
        dye[rows] = (dyh * entry[one]).astype(BF16)
        kept = jnp.sum(dnew[rows] * old[rows] * keep[one], axis=0, keepdims=True)
        ystat[one] = kept
        dstate[rows] = dnew[rows] * keep[one]
    dcross_low = jnp.where(allowed, dcross, 0.0).astype(BF16)
    dout = mm(in_low, dcross_low, 1, 1) + mm(old_low, dye[...], 0, 0)
    din = mm(out_low, dcross_low, 1, 0) + mm(dnew_low, xdt[...], 0, 0)
    dstate[...] += mm(dye[...], out_low, 1, 1)
    inner = upstream.shape[0]
    dm_ref[:inner] = (upstream * yrow[...] * sig * (1.0 + gate * (1.0 - sig))).astype(dm_ref.dtype)
    prod = dy * act
    accs[...] += sum(prod[:, c : c + 128] for c in range(0, block, 128))
    lower = jnp.transpose(upper)
    kept_total = jnp.sum(ystat[...], axis=1, keepdims=True)
    dlog = (
        mm_exact(rowterm[...] - colin[...], lower)
        + mm_exact(colst[...], upper)
        - colst[...]
        + kept_total
    )
    dstep = direct[...] + rate * dlog
    dstep_ref[...] = dstep * jax.nn.sigmoid(raw)
    drate_ref[...] = dlog * step

    def conv_back(dvals, conv, sigm, prev_ref, cur_ref, tap_ref, after, acc, out_ref):
        dconv = dvals * sigm * (1.0 + conv * (1.0 - sigm))
        taps = tap_ref[...]
        cur = cur_ref[...].astype(F32)
        prev = jnp.where(is_first, 0.0, prev_ref[...].astype(F32))
        result = taps[:, 3:4] * dconv
        acc[4] += sum(dconv[:, c : c + 128] for c in range(0, block, 128))
        prod = dconv * cur
        acc[3] += sum(prod[:, c : c + 128] for c in range(0, block, 128))
        following = after[...]
        for offset in range(1, 4):
            keep_cur = (run_row >= float(offset)).astype(F32)
            keep_next = (runn_ref[0:1, :] >= float(offset)).astype(F32)
            masked = dconv * keep_cur
            result = result + taps[:, 3 - offset : 4 - offset] * shift_left(
                masked, following * keep_next, offset
            )
            prod = masked * shift_right(prev, cur, offset)
            acc[3 - offset] += sum(prod[:, c : c + 128] for c in range(0, block, 128))
        after[...] = dconv[:, :128]
        out_ref[...] = result.astype(out_ref.dtype)

    conv_back(dact[...], convx, sigx, xp_ref, x_ref, tapx_ref, nextx, accx, dm_ref.at[inner:])
    conv_back(
        jnp.concatenate([din, dout], axis=0), convb, sigb, bp_ref, b_ref, tapb_ref, nextb, accb, db_ref
    )

    @pl.when(is_first)
    def _():
        def spread(acc, out_ref):
            lanes = lax.broadcasted_iota(jnp.int32, out_ref.shape, 1)
            result = jnp.zeros(out_ref.shape, F32)
            for item in range(5):
                total = jnp.sum(acc[item], axis=1, keepdims=True)
                result = jnp.where(lanes == item, total, result)
            out_ref[...] = result

        spread(accx, dtapx_ref)
        spread(accb, dtapb_ref)
        dskip_ref[...] = jnp.broadcast_to(
            jnp.sum(accs[...], axis=1, keepdims=True), dskip_ref.shape
        )


def ssd_specs(block, inner, vec, rows16, chunk_of):
    wide = lambda i: (0, chunk_of(i))
    per = block // 128
    before = lambda i: (0, jnp.maximum(chunk_of(i) * per - 1, 0))
    whole = lambda i: (0, 0)
    return [
        pl.BlockSpec((inner, block), wide),
        pl.BlockSpec((inner, block), lambda i: (1, chunk_of(i))),
        pl.BlockSpec((inner, 128), lambda i: (1, before(i)[1])),
        pl.BlockSpec((vec, block), wide),
        pl.BlockSpec((vec, 128), before),
        pl.BlockSpec((rows16, block), wide),
        pl.BlockSpec((8, block), wide),
        pl.BlockSpec((block, 128), lambda i: (chunk_of(i), 0)),
        pl.BlockSpec((inner, 128), whole),
        pl.BlockSpec((vec, 128), whole),
        pl.BlockSpec((rows16, 128), whole),
        pl.BlockSpec((inner, 128), whole),
    ]


def ssd_forward(mixer_t, vec_t, step_t, run8, run_col, tap_x, tap_b, head_cols, skip_col, heads, head_dim, block):
    inner = mixer_t.shape[0] // 2
    seq = mixer_t.shape[1]
    vec = vec_t.shape[0]
    rows16 = step_t.shape[0]
    chunks = seq // block
    state_dim = vec // 2
    return pl.pallas_call(
        functools.partial(ssd_forward_kernel, block, heads, head_dim),
        grid=(chunks,),
        in_specs=ssd_specs(block, inner, vec, rows16, lambda i: i),
        out_specs=[
            pl.BlockSpec((inner, block), lambda i: (0, i)),
            pl.BlockSpec((1, inner, state_dim), lambda i: (i, 0, 0)),
        ],
        out_shape=[
            jax.ShapeDtypeStruct((inner, seq), BF16),
            jax.ShapeDtypeStruct((chunks, inner, state_dim), BF16),
        ],
        scratch_shapes=[
            pltpu.VMEM((inner, state_dim), F32),
            pltpu.VMEM((inner, block), BF16),
            pltpu.VMEM((inner, block), F32),
        ],
        compiler_params=pltpu.CompilerParams(vmem_limit_bytes=48 << 20),
        cost_estimate=pl.CostEstimate(flops=10**9, bytes_accessed=10**7, transcendentals=10**7),
        name="ssd_forward",
    )(mixer_t, mixer_t, mixer_t, vec_t, vec_t, step_t, run8, run_col, tap_x, tap_b, head_cols, skip_col)


def ssd_backward(mixer_t, vec_t, step_t, run8, run_col, tap_x, tap_b, head_cols, skip_col, entry, grad_t, heads, head_dim, block):
    inner = mixer_t.shape[0] // 2
    seq = mixer_t.shape[1]
    vec = vec_t.shape[0]
    rows16 = step_t.shape[0]
    chunks = seq // block
    state_dim = vec // 2
    per = block // 128
    chunk_of = lambda i: chunks - 1 - i
    wide = lambda i: (0, chunk_of(i))
    whole = lambda i: (0, 0)
    return pl.pallas_call(
        functools.partial(ssd_backward_kernel, block, heads, head_dim),
        grid=(chunks,),
        in_specs=ssd_specs(block, inner, vec, rows16, chunk_of)
        + [
            pl.BlockSpec((1, inner, state_dim), lambda i: (chunk_of(i), 0, 0)),
            pl.BlockSpec((inner, block), wide),
            pl.BlockSpec((8, 128), lambda i: (0, jnp.minimum(chunk_of(i) * per + per, chunks * per - 1))),
        ],
        out_specs=[
            pl.BlockSpec((2 * inner, block), wide),
            pl.BlockSpec((vec, block), wide),
            pl.BlockSpec((rows16, block), wide),
            pl.BlockSpec((rows16, block), wide),
            pl.BlockSpec((inner, 128), whole),
            pl.BlockSpec((vec, 128), whole),
            pl.BlockSpec((inner, 128), whole),
        ],
        out_shape=[
            jax.ShapeDtypeStruct((2 * inner, seq), BF16),
            jax.ShapeDtypeStruct((vec, seq), BF16),
            jax.ShapeDtypeStruct((rows16, seq), F32),
            jax.ShapeDtypeStruct((rows16, seq), F32),
            jax.ShapeDtypeStruct((inner, 128), F32),
            jax.ShapeDtypeStruct((vec, 128), F32),
            jax.ShapeDtypeStruct((inner, 128), F32),
        ],
        scratch_shapes=[
            pltpu.VMEM((inner, state_dim), F32),
            pltpu.VMEM((inner, 128), F32),
            pltpu.VMEM((vec, 128), F32),
            pltpu.VMEM((5, inner, 128), F32),
            pltpu.VMEM((5, vec, 128), F32),
            pltpu.VMEM((inner, 128), F32),
            pltpu.VMEM((inner, block), F32),
            pltpu.VMEM((inner, block), F32),
            pltpu.VMEM((inner, block), BF16),
            pltpu.VMEM((inner, block), BF16),
            pltpu.VMEM((rows16, block), F32),
            pltpu.VMEM((rows16, block), F32),
            pltpu.VMEM((rows16, block), F32),
            pltpu.VMEM((rows16, block), F32),
            pltpu.VMEM((rows16, state_dim), F32),
        ],
        compiler_params=pltpu.CompilerParams(vmem_limit_bytes=48 << 20),
        cost_estimate=pl.CostEstimate(flops=3 * 10**9, bytes_accessed=2 * 10**7, transcendentals=3 * 10**7),
        name="ssd_backward",
    )(
        mixer_t, mixer_t, mixer_t, vec_t, vec_t, step_t, run8, run_col, tap_x, tap_b, head_cols, skip_col,
        entry, grad_t, run8,
    )


def rotate_rows(values, cosine, sine):
    half = values.shape[0] // 2
    first, second = values[:half], values[half:]
    return jnp.concatenate(
        [first * cosine - second * sine, second * cosine + first * sine], axis=0
    )


def window_of(block_index, block, reach):
    low = max(0, (block_index * block - (reach - 1)) // block)
    return low * block, (block_index + 1) * block


def allowed_of(run_ref, begin, stop, block):
    start, end = stop
    keys = lax.broadcasted_iota(jnp.int32, (end - start, block), 0) + start
    queries = lax.broadcasted_iota(jnp.int32, (end - start, block), 1) + begin
    gap = (queries - keys).astype(F32)
    return (gap >= 0.0) & (gap <= run_ref[0:1, begin : begin + block])


def attention_forward_kernel(
    heads, groups, head_dim, block, reach, scale,
    proj_ref, cos_ref, sin_ref, run_ref, out_ref, rot_ref, lse_ref,
):
    seq = proj_ref.shape[1]
    cosine, sine = cos_ref[...], sin_ref[...]
    total = heads + groups
    for item in range(total):
        rows = slice(item * head_dim, (item + 1) * head_dim)
        rot_ref[rows] = rotate_rows(proj_ref[rows].astype(F32), cosine, sine).astype(BF16)
    for index in range(seq // block):
        begin = index * block
        span = window_of(index, block, reach)
        allowed = allowed_of(run_ref, begin, span, block)
        for h in range(heads):
            group = h * groups // heads
            rows = slice(h * head_dim, (h + 1) * head_dim)
            krows = slice((heads + group) * head_dim, (heads + group + 1) * head_dim)
            vrows = slice((heads + groups + group) * head_dim, (heads + groups + group + 1) * head_dim)
            query = rot_ref[rows, begin : begin + block]
            key = rot_ref[krows, span[0] : span[1]]
            value = proj_ref[vrows, span[0] : span[1]].astype(BF16)
            logits = jnp.where(allowed, mm(key, query, 0, 0) * scale, -1e30)
            peak = jnp.max(logits, axis=0, keepdims=True)
            powered = jnp.exp(logits - peak)
            mass = jnp.sum(powered, axis=0, keepdims=True)
            probs = (powered * (1.0 / mass)).astype(BF16)
            out_ref[rows, begin : begin + block] = mm(value, probs, 1, 0).astype(out_ref.dtype)
            lse_ref[h : h + 1, begin : begin + block] = peak + jnp.log(mass)


def attention_backward_kernel(
    heads, groups, head_dim, block, reach, scale,
    proj_ref, rot_ref, cos_ref, sin_ref, run_ref, lse_ref, out_in_ref, grad_ref, back_ref,
    acc_key, acc_value,
):
    seq = proj_ref.shape[1]
    acc_key[...] = jnp.zeros_like(acc_key)
    acc_value[...] = jnp.zeros_like(acc_value)
    for index in range(seq // block):
        begin = index * block
        span = window_of(index, block, reach)
        allowed = allowed_of(run_ref, begin, span, block)
        cosine, sine = cos_ref[:, begin : begin + block], sin_ref[:, begin : begin + block]
        for h in range(heads):
            group = h * groups // heads
            rows = slice(h * head_dim, (h + 1) * head_dim)
            krows = slice((heads + group) * head_dim, (heads + group + 1) * head_dim)
            vrows = slice((heads + groups + group) * head_dim, (heads + groups + group + 1) * head_dim)
            grows = slice(group * head_dim, (group + 1) * head_dim)
            query = rot_ref[rows, begin : begin + block]
            key = rot_ref[krows, span[0] : span[1]]
            value = proj_ref[vrows, span[0] : span[1]].astype(BF16)
            grad = grad_ref[rows, begin : begin + block]
            logits = jnp.where(allowed, mm(key, query, 0, 0) * scale, -1e30)
            probs = jnp.exp(logits - lse_ref[h : h + 1, begin : begin + block])
            dprobs = mm(value, grad, 0, 0)
            centre = jnp.sum(probs * dprobs, axis=0, keepdims=True)
            dscore = (probs * (dprobs - centre) * scale).astype(BF16)
            dquery = mm(key, dscore, 1, 0)
            back_ref[rows, begin : begin + block] = rotate_rows(dquery, cosine, -sine).astype(BF16)
            acc_key[grows, span[0] : span[1]] += mm(query, dscore, 1, 1)
            acc_value[grows, span[0] : span[1]] += mm(grad, probs.astype(BF16), 1, 1)
    for group in range(groups):
        grows = slice(group * head_dim, (group + 1) * head_dim)
        krows = slice((heads + group) * head_dim, (heads + group + 1) * head_dim)
        vrows = slice((heads + groups + group) * head_dim, (heads + groups + group + 1) * head_dim)
        back_ref[krows] = rotate_rows(acc_key[grows], cos_ref[...], -sin_ref[...]).astype(BF16)
        back_ref[vrows] = acc_value[grows].astype(BF16)


def attention_forward(proj_t, cosine, sine, run8, heads, groups, head_dim, block, reach):
    seq = proj_t.shape[1]
    return pl.pallas_call(
        functools.partial(attention_forward_kernel, heads, groups, head_dim, block, reach, head_dim**-0.5),
        out_shape=[
            jax.ShapeDtypeStruct((heads * head_dim, seq), BF16),
            jax.ShapeDtypeStruct(((heads + groups) * head_dim, seq), BF16),
            jax.ShapeDtypeStruct((max(heads, 8), seq), F32),
        ],
        compiler_params=pltpu.CompilerParams(vmem_limit_bytes=48 << 20),
        cost_estimate=pl.CostEstimate(flops=2 * 10**9, bytes_accessed=10**7, transcendentals=4 * 10**6),
        name="attention_forward",
    )(proj_t, cosine, sine, run8)


def attention_backward(proj_t, rot_t, cosine, sine, run8, lse, out_t, grad_t, heads, groups, head_dim, block, reach):
    seq = proj_t.shape[1]
    return pl.pallas_call(
        functools.partial(attention_backward_kernel, heads, groups, head_dim, block, reach, head_dim**-0.5),
        out_shape=jax.ShapeDtypeStruct(proj_t.shape, BF16),
        scratch_shapes=[
            pltpu.VMEM((groups * head_dim, seq), F32),
            pltpu.VMEM((groups * head_dim, seq), F32),
        ],
        compiler_params=pltpu.CompilerParams(vmem_limit_bytes=48 << 20),
        cost_estimate=pl.CostEstimate(flops=5 * 10**9, bytes_accessed=10**7, transcendentals=4 * 10**6),
        name="attention_backward",
    )(proj_t, rot_t, cosine, sine, run8, lse, out_t, grad_t)


def ffn_kernel(norm_ref, cot_ref, gate_ref, up_ref, down_ref, out_ref, back_ref, act_ref, dgate_ref, dup_ref):
    @pl.when(pl.program_id(0) == 0)
    def _():
        out_ref[...] = jnp.zeros_like(out_ref)
        back_ref[...] = jnp.zeros_like(back_ref)

    normed, cot = norm_ref[...], cot_ref[...]
    gate_w, up_w, down_w = gate_ref[...], up_ref[...], down_ref[...]
    gate = mm(normed, gate_w, 1, 0)
    up = mm(normed, up_w, 1, 0)
    grad_act = mm(cot, down_w, 1, 1)
    sig = jax.nn.sigmoid(gate)
    silu = gate * sig
    act = (silu * up).astype(BF16)
    dgate = (grad_act * up * sig * (1.0 + gate * (1.0 - sig))).astype(BF16)
    dup = (grad_act * silu).astype(BF16)
    act_ref[...] = act
    dgate_ref[...] = dgate
    dup_ref[...] = dup
    out_ref[...] += mm(act, down_w, 1, 0)
    back_ref[...] += mm(dgate, gate_w, 1, 1) + mm(dup, up_w, 1, 1)


def feed_forward(normed, cot, gate_w, up_w, down_w, tile):
    rows, width = normed.shape
    hidden = gate_w.shape[1]
    whole = lambda i: (0, 0)
    return pl.pallas_call(
        ffn_kernel,
        grid=(hidden // tile,),
        in_specs=[
            pl.BlockSpec((rows, width), whole),
            pl.BlockSpec((rows, width), whole),
            pl.BlockSpec((width, tile), lambda i: (0, i)),
            pl.BlockSpec((width, tile), lambda i: (0, i)),
            pl.BlockSpec((tile, width), lambda i: (i, 0)),
        ],
        out_specs=[
            pl.BlockSpec((rows, width), whole),
            pl.BlockSpec((rows, width), whole),
            pl.BlockSpec((rows, tile), lambda i: (0, i)),
            pl.BlockSpec((rows, tile), lambda i: (0, i)),
            pl.BlockSpec((rows, tile), lambda i: (0, i)),
        ],
        out_shape=[
            jax.ShapeDtypeStruct((rows, width), F32),
            jax.ShapeDtypeStruct((rows, width), F32),
            jax.ShapeDtypeStruct((rows, hidden), BF16),
            jax.ShapeDtypeStruct((rows, hidden), BF16),
            jax.ShapeDtypeStruct((rows, hidden), BF16),
        ],
        compiler_params=pltpu.CompilerParams(vmem_limit_bytes=48 << 20),
        cost_estimate=pl.CostEstimate(flops=6 * 2 * rows * width * hidden, bytes_accessed=3 * 10**7, transcendentals=rows * hidden),
        name="feed_forward",
    )(normed, cot, gate_w, up_w, down_w)


def ffn_wgrad_kernel(norm_ref, cot_ref, act_ref, dgate_ref, dup_ref, gate_ref, up_ref, down_ref):
    normed, cot = norm_ref[...], cot_ref[...]
    gate_ref[...] = mm(dgate_ref[...], normed, 0, 0).astype(BF16)
    up_ref[...] = mm(dup_ref[...], normed, 0, 0).astype(BF16)
    down_ref[...] = mm(act_ref[...], cot, 0, 0).astype(BF16)


def ffn_wgrads(normed, cot, act, dgate, dup, tile):
    rows, width = normed.shape
    hidden = act.shape[1]
    whole = lambda i: (0, 0)
    return pl.pallas_call(
        ffn_wgrad_kernel,
        grid=(hidden // tile,),
        in_specs=[pl.BlockSpec((rows, width), whole)] * 2
        + [pl.BlockSpec((rows, tile), lambda i: (0, i))] * 3,
        out_specs=[pl.BlockSpec((tile, width), lambda i: (i, 0))] * 3,
        out_shape=[jax.ShapeDtypeStruct((hidden, width), BF16)] * 3,
        compiler_params=pltpu.CompilerParams(vmem_limit_bytes=48 << 20),
        cost_estimate=pl.CostEstimate(flops=3 * 2 * rows * width * hidden, bytes_accessed=2 * 10**7, transcendentals=0),
        name="ffn_wgrads",
    )(normed, cot, act, dgate, dup)


def bits_of(count):
    return count.bit_length() - 1


def swap_halves(values, axis_name, bit, size):
    pairs = [(item, item ^ (1 << bit)) for item in range(size)]
    return lax.ppermute(values, axis_name, pairs)


def halve(values, place, my_bit, axis_name, bit, size):
    owners = values.shape[0]
    high = 1 << place
    parts = values.reshape((high, 2, owners // (2 * high)) + values.shape[1:])
    sent = lax.dynamic_index_in_dim(parts, 1 - my_bit, 1, keepdims=False)
    kept = lax.dynamic_index_in_dim(parts, my_bit, 1, keepdims=False)
    got = swap_halves(sent, axis_name, bit, size)
    total = (kept.astype(jnp.float32) + got.astype(jnp.float32)).astype(values.dtype)
    return total.reshape((owners // 2,) + values.shape[1:])


def scatter_sum(values, digits, order):
    left = list(digits)
    for digit in order:
        axis_name, bit, size = digit
        my_bit = (lax.axis_index(axis_name) >> bit) & 1
        values = halve(values, left.index(digit), my_bit, axis_name, bit, size)
        left.remove(digit)
    return values[0]


def gather_all(values, digits, order):
    values = values[None]
    left = []
    for digit in order:
        axis_name, bit, size = digit
        my_bit = (lax.axis_index(axis_name) >> bit) & 1
        got = swap_halves(values, axis_name, bit, size)
        place = sum(1 for item in left if digits.index(item) < digits.index(digit))
        high = 1 << place
        owners = values.shape[0]
        mine = values.reshape((high, 1, owners // high) + values.shape[1:])
        other = got.reshape(mine.shape)
        first = jnp.where(my_bit == 0, mine, other)
        second = jnp.where(my_bit == 0, other, mine)
        values = jnp.concatenate([first, second], axis=1).reshape((owners * 2,) + values.shape[1:])
        left.append(digit)
    return values


def other_branch(values):
    return lax.ppermute(values, "branch", [(0, 1), (1, 0)])


def rms_scale(values):
    return lax.rsqrt(jnp.mean(values * values, axis=-1, keepdims=True) + EPSILON)


def rms_back(upstream, values, scales, gain):
    weighted = upstream * gain
    return scales * weighted - values * scales**3 * jnp.mean(
        weighted * values, axis=-1, keepdims=True
    )


def token_runs(length_row, seq_len, doc_count):
    order = jnp.arange(doc_count, dtype=jnp.int32)
    ends = jnp.sum(jnp.where(order[:, None] >= order[None, :], length_row[None, :], 0), axis=1)
    places = jnp.arange(seq_len, dtype=jnp.int32)
    passed = places[:, None] >= ends[None, :]
    starts = jnp.sum(jnp.where(passed, length_row[None, :], 0), axis=1)
    return (places - starts).astype(F32), jnp.sum(length_row)


def join(mine, other, branch_pos, axis):
    return jnp.concatenate(
        [jnp.where(branch_pos == 0, mine, other), jnp.where(branch_pos == 0, other, mine)], axis=axis
    )


def columns_of(items, rows):
    stacked = jnp.stack(items, axis=1)
    return jnp.pad(stacked, ((0, rows - stacked.shape[0]), (0, 128 - stacked.shape[1])))


def per_device(
    inputs,
    lengths,
    norm_gain,
    query_weight,
    keyval_weight,
    mixer_weight,
    state_weight,
    step_weight,
    conv_mixer,
    conv_state,
    bias_mixer,
    bias_state,
    step_bias,
    decay_log,
    skip_gain,
    ssd_gain,
    attn_output,
    ssd_output,
    ffn_gain,
    gate_weight,
    up_weight,
    down_weight,
    cotangent,
):
    branch_pos = lax.axis_index("branch")
    row_pos = lax.axis_index("rows")
    row_count = lax.axis_size("rows")
    row_bits = bits_of(row_count)
    row_digits = [("rows", bit, row_count) for bit in range(row_bits - 1, -1, -1)]
    branch_digit = ("branch", 0, 2)
    all_digits = [branch_digit] + row_digits
    upward = row_digits[::-1]
    turned = upward[:1] + upward[2:] + upward[1:2]
    order_a = upward + [branch_digit]
    order_b = turned + [branch_digit]
    order_c = upward[:1] + [branch_digit] + upward[1:]

    own_rows = inputs[0].astype(F32)
    upstream = cotangent[0]
    half_len, model_dim = own_rows.shape
    seq_len = 2 * half_len
    local_query = query_weight.shape[1] // HD
    local_keyval = keyval_weight.shape[2] // HD
    local_heads = step_bias.shape[0]
    local_inner = bias_mixer.shape[0]
    inner_dim = 2 * local_inner
    head_rows = -(-local_heads // 8) * 8
    own_begin = branch_pos * half_len

    run, used = token_runs(lengths[0], seq_len, lengths.shape[1])
    run8 = jnp.broadcast_to(run[None, :], (8, seq_len))
    run_col = jnp.broadcast_to(run[:, None], (seq_len, 128))
    frequency = ROPE_BASE ** (-(jnp.arange(HD // 2, dtype=F32) * 2.0) / HD)
    angles = frequency[:, None] * run[None, :]
    cosine, sine = jnp.cos(angles), jnp.sin(angles)
    own_valid = (own_begin + jnp.arange(half_len, dtype=jnp.int32) < used).astype(F32)[:, None]

    own_scale = rms_scale(own_rows)
    own_hat = own_rows * own_scale
    normed = (own_hat * norm_gain).astype(BF16)
    full_normed = join(normed, other_branch(normed), branch_pos, 0)

    qkv_flat = jnp.concatenate([query_weight, keyval_weight.reshape(model_dim, -1)], axis=1)
    mixer_flat = mixer_weight.reshape(model_dim, -1)
    state_flat = state_weight.reshape(model_dim, -1)
    step_flat = jnp.pad(step_weight, ((0, 0), (0, head_rows - local_heads)))

    mixer_t = mm(mixer_flat, full_normed, 0, 1).astype(BF16)
    vec_t = mm(state_flat, full_normed, 0, 1).astype(BF16)
    qkv_t = mm(qkv_flat, full_normed, 0, 1).astype(BF16)
    step_t = mm(step_flat, full_normed, 0, 1)

    taps = [conv_mixer[item] for item in range(4)] + [bias_mixer]
    tap_x = columns_of(taps, local_inner)
    state_taps = [conv_state[item].reshape(-1) for item in range(4)] + [bias_state.reshape(-1)]
    tap_b = columns_of(state_taps, state_flat.shape[1])
    rates = -jnp.exp(decay_log)
    head_cols = columns_of([step_bias, rates], head_rows)
    skip_col = jnp.broadcast_to(jnp.repeat(skip_gain, SP)[:, None], (local_inner, 128))
    ssd_args = (mixer_t, vec_t, step_t, run8, run_col, tap_x, tap_b, head_cols, skip_col)

    gated_t, entry = ssd_forward(*ssd_args, local_heads, SP, BLOCK)
    attn_t, rot_t, log_sums = attention_forward(
        qkv_t, cosine, sine, run8, local_query, local_keyval, HD, BLOCK, REACH
    )

    def own_tokens(values, pos):
        return lax.dynamic_slice_in_dim(values, pos * half_len, half_len, 1)

    def to_owner(values):
        got = other_branch(own_tokens(values, 1 - branch_pos))
        return join(own_tokens(values, branch_pos), got, branch_pos, 0)

    def own_channels(values, pos):
        size = values.shape[0] // 2
        return lax.dynamic_slice_in_dim(values, pos * size, size, 0)

    def to_heads(values):
        got = other_branch(own_channels(values, 1 - branch_pos))
        return join(own_channels(values, branch_pos), got, branch_pos, 1)

    all_gated = to_owner(gated_t)
    all_attn = to_owner(attn_t)
    attn_full = join(attn_output, other_branch(attn_output), branch_pos, 0)
    ssd_full = join(ssd_output, other_branch(ssd_output), branch_pos, 0)
    gain_full = join(ssd_gain, other_branch(ssd_gain), branch_pos, 0)[:, None]

    gated = all_gated.astype(F32)
    gated_scale = lax.rsqrt(jnp.mean(gated * gated, axis=0, keepdims=True) + EPSILON)
    ssd_low = (gated * gated_scale * gain_full).astype(BF16)
    mixer_sum = mm(all_attn, attn_full, 0, 0) + mm(ssd_low, ssd_full, 0, 0)
    hidden = own_rows + own_valid * mixer_sum
    hidden_scale = rms_scale(hidden)
    hidden_hat = hidden * hidden_scale
    normed_ffn = (hidden_hat * ffn_gain).astype(BF16)

    ffn_out, grad_normed_ffn, act_low, grad_gate, grad_up = feed_forward(
        normed_ffn, upstream, gate_weight, up_weight, down_weight, 256
    )
    block_out = (hidden + ffn_out).astype(BF16)[None]
    grad_hidden = upstream.astype(F32) + rms_back(grad_normed_ffn, hidden, hidden_scale, ffn_gain)
    ffn_gain_grad = jnp.sum(grad_normed_ffn * hidden_hat, axis=0)
    grad_mixer = (own_valid * grad_hidden).astype(BF16)

    grad_attn = mm(attn_full, grad_mixer, 1, 1).astype(BF16)
    grad_ssd = mm(ssd_full, grad_mixer, 1, 1)
    ssd_gain_wgrad = jnp.sum(grad_ssd * gated * gated_scale, axis=1)
    weighted = grad_ssd * gain_full
    row_inner = jnp.mean(weighted * gated, axis=0, keepdims=True)
    grad_gated = (gated_scale * weighted - gated * gated_scale**3 * row_inner).astype(BF16)
    head_gated = to_heads(grad_gated)
    head_attn = to_heads(grad_attn)

    gate_wgrad, up_wgrad, down_wgrad = ffn_wgrads(
        normed_ffn, upstream, act_low, grad_gate, grad_up, 512
    )

    def owner_rows(partial):
        return partial.reshape((2 * row_count, -1) + partial.shape[1:])

    ffn_sums = [
        scatter_sum(owner_rows(item), all_digits, order)
        for item, order in ((gate_wgrad, order_a), (up_wgrad, order_b), (down_wgrad, order_c))
    ]
    ffn_grads = (
        ffn_sums[0].astype(F32).T,
        ffn_sums[1].astype(F32).T,
        ffn_sums[2].astype(F32),
    )

    def out_wgrad(channels, order):
        parts = [
            mm(grad_mixer, own_channels(channels, pos), 0, 1).astype(BF16) for pos in (0, 1)
        ]
        stacked = jnp.stack(parts)
        return scatter_sum(owner_rows(stacked.reshape((-1,) + stacked.shape[2:])), all_digits, order)

    attn_out_sum = out_wgrad(all_attn, order_a).astype(F32).T
    ssd_out_sum = out_wgrad(ssd_low, order_b).astype(F32).T

    dmixer_t, dvec_t, dstep_t, dlog_t, dtap_x, dtap_b, dskip = ssd_backward(
        *ssd_args, entry, head_gated, local_heads, SP, BLOCK
    )
    dqkv_t = attention_backward(
        qkv_t, rot_t, cosine, sine, run8, log_sums, attn_t, head_attn, local_query, local_keyval, HD, BLOCK, REACH
    )
    dstep_low = dstep_t.astype(BF16)

    partial_normed = (
        mm(dmixer_t, mixer_flat, 0, 1)
        + mm(dvec_t, state_flat, 0, 1)
        + mm(dqkv_t, qkv_flat, 0, 1)
        + mm(dstep_low, step_flat, 0, 1)
    ).astype(BF16)
    sent = lax.dynamic_slice_in_dim(partial_normed, (1 - branch_pos) * half_len, half_len, 0)
    kept = lax.dynamic_slice_in_dim(partial_normed, own_begin, half_len, 0)
    own_grad_normed = kept.astype(F32) + other_branch(sent).astype(F32)
    input_grad = (grad_hidden + rms_back(own_grad_normed, own_rows, own_scale, norm_gain)).astype(
        BF16
    )[None]
    norm_gain_wgrad = jnp.sum(own_grad_normed * own_hat, axis=0)

    def row_sum(partial, order):
        return scatter_sum(
            partial.reshape((row_count, -1) + partial.shape[1:]), row_digits, order
        ).astype(F32)

    def weight_grad(grads_t):
        return mm(full_normed, grads_t, 0, 1).astype(BF16)

    state_part = scatter_sum(owner_rows(weight_grad(dvec_t)), all_digits, order_c)
    state_sum = gather_all(state_part, all_digits, order_c[::-1]).astype(F32)
    gate_sum = row_sum(weight_grad(dmixer_t[:local_inner]), upward)
    mixer_in_sum = row_sum(weight_grad(dmixer_t[local_inner:]), turned)
    qkvs_sum = row_sum(weight_grad(jnp.concatenate([dqkv_t, dstep_low], axis=0)), upward)
    query_cols = local_query * HD
    qkv_cols = dqkv_t.shape[0]
    query_sum = qkvs_sum[:, :query_cols]
    keyval_sum = qkvs_sum[:, query_cols:qkv_cols].reshape((-1,) + keyval_weight.shape[1:])
    step_sum = qkvs_sum[:, qkv_cols : qkv_cols + local_heads]
    mixer_wsum = jnp.stack([gate_sum, mixer_in_sum], axis=1)

    def widen(values):
        full = jnp.zeros(values.shape[:-1] + (2 * values.shape[-1],), F32)
        return lax.dynamic_update_slice_in_dim(
            full, values, branch_pos * values.shape[-1], values.ndim - 1
        )

    heads = slice(0, local_heads)
    small = [
        norm_gain_wgrad,
        ffn_gain_grad,
        dtap_b[:, :4].T,
        dtap_b[:, 4],
        widen(jnp.sum(dstep_t[heads], axis=1)),
        widen(jnp.sum(dlog_t[heads], axis=1) * rates),
        widen(jnp.sum(dskip[:, 0].reshape(local_heads, SP), axis=1)),
        widen(dtap_x[:, :4].T),
        widen(dtap_x[:, 4]),
        ssd_gain_wgrad,
    ]
    flat = jnp.concatenate([item.reshape(-1) for item in small])
    unit = 2 * row_count * 128
    padded = -(-flat.shape[0] // unit) * unit
    flat = jnp.pad(flat, (0, padded - flat.shape[0]))
    flat_part = scatter_sum(flat.reshape(2 * row_count, -1, 128), all_digits, order_c)
    flat_sum = gather_all(flat_part, all_digits, order_c[::-1]).reshape(-1)
    sums = []
    begin = 0
    for item in small:
        sums.append(flat_sum[begin : begin + item.size].reshape(item.shape))
        begin += item.size

    def own_columns(total):
        width = local_inner // row_count
        return lax.dynamic_slice_in_dim(
            total, branch_pos * local_inner + row_pos * width, width, total.ndim - 1
        )

    return (
        block_out,
        input_grad,
        sums[0],
        query_sum,
        keyval_sum,
        mixer_wsum.reshape((-1,) + mixer_weight.shape[1:]),
        state_sum.reshape(state_weight.shape),
        step_sum,
        own_columns(sums[7]),
        sums[2].reshape(conv_state.shape),
        own_columns(sums[8]),
        sums[3].reshape(bias_state.shape),
        sums[4],
        sums[5],
        sums[6],
        own_columns(sums[9]),
        attn_out_sum,
        ssd_out_sum,
        sums[1],
        ffn_grads[0],
        ffn_grads[1],
        ffn_grads[2],
    )


def solution(mesh):
    in_specs = (
        P("rows", "branch", None),
        P("rows", None),
        P(),
        P(None, "branch"),
        P(None, None, "branch"),
        P(None, None, "branch"),
        P(),
        P(None, "branch"),
        P(None, "branch"),
        P(),
        P("branch"),
        P(),
        P("branch"),
        P("branch"),
        P("branch"),
        P("branch"),
        P("branch", None),
        P("branch", None),
        P(),
        P(),
        P(),
        P(),
        P("rows", "branch", None),
    )
    out_specs = (
        P("rows", "branch", None),
        P("rows", "branch", None),
        P(),
        P("rows", "branch"),
        P("rows", None, "branch"),
        P("rows", None, "branch"),
        P(),
        P("rows", "branch"),
        P(None, ("branch", "rows")),
        P(),
        P(("branch", "rows")),
        P(),
        P(),
        P(),
        P(),
        P(("branch", "rows")),
        P("branch", "rows"),
        P("branch", "rows"),
        P(),
        P(None, ("branch", "rows")),
        P(None, ("branch", "rows")),
        P(("branch", "rows"), None),
    )
    return jax.shard_map(
        per_device, mesh=mesh, in_specs=in_specs, out_specs=out_specs, check_vma=False
    )
```

```python
import functools

import jax
import jax.numpy as jnp
from jax import lax
from jax.experimental import pallas as pl
from jax.experimental.pallas import tpu as pltpu
from jax.sharding import PartitionSpec as P

HD = 64
SH = 24
SP = 64
BLOCK = 256
REACH = 512
EPSILON = 1e-05
ROPE_BASE = 100000000000.0
F32 = jnp.float32
BF16 = jnp.bfloat16
PRECISE = lax.Precision.HIGHEST


def mm(left, right, left_dim, right_dim):
    return lax.dot_general(
        left, right, (((left_dim,), (right_dim,)), ((), ())), preferred_element_type=F32
    )


def mm_exact(left, right):
    return jnp.dot(left, right, preferred_element_type=F32, precision=PRECISE)


def shift_right(prev, cur, amount):
    joined = jnp.concatenate([prev, cur], axis=1)
    return pltpu.roll(joined, amount, 1)[:, prev.shape[1] :]


def shift_left(cur, after, amount):
    joined = jnp.concatenate([cur, after], axis=1)
    total = joined.shape[1]
    return pltpu.roll(joined, total - amount, 1)[:, : cur.shape[1]]


def conv_rows(prev_ref, cur_ref, tap_ref, run_row, is_first):
    cur = cur_ref[...].astype(F32)
    prev = jnp.where(is_first, 0.0, prev_ref[...].astype(F32))
    taps = tap_ref[...]
    result = taps[:, 4:5] + taps[:, 3:4] * cur
    for offset in range(1, 4):
        keep = (run_row >= float(offset)).astype(F32)
        moved = shift_right(prev, cur, offset) * keep
        result = result + taps[:, 3 - offset : 4 - offset] * moved
    return result


def step_rows(step_ref, head_ref):
    raw = step_ref[...] + head_ref[:, 0:1]
    return raw, jax.nn.softplus(raw)


def masks_of(run_col, block):
    rows = lax.broadcasted_iota(jnp.int32, (block, block), 0)
    cols = lax.broadcasted_iota(jnp.int32, (block, block), 1)
    gap = (rows - cols).astype(F32)
    return (gap >= 0.0) & (gap <= run_col)


def upper_ones(block):
    rows = lax.broadcasted_iota(jnp.int32, (block, block), 0)
    cols = lax.broadcasted_iota(jnp.int32, (block, block), 1)
    return (rows <= cols).astype(F32)


def ssd_forward_kernel(
    block, heads, head_dim,
    z_ref, x_ref, xp_ref, b_ref, bp_ref, step_ref, run_ref, runc_ref, tapx_ref, tapb_ref, head_ref, skip_ref,
    gated_ref, entry_ref,
    state, xdt, yrow,
):
    index = pl.program_id(0)
    is_first = index == 0

    @pl.when(is_first)
    def _():
        state[...] = jnp.zeros_like(state)

    run_row = run_ref[0:1, :]
    act = conv_rows(xp_ref, x_ref, tapx_ref, run_row, is_first)
    act = act * jax.nn.sigmoid(act)
    vec = conv_rows(bp_ref, b_ref, tapb_ref, run_row, is_first)
    vec = vec * jax.nn.sigmoid(vec)
    size = vec.shape[0] // 2
    in_low = vec[:size].astype(BF16)
    out_low = vec[size:].astype(BF16)
    raw, step = step_rows(step_ref, head_ref)
    rate = head_ref[:, 1:2]
    cum = mm_exact(step * rate, upper_ones(block))
    cum_col = jnp.transpose(cum)
    place = lax.broadcasted_iota(jnp.int32, (1, block), 1).astype(F32)
    carried = (run_row >= place + 1.0).astype(F32)
    last_run = run_row[:, block - 1 :]
    tail = (float(block - 1) - place <= last_run).astype(F32)
    last = cum[:, block - 1 :]
    entry = jnp.exp(cum) * carried
    to_end = jnp.exp(last - cum) * tail
    keep = jnp.exp(last) * carried[:, block - 1 :]
    allowed = masks_of(runc_ref[:, 0:1], block)
    cross = jnp.where(allowed, mm(out_low, in_low, 0, 0), 0.0)
    old = state[...]
    old_low = old.astype(BF16)
    entry_ref[0] = old_low
    y_off = mm(old_low, out_low, 1, 0)
    for h in range(heads):
        rows = slice(h * head_dim, (h + 1) * head_dim)
        part = act[rows] * step[h : h + 1]
        part_low = part.astype(BF16)
        decay = jnp.exp(jnp.minimum(cum_col[:, h : h + 1] - cum[h : h + 1], 0.0))
        weight = (cross * decay).astype(BF16)
        y_in = mm(part_low, weight, 1, 1)
        yrow[rows] = y_in + y_off[rows] * entry[h : h + 1] + skip_ref[rows, 0:1] * act[rows]
        xdt[rows] = (part * to_end[h : h + 1]).astype(BF16)
        state[rows] = old[rows] * keep[h : h + 1]
    state[...] += mm(xdt[...], in_low, 1, 1)
    gate = z_ref[...].astype(F32)
    gated_ref[...] = (yrow[...] * gate * jax.nn.sigmoid(gate)).astype(gated_ref.dtype)


def ssd_backward_kernel(block, heads, head_dim, *refs):
    ssd_backward_body(
        block, heads, head_dim, pl.program_id(0), pl.num_programs(0), lambda h: None, *refs
    )


def ssd_backward_body(
    block, heads, head_dim, index, count, hook,
    z_ref, x_ref, xp_ref, b_ref, bp_ref, step_ref, run_ref, runc_ref, tapx_ref, tapb_ref, head_ref, skip_ref,
    entry_ref, grad_ref, runn_ref,
    dm_ref, db_ref, dstep_ref, drate_ref, dtapx_ref, dtapb_ref, dskip_ref,
    dstate, nextx, nextb, accx, accb, accs, yrow, dact, xdt, dye, rowterm, colin, colst, direct, ystat,
):
    is_first = index == count - 1

    @pl.when(index == 0)
    def _():
        dstate[...] = jnp.zeros_like(dstate)
        nextx[...] = jnp.zeros_like(nextx)
        nextb[...] = jnp.zeros_like(nextb)
        accx[...] = jnp.zeros_like(accx)
        accb[...] = jnp.zeros_like(accb)
        accs[...] = jnp.zeros_like(accs)
        rowterm[...] = jnp.zeros_like(rowterm)
        colin[...] = jnp.zeros_like(colin)
        colst[...] = jnp.zeros_like(colst)
        direct[...] = jnp.zeros_like(direct)
        ystat[...] = jnp.zeros_like(ystat)

    run_row = run_ref[0:1, :]
    convx = conv_rows(xp_ref, x_ref, tapx_ref, run_row, is_first)
    sigx = jax.nn.sigmoid(convx)
    act = convx * sigx
    convb = conv_rows(bp_ref, b_ref, tapb_ref, run_row, is_first)
    sigb = jax.nn.sigmoid(convb)
    vec = convb * sigb
    size = vec.shape[0] // 2
    in_low = vec[:size].astype(BF16)
    out_low = vec[size:].astype(BF16)
    raw, step = step_rows(step_ref, head_ref)
    rate = head_ref[:, 1:2]
    upper = upper_ones(block)
    cum = mm_exact(step * rate, upper)
    cum_col = jnp.transpose(cum)
    place = lax.broadcasted_iota(jnp.int32, (1, block), 1).astype(F32)
    carried = (run_row >= place + 1.0).astype(F32)
    last_run = run_row[:, block - 1 :]
    tail = (float(block - 1) - place <= last_run).astype(F32)
    last = cum[:, block - 1 :]
    entry = jnp.exp(cum) * carried
    to_end = jnp.exp(last - cum) * tail
    keep = jnp.exp(last) * carried[:, block - 1 :]
    allowed = masks_of(runc_ref[:, 0:1], block)
    cross = jnp.where(allowed, mm(out_low, in_low, 0, 0), 0.0)
    old_low = entry_ref[0]
    old = old_low.astype(F32)
    dnew = dstate[...]
    dnew_low = dnew.astype(BF16)
    y_off = mm(old_low, out_low, 1, 0)
    u_off = mm(dnew_low, in_low, 1, 0)
    gate = z_ref[...].astype(F32)
    sig = jax.nn.sigmoid(gate)
    upstream = grad_ref[...].astype(F32)
    dy = upstream * gate * sig
    dcross = jnp.zeros((block, block), F32)
    for h in range(heads):
        rows = slice(h * head_dim, (h + 1) * head_dim)
        one = slice(h, h + 1)
        xh = act[rows]
        part = xh * step[one]
        part_low = part.astype(BF16)
        dyh = dy[rows]
        dy_low = dyh.astype(BF16)
        decay = jnp.exp(jnp.minimum(cum_col[:, one] - cum[one], 0.0))
        weight = (cross * decay).astype(BF16)
        y_in = mm(part_low, weight, 1, 1)
        y_scan = y_in + y_off[rows] * entry[one]
        u_in = mm(dy_low, weight, 1, 0)
        u_st = u_off[rows] * to_end[one]
        dcross = dcross + mm(dy_low, part_low, 0, 0) * decay
        part_f = part_low.astype(F32)
        u_all = u_in + u_st
        rowterm[one] = jnp.sum(dy_low.astype(F32) * y_scan, axis=0, keepdims=True)
        colin[one] = jnp.sum(part_f * u_in, axis=0, keepdims=True)
        colst[one] = jnp.sum(part_f * u_st, axis=0, keepdims=True)
        direct[one] = jnp.sum(xh * u_all, axis=0, keepdims=True)
        skip = skip_ref[rows, 0:1]
        yrow[rows] = y_scan + skip * xh
        dact[rows] = step[one] * u_all + skip * dyh
        xdt[rows] = (part * to_end[one]).astype(BF16)
        dye[rows] = (dyh * entry[one]).astype(BF16)
        kept = jnp.sum(dnew[rows] * old[rows] * keep[one], axis=0, keepdims=True)
        ystat[one] = kept
        dstate[rows] = dnew[rows] * keep[one]
        hook(h)
    dcross_low = jnp.where(allowed, dcross, 0.0).astype(BF16)
    dout = mm(in_low, dcross_low, 1, 1) + mm(old_low, dye[...], 0, 0)
    din = mm(out_low, dcross_low, 1, 0) + mm(dnew_low, xdt[...], 0, 0)
    dstate[...] += mm(dye[...], out_low, 1, 1)
    inner = upstream.shape[0]
    dm_ref[:inner] = (upstream * yrow[...] * sig * (1.0 + gate * (1.0 - sig))).astype(dm_ref.dtype)
    prod = dy * act
    accs[...] += sum(prod[:, c : c + 128] for c in range(0, block, 128))
    lower = jnp.transpose(upper)
    kept_total = jnp.sum(ystat[...], axis=1, keepdims=True)
    dlog = (
        mm_exact(rowterm[...] - colin[...], lower)
        + mm_exact(colst[...], upper)
        - colst[...]
        + kept_total
    )
    dstep = direct[...] + rate * dlog
    dstep_ref[...] = dstep * jax.nn.sigmoid(raw)
    drate_ref[...] = dlog * step

    def conv_back(dvals, conv, sigm, prev_ref, cur_ref, tap_ref, after, acc, out_ref):
        dconv = dvals * sigm * (1.0 + conv * (1.0 - sigm))
        taps = tap_ref[...]
        cur = cur_ref[...].astype(F32)
        prev = jnp.where(is_first, 0.0, prev_ref[...].astype(F32))
        result = taps[:, 3:4] * dconv
        acc[4] += sum(dconv[:, c : c + 128] for c in range(0, block, 128))
        prod = dconv * cur
        acc[3] += sum(prod[:, c : c + 128] for c in range(0, block, 128))
        following = after[...]
        for offset in range(1, 4):
            keep_cur = (run_row >= float(offset)).astype(F32)
            keep_next = (runn_ref[0:1, :] >= float(offset)).astype(F32)
            masked = dconv * keep_cur
            result = result + taps[:, 3 - offset : 4 - offset] * shift_left(
                masked, following * keep_next, offset
            )
            prod = masked * shift_right(prev, cur, offset)
            acc[3 - offset] += sum(prod[:, c : c + 128] for c in range(0, block, 128))
        after[...] = dconv[:, :128]
        out_ref[...] = result.astype(out_ref.dtype)

    conv_back(dact[...], convx, sigx, xp_ref, x_ref, tapx_ref, nextx, accx, dm_ref.at[inner:])
    conv_back(
        jnp.concatenate([din, dout], axis=0), convb, sigb, bp_ref, b_ref, tapb_ref, nextb, accb, db_ref
    )

    @pl.when(is_first)
    def _():
        def spread(acc, out_ref):
            lanes = lax.broadcasted_iota(jnp.int32, out_ref.shape, 1)
            result = jnp.zeros(out_ref.shape, F32)
            for item in range(5):
                total = jnp.sum(acc[item], axis=1, keepdims=True)
                result = jnp.where(lanes == item, total, result)
            out_ref[...] = result

        spread(accx, dtapx_ref)
        spread(accb, dtapb_ref)
        dskip_ref[...] = jnp.broadcast_to(
            jnp.sum(accs[...], axis=1, keepdims=True), dskip_ref.shape
        )


def ssd_specs(block, inner, vec, rows16, chunk_of):
    wide = lambda i: (0, chunk_of(i))
    per = block // 128
    before = lambda i: (0, jnp.maximum(chunk_of(i) * per - 1, 0))
    whole = lambda i: (0, 0)
    return [
        pl.BlockSpec((inner, block), wide),
        pl.BlockSpec((inner, block), lambda i: (1, chunk_of(i))),
        pl.BlockSpec((inner, 128), lambda i: (1, before(i)[1])),
        pl.BlockSpec((vec, block), wide),
        pl.BlockSpec((vec, 128), before),
        pl.BlockSpec((rows16, block), wide),
        pl.BlockSpec((8, block), wide),
        pl.BlockSpec((block, 128), lambda i: (chunk_of(i), 0)),
        pl.BlockSpec((inner, 128), whole),
        pl.BlockSpec((vec, 128), whole),
        pl.BlockSpec((rows16, 128), whole),
        pl.BlockSpec((inner, 128), whole),
    ]


def ssd_forward(mixer_t, vec_t, step_t, run8, run_col, tap_x, tap_b, head_cols, skip_col, heads, head_dim, block):
    inner = mixer_t.shape[0] // 2
    seq = mixer_t.shape[1]
    vec = vec_t.shape[0]
    rows16 = step_t.shape[0]
    chunks = seq // block
    state_dim = vec // 2
    return pl.pallas_call(
        functools.partial(ssd_forward_kernel, block, heads, head_dim),
        grid=(chunks,),
        in_specs=ssd_specs(block, inner, vec, rows16, lambda i: i),
        out_specs=[
            pl.BlockSpec((inner, block), lambda i: (0, i)),
            pl.BlockSpec((1, inner, state_dim), lambda i: (i, 0, 0)),
        ],
        out_shape=[
            jax.ShapeDtypeStruct((inner, seq), BF16),
            jax.ShapeDtypeStruct((chunks, inner, state_dim), BF16),
        ],
        scratch_shapes=[
            pltpu.VMEM((inner, state_dim), F32),
            pltpu.VMEM((inner, block), BF16),
            pltpu.VMEM((inner, block), F32),
        ],
        compiler_params=pltpu.CompilerParams(vmem_limit_bytes=48 << 20),
        cost_estimate=pl.CostEstimate(flops=10**9, bytes_accessed=10**7, transcendentals=10**7),
        name="ssd_forward",
    )(mixer_t, mixer_t, mixer_t, vec_t, vec_t, step_t, run8, run_col, tap_x, tap_b, head_cols, skip_col)


def ssd_backward(mixer_t, vec_t, step_t, run8, run_col, tap_x, tap_b, head_cols, skip_col, entry, grad_t, heads, head_dim, block):
    inner = mixer_t.shape[0] // 2
    seq = mixer_t.shape[1]
    vec = vec_t.shape[0]
    rows16 = step_t.shape[0]
    chunks = seq // block
    state_dim = vec // 2
    per = block // 128
    chunk_of = lambda i: chunks - 1 - i
    wide = lambda i: (0, chunk_of(i))
    whole = lambda i: (0, 0)
    return pl.pallas_call(
        functools.partial(ssd_backward_kernel, block, heads, head_dim),
        grid=(chunks,),
        in_specs=ssd_specs(block, inner, vec, rows16, chunk_of)
        + [
            pl.BlockSpec((1, inner, state_dim), lambda i: (chunk_of(i), 0, 0)),
            pl.BlockSpec((inner, block), wide),
            pl.BlockSpec((8, 128), lambda i: (0, jnp.minimum(chunk_of(i) * per + per, chunks * per - 1))),
        ],
        out_specs=[
            pl.BlockSpec((2 * inner, block), wide),
            pl.BlockSpec((vec, block), wide),
            pl.BlockSpec((rows16, block), wide),
            pl.BlockSpec((rows16, block), wide),
            pl.BlockSpec((inner, 128), whole),
            pl.BlockSpec((vec, 128), whole),
            pl.BlockSpec((inner, 128), whole),
        ],
        out_shape=[
            jax.ShapeDtypeStruct((2 * inner, seq), BF16),
            jax.ShapeDtypeStruct((vec, seq), BF16),
            jax.ShapeDtypeStruct((rows16, seq), F32),
            jax.ShapeDtypeStruct((rows16, seq), F32),
            jax.ShapeDtypeStruct((inner, 128), F32),
            jax.ShapeDtypeStruct((vec, 128), F32),
            jax.ShapeDtypeStruct((inner, 128), F32),
        ],
        scratch_shapes=[
            pltpu.VMEM((inner, state_dim), F32),
            pltpu.VMEM((inner, 128), F32),
            pltpu.VMEM((vec, 128), F32),
            pltpu.VMEM((5, inner, 128), F32),
            pltpu.VMEM((5, vec, 128), F32),
            pltpu.VMEM((inner, 128), F32),
            pltpu.VMEM((inner, block), F32),
            pltpu.VMEM((inner, block), F32),
            pltpu.VMEM((inner, block), BF16),
            pltpu.VMEM((inner, block), BF16),
            pltpu.VMEM((rows16, block), F32),
            pltpu.VMEM((rows16, block), F32),
            pltpu.VMEM((rows16, block), F32),
            pltpu.VMEM((rows16, block), F32),
            pltpu.VMEM((rows16, state_dim), F32),
        ],
        compiler_params=pltpu.CompilerParams(vmem_limit_bytes=48 << 20),
        cost_estimate=pl.CostEstimate(flops=3 * 10**9, bytes_accessed=2 * 10**7, transcendentals=3 * 10**7),
        name="ssd_backward",
    )(
        mixer_t, mixer_t, mixer_t, vec_t, vec_t, step_t, run8, run_col, tap_x, tap_b, head_cols, skip_col,
        entry, grad_t, run8,
    )


def rotate_rows(values, cosine, sine):
    half = values.shape[0] // 2
    first, second = values[:half], values[half:]
    return jnp.concatenate(
        [first * cosine - second * sine, second * cosine + first * sine], axis=0
    )


def window_of(block_index, block, reach):
    low = max(0, (block_index * block - (reach - 1)) // block)
    return low * block, (block_index + 1) * block


def allowed_of(run_ref, begin, stop, block):
    start, end = stop
    keys = lax.broadcasted_iota(jnp.int32, (end - start, block), 0) + start
    queries = lax.broadcasted_iota(jnp.int32, (end - start, block), 1) + begin
    gap = (queries - keys).astype(F32)
    return (gap >= 0.0) & (gap <= run_ref[0:1, begin : begin + block])


def attention_forward_kernel(
    heads, groups, head_dim, block, reach, scale,
    proj_ref, cos_ref, sin_ref, run_ref, out_ref, rot_ref, lse_ref,
):
    seq = proj_ref.shape[1]
    cosine, sine = cos_ref[...], sin_ref[...]
    total = heads + groups
    for item in range(total):
        rows = slice(item * head_dim, (item + 1) * head_dim)
        rot_ref[rows] = rotate_rows(proj_ref[rows].astype(F32), cosine, sine).astype(BF16)
    for index in range(seq // block):
        begin = index * block
        span = window_of(index, block, reach)
        allowed = allowed_of(run_ref, begin, span, block)
        for h in range(heads):
            group = h * groups // heads
            rows = slice(h * head_dim, (h + 1) * head_dim)
            krows = slice((heads + group) * head_dim, (heads + group + 1) * head_dim)
            vrows = slice((heads + groups + group) * head_dim, (heads + groups + group + 1) * head_dim)
            query = rot_ref[rows, begin : begin + block]
            key = rot_ref[krows, span[0] : span[1]]
            value = proj_ref[vrows, span[0] : span[1]].astype(BF16)
            logits = jnp.where(allowed, mm(key, query, 0, 0) * scale, -1e30)
            peak = jnp.max(logits, axis=0, keepdims=True)
            powered = jnp.exp(logits - peak)
            mass = jnp.sum(powered, axis=0, keepdims=True)
            probs = (powered * (1.0 / mass)).astype(BF16)
            out_ref[rows, begin : begin + block] = mm(value, probs, 1, 0).astype(out_ref.dtype)
            lse_ref[h : h + 1, begin : begin + block] = peak + jnp.log(mass)


def attention_backward_kernel(
    heads, groups, head_dim, block, reach, scale,
    proj_ref, rot_ref, cos_ref, sin_ref, run_ref, lse_ref, out_in_ref, grad_ref, back_ref,
    acc_key, acc_value,
):
    seq = proj_ref.shape[1]
    acc_key[...] = jnp.zeros_like(acc_key)
    acc_value[...] = jnp.zeros_like(acc_value)
    for index in range(seq // block):
        begin = index * block
        span = window_of(index, block, reach)
        allowed = allowed_of(run_ref, begin, span, block)
        cosine, sine = cos_ref[:, begin : begin + block], sin_ref[:, begin : begin + block]
        for h in range(heads):
            group = h * groups // heads
            rows = slice(h * head_dim, (h + 1) * head_dim)
            krows = slice((heads + group) * head_dim, (heads + group + 1) * head_dim)
            vrows = slice((heads + groups + group) * head_dim, (heads + groups + group + 1) * head_dim)
            grows = slice(group * head_dim, (group + 1) * head_dim)
            query = rot_ref[rows, begin : begin + block]
            key = rot_ref[krows, span[0] : span[1]]
            value = proj_ref[vrows, span[0] : span[1]].astype(BF16)
            grad = grad_ref[rows, begin : begin + block]
            logits = jnp.where(allowed, mm(key, query, 0, 0) * scale, -1e30)
            probs = jnp.exp(logits - lse_ref[h : h + 1, begin : begin + block])
            dprobs = mm(value, grad, 0, 0)
            centre = jnp.sum(probs * dprobs, axis=0, keepdims=True)
            dscore = (probs * (dprobs - centre) * scale).astype(BF16)
            dquery = mm(key, dscore, 1, 0)
            back_ref[rows, begin : begin + block] = rotate_rows(dquery, cosine, -sine).astype(BF16)
            acc_key[grows, span[0] : span[1]] += mm(query, dscore, 1, 1)
            acc_value[grows, span[0] : span[1]] += mm(grad, probs.astype(BF16), 1, 1)
    for group in range(groups):
        grows = slice(group * head_dim, (group + 1) * head_dim)
        krows = slice((heads + group) * head_dim, (heads + group + 1) * head_dim)
        vrows = slice((heads + groups + group) * head_dim, (heads + groups + group + 1) * head_dim)
        back_ref[krows] = rotate_rows(acc_key[grows], cos_ref[...], -sin_ref[...]).astype(BF16)
        back_ref[vrows] = acc_value[grows].astype(BF16)


def attention_forward(proj_t, cosine, sine, run8, heads, groups, head_dim, block, reach):
    seq = proj_t.shape[1]
    return pl.pallas_call(
        functools.partial(attention_forward_kernel, heads, groups, head_dim, block, reach, head_dim**-0.5),
        out_shape=[
            jax.ShapeDtypeStruct((heads * head_dim, seq), BF16),
            jax.ShapeDtypeStruct(((heads + groups) * head_dim, seq), BF16),
            jax.ShapeDtypeStruct((max(heads, 8), seq), F32),
        ],
        compiler_params=pltpu.CompilerParams(vmem_limit_bytes=48 << 20),
        cost_estimate=pl.CostEstimate(flops=2 * 10**9, bytes_accessed=10**7, transcendentals=4 * 10**6),
        name="attention_forward",
    )(proj_t, cosine, sine, run8)


def attention_backward(proj_t, rot_t, cosine, sine, run8, lse, out_t, grad_t, heads, groups, head_dim, block, reach):
    seq = proj_t.shape[1]
    return pl.pallas_call(
        functools.partial(attention_backward_kernel, heads, groups, head_dim, block, reach, head_dim**-0.5),
        out_shape=jax.ShapeDtypeStruct(proj_t.shape, BF16),
        scratch_shapes=[
            pltpu.VMEM((groups * head_dim, seq), F32),
            pltpu.VMEM((groups * head_dim, seq), F32),
        ],
        compiler_params=pltpu.CompilerParams(vmem_limit_bytes=48 << 20),
        cost_estimate=pl.CostEstimate(flops=5 * 10**9, bytes_accessed=10**7, transcendentals=4 * 10**6),
        name="attention_backward",
    )(proj_t, rot_t, cosine, sine, run8, lse, out_t, grad_t)


def ffn_kernel(norm_ref, cot_ref, gate_ref, up_ref, down_ref, out_ref, back_ref, act_ref, dgate_ref, dup_ref):
    @pl.when(pl.program_id(0) == 0)
    def _():
        out_ref[...] = jnp.zeros_like(out_ref)
        back_ref[...] = jnp.zeros_like(back_ref)

    normed, cot = norm_ref[...], cot_ref[...]
    gate_w, up_w, down_w = gate_ref[...], up_ref[...], down_ref[...]
    gate = mm(normed, gate_w, 1, 0)
    up = mm(normed, up_w, 1, 0)
    grad_act = mm(cot, down_w, 1, 1)
    sig = jax.nn.sigmoid(gate)
    silu = gate * sig
    act = (silu * up).astype(BF16)
    dgate = (grad_act * up * sig * (1.0 + gate * (1.0 - sig))).astype(BF16)
    dup = (grad_act * silu).astype(BF16)
    act_ref[...] = act
    dgate_ref[...] = dgate
    dup_ref[...] = dup
    out_ref[...] += mm(act, down_w, 1, 0)
    back_ref[...] += mm(dgate, gate_w, 1, 1) + mm(dup, up_w, 1, 1)


def feed_forward(normed, cot, gate_w, up_w, down_w, tile):
    rows, width = normed.shape
    hidden = gate_w.shape[1]
    whole = lambda i: (0, 0)
    return pl.pallas_call(
        ffn_kernel,
        grid=(hidden // tile,),
        in_specs=[
            pl.BlockSpec((rows, width), whole),
            pl.BlockSpec((rows, width), whole),
            pl.BlockSpec((width, tile), lambda i: (0, i)),
            pl.BlockSpec((width, tile), lambda i: (0, i)),
            pl.BlockSpec((tile, width), lambda i: (i, 0)),
        ],
        out_specs=[
            pl.BlockSpec((rows, width), whole),
            pl.BlockSpec((rows, width), whole),
            pl.BlockSpec((rows, tile), lambda i: (0, i)),
            pl.BlockSpec((rows, tile), lambda i: (0, i)),
            pl.BlockSpec((rows, tile), lambda i: (0, i)),
        ],
        out_shape=[
            jax.ShapeDtypeStruct((rows, width), F32),
            jax.ShapeDtypeStruct((rows, width), F32),
            jax.ShapeDtypeStruct((rows, hidden), BF16),
            jax.ShapeDtypeStruct((rows, hidden), BF16),
            jax.ShapeDtypeStruct((rows, hidden), BF16),
        ],
        compiler_params=pltpu.CompilerParams(vmem_limit_bytes=48 << 20),
        cost_estimate=pl.CostEstimate(flops=6 * 2 * rows * width * hidden, bytes_accessed=3 * 10**7, transcendentals=rows * hidden),
        name="feed_forward",
    )(normed, cot, gate_w, up_w, down_w)


def ffn_wgrad_kernel(norm_ref, cot_ref, act_ref, dgate_ref, dup_ref, gate_ref, up_ref, down_ref):
    normed, cot = norm_ref[...], cot_ref[...]
    gate_ref[...] = mm(dgate_ref[...], normed, 0, 0).astype(BF16)
    up_ref[...] = mm(dup_ref[...], normed, 0, 0).astype(BF16)
    down_ref[...] = mm(act_ref[...], cot, 0, 0).astype(BF16)


def ffn_wgrads(normed, cot, act, dgate, dup, tile):
    rows, width = normed.shape
    hidden = act.shape[1]
    whole = lambda i: (0, 0)
    return pl.pallas_call(
        ffn_wgrad_kernel,
        grid=(hidden // tile,),
        in_specs=[pl.BlockSpec((rows, width), whole)] * 2
        + [pl.BlockSpec((rows, tile), lambda i: (0, i))] * 3,
        out_specs=[pl.BlockSpec((tile, width), lambda i: (i, 0))] * 3,
        out_shape=[jax.ShapeDtypeStruct((hidden, width), BF16)] * 3,
        compiler_params=pltpu.CompilerParams(vmem_limit_bytes=48 << 20),
        cost_estimate=pl.CostEstimate(flops=3 * 2 * rows * width * hidden, bytes_accessed=2 * 10**7, transcendentals=0),
        name="ffn_wgrads",
    )(normed, cot, act, dgate, dup)


def digit_of(digit):
    axis_name, bit, size = digit
    return (lax.axis_index(axis_name) // (1 << bit)) % 2


def partner_of(digit):
    axis_name, bit, size = digit
    place = lax.axis_index(axis_name)
    return {axis_name: place + (1 - 2 * digit_of(digit)) * (1 << bit)}


def greet(digits):
    barrier = pltpu.get_barrier_semaphore()
    for digit in digits:
        pl.semaphore_signal(
            barrier, inc=1, device_id=partner_of(digit), device_id_type=pl.DeviceIdType.MESH
        )
    pl.semaphore_wait(barrier, len(digits))


def pair_kernel(products, tiles, group, rows, digit, left_count, *refs):
    count = len(products)
    right_count = 1 + max(right for _, right, _, _ in products)
    lefts, refs = refs[:left_count], refs[left_count:]
    rights, refs = refs[:right_count], refs[right_count:]
    outs, refs = refs[:count], refs[count:]
    fulls, refs = refs[:count], refs[count:]
    gots, (send_sem, recv_sem) = refs[:count], refs[count:]
    step = pl.program_id(0)
    mine = digit_of(digit)

    def copy_of(item, tile):
        return pltpu.make_async_remote_copy(
            src_ref=fulls[item].at[tile, :, 1 - mine],
            dst_ref=gots[item].at[tile],
            send_sem=send_sem.at[item, tile],
            recv_sem=recv_sem.at[item, tile],
            device_id=partner_of(digit),
            device_id_type=pl.DeviceIdType.MESH,
        )

    @pl.when(step == 0)
    def _():
        greet([digit])

    @pl.when(step < tiles)
    def _():
        for item, (left, right, right_dim, _) in enumerate(products):
            value = mm(lefts[left][...], rights[right][...], 0, right_dim)
            fulls[item][step] = value.astype(BF16).reshape((group, 2, rows, value.shape[1]))
            copy_of(item, step).start()

    @pl.when(step > 0)
    def _():
        done = step - 1
        for item in range(count):
            copy_of(item, done).wait()
            total = fulls[item][done, :, mine].astype(F32) + gots[item][done].astype(F32)
            width = outs[item].shape[3]
            for part in range(outs[item].shape[0]):
                outs[item][part] = total[:, :, part * width : (part + 1) * width].astype(BF16)


def pair_wgrads(lefts, rights, products, owners, tile, digit, collective_id, name):
    tokens, height = lefts[0].shape
    tiles = height // tile
    rows = height // owners
    group = tile // (2 * rows)
    widths = [rights[right].shape[1 - right_dim] for _, right, right_dim, _ in products]
    splits = [split for _, _, _, split in products]
    whole = lambda i: (0, 0)
    results = pl.pallas_call(
        functools.partial(pair_kernel, products, tiles, group, rows, digit, len(lefts)),
        grid=(tiles + 1,),
        in_specs=[pl.BlockSpec((tokens, tile), lambda i: (0, jnp.minimum(i, tiles - 1)))] * len(lefts)
        + [pl.BlockSpec(item.shape, whole) for item in rights],
        out_specs=[
            pl.BlockSpec((split, group, rows, width // split), lambda i: (0, jnp.maximum(i - 1, 0), 0, 0))
            for width, split in zip(widths, splits)
        ],
        out_shape=[
            jax.ShapeDtypeStruct((split, owners // 2, rows, width // split), BF16)
            for width, split in zip(widths, splits)
        ],
        scratch_shapes=[pltpu.VMEM((tiles, group, 2, rows, width), BF16) for width in widths]
        + [pltpu.VMEM((tiles, group, rows, width), BF16) for width in widths]
        + [
            pltpu.SemaphoreType.DMA((len(products), tiles)),
            pltpu.SemaphoreType.DMA((len(products), tiles)),
        ],
        compiler_params=pltpu.CompilerParams(
            vmem_limit_bytes=56 << 20, collective_id=collective_id, has_side_effects=True
        ),
        cost_estimate=pl.CostEstimate(
            flops=2 * tokens * height * sum(widths), bytes_accessed=2 * 10**7, transcendentals=0
        ),
        name=name,
    )(*lefts, *rights)
    return [item.reshape((-1,) + item.shape[2:]) for item in results]


class Reducer:
    def __init__(self, arrays, specs):
        self.pieces, self.plans = [], []
        for item, (digits, order, gather) in zip(arrays, specs):
            assert gather is None or list(digits) == list(order)
            left, count, stages = list(digits), item.shape[0], []
            for digit in order:
                high = 1 << left.index(digit)
                stages.append((digit, high, count // (2 * high)))
                left.remove(digit)
                count //= 2
            self.pieces.append((count,) + item.shape[1:] + (item.dtype, gather))
            self.plans.append(stages)
        self.count = len(self.pieces)
        self.inputs = [
            item.reshape((stages[0][1], 2, stages[0][2]) + item.shape[1:])
            for item, stages in zip(arrays, self.plans)
        ]

    def held(self, item):
        return list(self.pieces[item][4]) + [stage[0] for stage in self.plans[item]]

    def turns(self, item):
        gather = self.pieces[item][4]
        return len(self.plans[item]) + (0 if gather is None else len(self.held(item)))

    def out_shapes(self):
        shapes = []
        for item, (owners, rows, cols, dtype, gather) in enumerate(self.pieces):
            if gather is not None:
                shapes.append(jax.ShapeDtypeStruct((1 << len(self.held(item)), rows, cols), F32))
            elif owners == 1:
                shapes.append(jax.ShapeDtypeStruct((rows, cols), F32))
            else:
                shapes.append(jax.ShapeDtypeStruct((owners, rows, cols), dtype))
        return shapes

    def scratch(self):
        shapes = []
        for item, (owners, rows, cols, dtype, gather) in enumerate(self.pieces):
            stages = self.plans[item]
            for stage, (digit, high, low) in enumerate(stages):
                shapes.append(pltpu.VMEM(((high, low) if stage == 0 else (high, 2, low)) + (rows, cols), dtype))
            for digit, high, low in stages:
                shapes.append(pltpu.VMEM((high, low, rows, cols), dtype))
            if gather is not None:
                shapes.append(pltpu.VMEM((1 << len(self.held(item)), rows, cols), dtype))
        most = max(self.turns(item) for item in range(self.count))
        shapes += [pltpu.SemaphoreType.DMA((self.count, most))] * 2
        return shapes + [pltpu.SemaphoreType.DMA((self.count,))]

    def bind(self, ins, outs, refs):
        self.ins, self.outs = ins, outs
        self.keeps, self.gots, self.alls = [], [], []
        for item, stages in enumerate(self.plans):
            self.keeps.append(refs[: len(stages)])
            self.gots.append(refs[len(stages) : 2 * len(stages)])
            refs = refs[2 * len(stages) :]
            if self.pieces[item][4] is not None:
                self.alls.append(refs[0])
                refs = refs[1:]
            else:
                self.alls.append(None)
        self.send_sem, self.recv_sem, self.local_sem = refs

    def copy_of(self, item, stage):
        digit, high, low = self.plans[item][stage]
        source = self.ins[item] if stage == 0 else self.keeps[item][stage]
        return pltpu.make_async_remote_copy(
            src_ref=source.at[:, 1 - digit_of(digit)],
            dst_ref=self.gots[item][stage],
            send_sem=self.send_sem.at[item, stage],
            recv_sem=self.recv_sem.at[item, stage],
            device_id=partner_of(digit),
            device_id_type=pl.DeviceIdType.MESH,
        )

    def load_of(self, item):
        mine = digit_of(self.plans[item][0][0])
        return pltpu.make_async_copy(
            self.ins[item].at[:, mine], self.keeps[item][0], self.local_sem.at[item]
        )

    def place_of(self, digits):
        place = 0
        for digit in digits:
            place = place * 2 + digit_of(digit)
        return place

    def spread_of(self, item, stage):
        held = self.held(item)
        begin = self.place_of(held[: len(held) - stage]) * (1 << stage)
        region = self.alls[item].at[pl.ds(begin, 1 << stage)]
        turn = len(self.plans[item]) + stage
        return pltpu.make_async_remote_copy(
            src_ref=region,
            dst_ref=region,
            send_sem=self.send_sem.at[item, turn],
            recv_sem=self.recv_sem.at[item, turn],
            device_id=partner_of(held[len(held) - 1 - stage]),
            device_id_type=pl.DeviceIdType.MESH,
        )

    def start(self, item):
        self.copy_of(item, 0).start()
        self.load_of(item).start()

    def advance(self, item, turn):
        stages = self.plans[item]
        owners, rows, cols, dtype, gather = self.pieces[item]
        if turn >= len(stages):
            stage = turn - len(stages)
            self.spread_of(item, stage).wait()
            if stage + 1 < len(self.held(item)):
                self.spread_of(item, stage + 1).start()
            else:
                self.outs[item][...] = self.alls[item][...].astype(F32)
            return
        digit, high, low = stages[turn]
        self.copy_of(item, turn).wait()
        if turn == 0:
            self.load_of(item).wait()
        last = turn + 1 == len(stages)
        for h in range(high):
            for l in range(low):
                if turn == 0:
                    mine = self.keeps[item][0][h, l]
                else:
                    mine = self.keeps[item][turn][h, digit_of(digit), l]
                value = mine.astype(F32) + self.gots[item][turn][h, l].astype(F32)
                index = h * low + l
                if not last:
                    next_low = stages[turn + 1][2]
                    part, rest = index // (2 * next_low), index % (2 * next_low)
                    self.keeps[item][turn + 1][part, rest // next_low, rest % next_low] = value.astype(dtype)
                elif gather is not None:
                    self.alls[item][self.place_of(self.held(item))] = value.astype(dtype)
                elif owners == 1:
                    self.outs[item][...] = value
                else:
                    self.outs[item][index] = value.astype(dtype)
        if not last:
            self.copy_of(item, turn + 1).start()
        elif gather is not None:
            self.spread_of(item, 0).start()

    def events(self):
        depth = max(self.turns(item) for item in range(self.count))
        return [
            (item, turn) for turn in range(depth) for item in range(self.count) if turn < self.turns(item)
        ]


def reduce_kernel(reducer, partners, *refs):
    count = reducer.count
    reducer.bind(refs[:count], refs[count : 2 * count], refs[2 * count :])
    greet(partners)
    for item in range(count):
        reducer.start(item)
    for item, turn in reducer.events():
        reducer.advance(item, turn)


def reduce_all(arrays, specs, partners, collective_id):
    reducer = Reducer(arrays, specs)
    return pl.pallas_call(
        functools.partial(reduce_kernel, reducer, partners),
        in_specs=[pl.BlockSpec(memory_space=pl.ANY)] * len(arrays),
        out_specs=[pl.BlockSpec(memory_space=pltpu.VMEM)] * len(arrays),
        out_shape=reducer.out_shapes(),
        scratch_shapes=reducer.scratch(),
        compiler_params=pltpu.CompilerParams(
            vmem_limit_bytes=56 << 20, collective_id=collective_id, has_side_effects=True
        ),
        cost_estimate=pl.CostEstimate(flops=10**7, bytes_accessed=10**8, transcendentals=0),
        name="reduce_all",
    )(*reducer.inputs)


def backward_kernel(
    attention_part, ssd_part, reducer, partners, hooks, attention_count, ssd_count, ssd_outs, scratch_counts, *refs
):
    step = pl.program_id(0)
    steps = pl.num_programs(0)
    pieces = reducer.count
    attention_in, refs = refs[:attention_count], refs[attention_count:]
    ssd_in, refs = refs[:ssd_count], refs[ssd_count:]
    part_in, refs = refs[:pieces], refs[pieces:]
    attention_out, refs = refs[:1], refs[1:]
    ssd_out, refs = refs[:ssd_outs], refs[ssd_outs:]
    part_out, refs = refs[:pieces], refs[pieces:]
    attention_scratch, refs = refs[: scratch_counts[0]], refs[scratch_counts[0] :]
    ssd_scratch, refs = refs[: scratch_counts[1]], refs[scratch_counts[1] :]
    reducer.bind(part_in, part_out, refs)

    @pl.when(step == 0)
    def _():
        greet(partners)
        for item in range(pieces):
            reducer.start(item)
        attention_part(*attention_in, *attention_out, *attention_scratch)

    @pl.when(step > 0)
    def _():
        def hook(h):
            for (at_step, at_head), events in hooks.items():
                if at_head == h:
                    @pl.when(step == at_step)
                    def _():
                        for item, turn in events:
                            reducer.advance(item, turn)

        ssd_part(step - 1, steps - 1, hook, *ssd_in, *ssd_out, *ssd_scratch)

    late = [event for event in reducer.events() if not any(event in events for events in hooks.values())]

    @pl.when(step == steps - 1)
    def _():
        for item, turn in late:
            reducer.advance(item, turn)


def mixer_backward(attention_args, ssd_args, entry, grad_t, arrays, specs, partners, hooks, sizes, collective_id):
    query_heads, groups, head_dim, heads, ssd_dim, block, reach = sizes
    mixer_t, vec_t, step_t, run8, run_col, tap_x, tap_b, head_cols, skip_col = ssd_args
    inner = mixer_t.shape[0] // 2
    seq = mixer_t.shape[1]
    vec = vec_t.shape[0]
    rows16 = step_t.shape[0]
    chunks = seq // block
    state_dim = vec // 2
    per = block // 128
    chunk_of = lambda i: jnp.minimum(chunks - i, chunks - 1)
    wide = lambda i: (0, chunk_of(i))
    whole = lambda i: (0, 0)
    reducer = Reducer(arrays, specs)
    proj_t = attention_args[0]
    ssd_in = [mixer_t, mixer_t, mixer_t, vec_t, vec_t, step_t, run8, run_col, tap_x, tap_b, head_cols, skip_col]
    ssd_in += [entry, grad_t, run8]
    in_specs = [pl.BlockSpec(item.shape, whole) for item in attention_args]
    in_specs += ssd_specs(block, inner, vec, rows16, chunk_of)
    in_specs += [
        pl.BlockSpec((1, inner, state_dim), lambda i: (chunk_of(i), 0, 0)),
        pl.BlockSpec((inner, block), wide),
        pl.BlockSpec((8, 128), lambda i: (0, jnp.minimum(chunk_of(i) * per + per, chunks * per - 1))),
    ]
    in_specs += [pl.BlockSpec(memory_space=pl.ANY)] * len(arrays)
    ssd_out = [
        (2 * inner, seq, block, BF16),
        (vec, seq, block, BF16),
        (rows16, seq, block, F32),
        (rows16, seq, block, F32),
        (inner, 128, 128, F32),
        (vec, 128, 128, F32),
        (inner, 128, 128, F32),
    ]
    out_specs = [pl.BlockSpec(proj_t.shape, whole)]
    out_specs += [pl.BlockSpec((rows, width), wide if width == block and full == seq else whole) for rows, full, width, _ in ssd_out]
    part_shapes = reducer.out_shapes()
    out_specs += [
        pl.BlockSpec(item.shape, functools.partial(lambda rank, i: (0,) * rank, len(item.shape))) for item in part_shapes
    ]
    attention_scratch = [pltpu.VMEM((groups * head_dim, seq), F32)] * 2
    ssd_scratch = [
        pltpu.VMEM((inner, state_dim), F32),
        pltpu.VMEM((inner, 128), F32),
        pltpu.VMEM((vec, 128), F32),
        pltpu.VMEM((5, inner, 128), F32),
        pltpu.VMEM((5, vec, 128), F32),
        pltpu.VMEM((inner, 128), F32),
        pltpu.VMEM((inner, block), F32),
        pltpu.VMEM((inner, block), F32),
        pltpu.VMEM((inner, block), BF16),
        pltpu.VMEM((inner, block), BF16),
        pltpu.VMEM((rows16, block), F32),
        pltpu.VMEM((rows16, block), F32),
        pltpu.VMEM((rows16, block), F32),
        pltpu.VMEM((rows16, block), F32),
        pltpu.VMEM((rows16, state_dim), F32),
    ]
    results = pl.pallas_call(
        functools.partial(
            backward_kernel,
            functools.partial(attention_backward_kernel, query_heads, groups, head_dim, block, reach, head_dim**-0.5),
            functools.partial(ssd_backward_body, block, heads, ssd_dim),
            reducer,
            partners,
            hooks,
            len(attention_args),
            len(ssd_in),
            len(ssd_out),
            (len(attention_scratch), len(ssd_scratch)),
        ),
        grid=(chunks + 1,),
        in_specs=in_specs,
        out_specs=out_specs,
        out_shape=[jax.ShapeDtypeStruct(proj_t.shape, BF16)]
        + [jax.ShapeDtypeStruct((rows, full), dtype) for rows, full, _, dtype in ssd_out]
        + part_shapes,
        scratch_shapes=attention_scratch + ssd_scratch + reducer.scratch(),
        compiler_params=pltpu.CompilerParams(
            vmem_limit_bytes=60 << 20, collective_id=collective_id, has_side_effects=True
        ),
        cost_estimate=pl.CostEstimate(flops=5 * 10**10, bytes_accessed=3 * 10**7, transcendentals=3 * 10**7),
        name="mixer_backward",
    )(*attention_args, *ssd_in, *reducer.inputs)
    return results[0], results[1:8], results[8:]


def bits_of(count):
    return count.bit_length() - 1


def swap_halves(values, axis_name, bit, size):
    pairs = [(item, item ^ (1 << bit)) for item in range(size)]
    return lax.ppermute(values, axis_name, pairs)


def halve(values, place, my_bit, axis_name, bit, size):
    owners = values.shape[0]
    high = 1 << place
    parts = values.reshape((high, 2, owners // (2 * high)) + values.shape[1:])
    sent = lax.dynamic_index_in_dim(parts, 1 - my_bit, 1, keepdims=False)
    kept = lax.dynamic_index_in_dim(parts, my_bit, 1, keepdims=False)
    got = swap_halves(sent, axis_name, bit, size)
    total = (kept.astype(jnp.float32) + got.astype(jnp.float32)).astype(values.dtype)
    return total.reshape((owners // 2,) + values.shape[1:])


def scatter_sum(values, digits, order):
    left = list(digits)
    for digit in order:
        axis_name, bit, size = digit
        my_bit = (lax.axis_index(axis_name) >> bit) & 1
        values = halve(values, left.index(digit), my_bit, axis_name, bit, size)
        left.remove(digit)
    return values[0]


def gather_all(values, digits, order):
    values = values[None]
    left = []
    for digit in order:
        axis_name, bit, size = digit
        my_bit = (lax.axis_index(axis_name) >> bit) & 1
        got = swap_halves(values, axis_name, bit, size)
        place = sum(1 for item in left if digits.index(item) < digits.index(digit))
        high = 1 << place
        owners = values.shape[0]
        mine = values.reshape((high, 1, owners // high) + values.shape[1:])
        other = got.reshape(mine.shape)
        first = jnp.where(my_bit == 0, mine, other)
        second = jnp.where(my_bit == 0, other, mine)
        values = jnp.concatenate([first, second], axis=1).reshape((owners * 2,) + values.shape[1:])
        left.append(digit)
    return values


def other_branch(values):
    return lax.ppermute(values, "branch", [(0, 1), (1, 0)])


def rms_scale(values):
    return lax.rsqrt(jnp.mean(values * values, axis=-1, keepdims=True) + EPSILON)


def rms_back(upstream, values, scales, gain):
    weighted = upstream * gain
    return scales * weighted - values * scales**3 * jnp.mean(
        weighted * values, axis=-1, keepdims=True
    )


def token_runs(length_row, seq_len, doc_count):
    order = jnp.arange(doc_count, dtype=jnp.int32)
    ends = jnp.sum(jnp.where(order[:, None] >= order[None, :], length_row[None, :], 0), axis=1)
    places = jnp.arange(seq_len, dtype=jnp.int32)
    passed = places[:, None] >= ends[None, :]
    starts = jnp.sum(jnp.where(passed, length_row[None, :], 0), axis=1)
    return (places - starts).astype(F32), jnp.sum(length_row)


def join(mine, other, branch_pos, axis):
    return jnp.concatenate(
        [jnp.where(branch_pos == 0, mine, other), jnp.where(branch_pos == 0, other, mine)], axis=axis
    )


def both_weights(weight, core, branch_pos):
    half = weight.shape[0] // 2
    my_core = lax.axis_index("rows") & 1
    sent = lax.dynamic_slice_in_dim(weight, my_core * half, half, 0)
    got = other_branch(sent)
    rest = swap_halves(got, *core)
    other = jnp.concatenate(
        [jnp.where(my_core == 0, got, rest), jnp.where(my_core == 0, rest, got)], axis=0
    )
    return join(weight, other, branch_pos, 0)


def columns_of(items, rows):
    stacked = jnp.stack(items, axis=1)
    return jnp.pad(stacked, ((0, rows - stacked.shape[0]), (0, 128 - stacked.shape[1])))


def per_device(
    inputs,
    lengths,
    norm_gain,
    query_weight,
    keyval_weight,
    mixer_weight,
    state_weight,
    step_weight,
    conv_mixer,
    conv_state,
    bias_mixer,
    bias_state,
    step_bias,
    decay_log,
    skip_gain,
    ssd_gain,
    attn_output,
    ssd_output,
    ffn_gain,
    gate_weight,
    up_weight,
    down_weight,
    cotangent,
):
    branch_pos = lax.axis_index("branch")
    row_pos = lax.axis_index("rows")
    row_count = lax.axis_size("rows")
    row_bits = bits_of(row_count)
    row_digits = [("rows", bit, row_count) for bit in range(row_bits - 1, -1, -1)]
    across = ("branch", 0, 2)
    core = row_digits[-1]
    chip_digits = row_digits[:-1]
    near, others = chip_digits[-1], chip_digits[:-1][::-1]
    partners = [across] + row_digits
    fast = gate_weight.shape[1] // (2 * row_count) % 16 == 0

    own_rows = inputs[0].astype(F32)
    upstream = cotangent[0]
    half_len, model_dim = own_rows.shape
    seq_len = 2 * half_len
    local_query = query_weight.shape[1] // HD
    local_keyval = keyval_weight.shape[2] // HD
    local_heads = step_bias.shape[0]
    local_inner = bias_mixer.shape[0]
    inner_dim = 2 * local_inner
    head_rows = -(-local_heads // 8) * 8
    own_begin = branch_pos * half_len

    run, used = token_runs(lengths[0], seq_len, lengths.shape[1])
    run8 = jnp.broadcast_to(run[None, :], (8, seq_len))
    run_col = jnp.broadcast_to(run[:, None], (seq_len, 128))
    frequency = ROPE_BASE ** (-(jnp.arange(HD // 2, dtype=F32) * 2.0) / HD)
    angles = frequency[:, None] * run[None, :]
    cosine, sine = jnp.cos(angles), jnp.sin(angles)
    own_valid = (own_begin + jnp.arange(half_len, dtype=jnp.int32) < used).astype(F32)[:, None]

    own_scale = rms_scale(own_rows)
    own_hat = own_rows * own_scale
    normed = (own_hat * norm_gain).astype(BF16)
    full_normed = join(normed, other_branch(normed), branch_pos, 0)

    out_weight = jnp.concatenate([attn_output, ssd_output], axis=0)
    out_full = both_weights(out_weight, core, branch_pos)
    gain_full = join(ssd_gain, other_branch(ssd_gain), branch_pos, 0)

    qkv_flat = jnp.concatenate([query_weight, keyval_weight.reshape(model_dim, -1)], axis=1)
    mixer_flat = mixer_weight.reshape(model_dim, -1)
    state_flat = state_weight.reshape(model_dim, -1)
    step_flat = jnp.pad(step_weight, ((0, 0), (0, head_rows - local_heads)))

    mixer_t = mm(mixer_flat, full_normed, 0, 1).astype(BF16)
    vec_t = mm(state_flat, full_normed, 0, 1).astype(BF16)
    qkv_t = mm(qkv_flat, full_normed, 0, 1).astype(BF16)
    step_t = mm(step_flat, full_normed, 0, 1)

    taps = [conv_mixer[item] for item in range(4)] + [bias_mixer]
    tap_x = columns_of(taps, local_inner)
    state_taps = [conv_state[item].reshape(-1) for item in range(4)] + [bias_state.reshape(-1)]
    tap_b = columns_of(state_taps, state_flat.shape[1])
    rates = -jnp.exp(decay_log)
    head_cols = columns_of([step_bias, rates], head_rows)
    skip_col = jnp.broadcast_to(jnp.repeat(skip_gain, SP)[:, None], (local_inner, 128))
    ssd_args = (mixer_t, vec_t, step_t, run8, run_col, tap_x, tap_b, head_cols, skip_col)

    gated_t, entry = ssd_forward(*ssd_args, local_heads, SP, BLOCK)
    attn_t, rot_t, log_sums = attention_forward(
        qkv_t, cosine, sine, run8, local_query, local_keyval, HD, BLOCK, REACH
    )

    def own_tokens(values, pos):
        return lax.dynamic_slice_in_dim(values, pos * half_len, half_len, 1)

    def to_owner(values):
        got = other_branch(own_tokens(values, 1 - branch_pos))
        mine = own_tokens(values, branch_pos)
        return jnp.where(branch_pos == 0, mine, got), jnp.where(branch_pos == 0, got, mine)

    def to_heads(first, second):
        got = other_branch(jnp.where(branch_pos == 0, second, first))
        return join(jnp.where(branch_pos == 0, first, second), got, branch_pos, 1)

    gated_pair = to_owner(gated_t)
    attn_pair = to_owner(attn_t)
    attn_rows = attn_t.shape[0]
    part_rows = attn_rows + local_inner

    gated = [item.astype(F32) for item in gated_pair]
    gains = [gain_full[:local_inner, None], gain_full[local_inner:, None]]
    square_sum = sum(jnp.sum(item * item, axis=0, keepdims=True) for item in gated)
    gated_scale = lax.rsqrt(square_sum / inner_dim + EPSILON)
    features = jnp.concatenate(
        [
            attn_pair[0],
            (gated[0] * gated_scale * gains[0]).astype(BF16),
            attn_pair[1],
            (gated[1] * gated_scale * gains[1]).astype(BF16),
        ],
        axis=0,
    )
    mixer_sum = mm(features, out_full, 0, 0)
    hidden = own_rows + own_valid * mixer_sum
    hidden_scale = rms_scale(hidden)
    hidden_hat = hidden * hidden_scale
    normed_ffn = (hidden_hat * ffn_gain).astype(BF16)

    ffn_out, grad_normed_ffn, act_low, grad_gate, grad_up = feed_forward(
        normed_ffn, upstream, gate_weight, up_weight, down_weight, 256
    )
    block_out = (hidden + ffn_out).astype(BF16)[None]
    grad_hidden = upstream.astype(F32) + rms_back(grad_normed_ffn, hidden, hidden_scale, ffn_gain)
    ffn_gain_grad = jnp.sum(grad_normed_ffn * hidden_hat, axis=0)
    grad_mixer = (own_valid * grad_hidden).astype(BF16)

    grad_features = mm(out_full, grad_mixer, 1, 1)
    grad_attn = [grad_features[begin : begin + attn_rows] for begin in (0, part_rows)]
    grad_ssd = [grad_features[begin + attn_rows : begin + part_rows] for begin in (0, part_rows)]
    ssd_gain_wgrad = jnp.concatenate(
        [jnp.sum(item * value * gated_scale, axis=1) for item, value in zip(grad_ssd, gated)]
    )
    weighted = [item * gain for item, gain in zip(grad_ssd, gains)]
    row_inner = (
        sum(jnp.sum(item * value, axis=0, keepdims=True) for item, value in zip(weighted, gated))
        / inner_dim
    )
    grad_gated = [
        (gated_scale * item - value * gated_scale**3 * row_inner).astype(BF16)
        for item, value in zip(weighted, gated)
    ]
    head_gated = to_heads(*grad_gated)
    head_attn = to_heads(*[item.astype(BF16) for item in grad_attn])

    def pair_products(lefts, rights, products, owners, collective_id, name):
        if fast:
            return pair_wgrads(lefts, rights, products, owners, 256, core, collective_id, name)
        results = []
        for left, right, right_dim, split in products:
            value = mm(lefts[left], rights[right], 0, right_dim).astype(BF16)
            value = jnp.swapaxes(value.reshape(value.shape[0], split, -1), 0, 1)
            value = value.reshape((split * owners, -1) + value.shape[2:])
            results.append(halve(value, bits_of(split * owners) - 1, row_pos & 1, *core))
        return results

    def step_sum_of(values, digits, digit):
        axis_name, bit, size = digit
        my_bit = (lax.axis_index(axis_name) >> bit) & 1
        left = [item for item in digits if item != digit]
        return halve(values, digits.index(digit), my_bit, axis_name, bit, size), left

    all_digits = [across] + chip_digits
    gate_part, up_part, down_part = pair_products(
        [grad_gate, grad_up, act_low],
        [normed_ffn, upstream],
        [(0, 0, 0, 1), (1, 0, 0, 1), (2, 1, 0, 1)],
        2 * row_count,
        1,
        "ffn_wgrads",
    )
    (out_part,) = pair_products(
        [grad_mixer], [features], [(0, 0, 1, 2)], row_count, 2, "out_wgrads"
    )
    out_part, out_left = step_sum_of(out_part, all_digits, across)

    attention_args = (qkv_t, rot_t, cosine, sine, run8, log_sums, attn_t, head_attn)
    gate_left = up_left = down_left = all_digits
    if fast:
        early = [
            [across, near] + others[:1],
            [near, across] + others[:1],
            others[:2],
        ]
        dqkv_t, ssd_grads, (gate_part, up_part, down_part) = mixer_backward(
            attention_args,
            ssd_args,
            entry,
            head_gated,
            [gate_part, up_part, down_part],
            [(all_digits, order, None) for order in early],
            partners[:-1],
            {(2, 8): [(0, 0), (1, 0), (2, 0)], (4, 2): [(0, 1), (1, 1)]},
            (local_query, local_keyval, HD, local_heads, SP, BLOCK, REACH),
            3,
        )
        gate_left, up_left, down_left = [
            [item for item in all_digits if item not in order] for order in early
        ]
    else:
        ssd_grads = ssd_backward(*ssd_args, entry, head_gated, local_heads, SP, BLOCK)
        dqkv_t = attention_backward(
            *attention_args, local_query, local_keyval, HD, BLOCK, REACH
        )
    dmixer_t, dvec_t, dstep_t, dlog_t, dtap_x, dtap_b, dskip = ssd_grads
    mixer_part, state_part = pair_products(
        [full_normed], [dmixer_t, dvec_t], [(0, 0, 1, 1), (0, 1, 1, 1)], row_count, 4, "mixer_wgrads"
    )
    mixer_part, mixer_left = step_sum_of(mixer_part, chip_digits, near)
    dstep_low = dstep_t.astype(BF16)

    partial_normed = (
        mm(dmixer_t, mixer_flat, 0, 1)
        + mm(dvec_t, state_flat, 0, 1)
        + mm(dqkv_t, qkv_flat, 0, 1)
        + mm(dstep_low, step_flat, 0, 1)
    ).astype(BF16)
    sent = lax.dynamic_slice_in_dim(partial_normed, (1 - branch_pos) * half_len, half_len, 0)
    kept = lax.dynamic_slice_in_dim(partial_normed, own_begin, half_len, 0)
    own_grad_normed = kept.astype(F32) + other_branch(sent).astype(F32)
    input_grad = (grad_hidden + rms_back(own_grad_normed, own_rows, own_scale, norm_gain)).astype(
        BF16
    )[None]
    norm_gain_wgrad = (
        jnp.sum(partial_normed.astype(F32) * full_normed.astype(F32), axis=0) / norm_gain
    )
    qkvs_part = mm(full_normed, jnp.concatenate([dqkv_t, dstep_low], axis=0), 0, 1).astype(BF16)
    qkvs_part = qkvs_part.reshape((row_count, -1) + qkvs_part.shape[1:])
    query_cols = local_query * HD
    qkv_cols = dqkv_t.shape[0]

    def widen(values):
        full = jnp.zeros((2, 1, 64), F32)
        padded = jnp.pad(values, (0, 64 - local_heads))[None, None]
        return lax.dynamic_update_slice(full, padded, (branch_pos, 0, 0)).reshape(1, 128)

    heads = slice(0, local_heads)
    shared = jnp.concatenate(
        [
            norm_gain_wgrad.reshape(-1, 128),
            ffn_gain_grad.reshape(-1, 128),
            dtap_b[:, :4].T.reshape(-1, 128),
            dtap_b[:, 4].reshape(-1, 128),
            widen(jnp.sum(dstep_t[heads], axis=1)),
            widen(jnp.sum(dlog_t[heads], axis=1) * rates),
            widen(jnp.sum(dskip[:, 0].reshape(local_heads, SP), axis=1)),
        ],
        axis=0,
    )
    shared_rows = -(-shared.shape[0] // (2 * row_count))
    shared = jnp.pad(shared, ((0, 2 * row_count * shared_rows - shared.shape[0]), (0, 0)))
    shared = shared.reshape(2 * row_count, shared_rows, 128)
    own_width = local_inner // row_count
    own_gain = lax.dynamic_slice_in_dim(ssd_gain_wgrad, branch_pos * local_inner, local_inner, 0)
    other_gain = lax.dynamic_slice_in_dim(
        ssd_gain_wgrad, (1 - branch_pos) * local_inner, local_inner, 0
    )
    own_gain = own_gain + other_branch(other_gain)
    own_part = jnp.concatenate([dtap_x[:, :5].T, own_gain[None]], axis=0)
    own_part = jnp.swapaxes(own_part.reshape(6, row_count, own_width), 0, 1)
    own_part = jnp.pad(own_part, ((0, 0), (0, 2), (0, 128 - own_width)))

    def finish(arrays, specs):
        if fast:
            return reduce_all(arrays, specs, partners, 5)
        results = []
        for item, (digits, order, gather) in zip(arrays, specs):
            value = scatter_sum(item, digits, order)
            if gather is not None:
                digits = list(gather) + list(digits)
                value = gather_all(value, digits, digits[::-1])
            results.append(value.astype(F32))
        return results

    wide_digits = [core, across] + chip_digits[::-1]
    state_digits = wide_digits[1:]
    state_rows = state_part.reshape((row_count, -1) + state_part.shape[2:])

    def outward(left):
        return sorted(left, key=lambda item: (item[0] == "rows", item[1]))

    gate_sum, up_sum, down_sum, out_sum, mixer_wsum, qkvs_sum, state_sum, own_sum, flat_sum = finish(
        [gate_part, up_part, down_part, out_part, mixer_part, qkvs_part, state_rows, own_part, shared],
        [
            (gate_left, outward(gate_left), None),
            (up_left, outward(up_left), None),
            (down_left, outward(down_left), None),
            (out_left, outward(out_left), None),
            (mixer_left, outward(mixer_left), None),
            (row_digits, outward(row_digits), None),
            (state_digits, state_digits, [core]),
            (row_digits, outward(row_digits), None),
            (wide_digits, wide_digits, []),
        ],
    )
    flat_sum = flat_sum.reshape(-1, 128)
    gain_rows = model_dim // 128
    tap_rows = 4 * state_flat.shape[1] // 128
    bias_rows = state_flat.shape[1] // 128
    head_begin = 2 * gain_rows + tap_rows + bias_rows

    def rows_of(begin, size, shape):
        return flat_sum[begin : begin + size].reshape(shape)

    def head_values(item):
        pair = flat_sum[head_begin + item].reshape(2, 64)
        return pair[:, :local_heads].reshape(-1)

    state_sum = state_sum.reshape((2, row_count // 2, -1, state_flat.shape[1]))
    state_sum = jnp.swapaxes(state_sum, 0, 1).reshape(state_weight.shape)
    return (
        block_out,
        input_grad,
        rows_of(0, gain_rows, norm_gain.shape),
        qkvs_sum[:, :query_cols],
        qkvs_sum[:, query_cols:qkv_cols].reshape((-1,) + keyval_weight.shape[1:]),
        mixer_wsum.reshape((-1,) + mixer_weight.shape[1:]),
        state_sum,
        qkvs_sum[:, qkv_cols : qkv_cols + local_heads],
        own_sum[:4, :own_width],
        rows_of(2 * gain_rows, tap_rows, conv_state.shape),
        own_sum[4, :own_width],
        rows_of(2 * gain_rows + tap_rows, bias_rows, bias_state.shape),
        head_values(0),
        head_values(1),
        head_values(2),
        own_sum[5, :own_width],
        out_sum[:, :attn_rows].T,
        out_sum[:, attn_rows:].T,
        rows_of(gain_rows, gain_rows, ffn_gain.shape),
        gate_sum.T,
        up_sum.T,
        down_sum,
    )


def solution(mesh):
    in_specs = (
        P("rows", "branch", None),
        P("rows", None),
        P(),
        P(None, "branch"),
        P(None, None, "branch"),
        P(None, None, "branch"),
        P(),
        P(None, "branch"),
        P(None, "branch"),
        P(),
        P("branch"),
        P(),
        P("branch"),
        P("branch"),
        P("branch"),
        P("branch"),
        P("branch", None),
        P("branch", None),
        P(),
        P(),
        P(),
        P(),
        P("rows", "branch", None),
    )
    out_specs = (
        P("rows", "branch", None),
        P("rows", "branch", None),
        P(),
        P("rows", "branch"),
        P("rows", None, "branch"),
        P("rows", None, "branch"),
        P(),
        P("rows", "branch"),
        P(None, ("branch", "rows")),
        P(),
        P(("branch", "rows")),
        P(),
        P(),
        P(),
        P(),
        P(("branch", "rows")),
        P("branch", "rows"),
        P("branch", "rows"),
        P(),
        P(None, ("branch", "rows")),
        P(None, ("branch", "rows")),
        P(("branch", "rows"), None),
    )
    return jax.shard_map(
        per_device, mesh=mesh, in_specs=in_specs, out_specs=out_specs, check_vma=False
    )
```

```python
import functools
import itertools

import jax
import jax.numpy as jnp
from jax import lax
from jax.experimental import pallas as pl
from jax.experimental.pallas import tpu as pltpu
from jax.sharding import PartitionSpec as P

HD = 64
SH = 24
SP = 64
BLOCK = 256
REACH = 512
EPSILON = 1e-05
ROPE_BASE = 100000000000.0
F32 = jnp.float32
BF16 = jnp.bfloat16
PRECISE = lax.Precision.HIGHEST


def mm(left, right, left_dim, right_dim):
    return lax.dot_general(
        left, right, (((left_dim,), (right_dim,)), ((), ())), preferred_element_type=F32
    )


def mm_exact(left, right):
    return jnp.dot(left, right, preferred_element_type=F32, precision=PRECISE)


def shift_right(prev, cur, amount):
    joined = jnp.concatenate([prev, cur], axis=1)
    return pltpu.roll(joined, amount, 1)[:, prev.shape[1] :]


def shift_left(cur, after, amount):
    joined = jnp.concatenate([cur, after], axis=1)
    total = joined.shape[1]
    return pltpu.roll(joined, total - amount, 1)[:, : cur.shape[1]]


def conv_inputs(prev_ref, cur_ref, rows, run_row, is_first):
    cur = cur_ref[rows].astype(F32)
    prev = jnp.where(is_first, 0.0, prev_ref[rows].astype(F32))
    moved = [
        shift_right(prev, cur, offset) * (run_row >= float(offset)).astype(F32) for offset in (3, 2, 1)
    ]
    return moved + [cur]


def conv_rows(items, taps):
    result = taps[:, 4:5] + taps[:, 3:4] * items[3]
    for place in range(3):
        result = result + taps[:, place : place + 1] * items[place]
    return result


def step_rows(step_ref, head_ref):
    raw = step_ref[...] + head_ref[:, 0:1]
    return raw, jax.nn.softplus(raw)


def masks_of(run_col, block):
    rows = lax.broadcasted_iota(jnp.int32, (block, block), 0)
    cols = lax.broadcasted_iota(jnp.int32, (block, block), 1)
    gap = (rows - cols).astype(F32)
    return (gap >= 0.0) & (gap <= run_col)


def upper_ones(block):
    rows = lax.broadcasted_iota(jnp.int32, (block, block), 0)
    cols = lax.broadcasted_iota(jnp.int32, (block, block), 1)
    return (rows <= cols).astype(F32)


def ssd_forward_kernel(
    block, heads, head_dim,
    z_ref, x_ref, xp_ref, b_ref, bp_ref, step_ref, run_ref, runc_ref, tapx_ref, tapb_ref, head_ref, skip_ref,
    gated_ref, entry_ref,
    state, xdt,
):
    index = pl.program_id(0)
    is_first = index == 0

    @pl.when(is_first)
    def _():
        state[...] = jnp.zeros_like(state)

    run_row = run_ref[0:1, :]
    everything = slice(0, b_ref.shape[0])
    vec = conv_rows(conv_inputs(bp_ref, b_ref, everything, run_row, is_first), tapb_ref[...])
    vec = vec * jax.nn.sigmoid(vec)
    size = vec.shape[0] // 2
    in_low = vec[:size].astype(BF16)
    out_low = vec[size:].astype(BF16)
    raw, step = step_rows(step_ref, head_ref)
    rate = head_ref[:, 1:2]
    cum = mm_exact(step * rate, upper_ones(block))
    cum_col = jnp.transpose(cum)
    place = lax.broadcasted_iota(jnp.int32, (1, block), 1).astype(F32)
    carried = (run_row >= place + 1.0).astype(F32)
    last_run = run_row[:, block - 1 :]
    tail = (float(block - 1) - place <= last_run).astype(F32)
    last = cum[:, block - 1 :]
    entry = jnp.exp(cum) * carried
    to_end = jnp.exp(last - cum) * tail
    keep = jnp.exp(last) * carried[:, block - 1 :]
    allowed = masks_of(runc_ref[:, 0:1], block)
    cross = jnp.where(allowed, mm(out_low, in_low, 0, 0), 0.0)
    old = state[...]
    old_low = old.astype(BF16)
    entry_ref[0] = old_low
    for h in range(heads):
        rows = slice(h * head_dim, (h + 1) * head_dim)
        act = conv_rows(conv_inputs(xp_ref, x_ref, rows, run_row, is_first), tapx_ref[rows])
        act = act * jax.nn.sigmoid(act)
        part = act * step[h : h + 1]
        part_low = part.astype(BF16)
        decay = jnp.exp(jnp.minimum(cum_col[:, h : h + 1] - cum[h : h + 1], 0.0))
        weight = (cross * decay).astype(BF16)
        y_in = mm(part_low, weight, 1, 1)
        y_off = mm(old_low[rows], out_low, 1, 0)
        y_all = y_in + y_off * entry[h : h + 1] + skip_ref[rows, 0:1] * act
        gate = z_ref[rows].astype(F32)
        gated_ref[rows] = (y_all * gate * jax.nn.sigmoid(gate)).astype(gated_ref.dtype)
        xdt[rows] = (part * to_end[h : h + 1]).astype(BF16)
        state[rows] = old[rows] * keep[h : h + 1]
    state[...] += mm(xdt[...], in_low, 1, 1)


def ssd_backward_kernel(block, heads, head_dim, *refs):
    grad_ref = refs[13]
    ssd_backward_body(
        block, heads, head_dim, pl.program_id(0), pl.num_programs(0), lambda h: None,
        lambda chunk, low, high: grad_ref[low:high], *refs[:13], *refs[14:],
    )


def ssd_backward_body(
    block, heads, head_dim, index, count, hook, grad_of,
    z_ref, x_ref, xp_ref, b_ref, bp_ref, step_ref, run_ref, runc_ref, tapx_ref, tapb_ref, head_ref, skip_ref,
    entry_ref, runn_ref,
    dm_ref, db_ref, dstep_ref, drate_ref, dtapx_ref, dtapb_ref, dskip_ref,
    dstate, nextx, nextb, accx, accb, accs, xdt, dye, rowterm, colin, colst, direct, ystat,
):
    is_first = index == count - 1

    @pl.when(index == 0)
    def _():
        dstate[...] = jnp.zeros_like(dstate)
        nextx[...] = jnp.zeros_like(nextx)
        nextb[...] = jnp.zeros_like(nextb)
        accx[...] = jnp.zeros_like(accx)
        accb[...] = jnp.zeros_like(accb)
        accs[...] = jnp.zeros_like(accs)
        rowterm[...] = jnp.zeros_like(rowterm)
        colin[...] = jnp.zeros_like(colin)
        colst[...] = jnp.zeros_like(colst)
        direct[...] = jnp.zeros_like(direct)
        ystat[...] = jnp.zeros_like(ystat)

    run_row = run_ref[0:1, :]
    everything = slice(0, b_ref.shape[0])
    items_b = conv_inputs(bp_ref, b_ref, everything, run_row, is_first)
    convb = conv_rows(items_b, tapb_ref[...])
    sigb = jax.nn.sigmoid(convb)
    vec = convb * sigb
    size = vec.shape[0] // 2
    in_low = vec[:size].astype(BF16)
    out_low = vec[size:].astype(BF16)
    raw, step = step_rows(step_ref, head_ref)
    rate = head_ref[:, 1:2]
    upper = upper_ones(block)
    cum = mm_exact(step * rate, upper)
    cum_col = jnp.transpose(cum)
    place = lax.broadcasted_iota(jnp.int32, (1, block), 1).astype(F32)
    carried = (run_row >= place + 1.0).astype(F32)
    last_run = run_row[:, block - 1 :]
    tail = (float(block - 1) - place <= last_run).astype(F32)
    last = cum[:, block - 1 :]
    entry = jnp.exp(cum) * carried
    to_end = jnp.exp(last - cum) * tail
    keep = jnp.exp(last) * carried[:, block - 1 :]
    allowed = masks_of(runc_ref[:, 0:1], block)
    cross = jnp.where(allowed, mm(out_low, in_low, 0, 0), 0.0)
    old_low = entry_ref[0]
    dnew_low = dstate[...].astype(BF16)
    inner = xdt.shape[0]
    y_off = mm(old_low, out_low, 1, 0)
    u_off = mm(dnew_low, in_low, 1, 0)

    def conv_back(dvals, conv, sigm, items, taps, rows, after, acc, out_ref, out_rows):
        dconv = dvals * sigm * (1.0 + conv * (1.0 - sigm))

        def add(place, values):
            acc[place, rows] += sum(values[:, c : c + 128] for c in range(0, block, 128))

        add(4, dconv)
        for place in range(4):
            add(place, dconv * items[place])
        result = taps[:, 3:4] * dconv
        following = after[rows]
        for offset in range(1, 4):
            keep_cur = (run_row >= float(offset)).astype(F32)
            keep_next = (runn_ref[0:1, :] >= float(offset)).astype(F32)
            result = result + taps[:, 3 - offset : 4 - offset] * shift_left(
                dconv * keep_cur, following * keep_next, offset
            )
        after[rows] = dconv[:, :128]
        out_ref[out_rows] = result.astype(out_ref.dtype)

    dcross = jnp.zeros((block, block), F32)
    for h in range(heads):
        rows = slice(h * head_dim, (h + 1) * head_dim)
        one = slice(h, h + 1)
        items = conv_inputs(xp_ref, x_ref, rows, run_row, is_first)
        taps = tapx_ref[rows]
        conv = conv_rows(items, taps)
        sigm = jax.nn.sigmoid(conv)
        xh = conv * sigm
        gate = z_ref[rows].astype(F32)
        sig = jax.nn.sigmoid(gate)
        upstream = grad_of(count - 1 - index, h * head_dim, (h + 1) * head_dim).astype(F32)
        dyh = upstream * gate * sig
        dnew = dstate[rows]
        part = xh * step[one]
        part_low = part.astype(BF16)
        dy_low = dyh.astype(BF16)
        decay = jnp.exp(jnp.minimum(cum_col[:, one] - cum[one], 0.0))
        weight = (cross * decay).astype(BF16)
        y_in = mm(part_low, weight, 1, 1)
        y_scan = y_in + y_off[rows] * entry[one]
        u_in = mm(dy_low, weight, 1, 0)
        u_st = u_off[rows] * to_end[one]
        dcross = dcross + mm(dy_low, part_low, 0, 0) * decay
        part_f = part_low.astype(F32)
        u_all = u_in + u_st
        rowterm[one] = jnp.sum(dy_low.astype(F32) * y_scan, axis=0, keepdims=True)
        colin[one] = jnp.sum(part_f * u_in, axis=0, keepdims=True)
        colst[one] = jnp.sum(part_f * u_st, axis=0, keepdims=True)
        direct[one] = jnp.sum(xh * u_all, axis=0, keepdims=True)
        skip = skip_ref[rows, 0:1]
        y_all = y_scan + skip * xh
        dm_ref[rows] = (upstream * y_all * sig * (1.0 + gate * (1.0 - sig))).astype(dm_ref.dtype)
        prod = dyh * xh
        accs[rows] += sum(prod[:, c : c + 128] for c in range(0, block, 128))
        dact = step[one] * u_all + skip * dyh
        below = slice(inner + h * head_dim, inner + (h + 1) * head_dim)
        conv_back(dact, conv, sigm, items, taps, rows, nextx, accx, dm_ref, below)
        xdt[rows] = (part * to_end[one]).astype(BF16)
        dye[rows] = (dyh * entry[one]).astype(BF16)
        old = old_low[rows].astype(F32)
        ystat[one] = jnp.sum(dnew * old * keep[one], axis=0, keepdims=True)
        dstate[rows] = dnew * keep[one]
        hook(h)
    dcross_low = jnp.where(allowed, dcross, 0.0).astype(BF16)
    dout = mm(in_low, dcross_low, 1, 1) + mm(old_low, dye[...], 0, 0)
    din = mm(out_low, dcross_low, 1, 0) + mm(dnew_low, xdt[...], 0, 0)
    dstate[...] += mm(dye[...], out_low, 1, 1)
    lower = jnp.transpose(upper)
    kept_total = jnp.sum(ystat[...], axis=1, keepdims=True)
    dlog = (
        mm_exact(rowterm[...] - colin[...], lower)
        + mm_exact(colst[...], upper)
        - colst[...]
        + kept_total
    )
    dstep = direct[...] + rate * dlog
    dstep_ref[...] = dstep * jax.nn.sigmoid(raw)
    drate_ref[...] = dlog * step

    conv_back(
        jnp.concatenate([din, dout], axis=0), convb, sigb, items_b, tapb_ref[...], everything, nextb, accb,
        db_ref, everything,
    )

    @pl.when(is_first)
    def _():
        def spread(acc, out_ref):
            lanes = lax.broadcasted_iota(jnp.int32, out_ref.shape, 1)
            result = jnp.zeros(out_ref.shape, F32)
            for item in range(5):
                total = jnp.sum(acc[item], axis=1, keepdims=True)
                result = jnp.where(lanes == item, total, result)
            out_ref[...] = result

        spread(accx, dtapx_ref)
        spread(accb, dtapb_ref)
        dskip_ref[...] = jnp.broadcast_to(
            jnp.sum(accs[...], axis=1, keepdims=True), dskip_ref.shape
        )


def ssd_specs(block, inner, vec, rows16, chunk_of):
    wide = lambda i: (0, chunk_of(i))
    per = block // 128
    before = lambda i: (0, jnp.maximum(chunk_of(i) * per - 1, 0))
    whole = lambda i: (0, 0)
    return [
        pl.BlockSpec((inner, block), wide),
        pl.BlockSpec((inner, block), lambda i: (1, chunk_of(i))),
        pl.BlockSpec((inner, 128), lambda i: (1, before(i)[1])),
        pl.BlockSpec((vec, block), wide),
        pl.BlockSpec((vec, 128), before),
        pl.BlockSpec((rows16, block), wide),
        pl.BlockSpec((8, block), wide),
        pl.BlockSpec((block, 128), lambda i: (chunk_of(i), 0)),
        pl.BlockSpec((inner, 128), whole),
        pl.BlockSpec((vec, 128), whole),
        pl.BlockSpec((rows16, 128), whole),
        pl.BlockSpec((inner, 128), whole),
    ]


def ssd_forward(mixer_t, vec_t, step_t, run8, run_col, tap_x, tap_b, head_cols, skip_col, heads, head_dim, block):
    inner = mixer_t.shape[0] // 2
    seq = mixer_t.shape[1]
    vec = vec_t.shape[0]
    rows16 = step_t.shape[0]
    chunks = seq // block
    state_dim = vec // 2
    return pl.pallas_call(
        functools.partial(ssd_forward_kernel, block, heads, head_dim),
        grid=(chunks,),
        in_specs=ssd_specs(block, inner, vec, rows16, lambda i: i),
        out_specs=[
            pl.BlockSpec((inner, block), lambda i: (0, i)),
            pl.BlockSpec((1, inner, state_dim), lambda i: (i, 0, 0)),
        ],
        out_shape=[
            jax.ShapeDtypeStruct((inner, seq), BF16),
            jax.ShapeDtypeStruct((chunks, inner, state_dim), BF16),
        ],
        scratch_shapes=[
            pltpu.VMEM((inner, state_dim), F32),
            pltpu.VMEM((inner, block), BF16),
        ],
        compiler_params=pltpu.CompilerParams(vmem_limit_bytes=48 << 20),
        cost_estimate=pl.CostEstimate(flops=10**9, bytes_accessed=10**7, transcendentals=10**7),
        name="ssd_forward",
    )(mixer_t, mixer_t, mixer_t, vec_t, vec_t, step_t, run8, run_col, tap_x, tap_b, head_cols, skip_col)


def ssd_backward(mixer_t, vec_t, step_t, run8, run_col, tap_x, tap_b, head_cols, skip_col, entry, grad_t, heads, head_dim, block):
    inner = mixer_t.shape[0] // 2
    seq = mixer_t.shape[1]
    vec = vec_t.shape[0]
    rows16 = step_t.shape[0]
    chunks = seq // block
    state_dim = vec // 2
    per = block // 128
    chunk_of = lambda i: chunks - 1 - i
    wide = lambda i: (0, chunk_of(i))
    whole = lambda i: (0, 0)
    return pl.pallas_call(
        functools.partial(ssd_backward_kernel, block, heads, head_dim),
        grid=(chunks,),
        in_specs=ssd_specs(block, inner, vec, rows16, chunk_of)
        + [
            pl.BlockSpec((1, inner, state_dim), lambda i: (chunk_of(i), 0, 0)),
            pl.BlockSpec((inner, block), wide),
            pl.BlockSpec((8, 128), lambda i: (0, jnp.minimum(chunk_of(i) * per + per, chunks * per - 1))),
        ],
        out_specs=[
            pl.BlockSpec((2 * inner, block), wide),
            pl.BlockSpec((vec, block), wide),
            pl.BlockSpec((rows16, block), wide),
            pl.BlockSpec((rows16, block), wide),
            pl.BlockSpec((inner, 128), whole),
            pl.BlockSpec((vec, 128), whole),
            pl.BlockSpec((inner, 128), whole),
        ],
        out_shape=[
            jax.ShapeDtypeStruct((2 * inner, seq), BF16),
            jax.ShapeDtypeStruct((vec, seq), BF16),
            jax.ShapeDtypeStruct((rows16, seq), F32),
            jax.ShapeDtypeStruct((rows16, seq), F32),
            jax.ShapeDtypeStruct((inner, 128), F32),
            jax.ShapeDtypeStruct((vec, 128), F32),
            jax.ShapeDtypeStruct((inner, 128), F32),
        ],
        scratch_shapes=[
            pltpu.VMEM((inner, state_dim), F32),
            pltpu.VMEM((inner, 128), F32),
            pltpu.VMEM((vec, 128), F32),
            pltpu.VMEM((5, inner, 128), F32),
            pltpu.VMEM((5, vec, 128), F32),
            pltpu.VMEM((inner, 128), F32),
            pltpu.VMEM((inner, block), BF16),
            pltpu.VMEM((inner, block), BF16),
            pltpu.VMEM((rows16, block), F32),
            pltpu.VMEM((rows16, block), F32),
            pltpu.VMEM((rows16, block), F32),
            pltpu.VMEM((rows16, block), F32),
            pltpu.VMEM((rows16, state_dim), F32),
        ],
        compiler_params=pltpu.CompilerParams(vmem_limit_bytes=48 << 20),
        cost_estimate=pl.CostEstimate(flops=3 * 10**9, bytes_accessed=2 * 10**7, transcendentals=3 * 10**7),
        name="ssd_backward",
    )(
        mixer_t, mixer_t, mixer_t, vec_t, vec_t, step_t, run8, run_col, tap_x, tap_b, head_cols, skip_col,
        entry, grad_t, run8,
    )


def rotate_rows(values, cosine, sine):
    half = values.shape[0] // 2
    first, second = values[:half], values[half:]
    return jnp.concatenate(
        [first * cosine - second * sine, second * cosine + first * sine], axis=0
    )


def window_of(block_index, block, reach):
    low = max(0, (block_index * block - (reach - 1)) // block)
    return low * block, (block_index + 1) * block


def allowed_of(run_ref, begin, stop, block):
    start, end = stop
    keys = lax.broadcasted_iota(jnp.int32, (end - start, block), 0) + start
    queries = lax.broadcasted_iota(jnp.int32, (end - start, block), 1) + begin
    gap = (queries - keys).astype(F32)
    return (gap >= 0.0) & (gap <= run_ref[0:1, begin : begin + block])


def attention_forward_kernel(
    heads, groups, head_dim, block, reach, scale,
    proj_ref, cos_ref, sin_ref, run_ref, out_ref, rot_ref, lse_ref,
):
    seq = proj_ref.shape[1]
    cosine, sine = cos_ref[...], sin_ref[...]
    total = heads + groups
    for item in range(total):
        rows = slice(item * head_dim, (item + 1) * head_dim)
        rot_ref[rows] = rotate_rows(proj_ref[rows].astype(F32), cosine, sine).astype(BF16)
    for index in range(seq // block):
        begin = index * block
        span = window_of(index, block, reach)
        allowed = allowed_of(run_ref, begin, span, block)
        for h in range(heads):
            group = h * groups // heads
            rows = slice(h * head_dim, (h + 1) * head_dim)
            krows = slice((heads + group) * head_dim, (heads + group + 1) * head_dim)
            vrows = slice((heads + groups + group) * head_dim, (heads + groups + group + 1) * head_dim)
            query = rot_ref[rows, begin : begin + block]
            key = rot_ref[krows, span[0] : span[1]]
            value = proj_ref[vrows, span[0] : span[1]].astype(BF16)
            logits = jnp.where(allowed, mm(key, query, 0, 0) * scale, -1e30)
            peak = jnp.max(logits, axis=0, keepdims=True)
            powered = jnp.exp(logits - peak)
            mass = jnp.sum(powered, axis=0, keepdims=True)
            probs = (powered * (1.0 / mass)).astype(BF16)
            out_ref[rows, begin : begin + block] = mm(value, probs, 1, 0).astype(out_ref.dtype)
            lse_ref[h : h + 1, begin : begin + block] = peak + jnp.log(mass)


def attention_backward_kernel(
    heads, groups, head_dim, block, reach, scale, grad_of, hook,
    proj_ref, rot_ref, cos_ref, sin_ref, run_ref, lse_ref, back_ref,
    acc_key, acc_value,
):
    seq = proj_ref.shape[1]
    acc_key[...] = jnp.zeros_like(acc_key)
    acc_value[...] = jnp.zeros_like(acc_value)
    for index in range(seq // block):
        begin = index * block
        span = window_of(index, block, reach)
        allowed = allowed_of(run_ref, begin, span, block)
        cosine, sine = cos_ref[:, begin : begin + block], sin_ref[:, begin : begin + block]
        for h in range(heads):
            group = h * groups // heads
            rows = slice(h * head_dim, (h + 1) * head_dim)
            krows = slice((heads + group) * head_dim, (heads + group + 1) * head_dim)
            vrows = slice((heads + groups + group) * head_dim, (heads + groups + group + 1) * head_dim)
            grows = slice(group * head_dim, (group + 1) * head_dim)
            query = rot_ref[rows, begin : begin + block]
            key = rot_ref[krows, span[0] : span[1]]
            value = proj_ref[vrows, span[0] : span[1]].astype(BF16)
            grad = grad_of(h * head_dim, (h + 1) * head_dim, begin)
            logits = jnp.where(allowed, mm(key, query, 0, 0) * scale, -1e30)
            probs = jnp.exp(logits - lse_ref[h : h + 1, begin : begin + block])
            dprobs = mm(value, grad, 0, 0)
            centre = jnp.sum(probs * dprobs, axis=0, keepdims=True)
            dscore = (probs * (dprobs - centre) * scale).astype(BF16)
            dquery = mm(key, dscore, 1, 0)
            back_ref[rows, begin : begin + block] = rotate_rows(dquery, cosine, -sine).astype(BF16)
            acc_key[grows, span[0] : span[1]] += mm(query, dscore, 1, 1)
            acc_value[grows, span[0] : span[1]] += mm(grad, probs.astype(BF16), 1, 1)
        hook(index)
    for group in range(groups):
        grows = slice(group * head_dim, (group + 1) * head_dim)
        krows = slice((heads + group) * head_dim, (heads + group + 1) * head_dim)
        vrows = slice((heads + groups + group) * head_dim, (heads + groups + group + 1) * head_dim)
        back_ref[krows] = rotate_rows(acc_key[grows], cos_ref[...], -sin_ref[...]).astype(BF16)
        back_ref[vrows] = acc_value[grows].astype(BF16)


def attention_forward(proj_t, cosine, sine, run8, heads, groups, head_dim, block, reach):
    seq = proj_t.shape[1]
    return pl.pallas_call(
        functools.partial(attention_forward_kernel, heads, groups, head_dim, block, reach, head_dim**-0.5),
        out_shape=[
            jax.ShapeDtypeStruct((heads * head_dim, seq), BF16),
            jax.ShapeDtypeStruct(((heads + groups) * head_dim, seq), BF16),
            jax.ShapeDtypeStruct((max(heads, 8), seq), F32),
        ],
        compiler_params=pltpu.CompilerParams(vmem_limit_bytes=48 << 20),
        cost_estimate=pl.CostEstimate(flops=2 * 10**9, bytes_accessed=10**7, transcendentals=4 * 10**6),
        name="attention_forward",
    )(proj_t, cosine, sine, run8)


def attention_backward_call(
    heads, groups, head_dim, block, reach, proj_ref, rot_ref, cos_ref, sin_ref, run_ref, lse_ref, grad_ref, *refs
):
    attention_backward_kernel(
        heads, groups, head_dim, block, reach, head_dim**-0.5,
        lambda low, high, begin: grad_ref[low:high, begin : begin + block], lambda index: None,
        proj_ref, rot_ref, cos_ref, sin_ref, run_ref, lse_ref, *refs,
    )


def attention_backward(proj_t, rot_t, cosine, sine, run8, lse, grad_t, heads, groups, head_dim, block, reach):
    seq = proj_t.shape[1]
    return pl.pallas_call(
        functools.partial(attention_backward_call, heads, groups, head_dim, block, reach),
        out_shape=jax.ShapeDtypeStruct(proj_t.shape, BF16),
        scratch_shapes=[
            pltpu.VMEM((groups * head_dim, seq), F32),
            pltpu.VMEM((groups * head_dim, seq), F32),
        ],
        compiler_params=pltpu.CompilerParams(vmem_limit_bytes=48 << 20),
        cost_estimate=pl.CostEstimate(flops=5 * 10**9, bytes_accessed=10**7, transcendentals=4 * 10**6),
        name="attention_backward",
    )(proj_t, rot_t, cosine, sine, run8, lse, grad_t)


def ffn_kernel(norm_ref, cot_ref, gate_ref, up_ref, down_ref, out_ref, back_ref, acts_ref):
    @pl.when(pl.program_id(0) == 0)
    def _():
        out_ref[...] = jnp.zeros_like(out_ref)
        back_ref[...] = jnp.zeros_like(back_ref)

    normed, cot = norm_ref[...], cot_ref[...]
    gate_w, up_w, down_w = gate_ref[...], up_ref[...], down_ref[...]
    gate = mm(normed, gate_w, 1, 0)
    up = mm(normed, up_w, 1, 0)
    grad_act = mm(cot, down_w, 1, 1)
    sig = jax.nn.sigmoid(gate)
    silu = gate * sig
    act = (silu * up).astype(BF16)
    dgate = (grad_act * up * sig * (1.0 + gate * (1.0 - sig))).astype(BF16)
    dup = (grad_act * silu).astype(BF16)
    acts_ref[0] = dgate
    acts_ref[1] = dup
    acts_ref[2] = act
    out_ref[...] += mm(act, down_w, 1, 0)
    back_ref[...] += mm(dgate, gate_w, 1, 1) + mm(dup, up_w, 1, 1)


def feed_forward(normed, cot, gate_w, up_w, down_w, tile):
    rows, width = normed.shape
    hidden = gate_w.shape[1]
    whole = lambda i: (0, 0)
    return pl.pallas_call(
        ffn_kernel,
        grid=(hidden // tile,),
        in_specs=[
            pl.BlockSpec((rows, width), whole),
            pl.BlockSpec((rows, width), whole),
            pl.BlockSpec((width, tile), lambda i: (0, i)),
            pl.BlockSpec((width, tile), lambda i: (0, i)),
            pl.BlockSpec((tile, width), lambda i: (i, 0)),
        ],
        out_specs=[
            pl.BlockSpec((rows, width), whole),
            pl.BlockSpec((rows, width), whole),
            pl.BlockSpec((3, rows, tile), lambda i: (0, 0, i)),
        ],
        out_shape=[
            jax.ShapeDtypeStruct((rows, width), F32),
            jax.ShapeDtypeStruct((rows, width), F32),
            jax.ShapeDtypeStruct((3, rows, hidden), BF16),
        ],
        compiler_params=pltpu.CompilerParams(vmem_limit_bytes=48 << 20),
        cost_estimate=pl.CostEstimate(flops=6 * 2 * rows * width * hidden, bytes_accessed=3 * 10**7, transcendentals=rows * hidden),
        name="feed_forward",
    )(normed, cot, gate_w, up_w, down_w)


def digit_of(digit):
    axis_name, bit, size = digit
    return (lax.axis_index(axis_name) // (1 << bit)) % 2


def partner_of(digit):
    axis_name, bit, size = digit
    place = lax.axis_index(axis_name)
    return {axis_name: place + (1 - 2 * digit_of(digit)) * (1 << bit)}


def send_to(digit, source, target, send_sem, recv_sem):
    return pltpu.make_async_remote_copy(
        src_ref=source,
        dst_ref=target,
        send_sem=send_sem,
        recv_sem=recv_sem,
        device_id=partner_of(digit),
        device_id_type=pl.DeviceIdType.MESH,
    )


def greet(digits):
    barrier = pltpu.get_barrier_semaphore()
    for digit in digits:
        pl.semaphore_signal(
            barrier, inc=1, device_id=partner_of(digit), device_id_type=pl.DeviceIdType.MESH
        )
    pl.semaphore_wait(barrier, len(digits))


class Summer:
    def __init__(self, pieces):
        self.pieces = pieces
        self.count = len(pieces)
        for rows, cols, dtype, digits, order, gather in pieces:
            assert sorted(digits) == sorted(order) and (gather is None or list(digits) == list(order))

    def held(self, item):
        return list(self.pieces[item][5]) + list(self.pieces[item][4])

    def turns(self, item):
        return len(self.pieces[item][4]) + (0 if self.pieces[item][5] is None else len(self.held(item)))

    def out_shapes(self):
        return [
            jax.ShapeDtypeStruct((rows, cols) if gather is None else (1 << len(self.held(item)), rows, cols), F32)
            for item, (rows, cols, dtype, digits, order, gather) in enumerate(self.pieces)
        ]

    def scratch(self):
        shapes = []
        for item, (rows, cols, dtype, digits, order, gather) in enumerate(self.pieces):
            shapes.append(pltpu.VMEM((2,) * len(digits) + (rows, cols), dtype))
            for stage in range(len(order)):
                shapes.append(pltpu.VMEM((2,) * (len(order) - 1 - stage) + (rows, cols), dtype))
            if gather is not None:
                shapes.append(pltpu.VMEM((1 << len(self.held(item)), rows, cols), dtype))
        most = max(self.turns(item) for item in range(self.count))
        return shapes + [pltpu.SemaphoreType.DMA((self.count, most))] * 2

    def bind(self, outs, refs):
        self.outs, self.full, self.gots, self.alls = outs, [], [], []
        for rows, cols, dtype, digits, order, gather in self.pieces:
            self.full.append(refs[0])
            self.gots.append(refs[1 : 1 + len(order)])
            refs = refs[1 + len(order) :]
            if gather is not None:
                self.alls.append(refs[0])
                refs = refs[1:]
            else:
                self.alls.append(None)
        self.send_sem, self.recv_sem = refs

    def copy_of(self, item, stage):
        rows, cols, dtype, digits, order, gather = self.pieces[item]
        done, now = order[:stage], order[stage]
        index = tuple(
            digit_of(digit) if digit in done else 1 - digit_of(digit) if digit == now else slice(None)
            for digit in digits
        )
        return send_to(
            now,
            self.full[item].at[index],
            self.gots[item][stage],
            self.send_sem.at[item, stage],
            self.recv_sem.at[item, stage],
        )

    def place_of(self, digits):
        place = 0
        for digit in digits:
            place = place * 2 + digit_of(digit)
        return place

    def spread_of(self, item, stage):
        held = self.held(item)
        begin = self.place_of(held[: len(held) - stage]) * (1 << stage)
        region = self.alls[item].at[pl.ds(begin, 1 << stage)]
        turn = len(self.pieces[item][4]) + stage
        return send_to(
            held[len(held) - 1 - stage],
            region,
            region,
            self.send_sem.at[item, turn],
            self.recv_sem.at[item, turn],
        )

    def start(self, item):
        self.copy_of(item, 0).start()

    def advance(self, item, turn):
        rows, cols, dtype, digits, order, gather = self.pieces[item]
        if turn >= len(order):
            stage = turn - len(order)
            self.spread_of(item, stage).wait()
            if stage + 1 < len(self.held(item)):
                self.spread_of(item, stage + 1).start()
            else:
                self.outs[item][...] = self.alls[item][...].astype(F32)
            return
        self.copy_of(item, turn).wait()
        done, left = order[: turn + 1], [digit for digit in digits if digit not in order[: turn + 1]]
        for bits in itertools.product((0, 1), repeat=len(left)):
            index = tuple(
                digit_of(digit) if digit in done else bits[left.index(digit)] for digit in digits
            )
            value = self.full[item][index].astype(F32) + self.gots[item][turn][bits].astype(F32)
            if left:
                self.full[item][index] = value.astype(dtype)
            elif gather is None:
                self.outs[item][...] = value
            else:
                self.alls[item][self.place_of(self.held(item))] = value.astype(dtype)
        if left:
            self.copy_of(item, turn + 1).start()
        elif gather is not None:
            self.spread_of(item, 0).start()


def backward_kernel(plan, sizes, attention_count, ssd_count, ssd_outs, scratch_counts, *refs):
    query_heads, groups, head_dim, heads, ssd_dim, block, reach = sizes
    summer, partners, across, hooks = plan
    step = pl.program_id(0)
    steps = pl.num_programs(0)
    pieces = summer.count
    (acts, rows, mixer_ref, feature_ref, pair_ref), refs = refs[:5], refs[5:]
    attention_in, refs = refs[:attention_count], refs[attention_count:]
    ssd_in, refs = refs[:ssd_count], refs[ssd_count:]
    attention_out, refs = refs[:1], refs[1:]
    ssd_out, refs = refs[:ssd_outs], refs[ssd_outs:]
    part_out, refs = refs[:pieces], refs[pieces:]
    attention_scratch, refs = refs[: scratch_counts[0]], refs[scratch_counts[0] :]
    ssd_scratch, refs = refs[: scratch_counts[1]], refs[scratch_counts[1] :]
    (head_grad, pair_sem), refs = refs[:2], refs[2:]
    summer.bind(part_out, refs)
    branch_pos = digit_of(across)
    attn_rows = query_heads * head_dim

    def exchange():
        return send_to(
            across, pair_ref.at[1 - branch_pos], head_grad.at[branch_pos], pair_sem.at[0], pair_sem.at[1]
        )

    def own_pair():
        return pltpu.make_async_copy(
            pair_ref.at[branch_pos], head_grad.at[branch_pos], pair_sem.at[2]
        )

    def run(events):
        for item, turn in events:
            summer.advance(item, turn)

    @pl.when(step == 0)
    def _():
        own_pair().start()
        greet(partners)
        exchange().start()

    for item in range(3):
        @pl.when(step == item)
        def _():
            run(hooks.get((item, "begin"), ()))
            tile = 256
            right = rows[0]

            @pl.loop(0, acts.shape[2] // tile)
            def _(t):
                left = acts[0, :, pl.ds(pl.multiple_of(t * tile, tile), tile)]
                value = mm(left, right, 0, 0).astype(BF16)
                shape = summer.full[item].shape
                summer.full[item][t // 4, (t // 2) % 2, t % 2] = value.reshape(shape[3:])

            summer.start(item)

    @pl.when(step == 3)
    def _():
        run(hooks.get((3, "begin"), ()))
        tile = 256
        half = feature_ref.shape[0] // 2
        for part in range(2):
            right = feature_ref[part * half : (part + 1) * half]

            @pl.loop(0, mixer_ref.shape[1] // tile)
            def _(t):
                left = mixer_ref[:, pl.ds(pl.multiple_of(t * tile, tile), tile)]
                value = mm(left, right, 0, 1).astype(BF16)
                shape = summer.full[3].shape
                summer.full[3][part, t // 2, t % 2] = value.reshape(shape[3:])

        summer.start(3)

    @pl.when(step == 4)
    def _():
        exchange().wait()
        own_pair().wait()
        run(hooks.get((4, "begin"), ()))

        def grad_of(low, high, begin):
            width = head_grad.shape[2]
            return head_grad[begin // width, low:high, begin % width : begin % width + block]

        attention_backward_kernel(
            query_heads, groups, head_dim, block, reach, head_dim**-0.5,
            grad_of, lambda index: run(hooks.get((4, index), ())), *attention_in, *attention_out, *attention_scratch,
        )

    @pl.when(step > 4)
    def _():
        def hook(h):
            for (at_step, at_head), events in hooks.items():
                if at_head == h and at_step > 4:
                    @pl.when(step == at_step)
                    def _():
                        run(events)

        def grad_of(chunk, low, high):
            per = head_grad.shape[2] // block
            begin = pl.multiple_of((chunk % per) * block, block)
            return head_grad[chunk // per, attn_rows + low : attn_rows + high, pl.ds(begin, block)]

        ssd_backward_body(block, heads, ssd_dim, step - 5, steps - 5, hook, grad_of, *ssd_in, *ssd_out, *ssd_scratch)

    early = [event for events in hooks.values() for event in events]
    depth = max(summer.turns(item) for item in range(pieces))
    late = [
        (item, turn) for turn in range(depth) for item in range(pieces)
        if turn < summer.turns(item) and (item, turn) not in early
    ]

    @pl.when(step == steps - 1)
    def _():
        run(late)


def mixer_backward(acts, ffn_rows, grad_mixer, features, grad_pair, attention_args, ssd_args, entry, plan, sizes, collective_id):
    query_heads, groups, head_dim, heads, ssd_dim, block, reach = sizes
    summer = plan[0]
    mixer_t, vec_t, step_t, run8, run_col, tap_x, tap_b, head_cols, skip_col = ssd_args
    inner = mixer_t.shape[0] // 2
    seq = mixer_t.shape[1]
    vec = vec_t.shape[0]
    rows16 = step_t.shape[0]
    chunks = seq // block
    state_dim = vec // 2
    per = block // 128
    before = 5
    chunk_of = lambda i: jnp.minimum(chunks - 1 + before - i, chunks - 1)
    wide = lambda i: (0, chunk_of(i))
    whole = lambda i: (0, 0)
    proj_t = attention_args[0]
    once = pl.Buffered(1)
    ssd_in = [mixer_t, mixer_t, mixer_t, vec_t, vec_t, step_t, run8, run_col, tap_x, tap_b, head_cols, skip_col]
    ssd_in += [entry, run8]
    in_specs = [
        pl.BlockSpec((1,) + acts.shape[1:], lambda i: (jnp.minimum(i, 2), 0, 0), pipeline_mode=once),
        pl.BlockSpec((1,) + ffn_rows.shape[1:], lambda i: (jnp.minimum(i // 2, 1), 0, 0), pipeline_mode=once),
        pl.BlockSpec(grad_mixer.shape, whole, pipeline_mode=once),
        pl.BlockSpec(features.shape, whole, pipeline_mode=once),
        pl.BlockSpec(memory_space=pl.ANY),
    ]
    in_specs += [pl.BlockSpec(item.shape, whole, pipeline_mode=once) for item in attention_args]
    in_specs += ssd_specs(block, inner, vec, rows16, chunk_of)
    in_specs += [
        pl.BlockSpec((1, inner, state_dim), lambda i: (chunk_of(i), 0, 0)),
        pl.BlockSpec((8, 128), lambda i: (0, jnp.minimum(chunk_of(i) * per + per, chunks * per - 1))),
    ]
    ssd_out = [
        (2 * inner, seq, block, BF16),
        (vec, seq, block, BF16),
        (rows16, seq, block, F32),
        (rows16, seq, block, F32),
        (inner, 128, 128, F32),
        (vec, 128, 128, F32),
        (inner, 128, 128, F32),
    ]
    out_specs = [pl.BlockSpec(proj_t.shape, whole)]
    out_specs += [
        pl.BlockSpec((rows, width), wide if full == seq else whole) for rows, full, width, _ in ssd_out
    ]
    part_shapes = summer.out_shapes()
    out_specs += [pl.BlockSpec(item.shape, whole) for item in part_shapes]
    attention_scratch = [pltpu.VMEM((groups * head_dim, seq), F32)] * 2
    ssd_scratch = [
        pltpu.VMEM((inner, state_dim), F32),
        pltpu.VMEM((inner, 128), F32),
        pltpu.VMEM((vec, 128), F32),
        pltpu.VMEM((5, inner, 128), F32),
        pltpu.VMEM((5, vec, 128), F32),
        pltpu.VMEM((inner, 128), F32),
        pltpu.VMEM((inner, block), BF16),
        pltpu.VMEM((inner, block), BF16),
        pltpu.VMEM((rows16, block), F32),
        pltpu.VMEM((rows16, block), F32),
        pltpu.VMEM((rows16, block), F32),
        pltpu.VMEM((rows16, block), F32),
        pltpu.VMEM((rows16, state_dim), F32),
    ]
    results = pl.pallas_call(
        functools.partial(
            backward_kernel, plan, sizes, len(attention_args), len(ssd_in), len(ssd_out),
            (len(attention_scratch), len(ssd_scratch)),
        ),
        grid=(chunks + before,),
        in_specs=in_specs,
        out_specs=out_specs,
        out_shape=[jax.ShapeDtypeStruct(proj_t.shape, BF16)]
        + [jax.ShapeDtypeStruct((rows, full), dtype) for rows, full, _, dtype in ssd_out]
        + part_shapes,
        scratch_shapes=attention_scratch
        + ssd_scratch
        + [pltpu.VMEM(grad_pair.shape, BF16), pltpu.SemaphoreType.DMA((3,))]
        + summer.scratch(),
        compiler_params=pltpu.CompilerParams(
            vmem_limit_bytes=63 << 20, collective_id=collective_id, has_side_effects=True
        ),
        cost_estimate=pl.CostEstimate(flops=7 * 10**10, bytes_accessed=5 * 10**7, transcendentals=3 * 10**7),
        name="mixer_backward",
    )(acts, ffn_rows, grad_mixer, features, grad_pair, *attention_args, *ssd_in)
    return results[0], results[1:8], results[8:]

def final_kernel(plan, eps, *refs):
    summer, partners, across = plan
    names = ("normed", "dmixer", "dvec", "dqkv", "dstep", "mixer_w", "state_w", "qkv_w", "step_w", "rows", "hidden")
    hbm = dict(zip(names, refs[: len(names)]))
    gain_ref, own_ref, shared_ref = refs[len(names) : len(names) + 3]
    refs = refs[len(names) + 3 :]
    input_out, refs = refs[0], refs[1:]
    part_out, refs = refs[: summer.count], refs[summer.count :]
    vmem = dict(zip(names, refs[: len(names)]))
    refs = refs[len(names) :]
    partial, sent, got, load_sem, swap_sem = refs[:5]
    summer.bind(part_out, refs[5:])
    branch_pos = digit_of(across)
    half = partial.shape[0]
    inner = vmem["dmixer"].shape[0] // 2

    def load(name):
        return pltpu.make_async_copy(hbm[name], vmem[name], load_sem.at[names.index(name)])

    for name in ("dmixer", "mixer_w", "dvec", "state_w", "dqkv", "qkv_w", "dstep", "step_w", "normed", "rows", "hidden"):
        load(name).start()
    greet(partners)

    gain = gain_ref[...]

    def fill_rows(full, values):
        digits = len(full.shape) - 2
        for owner in range(values.shape[0]):
            full[tuple((owner >> (digits - 1 - place)) & 1 for place in range(digits))] = values[owner]

    own_item, shared_item = summer.count - 2, summer.count - 1
    fill_rows(summer.full[own_item], own_ref)
    summer.start(own_item)
    for name in ("dmixer", "mixer_w", "dvec", "state_w", "dqkv", "qkv_w", "dstep", "step_w"):
        load(name).wait()

    def partial_of(begin):
        at = pl.ds(pl.multiple_of(begin, 256), 256)
        return (
            mm(vmem["dmixer"][:, at], vmem["mixer_w"][...], 0, 1)
            + mm(vmem["dvec"][:, at], vmem["state_w"][...], 0, 1)
            + mm(vmem["dqkv"][:, at], vmem["qkv_w"][...], 0, 1)
            + mm(vmem["dstep"][:, at].astype(BF16), vmem["step_w"][...], 0, 1)
        )

    def swap():
        return send_to(across, sent, got, swap_sem.at[0], swap_sem.at[1])

    @pl.loop(0, half // 256)
    def _(t):
        sent[pl.ds(pl.multiple_of(t * 256, 256), 256)] = partial_of((1 - branch_pos) * half + t * 256).astype(BF16)

    swap().start()
    load("normed").wait()
    tile = 256
    for item, begin in ((0, 0), (1, inner)):
        @pl.loop(0, vmem["normed"].shape[1] // tile)
        def _(t):
            left = vmem["normed"][:, pl.ds(pl.multiple_of(t * tile, tile), tile)]
            value = mm(left, vmem["dmixer"][begin : begin + inner], 0, 1).astype(BF16)
            shape = summer.full[item].shape
            summer.full[item][t // 2, t % 2] = value.reshape(shape[2:])

        summer.start(item)

    @pl.loop(0, vmem["normed"].shape[1] // tile)
    def _(t):
        left = vmem["normed"][:, pl.ds(pl.multiple_of(t * tile, tile), tile)]
        value = mm(left, vmem["dvec"][...], 0, 1).astype(BF16)
        summer.full[3][t // 2, t % 2] = value.reshape(summer.full[3].shape[2:])
        columns = vmem["dqkv"].shape[0]
        value = mm(left, vmem["dqkv"][...], 0, 1).astype(BF16)
        summer.full[2][t // 2, t % 2, :, :, :, :columns] = value.reshape(summer.full[2].shape[2:5] + (columns,))
        value = mm(left, vmem["dstep"][...].astype(BF16), 0, 1).astype(BF16)
        summer.full[2][t // 2, t % 2, :, :, :, columns:] = value.reshape(summer.full[2].shape[2:5] + (-1,))

    summer.start(3)
    summer.start(2)
    summer.advance(own_item, 0)

    def gain_sum(tokens, begin):
        return jnp.sum(
            tokens * vmem["normed"][pl.ds(pl.multiple_of(begin, 256), 256)].astype(F32), axis=0, keepdims=True
        )

    total = jnp.zeros((1, partial.shape[1]), F32)
    for t in range(half // 256):
        rows = slice(t * 256, (t + 1) * 256)
        total = total + gain_sum(sent[rows].astype(F32), (1 - branch_pos) * half + t * 256)
    summer.advance(0, 0)
    for t in range(half // 256):
        rows = slice(t * 256, (t + 1) * 256)
        begin = branch_pos * half + t * 256
        value = partial_of(begin)
        partial[rows] = value
        total = total + gain_sum(value, begin)
        summer.advance(1 - t if t < 1 else 3, 0)
    total = total / gain
    shared = summer.full[shared_item]
    fill_rows(shared, shared_ref)
    digits = len(shared.shape) - 2
    for row in range(total.shape[1] // 128):
        shared[tuple((row >> (digits - 1 - place)) & 1 for place in range(digits))] = total[:, row * 128 : (row + 1) * 128]
    summer.start(shared_item)
    early = [(own_item, 0), (0, 0), (1, 0), (3, 0)]

    depth = max(summer.turns(item) for item in range(summer.count))
    events = [
        (item, turn) for turn in range(depth) for item in (5, 3, 4, 2, 0, 1)
        if turn < summer.turns(item) and (item, turn) not in early
    ]
    cut = len(events) // 2
    for item, turn in events[:cut]:
        summer.advance(item, turn)
    load("rows").wait()
    load("hidden").wait()
    swap().wait()

    @pl.loop(0, half // 64)
    def _(t):
        rows = pl.ds(pl.multiple_of(t * 64, 64), 64)
        values = vmem["rows"][rows].astype(F32)
        scale = lax.rsqrt(jnp.mean(values * values, axis=1, keepdims=True) + eps)
        weighted = (partial[rows].astype(BF16).astype(F32) + got[rows].astype(F32)) * gain
        centre = jnp.mean(weighted * values, axis=1, keepdims=True)
        result = vmem["hidden"][rows] + scale * weighted - values * (scale * scale * scale * centre)
        input_out[rows] = result.astype(BF16)

    for item, turn in events[cut:]:
        summer.advance(item, turn)


def final_gradients(arrays, gain, own_part, shared, plan, eps, collective_id):
    summer = plan[0]
    half, width = arrays[9].shape
    vmem = pl.BlockSpec(memory_space=pltpu.VMEM)
    results = pl.pallas_call(
        functools.partial(final_kernel, plan, eps),
        in_specs=[pl.BlockSpec(memory_space=pl.ANY)] * len(arrays) + [vmem] * 3,
        out_specs=[vmem] * (1 + summer.count),
        out_shape=[jax.ShapeDtypeStruct((half, width), BF16)] + summer.out_shapes(),
        scratch_shapes=[pltpu.VMEM(item.shape, item.dtype) for item in arrays]
        + [
            pltpu.VMEM((half, width), F32),
            pltpu.VMEM((half, width), BF16),
            pltpu.VMEM((half, width), BF16),
            pltpu.SemaphoreType.DMA((len(arrays),)),
            pltpu.SemaphoreType.DMA((2,)),
        ]
        + summer.scratch(),
        compiler_params=pltpu.CompilerParams(
            vmem_limit_bytes=60 << 20, collective_id=collective_id, has_side_effects=True
        ),
        cost_estimate=pl.CostEstimate(flops=3 * 10**10, bytes_accessed=5 * 10**7, transcendentals=0),
        name="final_gradients",
    )(*arrays, gain.reshape(1, width), own_part, shared)
    return results[0], results[1:]


def bits_of(count):
    return count.bit_length() - 1


def swap_halves(values, axis_name, bit, size):
    pairs = [(item, item ^ (1 << bit)) for item in range(size)]
    return lax.ppermute(values, axis_name, pairs)


def halve(values, place, my_bit, axis_name, bit, size):
    owners = values.shape[0]
    high = 1 << place
    parts = values.reshape((high, 2, owners // (2 * high)) + values.shape[1:])
    sent = lax.dynamic_index_in_dim(parts, 1 - my_bit, 1, keepdims=False)
    kept = lax.dynamic_index_in_dim(parts, my_bit, 1, keepdims=False)
    got = swap_halves(sent, axis_name, bit, size)
    total = (kept.astype(jnp.float32) + got.astype(jnp.float32)).astype(values.dtype)
    return total.reshape((owners // 2,) + values.shape[1:])


def scatter_sum(values, digits, order):
    left = list(digits)
    for digit in order:
        axis_name, bit, size = digit
        my_bit = (lax.axis_index(axis_name) >> bit) & 1
        values = halve(values, left.index(digit), my_bit, axis_name, bit, size)
        left.remove(digit)
    return values[0]


def gather_all(values, digits, order):
    values = values[None]
    left = []
    for digit in order:
        axis_name, bit, size = digit
        my_bit = (lax.axis_index(axis_name) >> bit) & 1
        got = swap_halves(values, axis_name, bit, size)
        place = sum(1 for item in left if digits.index(item) < digits.index(digit))
        high = 1 << place
        owners = values.shape[0]
        mine = values.reshape((high, 1, owners // high) + values.shape[1:])
        other = got.reshape(mine.shape)
        first = jnp.where(my_bit == 0, mine, other)
        second = jnp.where(my_bit == 0, other, mine)
        values = jnp.concatenate([first, second], axis=1).reshape((owners * 2,) + values.shape[1:])
        left.append(digit)
    return values


def other_branch(values):
    return lax.ppermute(values, "branch", [(0, 1), (1, 0)])


def rms_scale(values):
    return lax.rsqrt(jnp.mean(values * values, axis=-1, keepdims=True) + EPSILON)


def rms_back(upstream, values, scales, gain):
    weighted = upstream * gain
    return scales * weighted - values * scales**3 * jnp.mean(
        weighted * values, axis=-1, keepdims=True
    )


def token_runs(length_row, seq_len, doc_count):
    order = jnp.arange(doc_count, dtype=jnp.int32)
    ends = jnp.sum(jnp.where(order[:, None] >= order[None, :], length_row[None, :], 0), axis=1)
    places = jnp.arange(seq_len, dtype=jnp.int32)
    passed = places[:, None] >= ends[None, :]
    starts = jnp.sum(jnp.where(passed, length_row[None, :], 0), axis=1)
    return (places - starts).astype(F32), jnp.sum(length_row)


def join(mine, other, branch_pos, axis):
    return jnp.concatenate(
        [jnp.where(branch_pos == 0, mine, other), jnp.where(branch_pos == 0, other, mine)], axis=axis
    )


def both_weights(weight, core, branch_pos):
    half = weight.shape[0] // 2
    my_core = lax.axis_index("rows") & 1
    sent = lax.dynamic_slice_in_dim(weight, my_core * half, half, 0)
    got = other_branch(sent)
    rest = swap_halves(got, *core)
    other = jnp.concatenate(
        [jnp.where(my_core == 0, got, rest), jnp.where(my_core == 0, rest, got)], axis=0
    )
    return join(weight, other, branch_pos, 0)


def columns_of(items, rows):
    stacked = jnp.stack(items, axis=1)
    return jnp.pad(stacked, ((0, rows - stacked.shape[0]), (0, 128 - stacked.shape[1])))


def per_device(
    inputs,
    lengths,
    norm_gain,
    query_weight,
    keyval_weight,
    mixer_weight,
    state_weight,
    step_weight,
    conv_mixer,
    conv_state,
    bias_mixer,
    bias_state,
    step_bias,
    decay_log,
    skip_gain,
    ssd_gain,
    attn_output,
    ssd_output,
    ffn_gain,
    gate_weight,
    up_weight,
    down_weight,
    cotangent,
):
    branch_pos = lax.axis_index("branch")
    row_pos = lax.axis_index("rows")
    row_count = lax.axis_size("rows")
    row_bits = bits_of(row_count)
    row_digits = [("rows", bit, row_count) for bit in range(row_bits - 1, -1, -1)]
    across = ("branch", 0, 2)
    core = row_digits[-1]
    chip_digits = row_digits[:-1]
    near, others = chip_digits[-1], chip_digits[:-1][::-1]
    partners = [across] + row_digits
    fast = row_bits == 4

    own_rows = inputs[0].astype(F32)
    upstream = cotangent[0]
    half_len, model_dim = own_rows.shape
    seq_len = 2 * half_len
    local_query = query_weight.shape[1] // HD
    local_keyval = keyval_weight.shape[2] // HD
    local_heads = step_bias.shape[0]
    local_inner = bias_mixer.shape[0]
    inner_dim = 2 * local_inner
    head_rows = -(-local_heads // 8) * 8
    own_begin = branch_pos * half_len

    run, used = token_runs(lengths[0], seq_len, lengths.shape[1])
    run8 = jnp.broadcast_to(run[None, :], (8, seq_len))
    run_col = jnp.broadcast_to(run[:, None], (seq_len, 128))
    frequency = ROPE_BASE ** (-(jnp.arange(HD // 2, dtype=F32) * 2.0) / HD)
    angles = frequency[:, None] * run[None, :]
    cosine, sine = jnp.cos(angles), jnp.sin(angles)
    own_valid = (own_begin + jnp.arange(half_len, dtype=jnp.int32) < used).astype(F32)[:, None]

    own_scale = rms_scale(own_rows)
    own_hat = own_rows * own_scale
    normed = (own_hat * norm_gain).astype(BF16)
    full_normed = join(normed, other_branch(normed), branch_pos, 0)

    out_weight = jnp.concatenate([attn_output, ssd_output], axis=0)
    out_full = both_weights(out_weight, core, branch_pos)
    gain_full = join(ssd_gain, other_branch(ssd_gain), branch_pos, 0)

    qkv_flat = jnp.concatenate([query_weight, keyval_weight.reshape(model_dim, -1)], axis=1)
    mixer_flat = mixer_weight.reshape(model_dim, -1)
    state_flat = state_weight.reshape(model_dim, -1)
    step_flat = jnp.pad(step_weight, ((0, 0), (0, head_rows - local_heads)))

    mixer_t = mm(mixer_flat, full_normed, 0, 1).astype(BF16)
    vec_t = mm(state_flat, full_normed, 0, 1).astype(BF16)
    qkv_t = mm(qkv_flat, full_normed, 0, 1).astype(BF16)
    step_t = mm(step_flat, full_normed, 0, 1)

    taps = [conv_mixer[item] for item in range(4)] + [bias_mixer]
    tap_x = columns_of(taps, local_inner)
    state_taps = [conv_state[item].reshape(-1) for item in range(4)] + [bias_state.reshape(-1)]
    tap_b = columns_of(state_taps, state_flat.shape[1])
    rates = -jnp.exp(decay_log)
    head_cols = columns_of([step_bias, rates], head_rows)
    skip_col = jnp.broadcast_to(jnp.repeat(skip_gain, SP)[:, None], (local_inner, 128))
    ssd_args = (mixer_t, vec_t, step_t, run8, run_col, tap_x, tap_b, head_cols, skip_col)

    gated_t, entry = ssd_forward(*ssd_args, local_heads, SP, BLOCK)
    attn_t, rot_t, log_sums = attention_forward(
        qkv_t, cosine, sine, run8, local_query, local_keyval, HD, BLOCK, REACH
    )

    def own_tokens(values, pos):
        return lax.dynamic_slice_in_dim(values, pos * half_len, half_len, 1)

    def to_owner(values):
        got = other_branch(own_tokens(values, 1 - branch_pos))
        mine = own_tokens(values, branch_pos)
        return jnp.where(branch_pos == 0, mine, got), jnp.where(branch_pos == 0, got, mine)

    def to_heads(first, second):
        got = other_branch(jnp.where(branch_pos == 0, second, first))
        return join(jnp.where(branch_pos == 0, first, second), got, branch_pos, 1)

    gated_pair = to_owner(gated_t)
    attn_pair = to_owner(attn_t)
    attn_rows = attn_t.shape[0]
    part_rows = attn_rows + local_inner

    raw = jnp.stack(
        [jnp.concatenate([first, second], axis=0) for first, second in zip(attn_pair, gated_pair)]
    )
    scanned_rows = (jnp.arange(part_rows) >= attn_rows)[None, :, None]
    gains = jnp.pad(gain_full.reshape(2, local_inner), ((0, 0), (attn_rows, 0)))[:, :, None]
    raw_values = raw.astype(F32)
    square_sum = jnp.sum(jnp.where(scanned_rows, raw_values * raw_values, 0.0), axis=(0, 1))
    gated_scale = lax.rsqrt(square_sum / inner_dim + EPSILON)[None, None, :]
    features = jnp.where(scanned_rows, (raw_values * gated_scale * gains).astype(BF16), raw)
    features = features.reshape(2 * part_rows, half_len)
    mixer_sum = mm(features, out_full, 0, 0)
    hidden = own_rows + own_valid * mixer_sum
    hidden_scale = rms_scale(hidden)
    hidden_hat = hidden * hidden_scale
    normed_ffn = (hidden_hat * ffn_gain).astype(BF16)

    ffn_out, grad_normed_ffn, acts = feed_forward(
        normed_ffn, upstream, gate_weight, up_weight, down_weight, 256
    )
    block_out = (hidden + ffn_out).astype(BF16)[None]
    grad_hidden = upstream.astype(F32) + rms_back(grad_normed_ffn, hidden, hidden_scale, ffn_gain)
    ffn_gain_grad = jnp.sum(grad_normed_ffn * hidden_hat, axis=0)
    grad_mixer = (own_valid * grad_hidden).astype(BF16)

    grad_features = mm(out_full, grad_mixer, 1, 1).reshape(2, part_rows, half_len)
    ssd_gain_wgrad = jnp.sum(grad_features * raw_values * gated_scale, axis=2)[:, attn_rows:].reshape(-1)
    weighted = grad_features * gains
    row_inner = jnp.sum(weighted * raw_values, axis=(0, 1), keepdims=True) / inner_dim
    grad_pair = jnp.where(
        scanned_rows,
        gated_scale * weighted - raw_values * (gated_scale**3 * row_inner),
        grad_features,
    ).astype(BF16)

    all_digits = [across] + row_digits
    attention_args = (qkv_t, rot_t, cosine, sine, run8, log_sums)
    ffn_rows = jnp.stack([normed_ffn, upstream])
    qkv_cols = qkv_t.shape[0]
    query_cols = local_query * HD
    if fast:
        x, y, z0, z1 = across, near, others[0], others[1]
        orders = [[core, y, x, z0, z1], [core, x, y, z0, z1], [core, z0, z1, y, x], [core, y, x, z0, z1]]
        part_row = gate_weight.shape[1] // (2 * row_count)
        summer = Summer([(part_row, model_dim, BF16, all_digits, order, None) for order in orders])
        hooks = {
            (3, "begin"): [(0, 0), (1, 0)],
            (4, "begin"): [(2, 0)],
            (4, 1): [(3, 0)],
            (6, 0): [(0, 1)],
            (6, 5): [(2, 1)],
            (6, 8): [(1, 1)],
            (7, 9): [(3, 1)],
            (7, 11): [(0, 2)],
            (8, 6): [(1, 2)],
            (8, 8): [(0, 3)],
        }
        dqkv_t, ssd_grads, ffn_sums = mixer_backward(
            acts,
            ffn_rows,
            grad_mixer,
            features,
            grad_pair,
            attention_args,
            ssd_args,
            entry,
            (summer, partners, across, hooks),
            (local_query, local_keyval, HD, local_heads, SP, BLOCK, REACH),
            1,
        )
        gate_sum, up_sum, down_sum, out_sum = ffn_sums
    else:
        got = other_branch(grad_pair[1 - branch_pos])
        head_grad = join(grad_pair[branch_pos], got, branch_pos, 1)
        ssd_grads = ssd_backward(*ssd_args, entry, head_grad[attn_rows:], local_heads, SP, BLOCK)
        dqkv_t = attention_backward(
            *attention_args, head_grad[:attn_rows], local_query, local_keyval, HD, BLOCK, REACH
        )
        gate_sum, up_sum, down_sum = [
            scatter_sum(
                mm(acts[item], ffn_rows[item // 2], 0, 0).astype(BF16).reshape(2 * row_count, -1, model_dim),
                all_digits,
                all_digits[::-1],
            ).astype(F32)
            for item in range(3)
        ]
        out_part = mm(grad_mixer, features, 0, 1).astype(BF16).reshape(row_count, -1, 2, part_rows)
        out_part = jnp.moveaxis(out_part, 2, 0).reshape(2 * row_count, -1, part_rows)
        out_sum = scatter_sum(out_part, all_digits, all_digits[::-1]).astype(F32)
    dmixer_t, dvec_t, dstep_t, dlog_t, dtap_x, dtap_b, dskip = ssd_grads

    def widen(values):
        full = jnp.zeros((2, 1, 64), F32)
        padded = jnp.pad(values, (0, 64 - local_heads))[None, None]
        return lax.dynamic_update_slice(full, padded, (branch_pos, 0, 0)).reshape(1, 128)

    heads = slice(0, local_heads)
    shared = jnp.concatenate(
        [
            jnp.zeros((model_dim // 128, 128), F32),
            ffn_gain_grad.reshape(-1, 128),
            dtap_b[:, :4].T.reshape(-1, 128),
            dtap_b[:, 4].reshape(-1, 128),
            widen(jnp.sum(dstep_t[heads], axis=1)),
            widen(jnp.sum(dlog_t[heads], axis=1) * rates),
            widen(jnp.sum(dskip[:, 0].reshape(local_heads, SP), axis=1)),
        ],
        axis=0,
    )
    shared_rows = -(-shared.shape[0] // (2 * row_count))
    shared = jnp.pad(shared, ((0, 2 * row_count * shared_rows - shared.shape[0]), (0, 0)))
    shared = shared.reshape(2 * row_count, shared_rows, 128)
    own_width = local_inner // row_count
    own_gain = lax.dynamic_slice_in_dim(ssd_gain_wgrad, branch_pos * local_inner, local_inner, 0)
    other_gain = lax.dynamic_slice_in_dim(
        ssd_gain_wgrad, (1 - branch_pos) * local_inner, local_inner, 0
    )
    own_gain = own_gain + other_branch(other_gain)
    own_part = jnp.concatenate([dtap_x[:, :5].T, own_gain[None]], axis=0)
    own_part = jnp.swapaxes(own_part.reshape(6, row_count, own_width), 0, 1)
    own_part = jnp.pad(own_part, ((0, 0), (0, 2), (0, 128 - own_width)))

    qkv_step_cols = qkv_cols + head_rows
    gather_digits = [core, near] + others + [across]
    if fast:
        row_part = model_dim // row_count
        first = [core, near] + others
        second = [core] + others + [near]
        summer = Summer(
            [
                (row_part, local_inner, BF16, row_digits, first, None),
                (row_part, local_inner, BF16, row_digits, second, None),
                (row_part, qkv_step_cols, BF16, row_digits, first, None),
                (row_part // 2, state_flat.shape[1], BF16, gather_digits, gather_digits, []),
                own_part.shape[1:] + (F32, row_digits, first, None),
                shared.shape[1:] + (F32, gather_digits, gather_digits, []),
            ]
        )
        arrays = [
            full_normed, dmixer_t, dvec_t, dqkv_t, dstep_t,
            mixer_flat, state_flat, qkv_flat, step_flat, inputs[0], grad_hidden,
        ]
        input_grad, sums = final_gradients(
            arrays, norm_gain, own_part, shared, (summer, partners, across), EPSILON, 2
        )
        gate_in_sum, mixer_in_sum, qkvs_sum, state_sum, own_sum, flat_sum = sums
        mixer_wsum = jnp.stack([gate_in_sum, mixer_in_sum], axis=1)
    else:
        dstep_low = dstep_t.astype(BF16)
        partial_normed = (
            mm(dmixer_t, mixer_flat, 0, 1)
            + mm(dvec_t, state_flat, 0, 1)
            + mm(dqkv_t, qkv_flat, 0, 1)
            + mm(dstep_low, step_flat, 0, 1)
        ).astype(BF16)
        sent = lax.dynamic_slice_in_dim(partial_normed, (1 - branch_pos) * half_len, half_len, 0)
        kept = lax.dynamic_slice_in_dim(partial_normed, own_begin, half_len, 0)
        own_grad_normed = kept.astype(F32) + other_branch(sent).astype(F32)
        input_grad = grad_hidden + rms_back(own_grad_normed, own_rows, own_scale, norm_gain)
        input_grad = input_grad.astype(BF16)
        gain_part = jnp.sum(partial_normed.astype(F32) * full_normed.astype(F32), axis=0) / norm_gain
        shared = shared.reshape(-1, 128).at[: model_dim // 128].set(gain_part.reshape(-1, 128)).reshape(shared.shape)

        def row_sum(grads_t):
            value = mm(full_normed, grads_t, 0, 1).astype(BF16)
            value = value.reshape((row_count, -1) + value.shape[1:])
            return scatter_sum(value, row_digits, row_digits[::-1]).astype(F32)

        mixer_wsum = row_sum(dmixer_t)
        qkvs_sum = row_sum(jnp.concatenate([dqkv_t, dstep_low], axis=0))
        own_sum = scatter_sum(own_part, row_digits, row_digits[::-1])

        def everywhere(value):
            value = scatter_sum(value, gather_digits, gather_digits)
            return gather_all(value, gather_digits, gather_digits[::-1])

        state_part = mm(full_normed, dvec_t, 0, 1).astype(BF16)
        state_sum = everywhere(state_part.reshape(2 * row_count, -1, state_part.shape[1])).astype(F32)
        flat_sum = everywhere(shared)
    flat_sum = flat_sum.reshape(-1, 128)
    gain_rows = model_dim // 128
    tap_rows = 4 * state_flat.shape[1] // 128
    bias_rows = state_flat.shape[1] // 128
    head_begin = 2 * gain_rows + tap_rows + bias_rows

    def rows_of(begin, size, shape):
        return flat_sum[begin : begin + size].reshape(shape)

    def head_values(item):
        pair = flat_sum[head_begin + item].reshape(2, 64)
        return pair[:, :local_heads].reshape(-1)

    state_sum = state_sum.reshape(state_weight.shape)
    return (
        block_out,
        input_grad[None],
        rows_of(0, gain_rows, norm_gain.shape),
        qkvs_sum[:, :query_cols],
        qkvs_sum[:, query_cols:qkv_cols].reshape((-1,) + keyval_weight.shape[1:]),
        mixer_wsum.reshape((-1,) + mixer_weight.shape[1:]),
        state_sum,
        qkvs_sum[:, qkv_cols : qkv_cols + local_heads],
        own_sum[:4, :own_width],
        rows_of(2 * gain_rows, tap_rows, conv_state.shape),
        own_sum[4, :own_width],
        rows_of(2 * gain_rows + tap_rows, bias_rows, bias_state.shape),
        head_values(0),
        head_values(1),
        head_values(2),
        own_sum[5, :own_width],
        out_sum[:, :attn_rows].T,
        out_sum[:, attn_rows:].T,
        rows_of(gain_rows, gain_rows, ffn_gain.shape),
        gate_sum.T,
        up_sum.T,
        down_sum,
    )


def solution(mesh):
    in_specs = (
        P("rows", "branch", None),
        P("rows", None),
        P(),
        P(None, "branch"),
        P(None, None, "branch"),
        P(None, None, "branch"),
        P(),
        P(None, "branch"),
        P(None, "branch"),
        P(),
        P("branch"),
        P(),
        P("branch"),
        P("branch"),
        P("branch"),
        P("branch"),
        P("branch", None),
        P("branch", None),
        P(),
        P(),
        P(),
        P(),
        P("rows", "branch", None),
    )
    out_specs = (
        P("rows", "branch", None),
        P("rows", "branch", None),
        P(),
        P("rows", "branch"),
        P("rows", None, "branch"),
        P("rows", None, "branch"),
        P(),
        P("rows", "branch"),
        P(None, ("branch", "rows")),
        P(),
        P(("branch", "rows")),
        P(),
        P(),
        P(),
        P(),
        P(("branch", "rows")),
        P("branch", "rows"),
        P("branch", "rows"),
        P(),
        P(None, ("branch", "rows")),
        P(None, ("branch", "rows")),
        P(("branch", "rows"), None),
    )
    return jax.shard_map(
        per_device, mesh=mesh, in_specs=in_specs, out_specs=out_specs, check_vma=False
    )
```

```python
import functools
import itertools

import jax
import jax.numpy as jnp
from jax import lax
from jax.experimental import pallas as pl
from jax.experimental.pallas import tpu as pltpu
from jax.sharding import PartitionSpec as P

HD = 64
SH = 24
SP = 64
BLOCK = 256
REACH = 512
EPSILON = 1e-05
ROPE_BASE = 100000000000.0
F32 = jnp.float32
BF16 = jnp.bfloat16
PRECISE = lax.Precision.HIGHEST


def mm(left, right, left_dim, right_dim):
    return lax.dot_general(
        left, right, (((left_dim,), (right_dim,)), ((), ())), preferred_element_type=F32
    )


def mm_exact(left, right):
    return jnp.dot(left, right, preferred_element_type=F32, precision=PRECISE)


def shift_right(prev, cur, amount):
    joined = jnp.concatenate([prev, cur], axis=1)
    return pltpu.roll(joined, amount, 1)[:, prev.shape[1] :]


def shift_left(cur, after, amount):
    joined = jnp.concatenate([cur, after], axis=1)
    total = joined.shape[1]
    return pltpu.roll(joined, total - amount, 1)[:, : cur.shape[1]]


def conv_inputs(prev_ref, cur_ref, rows, run_row, is_first):
    cur = cur_ref[rows].astype(F32)
    prev = jnp.where(is_first, 0.0, prev_ref[rows].astype(F32))
    moved = [
        shift_right(prev, cur, offset) * (run_row >= float(offset)).astype(F32) for offset in (3, 2, 1)
    ]
    return moved + [cur]


def conv_rows(items, taps):
    result = taps[:, 4:5] + taps[:, 3:4] * items[3]
    for place in range(3):
        result = result + taps[:, place : place + 1] * items[place]
    return result


def step_rows(step_ref, head_ref):
    raw = step_ref[...] + head_ref[:, 0:1]
    return raw, jax.nn.softplus(raw)


def masks_of(run_col, block):
    rows = lax.broadcasted_iota(jnp.int32, (block, block), 0)
    cols = lax.broadcasted_iota(jnp.int32, (block, block), 1)
    gap = (rows - cols).astype(F32)
    return (gap >= 0.0) & (gap <= run_col)


def upper_ones(block):
    rows = lax.broadcasted_iota(jnp.int32, (block, block), 0)
    cols = lax.broadcasted_iota(jnp.int32, (block, block), 1)
    return (rows <= cols).astype(F32)


def ssd_forward_kernel(
    block, heads, head_dim,
    z_ref, x_ref, xp_ref, b_ref, bp_ref, step_ref, run_ref, runc_ref, tapx_ref, tapb_ref, head_ref, skip_ref,
    gated_ref, entry_ref,
    state, xdt,
):
    index = pl.program_id(0)
    is_first = index == 0

    @pl.when(is_first)
    def _():
        state[...] = jnp.zeros_like(state)

    run_row = run_ref[0:1, :]
    everything = slice(0, b_ref.shape[0])
    vec = conv_rows(conv_inputs(bp_ref, b_ref, everything, run_row, is_first), tapb_ref[...])
    vec = vec * jax.nn.sigmoid(vec)
    size = vec.shape[0] // 2
    in_low = vec[:size].astype(BF16)
    out_low = vec[size:].astype(BF16)
    raw, step = step_rows(step_ref, head_ref)
    rate = head_ref[:, 1:2]
    cum = mm_exact(step * rate, upper_ones(block))
    cum_col = jnp.transpose(cum)
    place = lax.broadcasted_iota(jnp.int32, (1, block), 1).astype(F32)
    carried = (run_row >= place + 1.0).astype(F32)
    last_run = run_row[:, block - 1 :]
    tail = (float(block - 1) - place <= last_run).astype(F32)
    last = cum[:, block - 1 :]
    entry = jnp.exp(cum) * carried
    to_end = jnp.exp(last - cum) * tail
    keep = jnp.exp(last) * carried[:, block - 1 :]
    allowed = masks_of(runc_ref[:, 0:1], block)
    cross = jnp.where(allowed, mm(out_low, in_low, 0, 0), 0.0)
    old = state[...]
    old_low = old.astype(BF16)
    entry_ref[0] = old_low
    for h in range(heads):
        rows = slice(h * head_dim, (h + 1) * head_dim)
        act = conv_rows(conv_inputs(xp_ref, x_ref, rows, run_row, is_first), tapx_ref[rows])
        act = act * jax.nn.sigmoid(act)
        part = act * step[h : h + 1]
        part_low = part.astype(BF16)
        decay = jnp.exp(jnp.minimum(cum_col[:, h : h + 1] - cum[h : h + 1], 0.0))
        weight = (cross * decay).astype(BF16)
        y_in = mm(part_low, weight, 1, 1)
        y_off = mm(old_low[rows], out_low, 1, 0)
        y_all = y_in + y_off * entry[h : h + 1] + skip_ref[rows, 0:1] * act
        gate = z_ref[rows].astype(F32)
        gated_ref[rows] = (y_all * gate * jax.nn.sigmoid(gate)).astype(gated_ref.dtype)
        xdt[rows] = (part * to_end[h : h + 1]).astype(BF16)
        state[rows] = old[rows] * keep[h : h + 1]
    state[...] += mm(xdt[...], in_low, 1, 1)


def ssd_backward_kernel(block, heads, head_dim, *refs):
    grad_ref = refs[13]
    ssd_backward_body(
        block, heads, head_dim, pl.program_id(0), pl.num_programs(0), lambda h: None,
        lambda chunk, low, high: grad_ref[low:high], *refs[:13], *refs[14:],
    )


def ssd_backward_body(
    block, heads, head_dim, index, count, hook, grad_of,
    z_ref, x_ref, xp_ref, b_ref, bp_ref, step_ref, run_ref, runc_ref, tapx_ref, tapb_ref, head_ref, skip_ref,
    entry_ref, runn_ref,
    dm_ref, db_ref, dstep_ref, drate_ref, dtapx_ref, dtapb_ref, dskip_ref,
    dstate, nextx, nextb, accx, accb, accs, xdt, dye, rowterm, colin, colst, direct, ystat,
):
    is_first = index == count - 1

    @pl.when(index == 0)
    def _():
        dstate[...] = jnp.zeros_like(dstate)
        nextx[...] = jnp.zeros_like(nextx)
        nextb[...] = jnp.zeros_like(nextb)
        accx[...] = jnp.zeros_like(accx)
        accb[...] = jnp.zeros_like(accb)
        accs[...] = jnp.zeros_like(accs)
        rowterm[...] = jnp.zeros_like(rowterm)
        colin[...] = jnp.zeros_like(colin)
        colst[...] = jnp.zeros_like(colst)
        direct[...] = jnp.zeros_like(direct)
        ystat[...] = jnp.zeros_like(ystat)

    run_row = run_ref[0:1, :]
    everything = slice(0, b_ref.shape[0])
    items_b = conv_inputs(bp_ref, b_ref, everything, run_row, is_first)
    convb = conv_rows(items_b, tapb_ref[...])
    sigb = jax.nn.sigmoid(convb)
    vec = convb * sigb
    size = vec.shape[0] // 2
    in_low = vec[:size].astype(BF16)
    out_low = vec[size:].astype(BF16)
    raw, step = step_rows(step_ref, head_ref)
    rate = head_ref[:, 1:2]
    upper = upper_ones(block)
    cum = mm_exact(step * rate, upper)
    cum_col = jnp.transpose(cum)
    place = lax.broadcasted_iota(jnp.int32, (1, block), 1).astype(F32)
    carried = (run_row >= place + 1.0).astype(F32)
    last_run = run_row[:, block - 1 :]
    tail = (float(block - 1) - place <= last_run).astype(F32)
    last = cum[:, block - 1 :]
    entry = jnp.exp(cum) * carried
    to_end = jnp.exp(last - cum) * tail
    keep = jnp.exp(last) * carried[:, block - 1 :]
    allowed = masks_of(runc_ref[:, 0:1], block)
    cross = jnp.where(allowed, mm(out_low, in_low, 0, 0), 0.0)
    old_low = entry_ref[0]
    dnew_low = dstate[...].astype(BF16)
    inner = xdt.shape[0]
    y_off = mm(old_low, out_low, 1, 0)
    u_off = mm(dnew_low, in_low, 1, 0)

    def conv_back(dvals, conv, sigm, items, taps, rows, after, acc, out_ref, out_rows):
        dconv = dvals * sigm * (1.0 + conv * (1.0 - sigm))

        def add(place, values):
            acc[place, rows] += sum(values[:, c : c + 128] for c in range(0, block, 128))

        add(4, dconv)
        for place in range(4):
            add(place, dconv * items[place])
        result = taps[:, 3:4] * dconv
        following = after[rows]
        for offset in range(1, 4):
            keep_cur = (run_row >= float(offset)).astype(F32)
            keep_next = (runn_ref[0:1, :] >= float(offset)).astype(F32)
            result = result + taps[:, 3 - offset : 4 - offset] * shift_left(
                dconv * keep_cur, following * keep_next, offset
            )
        after[rows] = dconv[:, :128]
        out_ref[out_rows] = result.astype(out_ref.dtype)

    dcross = jnp.zeros((block, block), F32)
    for h in range(heads):
        rows = slice(h * head_dim, (h + 1) * head_dim)
        one = slice(h, h + 1)
        items = conv_inputs(xp_ref, x_ref, rows, run_row, is_first)
        taps = tapx_ref[rows]
        conv = conv_rows(items, taps)
        sigm = jax.nn.sigmoid(conv)
        xh = conv * sigm
        gate = z_ref[rows].astype(F32)
        sig = jax.nn.sigmoid(gate)
        upstream = grad_of(count - 1 - index, h * head_dim, (h + 1) * head_dim).astype(F32)
        dyh = upstream * gate * sig
        dnew = dstate[rows]
        part = xh * step[one]
        part_low = part.astype(BF16)
        dy_low = dyh.astype(BF16)
        decay = jnp.exp(jnp.minimum(cum_col[:, one] - cum[one], 0.0))
        weight = (cross * decay).astype(BF16)
        y_in = mm(part_low, weight, 1, 1)
        y_scan = y_in + y_off[rows] * entry[one]
        u_in = mm(dy_low, weight, 1, 0)
        u_st = u_off[rows] * to_end[one]
        dcross = dcross + mm(dy_low, part_low, 0, 0) * decay
        part_f = part_low.astype(F32)
        u_all = u_in + u_st
        rowterm[one] = jnp.sum(dy_low.astype(F32) * y_scan, axis=0, keepdims=True)
        colin[one] = jnp.sum(part_f * u_in, axis=0, keepdims=True)
        colst[one] = jnp.sum(part_f * u_st, axis=0, keepdims=True)
        direct[one] = jnp.sum(xh * u_all, axis=0, keepdims=True)
        skip = skip_ref[rows, 0:1]
        y_all = y_scan + skip * xh
        dm_ref[rows] = (upstream * y_all * sig * (1.0 + gate * (1.0 - sig))).astype(dm_ref.dtype)
        prod = dyh * xh
        accs[rows] += sum(prod[:, c : c + 128] for c in range(0, block, 128))
        dact = step[one] * u_all + skip * dyh
        below = slice(inner + h * head_dim, inner + (h + 1) * head_dim)
        conv_back(dact, conv, sigm, items, taps, rows, nextx, accx, dm_ref, below)
        xdt[rows] = (part * to_end[one]).astype(BF16)
        dye[rows] = (dyh * entry[one]).astype(BF16)
        old = old_low[rows].astype(F32)
        ystat[one] = jnp.sum(dnew * old * keep[one], axis=0, keepdims=True)
        dstate[rows] = dnew * keep[one]
        hook(h)
    dcross_low = jnp.where(allowed, dcross, 0.0).astype(BF16)
    dout = mm(in_low, dcross_low, 1, 1) + mm(old_low, dye[...], 0, 0)
    din = mm(out_low, dcross_low, 1, 0) + mm(dnew_low, xdt[...], 0, 0)
    dstate[...] += mm(dye[...], out_low, 1, 1)
    lower = jnp.transpose(upper)
    kept_total = jnp.sum(ystat[...], axis=1, keepdims=True)
    dlog = (
        mm_exact(rowterm[...] - colin[...], lower)
        + mm_exact(colst[...], upper)
        - colst[...]
        + kept_total
    )
    dstep = direct[...] + rate * dlog
    dstep_ref[...] = dstep * jax.nn.sigmoid(raw)
    drate_ref[...] = dlog * step

    conv_back(
        jnp.concatenate([din, dout], axis=0), convb, sigb, items_b, tapb_ref[...], everything, nextb, accb,
        db_ref, everything,
    )

    @pl.when(is_first)
    def _():
        def spread(acc, out_ref):
            lanes = lax.broadcasted_iota(jnp.int32, out_ref.shape, 1)
            result = jnp.zeros(out_ref.shape, F32)
            for item in range(5):
                total = jnp.sum(acc[item], axis=1, keepdims=True)
                result = jnp.where(lanes == item, total, result)
            out_ref[...] = result

        spread(accx, dtapx_ref)
        spread(accb, dtapb_ref)
        dskip_ref[...] = jnp.broadcast_to(
            jnp.sum(accs[...], axis=1, keepdims=True), dskip_ref.shape
        )


def ssd_specs(block, inner, vec, rows16, chunk_of):
    wide = lambda i: (0, chunk_of(i))
    per = block // 128
    before = lambda i: (0, jnp.maximum(chunk_of(i) * per - 1, 0))
    whole = lambda i: (0, 0)
    return [
        pl.BlockSpec((inner, block), wide),
        pl.BlockSpec((inner, block), lambda i: (1, chunk_of(i))),
        pl.BlockSpec((inner, 128), lambda i: (1, before(i)[1])),
        pl.BlockSpec((vec, block), wide),
        pl.BlockSpec((vec, 128), before),
        pl.BlockSpec((rows16, block), wide),
        pl.BlockSpec((8, block), wide),
        pl.BlockSpec((block, 128), lambda i: (chunk_of(i), 0)),
        pl.BlockSpec((inner, 128), whole),
        pl.BlockSpec((vec, 128), whole),
        pl.BlockSpec((rows16, 128), whole),
        pl.BlockSpec((inner, 128), whole),
    ]


def ssd_forward(mixer_t, vec_t, step_t, run8, run_col, tap_x, tap_b, head_cols, skip_col, heads, head_dim, block):
    inner = mixer_t.shape[0] // 2
    seq = mixer_t.shape[1]
    vec = vec_t.shape[0]
    rows16 = step_t.shape[0]
    chunks = seq // block
    state_dim = vec // 2
    return pl.pallas_call(
        functools.partial(ssd_forward_kernel, block, heads, head_dim),
        grid=(chunks,),
        in_specs=ssd_specs(block, inner, vec, rows16, lambda i: i),
        out_specs=[
            pl.BlockSpec((inner, block), lambda i: (0, i)),
            pl.BlockSpec((1, inner, state_dim), lambda i: (i, 0, 0)),
        ],
        out_shape=[
            jax.ShapeDtypeStruct((inner, seq), BF16),
            jax.ShapeDtypeStruct((chunks, inner, state_dim), BF16),
        ],
        scratch_shapes=[
            pltpu.VMEM((inner, state_dim), F32),
            pltpu.VMEM((inner, block), BF16),
        ],
        compiler_params=pltpu.CompilerParams(vmem_limit_bytes=48 << 20),
        cost_estimate=pl.CostEstimate(flops=10**9, bytes_accessed=10**7, transcendentals=10**7),
        name="ssd_forward",
    )(mixer_t, mixer_t, mixer_t, vec_t, vec_t, step_t, run8, run_col, tap_x, tap_b, head_cols, skip_col)


def ssd_backward(mixer_t, vec_t, step_t, run8, run_col, tap_x, tap_b, head_cols, skip_col, entry, grad_t, heads, head_dim, block):
    inner = mixer_t.shape[0] // 2
    seq = mixer_t.shape[1]
    vec = vec_t.shape[0]
    rows16 = step_t.shape[0]
    chunks = seq // block
    state_dim = vec // 2
    per = block // 128
    chunk_of = lambda i: chunks - 1 - i
    wide = lambda i: (0, chunk_of(i))
    whole = lambda i: (0, 0)
    return pl.pallas_call(
        functools.partial(ssd_backward_kernel, block, heads, head_dim),
        grid=(chunks,),
        in_specs=ssd_specs(block, inner, vec, rows16, chunk_of)
        + [
            pl.BlockSpec((1, inner, state_dim), lambda i: (chunk_of(i), 0, 0)),
            pl.BlockSpec((inner, block), wide),
            pl.BlockSpec((8, 128), lambda i: (0, jnp.minimum(chunk_of(i) * per + per, chunks * per - 1))),
        ],
        out_specs=[
            pl.BlockSpec((2 * inner, block), wide),
            pl.BlockSpec((vec, block), wide),
            pl.BlockSpec((rows16, block), wide),
            pl.BlockSpec((rows16, block), wide),
            pl.BlockSpec((inner, 128), whole),
            pl.BlockSpec((vec, 128), whole),
            pl.BlockSpec((inner, 128), whole),
        ],
        out_shape=[
            jax.ShapeDtypeStruct((2 * inner, seq), BF16),
            jax.ShapeDtypeStruct((vec, seq), BF16),
            jax.ShapeDtypeStruct((rows16, seq), F32),
            jax.ShapeDtypeStruct((rows16, seq), F32),
            jax.ShapeDtypeStruct((inner, 128), F32),
            jax.ShapeDtypeStruct((vec, 128), F32),
            jax.ShapeDtypeStruct((inner, 128), F32),
        ],
        scratch_shapes=[
            pltpu.VMEM((inner, state_dim), F32),
            pltpu.VMEM((inner, 128), F32),
            pltpu.VMEM((vec, 128), F32),
            pltpu.VMEM((5, inner, 128), F32),
            pltpu.VMEM((5, vec, 128), F32),
            pltpu.VMEM((inner, 128), F32),
            pltpu.VMEM((inner, block), BF16),
            pltpu.VMEM((inner, block), BF16),
            pltpu.VMEM((rows16, block), F32),
            pltpu.VMEM((rows16, block), F32),
            pltpu.VMEM((rows16, block), F32),
            pltpu.VMEM((rows16, block), F32),
            pltpu.VMEM((rows16, state_dim), F32),
        ],
        compiler_params=pltpu.CompilerParams(vmem_limit_bytes=48 << 20),
        cost_estimate=pl.CostEstimate(flops=3 * 10**9, bytes_accessed=2 * 10**7, transcendentals=3 * 10**7),
        name="ssd_backward",
    )(
        mixer_t, mixer_t, mixer_t, vec_t, vec_t, step_t, run8, run_col, tap_x, tap_b, head_cols, skip_col,
        entry, grad_t, run8,
    )


def rotate_rows(values, cosine, sine):
    half = values.shape[0] // 2
    first, second = values[:half], values[half:]
    return jnp.concatenate(
        [first * cosine - second * sine, second * cosine + first * sine], axis=0
    )


def window_of(block_index, block, reach):
    low = max(0, (block_index * block - (reach - 1)) // block)
    return low * block, (block_index + 1) * block


def allowed_of(run_ref, begin, stop, block):
    start, end = stop
    keys = lax.broadcasted_iota(jnp.int32, (end - start, block), 0) + start
    queries = lax.broadcasted_iota(jnp.int32, (end - start, block), 1) + begin
    gap = (queries - keys).astype(F32)
    return (gap >= 0.0) & (gap <= run_ref[0:1, begin : begin + block])


def attention_forward_kernel(
    heads, groups, head_dim, block, reach, scale,
    proj_ref, cos_ref, sin_ref, run_ref, out_ref, rot_ref, lse_ref,
):
    seq = proj_ref.shape[1]
    cosine, sine = cos_ref[...], sin_ref[...]
    total = heads + groups
    for item in range(total):
        rows = slice(item * head_dim, (item + 1) * head_dim)
        rot_ref[rows] = rotate_rows(proj_ref[rows].astype(F32), cosine, sine).astype(BF16)
    for index in range(seq // block):
        begin = index * block
        span = window_of(index, block, reach)
        allowed = allowed_of(run_ref, begin, span, block)
        for h in range(heads):
            group = h * groups // heads
            rows = slice(h * head_dim, (h + 1) * head_dim)
            krows = slice((heads + group) * head_dim, (heads + group + 1) * head_dim)
            vrows = slice((heads + groups + group) * head_dim, (heads + groups + group + 1) * head_dim)
            query = rot_ref[rows, begin : begin + block]
            key = rot_ref[krows, span[0] : span[1]]
            value = proj_ref[vrows, span[0] : span[1]].astype(BF16)
            logits = jnp.where(allowed, mm(key, query, 0, 0) * scale, -1e30)
            peak = jnp.max(logits, axis=0, keepdims=True)
            powered = jnp.exp(logits - peak)
            mass = jnp.sum(powered, axis=0, keepdims=True)
            probs = (powered * (1.0 / mass)).astype(BF16)
            out_ref[rows, begin : begin + block] = mm(value, probs, 1, 0).astype(out_ref.dtype)
            lse_ref[h : h + 1, begin : begin + block] = peak + jnp.log(mass)


def attention_backward_kernel(
    heads, groups, head_dim, block, reach, scale, grad_of, hook,
    proj_ref, rot_ref, cos_ref, sin_ref, run_ref, lse_ref, back_ref,
    acc_key, acc_value,
):
    seq = proj_ref.shape[1]
    acc_key[...] = jnp.zeros_like(acc_key)
    acc_value[...] = jnp.zeros_like(acc_value)
    for index in range(seq // block):
        begin = index * block
        span = window_of(index, block, reach)
        allowed = allowed_of(run_ref, begin, span, block)
        cosine, sine = cos_ref[:, begin : begin + block], sin_ref[:, begin : begin + block]
        for h in range(heads):
            group = h * groups // heads
            rows = slice(h * head_dim, (h + 1) * head_dim)
            krows = slice((heads + group) * head_dim, (heads + group + 1) * head_dim)
            vrows = slice((heads + groups + group) * head_dim, (heads + groups + group + 1) * head_dim)
            grows = slice(group * head_dim, (group + 1) * head_dim)
            query = rot_ref[rows, begin : begin + block]
            key = rot_ref[krows, span[0] : span[1]]
            value = proj_ref[vrows, span[0] : span[1]].astype(BF16)
            grad = grad_of(h * head_dim, (h + 1) * head_dim, begin)
            logits = jnp.where(allowed, mm(key, query, 0, 0) * scale, -1e30)
            probs = jnp.exp(logits - lse_ref[h : h + 1, begin : begin + block])
            dprobs = mm(value, grad, 0, 0)
            centre = jnp.sum(probs * dprobs, axis=0, keepdims=True)
            dscore = (probs * (dprobs - centre) * scale).astype(BF16)
            dquery = mm(key, dscore, 1, 0)
            back_ref[rows, begin : begin + block] = rotate_rows(dquery, cosine, -sine).astype(BF16)
            acc_key[grows, span[0] : span[1]] += mm(query, dscore, 1, 1)
            acc_value[grows, span[0] : span[1]] += mm(grad, probs.astype(BF16), 1, 1)
        hook(index)
    for group in range(groups):
        grows = slice(group * head_dim, (group + 1) * head_dim)
        krows = slice((heads + group) * head_dim, (heads + group + 1) * head_dim)
        vrows = slice((heads + groups + group) * head_dim, (heads + groups + group + 1) * head_dim)
        back_ref[krows] = rotate_rows(acc_key[grows], cos_ref[...], -sin_ref[...]).astype(BF16)
        back_ref[vrows] = acc_value[grows].astype(BF16)


def attention_forward(proj_t, cosine, sine, run8, heads, groups, head_dim, block, reach):
    seq = proj_t.shape[1]
    return pl.pallas_call(
        functools.partial(attention_forward_kernel, heads, groups, head_dim, block, reach, head_dim**-0.5),
        out_shape=[
            jax.ShapeDtypeStruct((heads * head_dim, seq), BF16),
            jax.ShapeDtypeStruct(((heads + groups) * head_dim, seq), BF16),
            jax.ShapeDtypeStruct((max(heads, 8), seq), F32),
        ],
        compiler_params=pltpu.CompilerParams(vmem_limit_bytes=48 << 20),
        cost_estimate=pl.CostEstimate(flops=2 * 10**9, bytes_accessed=10**7, transcendentals=4 * 10**6),
        name="attention_forward",
    )(proj_t, cosine, sine, run8)


def attention_backward_call(
    heads, groups, head_dim, block, reach, proj_ref, rot_ref, cos_ref, sin_ref, run_ref, lse_ref, grad_ref, *refs
):
    attention_backward_kernel(
        heads, groups, head_dim, block, reach, head_dim**-0.5,
        lambda low, high, begin: grad_ref[low:high, begin : begin + block], lambda index: None,
        proj_ref, rot_ref, cos_ref, sin_ref, run_ref, lse_ref, *refs,
    )


def attention_backward(proj_t, rot_t, cosine, sine, run8, lse, grad_t, heads, groups, head_dim, block, reach):
    seq = proj_t.shape[1]
    return pl.pallas_call(
        functools.partial(attention_backward_call, heads, groups, head_dim, block, reach),
        out_shape=jax.ShapeDtypeStruct(proj_t.shape, BF16),
        scratch_shapes=[
            pltpu.VMEM((groups * head_dim, seq), F32),
            pltpu.VMEM((groups * head_dim, seq), F32),
        ],
        compiler_params=pltpu.CompilerParams(vmem_limit_bytes=48 << 20),
        cost_estimate=pl.CostEstimate(flops=5 * 10**9, bytes_accessed=10**7, transcendentals=4 * 10**6),
        name="attention_backward",
    )(proj_t, rot_t, cosine, sine, run8, lse, grad_t)


def ffn_kernel(norm_ref, cot_ref, gate_ref, up_ref, down_ref, out_ref, back_ref, acts_ref):
    @pl.when(pl.program_id(0) == 0)
    def _():
        out_ref[...] = jnp.zeros_like(out_ref)
        back_ref[...] = jnp.zeros_like(back_ref)

    normed, cot = norm_ref[...], cot_ref[...]
    gate_w, up_w, down_w = gate_ref[...], up_ref[...], down_ref[...]
    gate = mm(normed, gate_w, 1, 0)
    up = mm(normed, up_w, 1, 0)
    grad_act = mm(cot, down_w, 1, 1)
    sig = jax.nn.sigmoid(gate)
    silu = gate * sig
    act = (silu * up).astype(BF16)
    dgate = (grad_act * up * sig * (1.0 + gate * (1.0 - sig))).astype(BF16)
    dup = (grad_act * silu).astype(BF16)
    acts_ref[0] = dgate
    acts_ref[1] = dup
    acts_ref[2] = act
    out_ref[...] += mm(act, down_w, 1, 0)
    back_ref[...] += mm(dgate, gate_w, 1, 1) + mm(dup, up_w, 1, 1)


def feed_forward(normed, cot, gate_w, up_w, down_w, tile):
    rows, width = normed.shape
    hidden = gate_w.shape[1]
    whole = lambda i: (0, 0)
    return pl.pallas_call(
        ffn_kernel,
        grid=(hidden // tile,),
        in_specs=[
            pl.BlockSpec((rows, width), whole),
            pl.BlockSpec((rows, width), whole),
            pl.BlockSpec((width, tile), lambda i: (0, i)),
            pl.BlockSpec((width, tile), lambda i: (0, i)),
            pl.BlockSpec((tile, width), lambda i: (i, 0)),
        ],
        out_specs=[
            pl.BlockSpec((rows, width), whole),
            pl.BlockSpec((rows, width), whole),
            pl.BlockSpec((3, rows, tile), lambda i: (0, 0, i)),
        ],
        out_shape=[
            jax.ShapeDtypeStruct((rows, width), F32),
            jax.ShapeDtypeStruct((rows, width), F32),
            jax.ShapeDtypeStruct((3, rows, hidden), BF16),
        ],
        compiler_params=pltpu.CompilerParams(vmem_limit_bytes=48 << 20),
        cost_estimate=pl.CostEstimate(flops=6 * 2 * rows * width * hidden, bytes_accessed=3 * 10**7, transcendentals=rows * hidden),
        name="feed_forward",
    )(normed, cot, gate_w, up_w, down_w)


def digit_of(digit):
    axis_name, bit, size = digit
    return (lax.axis_index(axis_name) // (1 << bit)) % 2


def partner_of(flipped):
    places = {}
    for digit in flipped:
        axis_name, bit, size = digit
        place = places.get(axis_name, lax.axis_index(axis_name))
        places[axis_name] = place + (1 - 2 * digit_of(digit)) * (1 << bit)
    return places


def send_to(flipped, source, target, send_sem, recv_sem):
    return pltpu.make_async_remote_copy(
        src_ref=source,
        dst_ref=target,
        send_sem=send_sem,
        recv_sem=recv_sem,
        device_id=partner_of(flipped),
        device_id_type=pl.DeviceIdType.MESH,
    )


def greet(partners):
    barrier = pltpu.get_barrier_semaphore()
    for flipped in partners:
        pl.semaphore_signal(
            barrier, inc=1, device_id=partner_of(flipped), device_id_type=pl.DeviceIdType.MESH
        )
    pl.semaphore_wait(barrier, len(partners))


def flips_of(group):
    return [
        tuple(digit for digit, bit in zip(group, bits) if bit)
        for bits in itertools.product((0, 1), repeat=len(group))
        if any(bits)
    ]


class Summer:
    def __init__(self, pieces):
        self.pieces = pieces
        self.count = len(pieces)
        for rows, cols, dtype, digits, order, gather in pieces:
            flat = [digit for group in order for digit in group]
            assert sorted(digits) == sorted(flat) and (not gather or list(digits) == flat)

    def turns(self, item):
        return len(self.pieces[item][4]) * (2 if self.pieces[item][5] else 1)

    def scratch(self):
        shapes = []
        for item, (rows, cols, dtype, digits, order, gather) in enumerate(self.pieces):
            shapes.append(pltpu.VMEM((2,) * len(digits) + (rows, cols), dtype))
            left = len(digits)
            for group in order:
                left -= len(group)
                shapes.append(pltpu.VMEM(((1 << len(group)) - 1,) + (2,) * left + (rows, cols), dtype))
            if gather:
                shapes.append(pltpu.VMEM((1 << len(digits), rows, cols), dtype))
        most = max(self.turns(item) for item in range(self.count))
        wide = max((1 << len(group)) - 1 for piece in self.pieces for group in piece[4])
        return shapes + [pltpu.SemaphoreType.DMA((self.count, most, wide))] * 2

    def bind(self, emits, refs):
        self.emits, self.full, self.gots, self.alls = emits, [], [], []
        for rows, cols, dtype, digits, order, gather in self.pieces:
            self.full.append(refs[0])
            self.gots.append(refs[1 : 1 + len(order)])
            refs = refs[1 + len(order) :]
            if gather:
                self.alls.append(refs[0])
                refs = refs[1:]
            else:
                self.alls.append(None)
        self.send_sem, self.recv_sem = refs

    def copies(self, item, turn):
        rows, cols, dtype, digits, order, gather = self.pieces[item]
        result = []
        if turn < len(order):
            done = [digit for group in order[:turn] for digit in group]
            group = order[turn]
        else:
            group = order[2 * len(order) - 1 - turn]
            ahead = [digit for group in order[: 2 * len(order) - 1 - turn] for digit in group]
            size = 1 << (len(digits) - len(ahead) - len(group))
            region = self.alls[item].at[pl.ds(self.place_of(ahead + list(group)) * size, size)]
        for slot, flipped in enumerate(flips_of(group)):
            if turn < len(order):
                index = tuple(
                    1 - digit_of(digit) if digit in flipped
                    else digit_of(digit) if digit in done or digit in group
                    else slice(None)
                    for digit in digits
                )
                source, target = self.full[item].at[index], self.gots[item][turn].at[slot]
            else:
                source = target = region
            result.append(
                send_to(
                    flipped, source, target, self.send_sem.at[item, turn, slot], self.recv_sem.at[item, turn, slot]
                )
            )
        return result

    def place_of(self, digits):
        place = 0
        for digit in digits:
            place = place * 2 + digit_of(digit)
        return place

    def start(self, item, turn=0):
        for copy in self.copies(item, turn):
            copy.start()

    def advance(self, item, turn):
        rows, cols, dtype, digits, order, gather = self.pieces[item]
        for copy in self.copies(item, turn):
            copy.wait()
        if turn >= len(order):
            if turn + 1 < 2 * len(order):
                self.start(item, turn + 1)
            else:
                self.emits[item](self.alls[item])
            return
        done = [digit for group in order[: turn + 1] for digit in group]
        left = [digit for digit in digits if digit not in done]
        for bits in itertools.product((0, 1), repeat=len(left)):
            index = tuple(
                digit_of(digit) if digit in done else bits[left.index(digit)] for digit in digits
            )
            value = self.full[item][index].astype(F32)
            for slot in range((1 << len(order[turn])) - 1):
                value = value + self.gots[item][turn][(slot,) + bits].astype(F32)
            if left:
                self.full[item][index] = value.astype(dtype)
            elif gather:
                self.alls[item][self.place_of(digits)] = value.astype(dtype)
            else:
                self.emits[item](value)
        if turn + 1 < self.turns(item):
            self.start(item, turn + 1)


def backward_kernel(plan, sizes, attention_count, ssd_count, ssd_outs, scratch_counts, *refs):
    query_heads, groups, head_dim, heads, ssd_dim, block, reach = sizes
    summer, partners, across, hooks = plan
    step = pl.program_id(0)
    steps = pl.num_programs(0)
    (acts, rows, mixer_ref, feature_ref, pair_ref), refs = refs[:5], refs[5:]
    attention_in, refs = refs[:attention_count], refs[attention_count:]
    ssd_in, refs = refs[:ssd_count], refs[ssd_count:]
    attention_out, refs = refs[:1], refs[1:]
    ssd_out, refs = refs[:ssd_outs], refs[ssd_outs:]
    part_out, refs = refs[:5], refs[5:]
    attention_scratch, refs = refs[: scratch_counts[0]], refs[scratch_counts[0] :]
    ssd_scratch, refs = refs[: scratch_counts[1]], refs[scratch_counts[1] :]
    (head_grad, pair_sem), refs = refs[:2], refs[2:]
    branch_pos = digit_of(across)
    attn_rows = query_heads * head_dim
    gate_out, up_out, down_out, attn_out, ssd_w_out = part_out

    def to_columns(out_ref, begin):
        def emit(value):
            out_ref[begin : begin + value.shape[1]] = jnp.transpose(value)

        return emit

    def to_rows(begin):
        def emit(value):
            down_out[:, begin : begin + value.shape[1]] = value

        return emit

    def to_outputs(value):
        attn_out[...] = jnp.transpose(value[:, :attn_rows])
        ssd_w_out[: value.shape[1] - attn_rows] = jnp.transpose(value[:, attn_rows:])

    width = rows.shape[2] // 2
    summer.bind(
        [
            to_columns(gate_out, 0), to_columns(gate_out, width),
            to_columns(up_out, 0), to_columns(up_out, width),
            to_rows(0), to_rows(width),
            to_outputs, to_columns(ssd_w_out, width - attn_rows),
        ],
        refs,
    )

    def exchange(part):
        low, high = ((0, attn_rows), (attn_rows, head_grad.shape[1]))[part]
        return send_to(
            (across,),
            pair_ref.at[1 - branch_pos, low:high],
            head_grad.at[branch_pos, low:high],
            pair_sem.at[2 * part],
            pair_sem.at[2 * part + 1],
        )

    def own_pair():
        return pltpu.make_async_copy(
            pair_ref.at[branch_pos], head_grad.at[branch_pos], pair_sem.at[4]
        )

    def run(events):
        for item, turn in events:
            summer.advance(item, turn)

    @pl.when(step == 0)
    def _():
        own_pair().start()
        greet(partners)
        exchange(0).start()
        exchange(1).start()

    for item in range(3):
        @pl.when(step == item)
        def _():
            run(hooks.get((item, "begin"), ()))
            tile = 256
            right = rows[0]

            @pl.loop(0, acts.shape[2] // tile)
            def _(t):
                left = acts[0, :, pl.ds(pl.multiple_of(t * tile, tile), tile)]
                value = mm(left, right, 0, 0).astype(BF16)
                for part in range(2):
                    full = summer.full[2 * item + part]
                    columns = value[:, part * width : (part + 1) * width]
                    full[t // 4, (t // 2) % 2, t % 2] = columns.reshape(full.shape[3:])

            summer.start(2 * item)
            summer.start(2 * item + 1)

    @pl.when(step == 3)
    def _():
        run(hooks.get((3, "begin"), ()))
        tile = 256
        half = feature_ref.shape[0] // 2
        for part in range(2):
            right = feature_ref[part * half : (part + 1) * half]

            @pl.loop(0, mixer_ref.shape[1] // tile)
            def _(t):
                left = mixer_ref[:, pl.ds(pl.multiple_of(t * tile, tile), tile)]
                value = mm(left, right, 0, 1).astype(BF16)
                for piece in range(2):
                    full = summer.full[6 + piece]
                    columns = value[:, piece * width : (piece + 1) * width]
                    full[part, t // 2, t % 2] = columns.reshape(full.shape[3:])

        summer.start(6)
        summer.start(7)

    @pl.when(step == 4)
    def _():
        exchange(0).wait()
        own_pair().wait()
        run(hooks.get((4, "begin"), ()))

        def grad_of(low, high, begin):
            width = head_grad.shape[2]
            return head_grad[begin // width, low:high, begin % width : begin % width + block]

        attention_backward_kernel(
            query_heads, groups, head_dim, block, reach, head_dim**-0.5,
            grad_of, lambda index: run(hooks.get((4, index), ())), *attention_in, *attention_out, *attention_scratch,
        )

    timed = [item for item in hooks.items() if item[0] != "late"]

    @pl.when(step == 5)
    def _():
        exchange(1).wait()

    @pl.when(step > 4)
    def _():
        def hook(h):
            for (at_step, at_head), events in timed:
                if at_head == h and at_step > 4:
                    @pl.when(step == at_step)
                    def _():
                        run(events)

        def grad_of(chunk, low, high):
            per = head_grad.shape[2] // block
            begin = pl.multiple_of((chunk % per) * block, block)
            return head_grad[chunk // per, attn_rows + low : attn_rows + high, pl.ds(begin, block)]

        ssd_backward_body(block, heads, ssd_dim, step - 5, steps - 5, hook, grad_of, *ssd_in, *ssd_out, *ssd_scratch)

    late = hooks.get("late", ())

    @pl.when(step == steps - 1)
    def _():
        run(late)


def mixer_backward(acts, ffn_rows, grad_mixer, features, grad_pair, attention_args, ssd_args, entry, plan, sizes, collective_id):
    query_heads, groups, head_dim, heads, ssd_dim, block, reach = sizes
    summer = plan[0]
    mixer_t, vec_t, step_t, run8, run_col, tap_x, tap_b, head_cols, skip_col = ssd_args
    inner = mixer_t.shape[0] // 2
    seq = mixer_t.shape[1]
    vec = vec_t.shape[0]
    rows16 = step_t.shape[0]
    chunks = seq // block
    state_dim = vec // 2
    per = block // 128
    before = 5
    chunk_of = lambda i: jnp.minimum(chunks - 1 + before - i, chunks - 1)
    wide = lambda i: (0, chunk_of(i))
    whole = lambda i: (0, 0)
    proj_t = attention_args[0]
    once = pl.Buffered(1)
    ssd_in = [mixer_t, mixer_t, mixer_t, vec_t, vec_t, step_t, run8, run_col, tap_x, tap_b, head_cols, skip_col]
    ssd_in += [entry, run8]
    in_specs = [
        pl.BlockSpec((1,) + acts.shape[1:], lambda i: (jnp.minimum(i, 2), 0, 0), pipeline_mode=once),
        pl.BlockSpec((1,) + ffn_rows.shape[1:], lambda i: (jnp.minimum(i // 2, 1), 0, 0), pipeline_mode=once),
        pl.BlockSpec(grad_mixer.shape, whole, pipeline_mode=once),
        pl.BlockSpec(features.shape, whole, pipeline_mode=once),
        pl.BlockSpec(memory_space=pl.ANY),
    ]
    in_specs += [pl.BlockSpec(item.shape, whole, pipeline_mode=once) for item in attention_args]
    in_specs += ssd_specs(block, inner, vec, rows16, chunk_of)
    in_specs += [
        pl.BlockSpec((1, inner, state_dim), lambda i: (chunk_of(i), 0, 0)),
        pl.BlockSpec((8, 128), lambda i: (0, jnp.minimum(chunk_of(i) * per + per, chunks * per - 1))),
    ]
    ssd_out = [
        (2 * inner, seq, block, BF16),
        (vec, seq, block, BF16),
        (rows16, seq, block, F32),
        (rows16, seq, block, F32),
        (inner, 128, 128, F32),
        (vec, 128, 128, F32),
        (inner, 128, 128, F32),
    ]
    out_specs = [pl.BlockSpec(proj_t.shape, whole)]
    out_specs += [
        pl.BlockSpec((rows, width), wide if full == seq else whole) for rows, full, width, _ in ssd_out
    ]
    part_row = summer.pieces[0][0]
    model_dim = ffn_rows.shape[2]
    part_shapes = [
        jax.ShapeDtypeStruct(shape, F32)
        for shape in (
            (model_dim, part_row),
            (model_dim, part_row),
            (part_row, model_dim),
            (query_heads * head_dim, part_row),
            (inner, part_row),
        )
    ]
    out_specs += [pl.BlockSpec(item.shape, whole) for item in part_shapes]
    attention_scratch = [pltpu.VMEM((groups * head_dim, seq), F32)] * 2
    ssd_scratch = [
        pltpu.VMEM((inner, state_dim), F32),
        pltpu.VMEM((inner, 128), F32),
        pltpu.VMEM((vec, 128), F32),
        pltpu.VMEM((5, inner, 128), F32),
        pltpu.VMEM((5, vec, 128), F32),
        pltpu.VMEM((inner, 128), F32),
        pltpu.VMEM((inner, block), BF16),
        pltpu.VMEM((inner, block), BF16),
        pltpu.VMEM((rows16, block), F32),
        pltpu.VMEM((rows16, block), F32),
        pltpu.VMEM((rows16, block), F32),
        pltpu.VMEM((rows16, block), F32),
        pltpu.VMEM((rows16, state_dim), F32),
    ]
    results = pl.pallas_call(
        functools.partial(
            backward_kernel, plan, sizes, len(attention_args), len(ssd_in), len(ssd_out),
            (len(attention_scratch), len(ssd_scratch)),
        ),
        grid=(chunks + before,),
        in_specs=in_specs,
        out_specs=out_specs,
        out_shape=[jax.ShapeDtypeStruct(proj_t.shape, BF16)]
        + [jax.ShapeDtypeStruct((rows, full), dtype) for rows, full, _, dtype in ssd_out]
        + part_shapes,
        scratch_shapes=attention_scratch
        + ssd_scratch
        + [pltpu.VMEM(grad_pair.shape, BF16), pltpu.SemaphoreType.DMA((5,))]
        + summer.scratch(),
        compiler_params=pltpu.CompilerParams(
            vmem_limit_bytes=63 << 20, collective_id=collective_id, has_side_effects=True
        ),
        cost_estimate=pl.CostEstimate(flops=7 * 10**10, bytes_accessed=5 * 10**7, transcendentals=3 * 10**7),
        name="mixer_backward",
    )(acts, ffn_rows, grad_mixer, features, grad_pair, *attention_args, *ssd_in)
    return results[0], results[1:8], results[8:]

def final_kernel(plan, eps, sizes, *refs):
    summer, partners, across, order = plan
    heads, head_dim = sizes
    names = ("normed", "dvec", "dmixer", "mixer_w", "state_w", "dqkv", "qkv_w", "dstep", "step_w", "rows", "hidden")
    hbm = dict(zip(names, refs[: len(names)]))
    refs = refs[len(names) :]
    (gain_ref, tapx_ref, tapb_ref, skip_ref, rate_ref, head_ref, ffn_gain_ref, ssd_gain_ref), refs = refs[:8], refs[8:]
    (
        input_out, query_out, keyval_out, mixer_out, state_out, step_out, taps_out, bias_out, gain_out, ffn_gain_out,
        state_taps_out, state_bias_out, bias_sum_out, rate_sum_out, skip_sum_out, ssd_gain_out,
    ), refs = refs[:16], refs[16:]
    vmem = dict(zip(names, refs[: len(names)]))
    refs = refs[len(names) :]
    partial, sent, got, load_sem, swap_sem = refs[:5]
    branch_pos = digit_of(across)
    half, width = partial.shape
    inner = vmem["dmixer"].shape[0] // 2
    query_cols = query_out.shape[1]
    key_cols = keyval_out.shape[2]
    gain_rows = width // 128
    state_rows = tapb_ref.shape[0] // 128

    def emit_mixer(part):
        def emit(value):
            mixer_out[:, part, :] = value

        return emit

    def emit_qkvs(value):
        query_out[...] = value[:, :query_cols]
        for part in range(2):
            keyval_out[:, part, :] = value[:, query_cols + part * key_cols : query_cols + (part + 1) * key_cols]
        begin = query_cols + 2 * key_cols
        step_out[...] = value[:, begin : begin + heads]

    def emit_state(parts):
        values = parts[...].astype(F32)
        columns = values.shape[2] // 2
        for part in range(2):
            piece = values[:, :, part * columns : (part + 1) * columns]
            state_out[:, part, :] = piece.reshape(-1, columns)

    def emit_own(value):
        turned = jnp.transpose(value)
        taps_out[...] = turned[:4]
        bias_out[...] = turned[4:5]

    def emit_shared(parts):
        per = parts.shape[1]
        row = lambda place: parts[place // per, place % per : place % per + 1]
        for place in range(gain_rows):
            gain_out[place : place + 1] = row(place)
            ffn_gain_out[place : place + 1] = row(gain_rows + place)
        begin = 2 * gain_rows
        for tap in range(4):
            for part in range(state_rows):
                state_taps_out[tap, part : part + 1] = row(begin + tap * state_rows + part)
        begin += 4 * state_rows
        for part in range(state_rows):
            state_bias_out[part : part + 1] = row(begin + part)
        begin += state_rows
        for place, out_ref in enumerate((bias_sum_out, rate_sum_out, skip_sum_out)):
            out_ref[...] = row(begin + place)[:, : out_ref.shape[1]]
        begin += 3
        for place in range(ssd_gain_out.shape[0]):
            ssd_gain_out[place : place + 1] = row(begin + place)

    summer.bind(
        [emit_mixer(0), emit_mixer(1), emit_qkvs, emit_state, emit_own, emit_shared], refs[5:]
    )

    def load(name):
        return pltpu.make_async_copy(hbm[name], vmem[name], load_sem.at[names.index(name)])

    for name in names:
        load(name).start()
    greet(partners)
    gain = gain_ref[...]

    def index_of(full, owner):
        digits = len(full.shape) - 2
        return tuple((owner >> (digits - 1 - place)) & 1 for place in range(digits))

    own = summer.full[4]
    own_rows = own.shape[-2]
    for owner in range(tapx_ref.shape[0] // own_rows):
        own[index_of(own, owner)] = tapx_ref[owner * own_rows : (owner + 1) * own_rows]
    summer.start(4)

    shared = summer.full[5]
    per = shared.shape[-2]

    def put(place, row):
        shared[index_of(shared, place // per) + (slice(place % per, place % per + 1),)] = row

    for place in range(gain_rows):
        put(gain_rows + place, ffn_gain_ref[place : place + 1])
    begin = 2 * gain_rows
    turned = jnp.transpose(tapb_ref[...])
    for tap in range(5):
        for part in range(state_rows):
            put(begin + tap * state_rows + part, turned[tap : tap + 1, part * 128 : (part + 1) * 128])
    begin += 5 * state_rows

    def head_row(column):
        row = jnp.transpose(jnp.broadcast_to(column, (column.shape[0], 128)))[0:1]
        row = jnp.concatenate([row, jnp.zeros((1, 128 - row.shape[1]), F32)], axis=1)
        lanes = lax.broadcasted_iota(jnp.int32, row.shape, 1)
        row = jnp.where(lanes < heads, row, 0.0)
        return jnp.where(branch_pos == 0, row, pltpu.roll(row, heads, 1))

    rate_column = jnp.sum(rate_ref[...], axis=1, keepdims=True) * head_ref[:, 1:2]
    put(begin + 1, head_row(rate_column))
    skips = jnp.sum(skip_ref[...].reshape(heads, head_dim, 128), axis=1)[:, 0:1]
    pad = rate_ref.shape[0] - heads
    put(begin + 2, head_row(jnp.concatenate([skips, jnp.zeros((pad, 1), F32)], axis=0)))
    for place in range(ssd_gain_ref.shape[0]):
        put(begin + 3 + place, ssd_gain_ref[place : place + 1])
    for place in range(begin + 3 + ssd_gain_ref.shape[0], per << (len(shared.shape) - 2)):
        put(place, jnp.zeros((1, 128), F32))

    def partial_of(begin):
        at = pl.ds(pl.multiple_of(begin, 256), 256)
        return (
            mm(vmem["dmixer"][:, at], vmem["mixer_w"][...], 0, 1)
            + mm(vmem["dvec"][:, at], vmem["state_w"][...], 0, 1)
            + mm(vmem["dqkv"][:, at], vmem["qkv_w"][...], 0, 1)
            + mm(vmem["dstep"][:, at].astype(BF16), vmem["step_w"][...], 0, 1)
        )

    chunks = half // 256

    def swap(part):
        rows = slice(part * 256, (part + 1) * 256)
        return send_to((across,), sent.at[rows], got.at[rows], swap_sem.at[0, part], swap_sem.at[1, part])

    tile = 256
    tiles = width // tile

    def left_tile(t):
        return vmem["normed"][:, pl.ds(pl.multiple_of(t * tile, tile), tile)]

    def gain_sum(tokens, begin):
        return jnp.sum(
            tokens * vmem["normed"][pl.ds(pl.multiple_of(begin, 256), 256)].astype(F32), axis=0, keepdims=True
        )

    load("normed").wait()
    load("dvec").wait()

    @pl.loop(0, tiles)
    def _(t):
        value = mm(left_tile(t), vmem["dvec"][...], 0, 1).astype(BF16)
        summer.full[3][t // 2, t % 2] = value.reshape(summer.full[3].shape[2:])

    summer.start(3)
    summer.advance(4, 0)
    load("dmixer").wait()
    for item, begin_row in ((1, inner), (0, 0)):
        @pl.loop(0, tiles)
        def _(t):
            value = mm(left_tile(t), vmem["dmixer"][begin_row : begin_row + inner], 0, 1).astype(BF16)
            summer.full[item][t // 2, t % 2] = value.reshape(summer.full[item].shape[2:])

        summer.start(item)
        summer.advance(*((3, 0) if item == 1 else (1, 0)))

    for name in ("mixer_w", "state_w", "dqkv", "qkv_w", "dstep", "step_w"):
        load(name).wait()
    total = jnp.zeros((1, width), F32)
    for t in range(chunks):
        rows = slice(t * 256, (t + 1) * 256)
        begin_other = (1 - branch_pos) * half + t * 256
        value = partial_of(begin_other)
        sent[rows] = value.astype(BF16)
        if t == 0:
            swap(0).start()
            summer.advance(0, 0)
            summer.advance(4, 1)
        total = total + gain_sum(value, begin_other)
    summer.advance(3, 1)
    for t in range(chunks):
        rows = slice(t * 256, (t + 1) * 256)
        begin_own = branch_pos * half + t * 256
        value = partial_of(begin_own)
        partial[rows] = value
        total = total + gain_sum(value, begin_own)
        if t == 0:
            summer.advance(4, 2)
    total = total / gain
    for place in range(gain_rows):
        put(place, total[:, place * 128 : (place + 1) * 128])
    put(begin, head_row(jnp.sum(vmem["dstep"][...], axis=1, keepdims=True)))
    summer.start(5)

    @pl.loop(0, tiles)
    def _(t):
        columns = vmem["dqkv"].shape[0]
        shape = summer.full[2].shape[2:5]
        value = mm(left_tile(t), vmem["dqkv"][...], 0, 1).astype(BF16)
        summer.full[2][t // 2, t % 2, :, :, :, :columns] = value.reshape(shape + (columns,))
        value = mm(left_tile(t), vmem["dstep"][...].astype(BF16), 0, 1).astype(BF16)
        summer.full[2][t // 2, t % 2, :, :, :, columns:] = value.reshape(shape + (value.shape[1],))

    summer.advance(5, 0)
    for part in range(1, chunks):
        swap(part).start()
    summer.start(2)

    for event in order:
        if event != "input":
            summer.advance(*event)
            continue
        load("rows").wait()
        load("hidden").wait()
        for part in range(chunks):
            swap(part).wait()

        @pl.loop(0, half // 64)
        def _(t):
            rows = pl.ds(pl.multiple_of(t * 64, 64), 64)
            values = vmem["rows"][rows].astype(F32)
            scale = lax.rsqrt(jnp.mean(values * values, axis=1, keepdims=True) + eps)
            weighted = (partial[rows].astype(BF16).astype(F32) + got[rows].astype(F32)) * gain
            centre = jnp.mean(weighted * values, axis=1, keepdims=True)
            result = vmem["hidden"][rows] + scale * weighted - values * (scale * scale * scale * centre)
            input_out[rows] = result.astype(BF16)


def final_gradients(arrays, smalls, outs, plan, eps, sizes, collective_id):
    summer = plan[0]
    half, width = arrays[9].shape
    vmem = pl.BlockSpec(memory_space=pltpu.VMEM)
    return pl.pallas_call(
        functools.partial(final_kernel, plan, eps, sizes),
        in_specs=[pl.BlockSpec(memory_space=pl.ANY)] * len(arrays) + [vmem] * len(smalls),
        out_specs=[vmem] * len(outs),
        out_shape=[jax.ShapeDtypeStruct(shape, dtype) for shape, dtype in outs],
        scratch_shapes=[pltpu.VMEM(item.shape, item.dtype) for item in arrays]
        + [
            pltpu.VMEM((half, width), F32),
            pltpu.VMEM((half, width), BF16),
            pltpu.VMEM((half, width), BF16),
            pltpu.SemaphoreType.DMA((len(arrays),)),
            pltpu.SemaphoreType.DMA((2, half // 256)),
        ]
        + summer.scratch(),
        compiler_params=pltpu.CompilerParams(
            vmem_limit_bytes=60 << 20, collective_id=collective_id, has_side_effects=True
        ),
        cost_estimate=pl.CostEstimate(flops=3 * 10**10, bytes_accessed=5 * 10**7, transcendentals=0),
        name="final_gradients",
    )(*arrays, *smalls)


def bits_of(count):
    return count.bit_length() - 1


def swap_halves(values, axis_name, bit, size):
    pairs = [(item, item ^ (1 << bit)) for item in range(size)]
    return lax.ppermute(values, axis_name, pairs)


def halve(values, place, my_bit, axis_name, bit, size):
    owners = values.shape[0]
    high = 1 << place
    parts = values.reshape((high, 2, owners // (2 * high)) + values.shape[1:])
    sent = lax.dynamic_index_in_dim(parts, 1 - my_bit, 1, keepdims=False)
    kept = lax.dynamic_index_in_dim(parts, my_bit, 1, keepdims=False)
    got = swap_halves(sent, axis_name, bit, size)
    total = (kept.astype(jnp.float32) + got.astype(jnp.float32)).astype(values.dtype)
    return total.reshape((owners // 2,) + values.shape[1:])


def scatter_sum(values, digits, order):
    left = list(digits)
    for digit in order:
        axis_name, bit, size = digit
        my_bit = (lax.axis_index(axis_name) >> bit) & 1
        values = halve(values, left.index(digit), my_bit, axis_name, bit, size)
        left.remove(digit)
    return values[0]


def gather_all(values, digits, order):
    values = values[None]
    left = []
    for digit in order:
        axis_name, bit, size = digit
        my_bit = (lax.axis_index(axis_name) >> bit) & 1
        got = swap_halves(values, axis_name, bit, size)
        place = sum(1 for item in left if digits.index(item) < digits.index(digit))
        high = 1 << place
        owners = values.shape[0]
        mine = values.reshape((high, 1, owners // high) + values.shape[1:])
        other = got.reshape(mine.shape)
        first = jnp.where(my_bit == 0, mine, other)
        second = jnp.where(my_bit == 0, other, mine)
        values = jnp.concatenate([first, second], axis=1).reshape((owners * 2,) + values.shape[1:])
        left.append(digit)
    return values


def other_branch(values):
    return lax.ppermute(values, "branch", [(0, 1), (1, 0)])


def rms_scale(values):
    return lax.rsqrt(jnp.mean(values * values, axis=-1, keepdims=True) + EPSILON)


def rms_back(upstream, values, scales, gain):
    weighted = upstream * gain
    return scales * weighted - values * scales**3 * jnp.mean(
        weighted * values, axis=-1, keepdims=True
    )


def token_runs(length_row, seq_len, doc_count):
    order = jnp.arange(doc_count, dtype=jnp.int32)
    ends = jnp.sum(jnp.where(order[:, None] >= order[None, :], length_row[None, :], 0), axis=1)
    places = jnp.arange(seq_len, dtype=jnp.int32)
    passed = places[:, None] >= ends[None, :]
    starts = jnp.sum(jnp.where(passed, length_row[None, :], 0), axis=1)
    return (places - starts).astype(F32), jnp.sum(length_row)


def join(mine, other, branch_pos, axis):
    return jnp.concatenate(
        [jnp.where(branch_pos == 0, mine, other), jnp.where(branch_pos == 0, other, mine)], axis=axis
    )


def both_weights(weight, core, branch_pos):
    half = weight.shape[0] // 2
    my_core = lax.axis_index("rows") & 1
    sent = lax.dynamic_slice_in_dim(weight, my_core * half, half, 0)
    got = other_branch(sent)
    rest = swap_halves(got, *core)
    other = jnp.concatenate(
        [jnp.where(my_core == 0, got, rest), jnp.where(my_core == 0, rest, got)], axis=0
    )
    return join(weight, other, branch_pos, 0)


def columns_of(items, rows):
    stacked = jnp.stack(items, axis=1)
    return jnp.pad(stacked, ((0, rows - stacked.shape[0]), (0, 128 - stacked.shape[1])))


def per_device(
    inputs,
    lengths,
    norm_gain,
    query_weight,
    keyval_weight,
    mixer_weight,
    state_weight,
    step_weight,
    conv_mixer,
    conv_state,
    bias_mixer,
    bias_state,
    step_bias,
    decay_log,
    skip_gain,
    ssd_gain,
    attn_output,
    ssd_output,
    ffn_gain,
    gate_weight,
    up_weight,
    down_weight,
    cotangent,
):
    branch_pos = lax.axis_index("branch")
    row_pos = lax.axis_index("rows")
    row_count = lax.axis_size("rows")
    row_bits = bits_of(row_count)
    row_digits = [("rows", bit, row_count) for bit in range(row_bits - 1, -1, -1)]
    across = ("branch", 0, 2)
    core = row_digits[-1]
    chip_digits = row_digits[:-1]
    near, others = chip_digits[-1], chip_digits[:-1][::-1]
    fast = row_bits == 4

    own_rows = inputs[0].astype(F32)
    upstream = cotangent[0]
    half_len, model_dim = own_rows.shape
    seq_len = 2 * half_len
    local_query = query_weight.shape[1] // HD
    local_keyval = keyval_weight.shape[2] // HD
    local_heads = step_bias.shape[0]
    local_inner = bias_mixer.shape[0]
    inner_dim = 2 * local_inner
    head_rows = -(-local_heads // 8) * 8
    own_begin = branch_pos * half_len

    run, used = token_runs(lengths[0], seq_len, lengths.shape[1])
    run8 = jnp.broadcast_to(run[None, :], (8, seq_len))
    run_col = jnp.broadcast_to(run[:, None], (seq_len, 128))
    frequency = ROPE_BASE ** (-(jnp.arange(HD // 2, dtype=F32) * 2.0) / HD)
    angles = frequency[:, None] * run[None, :]
    cosine, sine = jnp.cos(angles), jnp.sin(angles)
    own_valid = (own_begin + jnp.arange(half_len, dtype=jnp.int32) < used).astype(F32)[:, None]

    own_scale = rms_scale(own_rows)
    own_hat = own_rows * own_scale
    normed = (own_hat * norm_gain).astype(BF16)
    full_normed = join(normed, other_branch(normed), branch_pos, 0)

    out_weight = jnp.concatenate([attn_output, ssd_output], axis=0)
    out_full = both_weights(out_weight, core, branch_pos)
    gain_full = join(ssd_gain, other_branch(ssd_gain), branch_pos, 0)

    qkv_flat = jnp.concatenate([query_weight, keyval_weight.reshape(model_dim, -1)], axis=1)
    mixer_flat = mixer_weight.reshape(model_dim, -1)
    state_flat = state_weight.reshape(model_dim, -1)
    step_flat = jnp.pad(step_weight, ((0, 0), (0, head_rows - local_heads)))

    mixer_t = mm(mixer_flat, full_normed, 0, 1).astype(BF16)
    vec_t = mm(state_flat, full_normed, 0, 1).astype(BF16)
    qkv_t = mm(qkv_flat, full_normed, 0, 1).astype(BF16)
    step_t = mm(step_flat, full_normed, 0, 1)

    taps = [conv_mixer[item] for item in range(4)] + [bias_mixer]
    tap_x = columns_of(taps, local_inner)
    state_taps = [conv_state[item].reshape(-1) for item in range(4)] + [bias_state.reshape(-1)]
    tap_b = columns_of(state_taps, state_flat.shape[1])
    rates = -jnp.exp(decay_log)
    head_cols = columns_of([step_bias, rates], head_rows)
    skip_col = jnp.broadcast_to(jnp.repeat(skip_gain, SP)[:, None], (local_inner, 128))
    ssd_args = (mixer_t, vec_t, step_t, run8, run_col, tap_x, tap_b, head_cols, skip_col)

    gated_t, entry = ssd_forward(*ssd_args, local_heads, SP, BLOCK)
    attn_t, rot_t, log_sums = attention_forward(
        qkv_t, cosine, sine, run8, local_query, local_keyval, HD, BLOCK, REACH
    )

    def own_tokens(values, pos):
        return lax.dynamic_slice_in_dim(values, pos * half_len, half_len, 1)

    def to_owner(values):
        got = other_branch(own_tokens(values, 1 - branch_pos))
        mine = own_tokens(values, branch_pos)
        return jnp.where(branch_pos == 0, mine, got), jnp.where(branch_pos == 0, got, mine)

    def to_heads(first, second):
        got = other_branch(jnp.where(branch_pos == 0, second, first))
        return join(jnp.where(branch_pos == 0, first, second), got, branch_pos, 1)

    gated_pair = to_owner(gated_t)
    attn_pair = to_owner(attn_t)
    attn_rows = attn_t.shape[0]
    part_rows = attn_rows + local_inner

    raw = jnp.stack(
        [jnp.concatenate([first, second], axis=0) for first, second in zip(attn_pair, gated_pair)]
    )
    scanned_rows = (jnp.arange(part_rows) >= attn_rows)[None, :, None]
    gains = jnp.pad(gain_full.reshape(2, local_inner), ((0, 0), (attn_rows, 0)))[:, :, None]
    raw_values = raw.astype(F32)
    square_sum = jnp.sum(jnp.where(scanned_rows, raw_values * raw_values, 0.0), axis=(0, 1))
    gated_scale = lax.rsqrt(square_sum / inner_dim + EPSILON)[None, None, :]
    features = jnp.where(scanned_rows, (raw_values * gated_scale * gains).astype(BF16), raw)
    features = features.reshape(2 * part_rows, half_len)
    mixer_sum = mm(features, out_full, 0, 0)
    hidden = own_rows + own_valid * mixer_sum
    hidden_scale = rms_scale(hidden)
    hidden_hat = hidden * hidden_scale
    normed_ffn = (hidden_hat * ffn_gain).astype(BF16)

    ffn_out, grad_normed_ffn, acts = feed_forward(
        normed_ffn, upstream, gate_weight, up_weight, down_weight, 256
    )
    block_out = (hidden + ffn_out).astype(BF16)[None]
    grad_hidden = upstream.astype(F32) + rms_back(grad_normed_ffn, hidden, hidden_scale, ffn_gain)
    ffn_gain_grad = jnp.sum(grad_normed_ffn * hidden_hat, axis=0)
    grad_mixer = (own_valid * grad_hidden).astype(BF16)

    grad_features = mm(out_full, grad_mixer, 1, 1).reshape(2, part_rows, half_len)
    ssd_gain_wgrad = jnp.sum(grad_features * raw_values * gated_scale, axis=2)[:, attn_rows:].reshape(-1)
    weighted = grad_features * gains
    row_inner = jnp.sum(weighted * raw_values, axis=(0, 1), keepdims=True) / inner_dim
    grad_pair = jnp.where(
        scanned_rows,
        gated_scale * weighted - raw_values * (gated_scale**3 * row_inner),
        grad_features,
    ).astype(BF16)

    all_digits = [across] + row_digits
    attention_args = (qkv_t, rot_t, cosine, sine, run8, log_sums)
    ffn_rows = jnp.stack([normed_ffn, upstream])
    qkv_cols = qkv_t.shape[0]
    query_cols = local_query * HD
    if fast:
        x, y, z0, z1 = across, near, others[0], others[1]
        partners = [(item,) for item in all_digits] + [(x, y), (z0, z1)]
        orders = [
            [(core,), (y,), (z1,), (x,), (z0,)],
            [(core,), (z1,), (x,), (y,), (z0,)],
            [(core,), (x,), (z0,), (y,), (z1,)],
            [(core,), (y,), (x,), (z0,), (z1,)],
            [(core,), (x,), (y,), (z0,), (z1,)],
            [(core,), (z0,), (y,), (z1,), (x,)],
            [(core,), (y,), (z0,), (z1,), (x,)],
            [(core,), (x,), (y,), (z0,), (z1,)],
        ]
        part_row = gate_weight.shape[1] // (2 * row_count)
        summer = Summer([(part_row, model_dim // 2, BF16, all_digits, order, False) for order in orders])
        hooks = {
            (2, "begin"): [(0, 0)],
            (3, "begin"): [(1, 0), (2, 0)],
            (4, "begin"): [(3, 0), (4, 0), (5, 0)],
            (4, 1): [(0, 1), (6, 0)],
            (4, 2): [(7, 0)],
            (5, 5): [(3, 1)],
            (5, 8): [(2, 1)],
            (5, 10): [(5, 1), (1, 1)],
            (6, 6): [(6, 1)],
            (6, 10): [(4, 1)],
            (6, 11): [(2, 2)],
            (7, 0): [(0, 2)],
            (7, 1): [(5, 2)],
            (7, 6): [(6, 2)],
            (7, 10): [(4, 2)],
            (7, 11): [(7, 1)],
            (8, 1): [(2, 3), (5, 3)],
            (8, 6): [(3, 2)],
            (8, 8): [(4, 3), (6, 3)],
            (8, 11): [(7, 2), (2, 4)],
            "late": [
                (1, 2), (3, 3), (0, 3), (5, 4), (4, 4), (7, 3), (6, 4), (1, 3),
                (0, 4), (3, 4), (1, 4), (7, 4),
            ],
        }
        dqkv_t, ssd_grads, ffn_sums = mixer_backward(
            acts,
            ffn_rows,
            grad_mixer,
            features,
            grad_pair,
            attention_args,
            ssd_args,
            entry,
            (summer, partners[:-2], across, hooks),
            (local_query, local_keyval, HD, local_heads, SP, BLOCK, REACH),
            1,
        )
        gate_grad, up_grad, down_grad, attn_out_grad, ssd_out_grad = ffn_sums
    else:
        got = other_branch(grad_pair[1 - branch_pos])
        head_grad = join(grad_pair[branch_pos], got, branch_pos, 1)
        ssd_grads = ssd_backward(*ssd_args, entry, head_grad[attn_rows:], local_heads, SP, BLOCK)
        dqkv_t = attention_backward(
            *attention_args, head_grad[:attn_rows], local_query, local_keyval, HD, BLOCK, REACH
        )
        gate_sum, up_sum, down_sum = [
            scatter_sum(
                mm(acts[item], ffn_rows[item // 2], 0, 0).astype(BF16).reshape(2 * row_count, -1, model_dim),
                all_digits,
                all_digits[::-1],
            ).astype(F32)
            for item in range(3)
        ]
        out_part = mm(grad_mixer, features, 0, 1).astype(BF16).reshape(row_count, -1, 2, part_rows)
        out_part = jnp.moveaxis(out_part, 2, 0).reshape(2 * row_count, -1, part_rows)
        out_sum = scatter_sum(out_part, all_digits, all_digits[::-1]).astype(F32)
        gate_grad, up_grad, down_grad = gate_sum.T, up_sum.T, down_sum
        attn_out_grad, ssd_out_grad = out_sum[:, :attn_rows].T, out_sum[:, attn_rows:].T
    dmixer_t, dvec_t, dstep_t, dlog_t, dtap_x, dtap_b, dskip = ssd_grads

    qkv_step_cols = qkv_cols + head_rows
    gather_digits = [core, across, near] + others
    own_width = local_inner // row_count
    gain_rows = model_dim // 128
    tap_rows = 4 * state_flat.shape[1] // 128
    bias_rows = state_flat.shape[1] // 128
    inner_rows = inner_dim // 128
    if fast:
        row_part = model_dim // row_count
        rows_total = 2 * gain_rows + tap_rows + bias_rows + 3 + inner_rows
        shared_rows = -(-rows_total // (2 * row_count))
        first = [(core,), (y,), (z0,), (z1,)]
        second = [(core,), (z0,), (y,), (z1,)]
        gathered = [(core,), (x, y), (z0, z1)]
        gather_digits = [core, x, y, z0, z1]
        summer = Summer(
            [
                (row_part, local_inner, BF16, row_digits, first, False),
                (row_part, local_inner, BF16, row_digits, second, False),
                (row_part, qkv_step_cols, BF16, row_digits, first, False),
                (row_part // 2, state_flat.shape[1], BF16, gather_digits, gathered, True),
                (own_width, 128, F32, row_digits, [(core,), (y,), (z0, z1)], False),
                (shared_rows, 128, F32, gather_digits, gathered, True),
            ]
        )
        arrays = [
            full_normed, dvec_t, dmixer_t, mixer_flat, state_flat, dqkv_t, qkv_flat, dstep_t, step_flat,
            inputs[0], grad_hidden,
        ]
        smalls = [
            norm_gain.reshape(1, model_dim), dtap_x, dtap_b, dskip, dlog_t, head_cols,
            ffn_gain_grad.reshape(gain_rows, 128), ssd_gain_wgrad.reshape(inner_rows, 128),
        ]
        outs = [
            ((half_len, model_dim), BF16),
            ((row_part, query_cols), F32),
            ((row_part,) + keyval_weight.shape[1:], F32),
            ((row_part,) + mixer_weight.shape[1:], F32),
            (state_weight.shape, F32),
            ((row_part, local_heads), F32),
            ((4, own_width), F32),
            ((1, own_width), F32),
            ((gain_rows, 128), F32),
            ((gain_rows, 128), F32),
            (conv_state.shape, F32),
            (bias_state.shape, F32),
            ((1, 2 * local_heads), F32),
            ((1, 2 * local_heads), F32),
            ((1, 2 * local_heads), F32),
            ((inner_rows, 128), F32),
        ]
        order = [
            (1, 1), (0, 1), (3, 2), (2, 0), (5, 1), (0, 2), (1, 2), (3, 3), (5, 2), (2, 1), (0, 3), "input", (3, 4),
            (1, 3), (5, 3), (3, 5), (2, 2), (5, 4), (5, 5), (2, 3),
        ]
        (
            input_grad, query_grad, keyval_grad, mixer_grad, state_grad, step_grad, taps_grad, bias_grad, gain_grad,
            ffn_gain_sum, state_taps_grad, state_bias_grad, step_bias_grad, decay_grad, skip_grad, ssd_gain_rows,
        ) = final_gradients(
            arrays, smalls, outs, (summer, partners, across, order), EPSILON, (local_heads, SP), 2
        )
        ssd_gain_sum = ssd_gain_rows.reshape(-1)
        ffn_gain_sum = ffn_gain_sum.reshape(-1)
        gain_grad, bias_grad = gain_grad.reshape(-1), bias_grad.reshape(-1)
        step_bias_grad, decay_grad, skip_grad = [
            item.reshape(-1) for item in (step_bias_grad, decay_grad, skip_grad)
        ]
    else:
        dstep_low = dstep_t.astype(BF16)
        partial_normed = (
            mm(dmixer_t, mixer_flat, 0, 1)
            + mm(dvec_t, state_flat, 0, 1)
            + mm(dqkv_t, qkv_flat, 0, 1)
            + mm(dstep_low, step_flat, 0, 1)
        ).astype(BF16)
        sent = lax.dynamic_slice_in_dim(partial_normed, (1 - branch_pos) * half_len, half_len, 0)
        kept = lax.dynamic_slice_in_dim(partial_normed, own_begin, half_len, 0)
        own_grad_normed = kept.astype(F32) + other_branch(sent).astype(F32)
        input_grad = grad_hidden + rms_back(own_grad_normed, own_rows, own_scale, norm_gain)
        input_grad = input_grad.astype(BF16)
        norm_gain_part = jnp.sum(partial_normed.astype(F32) * full_normed.astype(F32), axis=0) / norm_gain

        def row_sum(grads_t):
            value = mm(full_normed, grads_t, 0, 1).astype(BF16)
            value = value.reshape((row_count, -1) + value.shape[1:])
            return scatter_sum(value, row_digits, row_digits[::-1]).astype(F32)

        def everywhere(value):
            value = scatter_sum(value, gather_digits, gather_digits)
            return gather_all(value, gather_digits, gather_digits[::-1])

        mixer_grad = row_sum(dmixer_t).reshape((-1,) + mixer_weight.shape[1:])
        qkvs_sum = row_sum(jnp.concatenate([dqkv_t, dstep_low], axis=0))
        query_grad = qkvs_sum[:, :query_cols]
        keyval_grad = qkvs_sum[:, query_cols:qkv_cols].reshape((-1,) + keyval_weight.shape[1:])
        step_grad = qkvs_sum[:, qkv_cols : qkv_cols + local_heads]
        own_part = jnp.swapaxes(dtap_x[:, :5].T.reshape(5, row_count, own_width), 0, 1)
        own_sum = scatter_sum(own_part, row_digits, row_digits[::-1])
        taps_grad, bias_grad = own_sum[:4], own_sum[4]
        state_part = mm(full_normed, dvec_t, 0, 1).astype(BF16)
        state_part = everywhere(state_part.reshape(2 * row_count, -1, state_part.shape[1]))
        state_grad = state_part.astype(F32).reshape(state_weight.shape)

        def widen(values):
            full = jnp.zeros((2 * local_heads,), F32)
            return lax.dynamic_update_slice_in_dim(full, values, branch_pos * local_heads, 0)

        heads = slice(0, local_heads)
        small = [
            norm_gain_part,
            ffn_gain_grad,
            dtap_b[:, :4].T,
            dtap_b[:, 4],
            widen(jnp.sum(dstep_t[heads], axis=1)),
            widen(jnp.sum(dlog_t[heads], axis=1) * rates),
            widen(jnp.sum(dskip[:, 0].reshape(local_heads, SP), axis=1)),
            ssd_gain_wgrad,
        ]
        flat = jnp.concatenate([item.reshape(-1) for item in small])
        unit = 2 * row_count * 128
        flat = jnp.pad(flat, (0, -flat.shape[0] % unit)).reshape(2 * row_count, -1, 128)
        flat = everywhere(flat).reshape(-1)
        sums, begin = [], 0
        for item in small:
            sums.append(flat[begin : begin + item.size])
            begin += item.size
        gain_grad, ffn_gain_sum, state_taps_grad, state_bias_grad = sums[:4]
        step_bias_grad, decay_grad, skip_grad, ssd_gain_sum = sums[4:]
    own_gain_grad = lax.dynamic_slice_in_dim(
        ssd_gain_sum, branch_pos * local_inner + row_pos * own_width, own_width, 0
    )
    return (
        block_out,
        input_grad[None],
        gain_grad,
        query_grad,
        keyval_grad,
        mixer_grad,
        state_grad,
        step_grad,
        taps_grad,
        state_taps_grad.reshape(conv_state.shape),
        bias_grad,
        state_bias_grad.reshape(bias_state.shape),
        step_bias_grad,
        decay_grad,
        skip_grad,
        own_gain_grad,
        attn_out_grad,
        ssd_out_grad,
        ffn_gain_sum,
        gate_grad,
        up_grad,
        down_grad,
    )


def solution(mesh):
    in_specs = (
        P("rows", "branch", None),
        P("rows", None),
        P(),
        P(None, "branch"),
        P(None, None, "branch"),
        P(None, None, "branch"),
        P(),
        P(None, "branch"),
        P(None, "branch"),
        P(),
        P("branch"),
        P(),
        P("branch"),
        P("branch"),
        P("branch"),
        P("branch"),
        P("branch", None),
        P("branch", None),
        P(),
        P(),
        P(),
        P(),
        P("rows", "branch", None),
    )
    out_specs = (
        P("rows", "branch", None),
        P("rows", "branch", None),
        P(),
        P("rows", "branch"),
        P("rows", None, "branch"),
        P("rows", None, "branch"),
        P(),
        P("rows", "branch"),
        P(None, ("branch", "rows")),
        P(),
        P(("branch", "rows")),
        P(),
        P(),
        P(),
        P(),
        P(("branch", "rows")),
        P("branch", "rows"),
        P("branch", "rows"),
        P(),
        P(None, ("branch", "rows")),
        P(None, ("branch", "rows")),
        P(("branch", "rows"), None),
    )
    return jax.shard_map(
        per_device, mesh=mesh, in_specs=in_specs, out_specs=out_specs, check_vma=False
    )
```

```python
import functools
import itertools

import jax
import jax.numpy as jnp
from jax import lax
from jax.experimental import pallas as pl
from jax.experimental.pallas import tpu as pltpu
from jax.sharding import PartitionSpec as P

HD = 64
SH = 24
SP = 64
BLOCK = 256
REACH = 512
EPSILON = 1e-05
ROPE_BASE = 100000000000.0
F32 = jnp.float32
BF16 = jnp.bfloat16
PRECISE = lax.Precision.HIGHEST


def mm(left, right, left_dim, right_dim):
    return lax.dot_general(
        left, right, (((left_dim,), (right_dim,)), ((), ())), preferred_element_type=F32
    )


def mm_exact(left, right):
    return jnp.dot(left, right, preferred_element_type=F32, precision=PRECISE)


def shift_right(prev, cur, amount):
    joined = jnp.concatenate([prev, cur], axis=1)
    return pltpu.roll(joined, amount, 1)[:, prev.shape[1] :]


def shift_left(cur, after, amount):
    joined = jnp.concatenate([cur, after], axis=1)
    total = joined.shape[1]
    return pltpu.roll(joined, total - amount, 1)[:, : cur.shape[1]]


def conv_inputs(prev_ref, cur_ref, rows, run_row, is_first):
    cur = cur_ref[rows].astype(F32)
    prev = jnp.where(is_first, 0.0, prev_ref[rows].astype(F32))
    moved = [
        shift_right(prev, cur, offset) * (run_row >= float(offset)).astype(F32) for offset in (3, 2, 1)
    ]
    return moved + [cur]


def conv_rows(items, taps):
    result = taps[:, 4:5] + taps[:, 3:4] * items[3]
    for place in range(3):
        result = result + taps[:, place : place + 1] * items[place]
    return result


def step_rows(step_ref, head_ref):
    raw = step_ref[...] + head_ref[:, 0:1]
    return raw, jax.nn.softplus(raw)


def masks_of(run_col, block):
    rows = lax.broadcasted_iota(jnp.int32, (block, block), 0)
    cols = lax.broadcasted_iota(jnp.int32, (block, block), 1)
    gap = (rows - cols).astype(F32)
    return (gap >= 0.0) & (gap <= run_col)


def upper_ones(block):
    rows = lax.broadcasted_iota(jnp.int32, (block, block), 0)
    cols = lax.broadcasted_iota(jnp.int32, (block, block), 1)
    return (rows <= cols).astype(F32)


def ssd_forward_kernel(
    block, heads, head_dim,
    z_ref, x_ref, xp_ref, b_ref, bp_ref, step_ref, run_ref, runc_ref, tapx_ref, tapb_ref, head_ref, skip_ref,
    gated_ref, entry_ref,
    state, xdt,
):
    index = pl.program_id(0)
    is_first = index == 0

    @pl.when(is_first)
    def _():
        state[...] = jnp.zeros_like(state)

    run_row = run_ref[0:1, :]
    everything = slice(0, b_ref.shape[0])
    vec = conv_rows(conv_inputs(bp_ref, b_ref, everything, run_row, is_first), tapb_ref[...])
    vec = vec * jax.nn.sigmoid(vec)
    size = vec.shape[0] // 2
    in_low = vec[:size].astype(BF16)
    out_low = vec[size:].astype(BF16)
    raw, step = step_rows(step_ref, head_ref)
    rate = head_ref[:, 1:2]
    cum = mm_exact(step * rate, upper_ones(block))
    cum_col = jnp.transpose(cum)
    place = lax.broadcasted_iota(jnp.int32, (1, block), 1).astype(F32)
    carried = (run_row >= place + 1.0).astype(F32)
    last_run = run_row[:, block - 1 :]
    tail = (float(block - 1) - place <= last_run).astype(F32)
    last = cum[:, block - 1 :]
    entry = jnp.exp(cum) * carried
    to_end = jnp.exp(last - cum) * tail
    keep = jnp.exp(last) * carried[:, block - 1 :]
    allowed = masks_of(runc_ref[:, 0:1], block)
    cross = jnp.where(allowed, mm(out_low, in_low, 0, 0), 0.0)
    old = state[...]
    old_low = old.astype(BF16)
    entry_ref[0] = old_low
    for h in range(heads):
        rows = slice(h * head_dim, (h + 1) * head_dim)
        act = conv_rows(conv_inputs(xp_ref, x_ref, rows, run_row, is_first), tapx_ref[rows])
        act = act * jax.nn.sigmoid(act)
        part = act * step[h : h + 1]
        part_low = part.astype(BF16)
        decay = jnp.exp(jnp.minimum(cum_col[:, h : h + 1] - cum[h : h + 1], 0.0))
        weight = (cross * decay).astype(BF16)
        y_in = mm(part_low, weight, 1, 1)
        y_off = mm(old_low[rows], out_low, 1, 0)
        y_all = y_in + y_off * entry[h : h + 1] + skip_ref[rows, 0:1] * act
        gate = z_ref[rows].astype(F32)
        gated_ref[rows] = (y_all * gate * jax.nn.sigmoid(gate)).astype(gated_ref.dtype)
        xdt[rows] = (part * to_end[h : h + 1]).astype(BF16)
        state[rows] = old[rows] * keep[h : h + 1]
    state[...] += mm(xdt[...], in_low, 1, 1)


def ssd_backward_kernel(block, heads, head_dim, *refs):
    grad_ref = refs[13]
    ssd_backward_body(
        block, heads, head_dim, pl.program_id(0), pl.num_programs(0), lambda h: None,
        lambda chunk, low, high: grad_ref[low:high], *refs[:13], *refs[14:],
    )


def ssd_backward_body(
    block, heads, head_dim, index, count, hook, grad_of,
    z_ref, x_ref, xp_ref, b_ref, bp_ref, step_ref, run_ref, runc_ref, tapx_ref, tapb_ref, head_ref, skip_ref,
    entry_ref, runn_ref,
    dm_ref, db_ref, dstep_ref, drate_ref, dtapx_ref, dtapb_ref, dskip_ref,
    dstate, nextx, nextb, accx, accb, accs, xdt, dye, rowterm, colin, colst, direct, ystat,
):
    is_first = index == count - 1

    @pl.when(index == 0)
    def _():
        dstate[...] = jnp.zeros_like(dstate)
        nextx[...] = jnp.zeros_like(nextx)
        nextb[...] = jnp.zeros_like(nextb)
        accx[...] = jnp.zeros_like(accx)
        accb[...] = jnp.zeros_like(accb)
        accs[...] = jnp.zeros_like(accs)
        rowterm[...] = jnp.zeros_like(rowterm)
        colin[...] = jnp.zeros_like(colin)
        colst[...] = jnp.zeros_like(colst)
        direct[...] = jnp.zeros_like(direct)
        ystat[...] = jnp.zeros_like(ystat)

    run_row = run_ref[0:1, :]
    everything = slice(0, b_ref.shape[0])
    items_b = conv_inputs(bp_ref, b_ref, everything, run_row, is_first)
    convb = conv_rows(items_b, tapb_ref[...])
    sigb = jax.nn.sigmoid(convb)
    vec = convb * sigb
    size = vec.shape[0] // 2
    in_low = vec[:size].astype(BF16)
    out_low = vec[size:].astype(BF16)
    raw, step = step_rows(step_ref, head_ref)
    rate = head_ref[:, 1:2]
    upper = upper_ones(block)
    cum = mm_exact(step * rate, upper)
    cum_col = jnp.transpose(cum)
    place = lax.broadcasted_iota(jnp.int32, (1, block), 1).astype(F32)
    carried = (run_row >= place + 1.0).astype(F32)
    last_run = run_row[:, block - 1 :]
    tail = (float(block - 1) - place <= last_run).astype(F32)
    last = cum[:, block - 1 :]
    entry = jnp.exp(cum) * carried
    to_end = jnp.exp(last - cum) * tail
    keep = jnp.exp(last) * carried[:, block - 1 :]
    allowed = masks_of(runc_ref[:, 0:1], block)
    cross = jnp.where(allowed, mm(out_low, in_low, 0, 0), 0.0)
    old_low = entry_ref[0]
    dnew_low = dstate[...].astype(BF16)
    inner = xdt.shape[0]
    y_off = mm(old_low, out_low, 1, 0)
    u_off = mm(dnew_low, in_low, 1, 0)

    def conv_back(dvals, conv, sigm, items, taps, rows, after, acc, out_ref, out_rows):
        dconv = dvals * sigm * (1.0 + conv * (1.0 - sigm))

        def add(place, values):
            acc[place, rows] += sum(values[:, c : c + 128] for c in range(0, block, 128))

        add(4, dconv)
        for place in range(4):
            add(place, dconv * items[place])
        result = taps[:, 3:4] * dconv
        following = after[rows]
        for offset in range(1, 4):
            keep_cur = (run_row >= float(offset)).astype(F32)
            keep_next = (runn_ref[0:1, :] >= float(offset)).astype(F32)
            result = result + taps[:, 3 - offset : 4 - offset] * shift_left(
                dconv * keep_cur, following * keep_next, offset
            )
        after[rows] = dconv[:, :128]
        out_ref[out_rows] = result.astype(out_ref.dtype)

    dcross = jnp.zeros((block, block), F32)
    for h in range(heads):
        rows = slice(h * head_dim, (h + 1) * head_dim)
        one = slice(h, h + 1)
        items = conv_inputs(xp_ref, x_ref, rows, run_row, is_first)
        taps = tapx_ref[rows]
        conv = conv_rows(items, taps)
        sigm = jax.nn.sigmoid(conv)
        xh = conv * sigm
        gate = z_ref[rows].astype(F32)
        sig = jax.nn.sigmoid(gate)
        upstream = grad_of(count - 1 - index, h * head_dim, (h + 1) * head_dim).astype(F32)
        dyh = upstream * gate * sig
        dnew = dstate[rows]
        part = xh * step[one]
        part_low = part.astype(BF16)
        dy_low = dyh.astype(BF16)
        decay = jnp.exp(jnp.minimum(cum_col[:, one] - cum[one], 0.0))
        weight = (cross * decay).astype(BF16)
        y_in = mm(part_low, weight, 1, 1)
        y_scan = y_in + y_off[rows] * entry[one]
        u_in = mm(dy_low, weight, 1, 0)
        u_st = u_off[rows] * to_end[one]
        dcross = dcross + mm(dy_low, part_low, 0, 0) * decay
        part_f = part_low.astype(F32)
        u_all = u_in + u_st
        rowterm[one] = jnp.sum(dy_low.astype(F32) * y_scan, axis=0, keepdims=True)
        colin[one] = jnp.sum(part_f * u_in, axis=0, keepdims=True)
        colst[one] = jnp.sum(part_f * u_st, axis=0, keepdims=True)
        direct[one] = jnp.sum(xh * u_all, axis=0, keepdims=True)
        skip = skip_ref[rows, 0:1]
        y_all = y_scan + skip * xh
        dm_ref[rows] = (upstream * y_all * sig * (1.0 + gate * (1.0 - sig))).astype(dm_ref.dtype)
        prod = dyh * xh
        accs[rows] += sum(prod[:, c : c + 128] for c in range(0, block, 128))
        dact = step[one] * u_all + skip * dyh
        below = slice(inner + h * head_dim, inner + (h + 1) * head_dim)
        conv_back(dact, conv, sigm, items, taps, rows, nextx, accx, dm_ref, below)
        xdt[rows] = (part * to_end[one]).astype(BF16)
        dye[rows] = (dyh * entry[one]).astype(BF16)
        old = old_low[rows].astype(F32)
        ystat[one] = jnp.sum(dnew * old * keep[one], axis=0, keepdims=True)
        dstate[rows] = dnew * keep[one]
        hook(h)
    dcross_low = jnp.where(allowed, dcross, 0.0).astype(BF16)
    dout = mm(in_low, dcross_low, 1, 1) + mm(old_low, dye[...], 0, 0)
    din = mm(out_low, dcross_low, 1, 0) + mm(dnew_low, xdt[...], 0, 0)
    dstate[...] += mm(dye[...], out_low, 1, 1)
    lower = jnp.transpose(upper)
    kept_total = jnp.sum(ystat[...], axis=1, keepdims=True)
    dlog = (
        mm_exact(rowterm[...] - colin[...], lower)
        + mm_exact(colst[...], upper)
        - colst[...]
        + kept_total
    )
    dstep = direct[...] + rate * dlog
    dstep_ref[...] = dstep * jax.nn.sigmoid(raw)
    drate_ref[...] = dlog * step

    conv_back(
        jnp.concatenate([din, dout], axis=0), convb, sigb, items_b, tapb_ref[...], everything, nextb, accb,
        db_ref, everything,
    )

    @pl.when(is_first)
    def _():
        def spread(acc, out_ref):
            lanes = lax.broadcasted_iota(jnp.int32, out_ref.shape, 1)
            result = jnp.zeros(out_ref.shape, F32)
            for item in range(5):
                total = jnp.sum(acc[item], axis=1, keepdims=True)
                result = jnp.where(lanes == item, total, result)
            out_ref[...] = result

        spread(accx, dtapx_ref)
        spread(accb, dtapb_ref)
        dskip_ref[...] = jnp.broadcast_to(
            jnp.sum(accs[...], axis=1, keepdims=True), dskip_ref.shape
        )


def ssd_specs(block, inner, vec, rows16, chunk_of):
    wide = lambda i: (0, chunk_of(i))
    per = block // 128
    before = lambda i: (0, jnp.maximum(chunk_of(i) * per - 1, 0))
    whole = lambda i: (0, 0)
    return [
        pl.BlockSpec((inner, block), wide),
        pl.BlockSpec((inner, block), lambda i: (1, chunk_of(i))),
        pl.BlockSpec((inner, 128), lambda i: (1, before(i)[1])),
        pl.BlockSpec((vec, block), wide),
        pl.BlockSpec((vec, 128), before),
        pl.BlockSpec((rows16, block), wide),
        pl.BlockSpec((8, block), wide),
        pl.BlockSpec((block, 128), lambda i: (chunk_of(i), 0)),
        pl.BlockSpec((inner, 128), whole),
        pl.BlockSpec((vec, 128), whole),
        pl.BlockSpec((rows16, 128), whole),
        pl.BlockSpec((inner, 128), whole),
    ]


def ssd_forward(mixer_t, vec_t, step_t, run8, run_col, tap_x, tap_b, head_cols, skip_col, heads, head_dim, block):
    inner = mixer_t.shape[0] // 2
    seq = mixer_t.shape[1]
    vec = vec_t.shape[0]
    rows16 = step_t.shape[0]
    chunks = seq // block
    state_dim = vec // 2
    return pl.pallas_call(
        functools.partial(ssd_forward_kernel, block, heads, head_dim),
        grid=(chunks,),
        in_specs=ssd_specs(block, inner, vec, rows16, lambda i: i),
        out_specs=[
            pl.BlockSpec((inner, block), lambda i: (0, i)),
            pl.BlockSpec((1, inner, state_dim), lambda i: (i, 0, 0)),
        ],
        out_shape=[
            jax.ShapeDtypeStruct((inner, seq), BF16),
            jax.ShapeDtypeStruct((chunks, inner, state_dim), BF16),
        ],
        scratch_shapes=[
            pltpu.VMEM((inner, state_dim), F32),
            pltpu.VMEM((inner, block), BF16),
        ],
        compiler_params=pltpu.CompilerParams(vmem_limit_bytes=48 << 20),
        cost_estimate=pl.CostEstimate(flops=10**9, bytes_accessed=10**7, transcendentals=10**7),
        name="ssd_forward",
    )(mixer_t, mixer_t, mixer_t, vec_t, vec_t, step_t, run8, run_col, tap_x, tap_b, head_cols, skip_col)


def ssd_backward(mixer_t, vec_t, step_t, run8, run_col, tap_x, tap_b, head_cols, skip_col, entry, grad_t, heads, head_dim, block):
    inner = mixer_t.shape[0] // 2
    seq = mixer_t.shape[1]
    vec = vec_t.shape[0]
    rows16 = step_t.shape[0]
    chunks = seq // block
    state_dim = vec // 2
    per = block // 128
    chunk_of = lambda i: chunks - 1 - i
    wide = lambda i: (0, chunk_of(i))
    whole = lambda i: (0, 0)
    return pl.pallas_call(
        functools.partial(ssd_backward_kernel, block, heads, head_dim),
        grid=(chunks,),
        in_specs=ssd_specs(block, inner, vec, rows16, chunk_of)
        + [
            pl.BlockSpec((1, inner, state_dim), lambda i: (chunk_of(i), 0, 0)),
            pl.BlockSpec((inner, block), wide),
            pl.BlockSpec((8, 128), lambda i: (0, jnp.minimum(chunk_of(i) * per + per, chunks * per - 1))),
        ],
        out_specs=[
            pl.BlockSpec((2 * inner, block), wide),
            pl.BlockSpec((vec, block), wide),
            pl.BlockSpec((rows16, block), wide),
            pl.BlockSpec((rows16, block), wide),
            pl.BlockSpec((inner, 128), whole),
            pl.BlockSpec((vec, 128), whole),
            pl.BlockSpec((inner, 128), whole),
        ],
        out_shape=[
            jax.ShapeDtypeStruct((2 * inner, seq), BF16),
            jax.ShapeDtypeStruct((vec, seq), BF16),
            jax.ShapeDtypeStruct((rows16, seq), F32),
            jax.ShapeDtypeStruct((rows16, seq), F32),
            jax.ShapeDtypeStruct((inner, 128), F32),
            jax.ShapeDtypeStruct((vec, 128), F32),
            jax.ShapeDtypeStruct((inner, 128), F32),
        ],
        scratch_shapes=[
            pltpu.VMEM((inner, state_dim), F32),
            pltpu.VMEM((inner, 128), F32),
            pltpu.VMEM((vec, 128), F32),
            pltpu.VMEM((5, inner, 128), F32),
            pltpu.VMEM((5, vec, 128), F32),
            pltpu.VMEM((inner, 128), F32),
            pltpu.VMEM((inner, block), BF16),
            pltpu.VMEM((inner, block), BF16),
            pltpu.VMEM((rows16, block), F32),
            pltpu.VMEM((rows16, block), F32),
            pltpu.VMEM((rows16, block), F32),
            pltpu.VMEM((rows16, block), F32),
            pltpu.VMEM((rows16, state_dim), F32),
        ],
        compiler_params=pltpu.CompilerParams(vmem_limit_bytes=48 << 20),
        cost_estimate=pl.CostEstimate(flops=3 * 10**9, bytes_accessed=2 * 10**7, transcendentals=3 * 10**7),
        name="ssd_backward",
    )(
        mixer_t, mixer_t, mixer_t, vec_t, vec_t, step_t, run8, run_col, tap_x, tap_b, head_cols, skip_col,
        entry, grad_t, run8,
    )


def rotate_rows(values, cosine, sine):
    half = values.shape[0] // 2
    first, second = values[:half], values[half:]
    return jnp.concatenate(
        [first * cosine - second * sine, second * cosine + first * sine], axis=0
    )


def window_of(block_index, block, reach):
    low = max(0, (block_index * block - (reach - 1)) // block)
    return low * block, (block_index + 1) * block


def allowed_of(run_ref, begin, stop, block):
    start, end = stop
    keys = lax.broadcasted_iota(jnp.int32, (end - start, block), 0) + start
    queries = lax.broadcasted_iota(jnp.int32, (end - start, block), 1) + begin
    gap = (queries - keys).astype(F32)
    return (gap >= 0.0) & (gap <= run_ref[0:1, begin : begin + block])


def attention_forward_kernel(
    heads, groups, head_dim, block, reach, scale,
    proj_ref, cos_ref, sin_ref, run_ref, out_ref, rot_ref, lse_ref,
):
    seq = proj_ref.shape[1]
    cosine, sine = cos_ref[...], sin_ref[...]
    total = heads + groups
    for item in range(total):
        rows = slice(item * head_dim, (item + 1) * head_dim)
        rot_ref[rows] = rotate_rows(proj_ref[rows].astype(F32), cosine, sine).astype(BF16)
    for index in range(seq // block):
        begin = index * block
        span = window_of(index, block, reach)
        allowed = allowed_of(run_ref, begin, span, block)
        for h in range(heads):
            group = h * groups // heads
            rows = slice(h * head_dim, (h + 1) * head_dim)
            krows = slice((heads + group) * head_dim, (heads + group + 1) * head_dim)
            vrows = slice((heads + groups + group) * head_dim, (heads + groups + group + 1) * head_dim)
            query = rot_ref[rows, begin : begin + block]
            key = rot_ref[krows, span[0] : span[1]]
            value = proj_ref[vrows, span[0] : span[1]].astype(BF16)
            logits = jnp.where(allowed, mm(key, query, 0, 0) * scale, -1e30)
            peak = jnp.max(logits, axis=0, keepdims=True)
            powered = jnp.exp(logits - peak)
            mass = jnp.sum(powered, axis=0, keepdims=True)
            probs = (powered * (1.0 / mass)).astype(BF16)
            out_ref[rows, begin : begin + block] = mm(value, probs, 1, 0).astype(out_ref.dtype)
            lse_ref[h : h + 1, begin : begin + block] = peak + jnp.log(mass)


def attention_backward_kernel(
    heads, groups, head_dim, block, reach, scale, grad_of, hook,
    proj_ref, rot_ref, cos_ref, sin_ref, run_ref, lse_ref, back_ref,
    acc_key, acc_value,
):
    seq = proj_ref.shape[1]
    acc_key[...] = jnp.zeros_like(acc_key)
    acc_value[...] = jnp.zeros_like(acc_value)
    for index in range(seq // block):
        begin = index * block
        span = window_of(index, block, reach)
        allowed = allowed_of(run_ref, begin, span, block)
        cosine, sine = cos_ref[:, begin : begin + block], sin_ref[:, begin : begin + block]
        for h in range(heads):
            group = h * groups // heads
            rows = slice(h * head_dim, (h + 1) * head_dim)
            krows = slice((heads + group) * head_dim, (heads + group + 1) * head_dim)
            vrows = slice((heads + groups + group) * head_dim, (heads + groups + group + 1) * head_dim)
            grows = slice(group * head_dim, (group + 1) * head_dim)
            query = rot_ref[rows, begin : begin + block]
            key = rot_ref[krows, span[0] : span[1]]
            value = proj_ref[vrows, span[0] : span[1]].astype(BF16)
            grad = grad_of(h * head_dim, (h + 1) * head_dim, begin)
            logits = jnp.where(allowed, mm(key, query, 0, 0) * scale, -1e30)
            probs = jnp.exp(logits - lse_ref[h : h + 1, begin : begin + block])
            dprobs = mm(value, grad, 0, 0)
            centre = jnp.sum(probs * dprobs, axis=0, keepdims=True)
            dscore = (probs * (dprobs - centre) * scale).astype(BF16)
            dquery = mm(key, dscore, 1, 0)
            back_ref[rows, begin : begin + block] = rotate_rows(dquery, cosine, -sine).astype(BF16)
            acc_key[grows, span[0] : span[1]] += mm(query, dscore, 1, 1)
            acc_value[grows, span[0] : span[1]] += mm(grad, probs.astype(BF16), 1, 1)
        hook(index)
    for group in range(groups):
        grows = slice(group * head_dim, (group + 1) * head_dim)
        krows = slice((heads + group) * head_dim, (heads + group + 1) * head_dim)
        vrows = slice((heads + groups + group) * head_dim, (heads + groups + group + 1) * head_dim)
        back_ref[krows] = rotate_rows(acc_key[grows], cos_ref[...], -sin_ref[...]).astype(BF16)
        back_ref[vrows] = acc_value[grows].astype(BF16)


def attention_forward(proj_t, cosine, sine, run8, heads, groups, head_dim, block, reach):
    seq = proj_t.shape[1]
    return pl.pallas_call(
        functools.partial(attention_forward_kernel, heads, groups, head_dim, block, reach, head_dim**-0.5),
        out_shape=[
            jax.ShapeDtypeStruct((heads * head_dim, seq), BF16),
            jax.ShapeDtypeStruct(((heads + groups) * head_dim, seq), BF16),
            jax.ShapeDtypeStruct((max(heads, 8), seq), F32),
        ],
        compiler_params=pltpu.CompilerParams(vmem_limit_bytes=48 << 20),
        cost_estimate=pl.CostEstimate(flops=2 * 10**9, bytes_accessed=10**7, transcendentals=4 * 10**6),
        name="attention_forward",
    )(proj_t, cosine, sine, run8)


def attention_backward_call(
    heads, groups, head_dim, block, reach, proj_ref, rot_ref, cos_ref, sin_ref, run_ref, lse_ref, grad_ref, *refs
):
    attention_backward_kernel(
        heads, groups, head_dim, block, reach, head_dim**-0.5,
        lambda low, high, begin: grad_ref[low:high, begin : begin + block], lambda index: None,
        proj_ref, rot_ref, cos_ref, sin_ref, run_ref, lse_ref, *refs,
    )


def attention_backward(proj_t, rot_t, cosine, sine, run8, lse, grad_t, heads, groups, head_dim, block, reach):
    seq = proj_t.shape[1]
    return pl.pallas_call(
        functools.partial(attention_backward_call, heads, groups, head_dim, block, reach),
        out_shape=jax.ShapeDtypeStruct(proj_t.shape, BF16),
        scratch_shapes=[
            pltpu.VMEM((groups * head_dim, seq), F32),
            pltpu.VMEM((groups * head_dim, seq), F32),
        ],
        compiler_params=pltpu.CompilerParams(vmem_limit_bytes=48 << 20),
        cost_estimate=pl.CostEstimate(flops=5 * 10**9, bytes_accessed=10**7, transcendentals=4 * 10**6),
        name="attention_backward",
    )(proj_t, rot_t, cosine, sine, run8, lse, grad_t)


def digit_of(digit):
    axis_name, bit, size = digit
    return (lax.axis_index(axis_name) // (1 << bit)) % 2


def partner_of(flipped):
    places = {}
    for digit in flipped:
        axis_name, bit, size = digit
        place = places.get(axis_name, lax.axis_index(axis_name))
        places[axis_name] = place + (1 - 2 * digit_of(digit)) * (1 << bit)
    return places


def send_to(flipped, source, target, send_sem, recv_sem):
    return pltpu.make_async_remote_copy(
        src_ref=source,
        dst_ref=target,
        send_sem=send_sem,
        recv_sem=recv_sem,
        device_id=partner_of(flipped),
        device_id_type=pl.DeviceIdType.MESH,
    )


def greet(partners):
    barrier = pltpu.get_barrier_semaphore()
    for flipped in partners:
        pl.semaphore_signal(
            barrier, inc=1, device_id=partner_of(flipped), device_id_type=pl.DeviceIdType.MESH
        )
    pl.semaphore_wait(barrier, len(partners))


def flips_of(group):
    return [
        tuple(digit for digit, bit in zip(group, bits) if bit)
        for bits in itertools.product((0, 1), repeat=len(group))
        if any(bits)
    ]


class Summer:
    def __init__(self, pieces):
        self.pieces = pieces
        self.count = len(pieces)
        for rows, cols, dtype, digits, order, gather in pieces:
            flat = [digit for group in order for digit in group]
            assert sorted(digits) == sorted(flat) and (not gather or list(digits) == flat)

    def turns(self, item):
        return len(self.pieces[item][4]) * (2 if self.pieces[item][5] else 1)

    def scratch(self):
        shapes = []
        for item, (rows, cols, dtype, digits, order, gather) in enumerate(self.pieces):
            shapes.append(pltpu.VMEM((2,) * len(digits) + (rows, cols), dtype))
            left = len(digits)
            for group in order:
                left -= len(group)
                shapes.append(pltpu.VMEM(((1 << len(group)) - 1,) + (2,) * left + (rows, cols), dtype))
            if gather:
                shapes.append(pltpu.VMEM((1 << len(digits), rows, cols), dtype))
        most = max(self.turns(item) for item in range(self.count))
        wide = max((1 << len(group)) - 1 for piece in self.pieces for group in piece[4])
        return shapes + [pltpu.SemaphoreType.DMA((self.count, most, wide))] * 2

    def bind(self, emits, refs):
        self.emits, self.full, self.gots, self.alls = emits, [], [], []
        for rows, cols, dtype, digits, order, gather in self.pieces:
            self.full.append(refs[0])
            self.gots.append(refs[1 : 1 + len(order)])
            refs = refs[1 + len(order) :]
            if gather:
                self.alls.append(refs[0])
                refs = refs[1:]
            else:
                self.alls.append(None)
        self.send_sem, self.recv_sem = refs

    def copies(self, item, turn):
        rows, cols, dtype, digits, order, gather = self.pieces[item]
        result = []
        if turn < len(order):
            done = [digit for group in order[:turn] for digit in group]
            group = order[turn]
        else:
            group = order[2 * len(order) - 1 - turn]
            ahead = [digit for group in order[: 2 * len(order) - 1 - turn] for digit in group]
            size = 1 << (len(digits) - len(ahead) - len(group))
            region = self.alls[item].at[pl.ds(self.place_of(ahead + list(group)) * size, size)]
        for slot, flipped in enumerate(flips_of(group)):
            if turn < len(order):
                index = tuple(
                    1 - digit_of(digit) if digit in flipped
                    else digit_of(digit) if digit in done or digit in group
                    else slice(None)
                    for digit in digits
                )
                source, target = self.full[item].at[index], self.gots[item][turn].at[slot]
            else:
                source = target = region
            result.append(
                send_to(
                    flipped, source, target, self.send_sem.at[item, turn, slot], self.recv_sem.at[item, turn, slot]
                )
            )
        return result

    def place_of(self, digits):
        place = 0
        for digit in digits:
            place = place * 2 + digit_of(digit)
        return place

    def start(self, item, turn=0):
        for copy in self.copies(item, turn):
            copy.start()

    def advance(self, item, turn):
        rows, cols, dtype, digits, order, gather = self.pieces[item]
        for copy in self.copies(item, turn):
            copy.wait()
        if turn >= len(order):
            if turn + 1 < 2 * len(order):
                self.start(item, turn + 1)
            else:
                self.emits[item](self.alls[item])
            return
        done = [digit for group in order[: turn + 1] for digit in group]
        left = [digit for digit in digits if digit not in done]
        for bits in itertools.product((0, 1), repeat=len(left)):
            index = tuple(
                digit_of(digit) if digit in done else bits[left.index(digit)] for digit in digits
            )
            value = self.full[item][index].astype(F32)
            for slot in range((1 << len(order[turn])) - 1):
                value = value + self.gots[item][turn][(slot,) + bits].astype(F32)
            if left:
                self.full[item][index] = value.astype(dtype)
            elif gather:
                self.alls[item][self.place_of(digits)] = value.astype(dtype)
            else:
                self.emits[item](value)
        if turn + 1 < self.turns(item):
            self.start(item, turn + 1)


def ffn_tile(eps, hidden_ref, valid_ref, gain_ref, cot_ref, gate_ref, up_ref, down_ref, act_ref, out_acc, back_acc, normed_ref):
    @pl.when(pl.program_id(0) == 0)
    def _():
        out_acc[...] = jnp.zeros_like(out_acc)
        back_acc[...] = jnp.zeros_like(back_acc)

        @pl.loop(0, normed_ref.shape[0] // 64)
        def _(t):
            at = pl.ds(pl.multiple_of(t * 64, 64), 64)
            values = hidden_ref[at]
            scale = lax.rsqrt(jnp.mean(values * values, axis=1, keepdims=True) + eps)
            normed_ref[at] = (values * scale * gain_ref[...]).astype(BF16)

    normed, cot = normed_ref[...], cot_ref[...]
    gate_w, up_w, down_w = gate_ref[...], up_ref[...], down_ref[...]
    gate = mm(normed, gate_w, 1, 0)
    up = mm(normed, up_w, 1, 0)
    grad_act = mm(cot, down_w, 1, 1)
    sig = jax.nn.sigmoid(gate)
    silu = gate * sig
    act = (silu * up).astype(BF16)
    dgate = (grad_act * up * sig * (1.0 + gate * (1.0 - sig))).astype(BF16)
    dup = (grad_act * silu).astype(BF16)
    act_ref[...] = act
    out_acc[...] += mm(act, down_w, 1, 0)
    back_acc[...] += mm(dgate, gate_w, 1, 1) + mm(dup, up_w, 1, 1)
    return normed, dgate, dup


def ffn_end(eps, hidden_ref, valid_ref, gain_ref, cot_ref, outs, out_acc, back_acc):
    block_ref, grad_ref, mixer_ref, gain_grad_ref = outs
    gain = gain_ref[...]
    gain_grad_ref[...] = jnp.zeros_like(gain_grad_ref)

    @pl.loop(0, out_acc.shape[0] // 64)
    def _(t):
        at = pl.ds(pl.multiple_of(t * 64, 64), 64)
        values = hidden_ref[at]
        scale = lax.rsqrt(jnp.mean(values * values, axis=1, keepdims=True) + eps)
        upstream = back_acc[at]
        weighted = upstream * gain
        centre = jnp.mean(weighted * values, axis=1, keepdims=True)
        grad = cot_ref[at].astype(F32) + scale * weighted - values * (scale * scale * scale * centre)
        block_ref[at] = (values + out_acc[at]).astype(BF16)
        grad_ref[at] = grad
        mixer_ref[at] = (valid_ref[at, 0:1] * grad).astype(BF16)
        gain_grad_ref[...] += jnp.sum(upstream * values * scale, axis=0, keepdims=True)


def ffn_plain_kernel(tiles, eps, *refs):
    ins, outs, accs = refs[:7], refs[7:14], refs[14:]
    normed, dgate, dup = ffn_tile(eps, *ins, outs[4], *accs)
    for wgrad_ref, grads in zip(outs[5:], (dgate, dup)):
        wgrad_ref[...] = mm(grads, normed, 0, 0).astype(BF16)

    @pl.when(pl.program_id(0) == tiles - 1)
    def _():
        ffn_end(eps, *ins[:4], outs[:4], *accs[:2])


def ffn_sum_kernel(digits, tiles, eps, *refs):
    core, near, far = digits
    ins, outs, accs = refs[:7], refs[7:14], refs[14:17]
    gate_out, up_out = outs[5:]
    full_gate, full_up, got_gate, got_up, far_gate, far_up, sems = refs[17:]
    fulls, gots = (full_gate, full_up), (got_gate, got_up)
    step = pl.program_id(0)
    mine, near_bit, far_bit = digit_of(core), digit_of(near), digit_of(far)

    def core_copy(item, tile):
        return send_to(
            (core,), fulls[item].at[tile, :, 1 - mine], gots[item].at[tile], sems.at[0, item, tile], sems.at[1, item, tile]
        )

    def near_copy(tile):
        return send_to(
            (near,), full_gate.at[tile, 1 - near_bit, mine], far_gate.at[tile], sems.at[2, 0, tile], sems.at[3, 0, tile]
        )

    def far_copy(pair):
        return send_to(
            (far,), full_up.at[2 * pair + 1 - far_bit, :, mine], far_up.at[pair], sems.at[2, 1, pair], sems.at[3, 1, pair]
        )

    def finish(tile):
        for item in range(2):
            core_copy(item, tile).wait()
            total = fulls[item][tile, :, mine].astype(F32) + gots[item][tile].astype(F32)
            fulls[item][tile, :, mine] = total.astype(BF16)
        near_copy(tile).start()

        @pl.when(tile % 2 == 1 - far_bit)
        def _():
            far_copy(tile // 2).start()

    @pl.when(step == 0)
    def _():
        greet([(item,) for item in digits])

    normed, dgate, dup = ffn_tile(eps, *ins, outs[4], *accs)
    for item, grads in enumerate((dgate, dup)):
        value = mm(grads, normed, 0, 0).astype(BF16)
        fulls[item][step] = value.reshape(fulls[item].shape[1:])
        core_copy(item, step).start()

    @pl.when(step > 0)
    def _():
        finish(step - 1)

    @pl.when(step == tiles - 1)
    def _():
        finish(step)
        ffn_end(eps, *ins[:4], outs[:4], *accs[:2])
        for tile in range(tiles):
            near_copy(tile).wait()
            total = full_gate[tile, near_bit, mine].astype(F32) + far_gate[tile].astype(F32)
            gate_out[tile] = total.astype(BF16)
        for pair in range(tiles // 2):
            far_copy(pair).wait()
            for other in range(2):
                total = full_up[2 * pair + far_bit, other, mine].astype(F32) + far_up[pair, other].astype(F32)
                up_out[2 * pair + other] = total.astype(BF16)


def feed_forward(hidden, valid, gain, cot, gate_w, up_w, down_w, tile, eps, digits, collective_id):
    rows, width = hidden.shape
    inner = gate_w.shape[1]
    tiles = inner // tile
    whole = lambda i: (0, 0)
    once = pl.Buffered(1)
    scratch = [pltpu.VMEM((rows, width), F32)] * 2 + [pltpu.VMEM((rows, width), BF16)]
    if digits is None:
        kernel = functools.partial(ffn_plain_kernel, tiles, eps)
        wgrads = [jax.ShapeDtypeStruct((inner, width), BF16)] * 2
        wgrad_specs = [pl.BlockSpec((tile, width), lambda i: (i, 0))] * 2
        params = pltpu.CompilerParams(vmem_limit_bytes=56 << 20)
    else:
        kernel = functools.partial(ffn_sum_kernel, digits, tiles, eps)
        part = tile // 4
        wgrads = [jax.ShapeDtypeStruct((tiles, part, width), BF16)] * 2
        wgrad_specs = [pl.BlockSpec((tiles, part, width), lambda i: (0, 0, 0))] * 2
        scratch += [pltpu.VMEM((tiles, 2, 2, part, width), BF16)] * 2
        scratch += [pltpu.VMEM((tiles, 2, part, width), BF16)] * 2
        scratch += [
            pltpu.VMEM((tiles, part, width), BF16),
            pltpu.VMEM((tiles // 2, 2, part, width), BF16),
            pltpu.SemaphoreType.DMA((4, 2, tiles)),
        ]
        params = pltpu.CompilerParams(
            vmem_limit_bytes=60 << 20, collective_id=collective_id, has_side_effects=True
        )
    return pl.pallas_call(
        kernel,
        grid=(tiles,),
        in_specs=[
            pl.BlockSpec((rows, width), whole, pipeline_mode=once),
            pl.BlockSpec((rows, 128), whole, pipeline_mode=once),
            pl.BlockSpec((1, width), whole, pipeline_mode=once),
            pl.BlockSpec((rows, width), whole, pipeline_mode=once),
            pl.BlockSpec((width, tile), lambda i: (0, i)),
            pl.BlockSpec((width, tile), lambda i: (0, i)),
            pl.BlockSpec((tile, width), lambda i: (i, 0)),
        ],
        out_specs=[
            pl.BlockSpec((rows, width), whole),
            pl.BlockSpec((rows, width), whole),
            pl.BlockSpec((rows, width), whole),
            pl.BlockSpec((1, width), whole),
            pl.BlockSpec((rows, tile), lambda i: (0, i)),
        ]
        + wgrad_specs,
        out_shape=[
            jax.ShapeDtypeStruct((rows, width), BF16),
            jax.ShapeDtypeStruct((rows, width), F32),
            jax.ShapeDtypeStruct((rows, width), BF16),
            jax.ShapeDtypeStruct((1, width), F32),
            jax.ShapeDtypeStruct((rows, inner), BF16),
        ]
        + wgrads,
        scratch_shapes=scratch,
        compiler_params=params,
        cost_estimate=pl.CostEstimate(
            flops=8 * 2 * rows * width * inner, bytes_accessed=3 * 10**7, transcendentals=rows * inner
        ),
        name="feed_forward",
    )(hidden, valid, gain.reshape(1, width), cot, gate_w, up_w, down_w)


def backward_kernel(plan, sizes, attention_count, ssd_count, ssd_outs, scratch_counts, *refs):
    query_heads, groups, head_dim, heads, ssd_dim, block, reach = sizes
    summer, partners, across, hooks = plan
    step = pl.program_id(0)
    steps = pl.num_programs(0)
    (act_ref, rows_ref, mixer_ref, feature_ref, pair_ref, gate_part, up_part), refs = refs[:7], refs[7:]
    attention_in, refs = refs[:attention_count], refs[attention_count:]
    ssd_in, refs = refs[:ssd_count], refs[ssd_count:]
    attention_out, refs = refs[:1], refs[1:]
    ssd_out, refs = refs[:ssd_outs], refs[ssd_outs:]
    part_out, refs = refs[:5], refs[5:]
    attention_scratch, refs = refs[: scratch_counts[0]], refs[scratch_counts[0] :]
    ssd_scratch, refs = refs[: scratch_counts[1]], refs[scratch_counts[1] :]
    (head_grad, pair_sem), refs = refs[:2], refs[2:]
    branch_pos = digit_of(across)
    attn_rows = query_heads * head_dim
    gate_out, up_out, down_out, attn_out, ssd_w_out = part_out

    def to_rows(out_ref, begin):
        def emit(value):
            out_ref[:, begin : begin + value.shape[1]] = value

        return emit

    def to_outputs(value):
        attn_out[...] = value[:, :attn_rows]
        ssd_w_out[:, : value.shape[1] - attn_rows] = value[:, attn_rows:]

    width = rows_ref.shape[1] // 2
    summer.bind(
        [
            to_rows(gate_out, 0), to_rows(up_out, 0), to_rows(down_out, 0), to_rows(down_out, width),
            to_outputs, to_rows(ssd_w_out, width - attn_rows),
        ],
        refs,
    )

    def exchange(part):
        low, high = ((0, attn_rows), (attn_rows, head_grad.shape[1]))[part]
        return send_to(
            (across,),
            pair_ref.at[1 - branch_pos, low:high],
            head_grad.at[branch_pos, low:high],
            pair_sem.at[2 * part],
            pair_sem.at[2 * part + 1],
        )

    def own_pair():
        return pltpu.make_async_copy(
            pair_ref.at[branch_pos], head_grad.at[branch_pos], pair_sem.at[4]
        )

    def run(events):
        for item, turn in events:
            summer.advance(item, turn)

    def load_of(item):
        return pltpu.make_async_copy((gate_part, up_part)[item], summer.full[item], pair_sem.at[5 + item])

    tile = 256

    @pl.when(step == 0)
    def _():
        load_of(0).start()
        load_of(1).start()
        own_pair().start()
        greet(partners)
        exchange(0).start()
        exchange(1).start()
        for item in range(2):
            load_of(item).wait()
            summer.start(item)
        right = rows_ref[...]

        @pl.loop(0, act_ref.shape[1] // tile, unroll=2)
        def _(t):
            left = act_ref[:, pl.ds(pl.multiple_of(t * tile, tile), tile)]
            value = mm(left, right, 0, 0).astype(BF16)
            for part in range(2):
                full = summer.full[2 + part]
                columns = value[:, part * width : (part + 1) * width]
                full[t // 4, (t // 2) % 2, t % 2] = columns.reshape(full.shape[3:])

        summer.start(2)
        summer.start(3)

    @pl.when(step == 1)
    def _():
        run(hooks.get((1, "begin"), ()))
        half = feature_ref.shape[0] // 2

        @pl.loop(0, mixer_ref.shape[1] // tile)
        def _(t):
            left = mixer_ref[:, pl.ds(pl.multiple_of(t * tile, tile), tile)]
            for part in range(2):
                value = mm(left, feature_ref[part * half : (part + 1) * half], 0, 1).astype(BF16)
                for piece in range(2):
                    full = summer.full[4 + piece]
                    columns = value[:, piece * width : (piece + 1) * width]
                    full[part, t // 2, t % 2] = columns.reshape(full.shape[3:])

        summer.start(4)
        summer.start(5)

    @pl.when(step == 2)
    def _():
        exchange(0).wait()
        own_pair().wait()
        run(hooks.get((2, "begin"), ()))

        def grad_of(low, high, begin):
            width = head_grad.shape[2]
            return head_grad[begin // width, low:high, begin % width : begin % width + block]

        attention_backward_kernel(
            query_heads, groups, head_dim, block, reach, head_dim**-0.5,
            grad_of, lambda index: run(hooks.get((2, index), ())), *attention_in, *attention_out, *attention_scratch,
        )

    timed = [item for item in hooks.items() if item[0] != "late"]

    @pl.when(step == 3)
    def _():
        exchange(1).wait()

    @pl.when(step > 2)
    def _():
        def hook(h):
            for (at_step, at_head), events in timed:
                if at_head == h and at_step > 2:
                    @pl.when(step == at_step)
                    def _():
                        run(events)

        def grad_of(chunk, low, high):
            per = head_grad.shape[2] // block
            begin = pl.multiple_of((chunk % per) * block, block)
            return head_grad[chunk // per, attn_rows + low : attn_rows + high, pl.ds(begin, block)]

        ssd_backward_body(block, heads, ssd_dim, step - 3, steps - 3, hook, grad_of, *ssd_in, *ssd_out, *ssd_scratch)

    late = hooks.get("late", ())

    @pl.when(step == steps - 1)
    def _():
        run(late)


def mixer_backward(act, rows, grad_mixer, features, grad_pair, gate_part, up_part, attention_args, ssd_args, entry, plan, sizes, collective_id):
    query_heads, groups, head_dim, heads, ssd_dim, block, reach = sizes
    summer = plan[0]
    mixer_t, vec_t, step_t, run8, run_col, tap_x, tap_b, head_cols, skip_col = ssd_args
    inner = mixer_t.shape[0] // 2
    seq = mixer_t.shape[1]
    vec = vec_t.shape[0]
    rows16 = step_t.shape[0]
    chunks = seq // block
    state_dim = vec // 2
    per = block // 128
    before = 3
    chunk_of = lambda i: jnp.minimum(chunks - 1 + before - i, chunks - 1)
    wide = lambda i: (0, chunk_of(i))
    whole = lambda i: (0, 0)
    proj_t = attention_args[0]
    once = pl.Buffered(1)
    ssd_in = [mixer_t, mixer_t, mixer_t, vec_t, vec_t, step_t, run8, run_col, tap_x, tap_b, head_cols, skip_col]
    ssd_in += [entry, run8]
    in_specs = [
        pl.BlockSpec(act.shape, whole, pipeline_mode=once),
        pl.BlockSpec(rows.shape, whole, pipeline_mode=once),
        pl.BlockSpec(grad_mixer.shape, whole, pipeline_mode=once),
        pl.BlockSpec(features.shape, whole, pipeline_mode=once),
        pl.BlockSpec(memory_space=pl.ANY),
        pl.BlockSpec(memory_space=pl.ANY),
        pl.BlockSpec(memory_space=pl.ANY),
    ]
    in_specs += [pl.BlockSpec(item.shape, whole, pipeline_mode=once) for item in attention_args]
    in_specs += ssd_specs(block, inner, vec, rows16, chunk_of)
    in_specs += [
        pl.BlockSpec((1, inner, state_dim), lambda i: (chunk_of(i), 0, 0)),
        pl.BlockSpec((8, 128), lambda i: (0, jnp.minimum(chunk_of(i) * per + per, chunks * per - 1))),
    ]
    ssd_out = [
        (2 * inner, seq, block, BF16),
        (vec, seq, block, BF16),
        (rows16, seq, block, F32),
        (rows16, seq, block, F32),
        (inner, 128, 128, F32),
        (vec, 128, 128, F32),
        (inner, 128, 128, F32),
    ]
    out_specs = [pl.BlockSpec(proj_t.shape, whole)]
    out_specs += [
        pl.BlockSpec((height, width), wide if full == seq else whole) for height, full, width, _ in ssd_out
    ]
    part_row = summer.pieces[0][0]
    model_dim = rows.shape[1]
    part_shapes = [
        jax.ShapeDtypeStruct(shape, F32)
        for shape in (
            (part_row, model_dim),
            (part_row, model_dim),
            (part_row, model_dim),
            (part_row, query_heads * head_dim),
            (part_row, inner),
        )
    ]
    out_specs += [pl.BlockSpec(item.shape, whole) for item in part_shapes]
    attention_scratch = [pltpu.VMEM((groups * head_dim, seq), F32)] * 2
    ssd_scratch = [
        pltpu.VMEM((inner, state_dim), F32),
        pltpu.VMEM((inner, 128), F32),
        pltpu.VMEM((vec, 128), F32),
        pltpu.VMEM((5, inner, 128), F32),
        pltpu.VMEM((5, vec, 128), F32),
        pltpu.VMEM((inner, 128), F32),
        pltpu.VMEM((inner, block), BF16),
        pltpu.VMEM((inner, block), BF16),
        pltpu.VMEM((rows16, block), F32),
        pltpu.VMEM((rows16, block), F32),
        pltpu.VMEM((rows16, block), F32),
        pltpu.VMEM((rows16, block), F32),
        pltpu.VMEM((rows16, state_dim), F32),
    ]
    results = pl.pallas_call(
        functools.partial(
            backward_kernel, plan, sizes, len(attention_args), len(ssd_in), len(ssd_out),
            (len(attention_scratch), len(ssd_scratch)),
        ),
        grid=(chunks + before,),
        in_specs=in_specs,
        out_specs=out_specs,
        out_shape=[jax.ShapeDtypeStruct(proj_t.shape, BF16)]
        + [jax.ShapeDtypeStruct((height, full), dtype) for height, full, _, dtype in ssd_out]
        + part_shapes,
        scratch_shapes=attention_scratch
        + ssd_scratch
        + [pltpu.VMEM(grad_pair.shape, BF16), pltpu.SemaphoreType.DMA((7,))]
        + summer.scratch(),
        compiler_params=pltpu.CompilerParams(
            vmem_limit_bytes=63 << 20, collective_id=collective_id, has_side_effects=True
        ),
        cost_estimate=pl.CostEstimate(flops=7 * 10**10, bytes_accessed=5 * 10**7, transcendentals=3 * 10**7),
        name="mixer_backward",
    )(act, rows, grad_mixer, features, grad_pair, gate_part, up_part, *attention_args, *ssd_in)
    return results[0], results[1:8], results[8:]

def final_kernel(plan, eps, sizes, *refs):
    summer, partners, across, order = plan
    heads, head_dim = sizes
    names = ("normed", "dvec", "dmixer", "mixer_w", "state_w", "dqkv", "qkv_w", "dstep", "step_w", "rows", "hidden")
    hbm = dict(zip(names, refs[: len(names)]))
    refs = refs[len(names) :]
    (gain_ref, tapx_ref, tapb_ref, skip_ref, rate_ref, head_ref, ffn_gain_ref, ssd_gain_ref), refs = refs[:8], refs[8:]
    (
        input_out, query_out, keyval_out, mixer_out, state_out, step_out, taps_out, bias_out, gain_out, ffn_gain_out,
        state_taps_out, state_bias_out, bias_sum_out, rate_sum_out, skip_sum_out, ssd_gain_out,
    ), refs = refs[:16], refs[16:]
    vmem = dict(zip(names, refs[: len(names)]))
    refs = refs[len(names) :]
    partial, sent, got, load_sem, swap_sem = refs[:5]
    branch_pos = digit_of(across)
    half, width = partial.shape
    inner = vmem["dmixer"].shape[0] // 2
    query_cols = query_out.shape[1]
    key_cols = keyval_out.shape[2]
    gain_rows = width // 128
    state_rows = tapb_ref.shape[0] // 128

    def emit_mixer(part):
        def emit(value):
            mixer_out[:, part, :] = value

        return emit

    def emit_qkvs(value):
        query_out[...] = value[:, :query_cols]
        for part in range(2):
            keyval_out[:, part, :] = value[:, query_cols + part * key_cols : query_cols + (part + 1) * key_cols]
        begin = query_cols + 2 * key_cols
        steps = value[:, begin:]
        steps = jnp.concatenate([steps, jnp.zeros((steps.shape[0], 128 - steps.shape[1]), F32)], axis=1)
        step_out[...] = jnp.transpose(steps)[:heads]

    def emit_state(parts):
        values = parts[...].astype(F32)
        columns = values.shape[2] // 2
        for part in range(2):
            piece = values[:, :, part * columns : (part + 1) * columns]
            state_out[:, part, :] = piece.reshape(-1, columns)

    def emit_own(value):
        turned = jnp.transpose(value)
        taps_out[...] = turned[:4]
        bias_out[...] = turned[4:5]

    def emit_shared(parts):
        per = parts.shape[1]
        row = lambda place: parts[place // per, place % per : place % per + 1]
        for place in range(gain_rows):
            gain_out[place : place + 1] = row(place)
            ffn_gain_out[place : place + 1] = row(gain_rows + place)
        begin = 2 * gain_rows
        for tap in range(4):
            for part in range(state_rows):
                state_taps_out[tap, part : part + 1] = row(begin + tap * state_rows + part)
        begin += 4 * state_rows
        for part in range(state_rows):
            state_bias_out[part : part + 1] = row(begin + part)
        begin += state_rows
        for place, out_ref in enumerate((bias_sum_out, rate_sum_out, skip_sum_out)):
            out_ref[...] = row(begin + place)[:, : out_ref.shape[1]]
        begin += 3
        for place in range(ssd_gain_out.shape[0]):
            ssd_gain_out[place : place + 1] = row(begin + place)

    summer.bind(
        [emit_mixer(0), emit_mixer(1), emit_qkvs, emit_state, emit_own, emit_shared], refs[5:]
    )

    def load(name):
        return pltpu.make_async_copy(hbm[name], vmem[name], load_sem.at[names.index(name)])

    for name in names:
        load(name).start()
    greet(partners)
    gain = gain_ref[...]

    def index_of(full, owner):
        digits = len(full.shape) - 2
        return tuple((owner >> (digits - 1 - place)) & 1 for place in range(digits))

    own = summer.full[4]
    own_rows = own.shape[-2]
    for owner in range(tapx_ref.shape[0] // own_rows):
        own[index_of(own, owner)] = tapx_ref[owner * own_rows : (owner + 1) * own_rows]
    summer.start(4)

    shared = summer.full[5]
    per = shared.shape[-2]

    def put(place, row):
        shared[index_of(shared, place // per) + (slice(place % per, place % per + 1),)] = row

    for place in range(gain_rows):
        put(gain_rows + place, ffn_gain_ref[place : place + 1])
    begin = 2 * gain_rows
    turned = jnp.transpose(tapb_ref[...])
    for tap in range(5):
        for part in range(state_rows):
            put(begin + tap * state_rows + part, turned[tap : tap + 1, part * 128 : (part + 1) * 128])
    begin += 5 * state_rows

    def head_row(column):
        row = jnp.transpose(jnp.broadcast_to(column, (column.shape[0], 128)))[0:1]
        row = jnp.concatenate([row, jnp.zeros((1, 128 - row.shape[1]), F32)], axis=1)
        lanes = lax.broadcasted_iota(jnp.int32, row.shape, 1)
        row = jnp.where(lanes < heads, row, 0.0)
        return jnp.where(branch_pos == 0, row, pltpu.roll(row, heads, 1))

    rate_column = jnp.sum(rate_ref[...], axis=1, keepdims=True) * head_ref[:, 1:2]
    put(begin + 1, head_row(rate_column))
    skips = jnp.sum(skip_ref[...].reshape(heads, head_dim, 128), axis=1)[:, 0:1]
    pad = rate_ref.shape[0] - heads
    put(begin + 2, head_row(jnp.concatenate([skips, jnp.zeros((pad, 1), F32)], axis=0)))
    for place in range(ssd_gain_ref.shape[0]):
        put(begin + 3 + place, ssd_gain_ref[place : place + 1])
    for place in range(begin + 3 + ssd_gain_ref.shape[0], per << (len(shared.shape) - 2)):
        put(place, jnp.zeros((1, 128), F32))

    def partial_of(begin):
        at = pl.ds(pl.multiple_of(begin, 256), 256)
        return (
            mm(vmem["dmixer"][:, at], vmem["mixer_w"][...], 0, 1)
            + mm(vmem["dvec"][:, at], vmem["state_w"][...], 0, 1)
            + mm(vmem["dqkv"][:, at], vmem["qkv_w"][...], 0, 1)
            + mm(vmem["dstep"][:, at].astype(BF16), vmem["step_w"][...], 0, 1)
        )

    chunks = half // 256

    def swap(part):
        rows = slice(part * 256, (part + 1) * 256)
        return send_to((across,), sent.at[rows], got.at[rows], swap_sem.at[0, part], swap_sem.at[1, part])

    tile = 256
    tiles = width // tile

    def left_tile(t):
        return vmem["normed"][:, pl.ds(pl.multiple_of(t * tile, tile), tile)]

    def gain_sum(tokens, begin):
        return jnp.sum(
            tokens * vmem["normed"][pl.ds(pl.multiple_of(begin, 256), 256)].astype(F32), axis=0, keepdims=True
        )

    load("normed").wait()
    load("dvec").wait()

    @pl.loop(0, tiles)
    def _(t):
        value = mm(left_tile(t), vmem["dvec"][...], 0, 1).astype(BF16)
        summer.full[3][t // 2, t % 2] = value.reshape(summer.full[3].shape[2:])

    summer.start(3)
    summer.advance(4, 0)
    load("dmixer").wait()
    for item, begin_row in ((1, inner), (0, 0)):
        @pl.loop(0, tiles)
        def _(t):
            value = mm(left_tile(t), vmem["dmixer"][begin_row : begin_row + inner], 0, 1).astype(BF16)
            summer.full[item][t // 2, t % 2] = value.reshape(summer.full[item].shape[2:])

        summer.start(item)
        summer.advance(*((3, 0) if item == 1 else (1, 0)))

    for name in ("mixer_w", "state_w", "dqkv", "qkv_w", "dstep", "step_w"):
        load(name).wait()
    total = jnp.zeros((1, width), F32)
    for t in range(chunks):
        rows = slice(t * 256, (t + 1) * 256)
        begin_other = (1 - branch_pos) * half + t * 256
        value = partial_of(begin_other)
        sent[rows] = value.astype(BF16)
        if t == 0:
            swap(0).start()
            summer.advance(0, 0)
            summer.advance(4, 1)
        total = total + gain_sum(value, begin_other)
    summer.advance(3, 1)
    for t in range(chunks):
        rows = slice(t * 256, (t + 1) * 256)
        begin_own = branch_pos * half + t * 256
        value = partial_of(begin_own)
        partial[rows] = value
        total = total + gain_sum(value, begin_own)
        if t == 0:
            summer.advance(4, 2)
    total = total / gain
    for place in range(gain_rows):
        put(place, total[:, place * 128 : (place + 1) * 128])
    put(begin, head_row(jnp.sum(vmem["dstep"][...], axis=1, keepdims=True)))
    summer.start(5)

    @pl.loop(0, tiles)
    def _(t):
        columns = vmem["dqkv"].shape[0]
        shape = summer.full[2].shape[2:5]
        value = mm(left_tile(t), vmem["dqkv"][...], 0, 1).astype(BF16)
        summer.full[2][t // 2, t % 2, :, :, :, :columns] = value.reshape(shape + (columns,))
        value = mm(left_tile(t), vmem["dstep"][...].astype(BF16), 0, 1).astype(BF16)
        summer.full[2][t // 2, t % 2, :, :, :, columns:] = value.reshape(shape + (value.shape[1],))

    summer.advance(5, 0)
    for part in range(1, chunks):
        swap(part).start()
    summer.start(2)

    for event in order:
        if event != "input":
            summer.advance(*event)
            continue
        load("rows").wait()
        load("hidden").wait()
        for part in range(chunks):
            swap(part).wait()

        @pl.loop(0, half // 64)
        def _(t):
            rows = pl.ds(pl.multiple_of(t * 64, 64), 64)
            values = vmem["rows"][rows].astype(F32)
            scale = lax.rsqrt(jnp.mean(values * values, axis=1, keepdims=True) + eps)
            weighted = (partial[rows].astype(BF16).astype(F32) + got[rows].astype(F32)) * gain
            centre = jnp.mean(weighted * values, axis=1, keepdims=True)
            result = vmem["hidden"][rows] + scale * weighted - values * (scale * scale * scale * centre)
            input_out[rows] = result.astype(BF16)


def final_gradients(arrays, smalls, outs, plan, eps, sizes, collective_id):
    summer = plan[0]
    half, width = arrays[9].shape
    vmem = pl.BlockSpec(memory_space=pltpu.VMEM)
    return pl.pallas_call(
        functools.partial(final_kernel, plan, eps, sizes),
        in_specs=[pl.BlockSpec(memory_space=pl.ANY)] * len(arrays) + [vmem] * len(smalls),
        out_specs=[vmem] * len(outs),
        out_shape=[jax.ShapeDtypeStruct(shape, dtype) for shape, dtype in outs],
        scratch_shapes=[pltpu.VMEM(item.shape, item.dtype) for item in arrays]
        + [
            pltpu.VMEM((half, width), F32),
            pltpu.VMEM((half, width), BF16),
            pltpu.VMEM((half, width), BF16),
            pltpu.SemaphoreType.DMA((len(arrays),)),
            pltpu.SemaphoreType.DMA((2, half // 256)),
        ]
        + summer.scratch(),
        compiler_params=pltpu.CompilerParams(
            vmem_limit_bytes=60 << 20, collective_id=collective_id, has_side_effects=True
        ),
        cost_estimate=pl.CostEstimate(flops=3 * 10**10, bytes_accessed=5 * 10**7, transcendentals=0),
        name="final_gradients",
    )(*arrays, *smalls)


def bits_of(count):
    return count.bit_length() - 1


def swap_halves(values, axis_name, bit, size):
    pairs = [(item, item ^ (1 << bit)) for item in range(size)]
    return lax.ppermute(values, axis_name, pairs)


def halve(values, place, my_bit, axis_name, bit, size):
    owners = values.shape[0]
    high = 1 << place
    parts = values.reshape((high, 2, owners // (2 * high)) + values.shape[1:])
    sent = lax.dynamic_index_in_dim(parts, 1 - my_bit, 1, keepdims=False)
    kept = lax.dynamic_index_in_dim(parts, my_bit, 1, keepdims=False)
    got = swap_halves(sent, axis_name, bit, size)
    total = (kept.astype(jnp.float32) + got.astype(jnp.float32)).astype(values.dtype)
    return total.reshape((owners // 2,) + values.shape[1:])


def scatter_sum(values, digits, order):
    left = list(digits)
    for digit in order:
        axis_name, bit, size = digit
        my_bit = (lax.axis_index(axis_name) >> bit) & 1
        values = halve(values, left.index(digit), my_bit, axis_name, bit, size)
        left.remove(digit)
    return values[0]


def gather_all(values, digits, order):
    values = values[None]
    left = []
    for digit in order:
        axis_name, bit, size = digit
        my_bit = (lax.axis_index(axis_name) >> bit) & 1
        got = swap_halves(values, axis_name, bit, size)
        place = sum(1 for item in left if digits.index(item) < digits.index(digit))
        high = 1 << place
        owners = values.shape[0]
        mine = values.reshape((high, 1, owners // high) + values.shape[1:])
        other = got.reshape(mine.shape)
        first = jnp.where(my_bit == 0, mine, other)
        second = jnp.where(my_bit == 0, other, mine)
        values = jnp.concatenate([first, second], axis=1).reshape((owners * 2,) + values.shape[1:])
        left.append(digit)
    return values


def other_branch(values):
    return lax.ppermute(values, "branch", [(0, 1), (1, 0)])


def rms_scale(values):
    return lax.rsqrt(jnp.mean(values * values, axis=-1, keepdims=True) + EPSILON)


def rms_back(upstream, values, scales, gain):
    weighted = upstream * gain
    return scales * weighted - values * scales**3 * jnp.mean(
        weighted * values, axis=-1, keepdims=True
    )


def token_runs(length_row, seq_len, doc_count):
    order = jnp.arange(doc_count, dtype=jnp.int32)
    ends = jnp.sum(jnp.where(order[:, None] >= order[None, :], length_row[None, :], 0), axis=1)
    places = jnp.arange(seq_len, dtype=jnp.int32)
    passed = places[:, None] >= ends[None, :]
    starts = jnp.sum(jnp.where(passed, length_row[None, :], 0), axis=1)
    return (places - starts).astype(F32), jnp.sum(length_row)


def join(mine, other, branch_pos, axis):
    return jnp.concatenate(
        [jnp.where(branch_pos == 0, mine, other), jnp.where(branch_pos == 0, other, mine)], axis=axis
    )


def both_weights(weight, core, branch_pos):
    half = weight.shape[0] // 2
    my_core = lax.axis_index("rows") & 1
    sent = lax.dynamic_slice_in_dim(weight, my_core * half, half, 0)
    got = other_branch(sent)
    rest = swap_halves(got, *core)
    other = jnp.concatenate(
        [jnp.where(my_core == 0, got, rest), jnp.where(my_core == 0, rest, got)], axis=0
    )
    return join(weight, other, branch_pos, 0)


def hand_over_kernel(count, *refs):
    ins, outs, bufs, sems = refs[:count], refs[count : 2 * count], refs[2 * count : 3 * count], refs[3 * count]
    loads = [pltpu.make_async_copy(ins[item], bufs[item], sems.at[0, item]) for item in range(count)]
    stores = [pltpu.make_async_copy(bufs[item], outs[item], sems.at[1, item]) for item in range(count)]
    for copy in loads:
        copy.start()
    for load, store in zip(loads, stores):
        load.wait()
        store.start()
    for copy in stores:
        copy.wait()


def hand_over(arrays):
    anywhere = pl.BlockSpec(memory_space=pl.ANY)
    return pl.pallas_call(
        functools.partial(hand_over_kernel, len(arrays)),
        in_specs=[anywhere] * len(arrays),
        out_specs=[anywhere] * len(arrays),
        out_shape=[jax.ShapeDtypeStruct(item.shape, item.dtype) for item in arrays],
        scratch_shapes=[pltpu.VMEM(item.shape, item.dtype) for item in arrays]
        + [pltpu.SemaphoreType.DMA((2, len(arrays)))],
        compiler_params=pltpu.CompilerParams(vmem_limit_bytes=63 << 20),
        cost_estimate=pl.CostEstimate(flops=0, bytes_accessed=10**7, transcendentals=0),
        name="hand_over",
    )(*arrays)


def columns_of(items, rows):
    stacked = jnp.stack(items, axis=1)
    return jnp.pad(stacked, ((0, rows - stacked.shape[0]), (0, 128 - stacked.shape[1])))


def per_device(
    inputs,
    lengths,
    norm_gain,
    query_weight,
    keyval_weight,
    mixer_weight,
    state_weight,
    step_weight,
    conv_mixer,
    conv_state,
    bias_mixer,
    bias_state,
    step_bias,
    decay_log,
    skip_gain,
    ssd_gain,
    attn_output,
    ssd_output,
    ffn_gain,
    gate_weight,
    up_weight,
    down_weight,
    cotangent,
):
    branch_pos = lax.axis_index("branch")
    row_pos = lax.axis_index("rows")
    row_count = lax.axis_size("rows")
    row_bits = bits_of(row_count)
    row_digits = [("rows", bit, row_count) for bit in range(row_bits - 1, -1, -1)]
    across = ("branch", 0, 2)
    core = row_digits[-1]
    chip_digits = row_digits[:-1]
    near, others = chip_digits[-1], chip_digits[:-1][::-1]
    fast = row_bits == 4

    own_rows = inputs[0].astype(F32)
    upstream = cotangent[0]
    half_len, model_dim = own_rows.shape
    seq_len = 2 * half_len
    local_query = query_weight.shape[1] // HD
    local_keyval = keyval_weight.shape[2] // HD
    local_heads = step_bias.shape[0]
    local_inner = bias_mixer.shape[0]
    inner_dim = 2 * local_inner
    head_rows = -(-local_heads // 8) * 8
    own_begin = branch_pos * half_len

    run, used = token_runs(lengths[0], seq_len, lengths.shape[1])
    run8 = jnp.broadcast_to(run[None, :], (8, seq_len))
    run_col = jnp.broadcast_to(run[:, None], (seq_len, 128))
    frequency = ROPE_BASE ** (-(jnp.arange(HD // 2, dtype=F32) * 2.0) / HD)
    angles = frequency[:, None] * run[None, :]
    cosine, sine = jnp.cos(angles), jnp.sin(angles)
    own_valid = (own_begin + jnp.arange(half_len, dtype=jnp.int32) < used).astype(F32)[:, None]

    own_scale = rms_scale(own_rows)
    own_hat = own_rows * own_scale
    normed = (own_hat * norm_gain).astype(BF16)
    full_normed = join(normed, other_branch(normed), branch_pos, 0)

    out_weight = jnp.concatenate([attn_output, ssd_output], axis=0)
    out_full = both_weights(out_weight, core, branch_pos)
    gain_full = join(ssd_gain, other_branch(ssd_gain), branch_pos, 0)

    qkv_flat = jnp.concatenate([query_weight, keyval_weight.reshape(model_dim, -1)], axis=1)
    mixer_flat = mixer_weight.reshape(model_dim, -1)
    state_flat = state_weight.reshape(model_dim, -1)
    step_flat = jnp.pad(step_weight, ((0, 0), (0, head_rows - local_heads)))

    mixer_t = mm(mixer_flat, full_normed, 0, 1).astype(BF16)
    vec_t = mm(state_flat, full_normed, 0, 1).astype(BF16)
    qkv_t = mm(qkv_flat, full_normed, 0, 1).astype(BF16)
    step_t = mm(step_flat, full_normed, 0, 1)

    taps = [conv_mixer[item] for item in range(4)] + [bias_mixer]
    tap_x = columns_of(taps, local_inner)
    state_taps = [conv_state[item].reshape(-1) for item in range(4)] + [bias_state.reshape(-1)]
    tap_b = columns_of(state_taps, state_flat.shape[1])
    rates = -jnp.exp(decay_log)
    head_cols = columns_of([step_bias, rates], head_rows)
    skip_col = jnp.broadcast_to(jnp.repeat(skip_gain, SP)[:, None], (local_inner, 128))
    ssd_args = (mixer_t, vec_t, step_t, run8, run_col, tap_x, tap_b, head_cols, skip_col)

    gated_t, entry = ssd_forward(*ssd_args, local_heads, SP, BLOCK)
    attn_t, rot_t, log_sums = attention_forward(
        qkv_t, cosine, sine, run8, local_query, local_keyval, HD, BLOCK, REACH
    )

    def own_tokens(values, pos):
        return lax.dynamic_slice_in_dim(values, pos * half_len, half_len, 1)

    def to_owner(values):
        got = other_branch(own_tokens(values, 1 - branch_pos))
        mine = own_tokens(values, branch_pos)
        return jnp.where(branch_pos == 0, mine, got), jnp.where(branch_pos == 0, got, mine)

    def to_heads(first, second):
        got = other_branch(jnp.where(branch_pos == 0, second, first))
        return join(jnp.where(branch_pos == 0, first, second), got, branch_pos, 1)

    gated_pair = to_owner(gated_t)
    attn_pair = to_owner(attn_t)
    attn_rows = attn_t.shape[0]
    part_rows = attn_rows + local_inner

    raw = jnp.stack(
        [jnp.concatenate([first, second], axis=0) for first, second in zip(attn_pair, gated_pair)]
    )
    scanned_rows = (jnp.arange(part_rows) >= attn_rows)[None, :, None]
    gains = jnp.pad(gain_full.reshape(2, local_inner), ((0, 0), (attn_rows, 0)))[:, :, None]
    raw_values = raw.astype(F32)
    square_sum = jnp.sum(jnp.where(scanned_rows, raw_values * raw_values, 0.0), axis=(0, 1))
    gated_scale = lax.rsqrt(square_sum / inner_dim + EPSILON)[None, None, :]
    features = jnp.where(scanned_rows, (raw_values * gated_scale * gains).astype(BF16), raw)
    features = features.reshape(2 * part_rows, half_len)
    mixer_sum = mm(features, out_full, 0, 0)
    hidden = own_rows + own_valid * mixer_sum
    block_out, grad_hidden, grad_mixer, ffn_gain_grad, act_low, gate_part, up_part = feed_forward(
        hidden, jnp.broadcast_to(own_valid, (half_len, 128)), ffn_gain, upstream, gate_weight, up_weight, down_weight,
        256, EPSILON, (core, near, others[0]) if fast else None, 3,
    )
    block_out = block_out[None]

    grad_features = mm(out_full, grad_mixer, 1, 1).reshape(2, part_rows, half_len)
    ssd_gain_wgrad = jnp.sum(grad_features * raw_values * gated_scale, axis=2)[:, attn_rows:].reshape(-1)
    weighted = grad_features * gains
    row_inner = jnp.sum(weighted * raw_values, axis=(0, 1), keepdims=True) / inner_dim
    grad_pair = jnp.where(
        scanned_rows,
        gated_scale * weighted - raw_values * (gated_scale**3 * row_inner),
        grad_features,
    ).astype(BF16)

    all_digits = [across] + row_digits
    attention_args = (qkv_t, rot_t, cosine, sine, run8, log_sums)
    qkv_cols = qkv_t.shape[0]
    query_cols = local_query * HD
    if fast:
        x, y, z0, z1 = across, near, others[0], others[1]
        partners = [(item,) for item in all_digits] + [(x, y), (z0, z1)]
        orders = [
            [(z0,), (z1,), (x,)],
            [(y,), (x,), (z1,)],
            [(core,), (y,), (z1,), (x,), (z0,)],
            [(core,), (x,), (z0,), (y,), (z1,)],
            [(core,), (z0,), (y,), (z1,), (x,)],
            [(core,), (y,), (x,), (z0,), (z1,)],
        ]
        part_row = gate_weight.shape[1] // (2 * row_count)
        piece_digits = [[x, z1, z0], [x, z1, y]] + [all_digits] * 4
        piece_cols = [model_dim] * 2 + [model_dim // 2] * 4
        summer = Summer(
            [
                (part_row, cols, BF16, digits, order, False)
                for cols, digits, order in zip(piece_cols, piece_digits, orders)
            ]
        )
        hooks = {
            (2, 0): [(2, 0), (3, 0), (0, 0), (1, 0)],
            (2, 1): [(4, 0)],
            (2, 2): [(5, 0)],
            (3, 6): [(2, 1)],
            (3, 7): [(0, 1)],
            (4, 2): [(4, 1)],
            (4, 3): [(3, 1)],
            (4, 10): [(5, 1)],
            (4, 11): [(1, 1)],
            (5, 3): [(0, 2)],
            (5, 6): [(3, 2), (4, 2)],
            (5, 7): [(2, 2)],
            (6, 0): [(5, 2)],
            (6, 3): [(1, 2)],
            (6, 4): [(3, 3)],
            (6, 5): [(2, 3)],
            (6, 10): [(5, 3)],
            (6, 11): [(4, 3)],
            "late": [(2, 4), (3, 4), (4, 4), (5, 4)],
        }
        dqkv_t, ssd_grads, ffn_sums = mixer_backward(
            act_low,
            upstream,
            grad_mixer,
            features,
            grad_pair,
            gate_part.reshape((2, 2, 2) + gate_part.shape[1:]),
            up_part.reshape((2, 2, 2) + up_part.shape[1:]),
            attention_args,
            ssd_args,
            entry,
            (summer, partners[:-2], across, hooks),
            (local_query, local_keyval, HD, local_heads, SP, BLOCK, REACH),
            1,
        )
        gate_grad, up_grad, down_grad, attn_out_grad, ssd_out_grad = ffn_sums
    else:
        got = other_branch(grad_pair[1 - branch_pos])
        head_grad = join(grad_pair[branch_pos], got, branch_pos, 1)
        ssd_grads = ssd_backward(*ssd_args, entry, head_grad[attn_rows:], local_heads, SP, BLOCK)
        dqkv_t = attention_backward(
            *attention_args, head_grad[:attn_rows], local_query, local_keyval, HD, BLOCK, REACH
        )
        down_part = mm(act_low, upstream, 0, 0).astype(BF16)
        gate_sum, up_sum, down_sum = [
            scatter_sum(item.reshape(2 * row_count, -1, model_dim), all_digits, all_digits[::-1]).astype(F32)
            for item in (gate_part, up_part, down_part)
        ]
        out_part = mm(grad_mixer, features, 0, 1).astype(BF16).reshape(row_count, -1, 2, part_rows)
        out_part = jnp.moveaxis(out_part, 2, 0).reshape(2 * row_count, -1, part_rows)
        out_sum = scatter_sum(out_part, all_digits, all_digits[::-1]).astype(F32)
        gate_grad, up_grad, down_grad = gate_sum.T, up_sum.T, down_sum
        attn_out_grad, ssd_out_grad = out_sum[:, :attn_rows].T, out_sum[:, attn_rows:].T
    dmixer_t, dvec_t, dstep_t, dlog_t, dtap_x, dtap_b, dskip = ssd_grads

    qkv_step_cols = qkv_cols + head_rows
    gather_digits = [core, across, near] + others
    own_width = local_inner // row_count
    gain_rows = model_dim // 128
    tap_rows = 4 * state_flat.shape[1] // 128
    bias_rows = state_flat.shape[1] // 128
    inner_rows = inner_dim // 128
    if fast:
        row_part = model_dim // row_count
        rows_total = 2 * gain_rows + tap_rows + bias_rows + 3 + inner_rows
        shared_rows = -(-rows_total // (2 * row_count))
        first = [(core,), (y,), (z0,), (z1,)]
        second = [(core,), (z0,), (y,), (z1,)]
        gathered = [(core,), (x, y), (z0, z1)]
        gather_digits = [core, x, y, z0, z1]
        summer = Summer(
            [
                (row_part, local_inner, BF16, row_digits, first, False),
                (row_part, local_inner, BF16, row_digits, second, False),
                (row_part, qkv_step_cols, BF16, row_digits, first, False),
                (row_part // 2, state_flat.shape[1], BF16, gather_digits, gathered, True),
                (own_width, 128, F32, row_digits, [(core,), (y,), (z0, z1)], False),
                (shared_rows, 128, F32, gather_digits, gathered, True),
            ]
        )
        arrays = [
            full_normed, dvec_t, dmixer_t, mixer_flat, state_flat, dqkv_t, qkv_flat, dstep_t, step_flat,
            inputs[0], grad_hidden,
        ]
        smalls = [
            norm_gain.reshape(1, model_dim), dtap_x, dtap_b, dskip, dlog_t, head_cols,
            ffn_gain_grad.reshape(gain_rows, 128), ssd_gain_wgrad.reshape(inner_rows, 128),
        ]
        outs = [
            ((half_len, model_dim), BF16),
            ((row_part, query_cols), F32),
            ((row_part,) + keyval_weight.shape[1:], F32),
            ((row_part,) + mixer_weight.shape[1:], F32),
            (state_weight.shape, F32),
            ((local_heads, row_part), F32),
            ((4, own_width), F32),
            ((1, own_width), F32),
            ((gain_rows, 128), F32),
            ((gain_rows, 128), F32),
            (conv_state.shape, F32),
            (bias_state.shape, F32),
            ((1, 2 * local_heads), F32),
            ((1, 2 * local_heads), F32),
            ((1, 2 * local_heads), F32),
            ((inner_rows, 128), F32),
        ]
        order = [
            (1, 1), (0, 1), (3, 2), (2, 0), (5, 1), (0, 2), (1, 2), (3, 3), (5, 2), (2, 1), (0, 3), "input", (3, 4),
            (1, 3), (5, 3), (3, 5), (2, 2), (5, 4), (5, 5), (2, 3),
        ]
        (
            input_grad, query_grad, keyval_grad, mixer_grad, state_grad, step_grad, taps_grad, bias_grad, gain_grad,
            ffn_gain_sum, state_taps_grad, state_bias_grad, step_bias_grad, decay_grad, skip_grad, ssd_gain_rows,
        ) = final_gradients(
            arrays, smalls, outs, (summer, partners, across, order), EPSILON, (local_heads, SP), 2
        )
        (
            block_out, gate_grad, up_grad, down_grad, attn_out_grad, ssd_out_grad,
            input_grad, query_grad, keyval_grad, mixer_grad, state_grad, step_grad, taps_grad, bias_grad, gain_grad,
            ffn_gain_sum, state_taps_grad, state_bias_grad, step_bias_grad, decay_grad, skip_grad,
        ) = hand_over(
            [
                block_out, gate_grad, up_grad, down_grad, attn_out_grad, ssd_out_grad,
                input_grad, query_grad, keyval_grad, mixer_grad, state_grad, step_grad, taps_grad, bias_grad, gain_grad,
                ffn_gain_sum, state_taps_grad, state_bias_grad, step_bias_grad, decay_grad, skip_grad,
            ]
        )
        gate_grad, up_grad, step_grad = gate_grad.T, up_grad.T, step_grad.T
        attn_out_grad, ssd_out_grad = attn_out_grad.T, ssd_out_grad.T
        ssd_gain_sum = ssd_gain_rows.reshape(-1)
        ffn_gain_sum = ffn_gain_sum.reshape(-1)
        gain_grad, bias_grad = gain_grad.reshape(-1), bias_grad.reshape(-1)
        step_bias_grad, decay_grad, skip_grad = [
            item.reshape(-1) for item in (step_bias_grad, decay_grad, skip_grad)
        ]
    else:
        dstep_low = dstep_t.astype(BF16)
        partial_normed = (
            mm(dmixer_t, mixer_flat, 0, 1)
            + mm(dvec_t, state_flat, 0, 1)
            + mm(dqkv_t, qkv_flat, 0, 1)
            + mm(dstep_low, step_flat, 0, 1)
        ).astype(BF16)
        sent = lax.dynamic_slice_in_dim(partial_normed, (1 - branch_pos) * half_len, half_len, 0)
        kept = lax.dynamic_slice_in_dim(partial_normed, own_begin, half_len, 0)
        own_grad_normed = kept.astype(F32) + other_branch(sent).astype(F32)
        input_grad = grad_hidden + rms_back(own_grad_normed, own_rows, own_scale, norm_gain)
        input_grad = input_grad.astype(BF16)
        norm_gain_part = jnp.sum(partial_normed.astype(F32) * full_normed.astype(F32), axis=0) / norm_gain

        def row_sum(grads_t):
            value = mm(full_normed, grads_t, 0, 1).astype(BF16)
            value = value.reshape((row_count, -1) + value.shape[1:])
            return scatter_sum(value, row_digits, row_digits[::-1]).astype(F32)

        def everywhere(value):
            value = scatter_sum(value, gather_digits, gather_digits)
            return gather_all(value, gather_digits, gather_digits[::-1])

        mixer_grad = row_sum(dmixer_t).reshape((-1,) + mixer_weight.shape[1:])
        qkvs_sum = row_sum(jnp.concatenate([dqkv_t, dstep_low], axis=0))
        query_grad = qkvs_sum[:, :query_cols]
        keyval_grad = qkvs_sum[:, query_cols:qkv_cols].reshape((-1,) + keyval_weight.shape[1:])
        step_grad = qkvs_sum[:, qkv_cols : qkv_cols + local_heads]
        own_part = jnp.swapaxes(dtap_x[:, :5].T.reshape(5, row_count, own_width), 0, 1)
        own_sum = scatter_sum(own_part, row_digits, row_digits[::-1])
        taps_grad, bias_grad = own_sum[:4], own_sum[4]
        state_part = mm(full_normed, dvec_t, 0, 1).astype(BF16)
        state_part = everywhere(state_part.reshape(2 * row_count, -1, state_part.shape[1]))
        state_grad = state_part.astype(F32).reshape(state_weight.shape)

        def widen(values):
            full = jnp.zeros((2 * local_heads,), F32)
            return lax.dynamic_update_slice_in_dim(full, values, branch_pos * local_heads, 0)

        heads = slice(0, local_heads)
        small = [
            norm_gain_part,
            ffn_gain_grad,
            dtap_b[:, :4].T,
            dtap_b[:, 4],
            widen(jnp.sum(dstep_t[heads], axis=1)),
            widen(jnp.sum(dlog_t[heads], axis=1) * rates),
            widen(jnp.sum(dskip[:, 0].reshape(local_heads, SP), axis=1)),
            ssd_gain_wgrad,
        ]
        flat = jnp.concatenate([item.reshape(-1) for item in small])
        unit = 2 * row_count * 128
        flat = jnp.pad(flat, (0, -flat.shape[0] % unit)).reshape(2 * row_count, -1, 128)
        flat = everywhere(flat).reshape(-1)
        sums, begin = [], 0
        for item in small:
            sums.append(flat[begin : begin + item.size])
            begin += item.size
        gain_grad, ffn_gain_sum, state_taps_grad, state_bias_grad = sums[:4]
        step_bias_grad, decay_grad, skip_grad, ssd_gain_sum = sums[4:]
    own_gain_grad = lax.dynamic_slice_in_dim(
        ssd_gain_sum, branch_pos * local_inner + row_pos * own_width, own_width, 0
    )
    return (
        block_out,
        input_grad[None],
        gain_grad,
        query_grad,
        keyval_grad,
        mixer_grad,
        state_grad,
        step_grad,
        taps_grad,
        state_taps_grad.reshape(conv_state.shape),
        bias_grad,
        state_bias_grad.reshape(bias_state.shape),
        step_bias_grad,
        decay_grad,
        skip_grad,
        own_gain_grad,
        attn_out_grad,
        ssd_out_grad,
        ffn_gain_sum,
        gate_grad,
        up_grad,
        down_grad,
    )


def solution(mesh):
    in_specs = (
        P("rows", "branch", None),
        P("rows", None),
        P(),
        P(None, "branch"),
        P(None, None, "branch"),
        P(None, None, "branch"),
        P(),
        P(None, "branch"),
        P(None, "branch"),
        P(),
        P("branch"),
        P(),
        P("branch"),
        P("branch"),
        P("branch"),
        P("branch"),
        P("branch", None),
        P("branch", None),
        P(),
        P(),
        P(),
        P(),
        P("rows", "branch", None),
    )
    out_specs = (
        P("rows", "branch", None),
        P("rows", "branch", None),
        P(),
        P("rows", "branch"),
        P("rows", None, "branch"),
        P("rows", None, "branch"),
        P(),
        P("rows", "branch"),
        P(None, ("branch", "rows")),
        P(),
        P(("branch", "rows")),
        P(),
        P(),
        P(),
        P(),
        P(("branch", "rows")),
        P("branch", "rows"),
        P("branch", "rows"),
        P(),
        P(None, ("branch", "rows")),
        P(None, ("branch", "rows")),
        P(("branch", "rows"), None),
    )
    return jax.shard_map(
        per_device, mesh=mesh, in_specs=in_specs, out_specs=out_specs, check_vma=False
    )
```

```python
import functools
import itertools

import jax
import jax.numpy as jnp
from jax import lax
from jax.experimental import pallas as pl
from jax.experimental.pallas import tpu as pltpu
from jax.sharding import PartitionSpec as P

HD = 64
SH = 24
SP = 64
BLOCK = 256
REACH = 512
EPSILON = 1e-05
ROPE_BASE = 100000000000.0
F32 = jnp.float32
BF16 = jnp.bfloat16
PRECISE = lax.Precision.HIGHEST


def mm(left, right, left_dim, right_dim):
    return lax.dot_general(
        left, right, (((left_dim,), (right_dim,)), ((), ())), preferred_element_type=F32
    )


def mm_exact(left, right):
    return jnp.dot(left, right, preferred_element_type=F32, precision=PRECISE)


def shift_right(prev, cur, amount):
    joined = jnp.concatenate([prev, cur], axis=1)
    return pltpu.roll(joined, amount, 1)[:, prev.shape[1] :]


def shift_left(cur, after, amount):
    joined = jnp.concatenate([cur, after], axis=1)
    total = joined.shape[1]
    return pltpu.roll(joined, total - amount, 1)[:, : cur.shape[1]]


def conv_inputs(prev_ref, cur_ref, rows, run_row, is_first):
    cur = cur_ref[rows].astype(F32)
    prev = jnp.where(is_first, 0.0, prev_ref[rows].astype(F32))
    moved = [
        shift_right(prev, cur, offset) * (run_row >= float(offset)).astype(F32) for offset in (3, 2, 1)
    ]
    return moved + [cur]


def conv_rows(items, taps):
    result = taps[:, 4:5] + taps[:, 3:4] * items[3]
    for place in range(3):
        result = result + taps[:, place : place + 1] * items[place]
    return result


def step_rows(step_ref, head_ref):
    raw = step_ref[...] + head_ref[:, 0:1]
    return raw, jax.nn.softplus(raw)


def masks_of(run_col, block):
    rows = lax.broadcasted_iota(jnp.int32, (block, block), 0)
    cols = lax.broadcasted_iota(jnp.int32, (block, block), 1)
    gap = (rows - cols).astype(F32)
    return (gap >= 0.0) & (gap <= run_col)


def upper_ones(block):
    rows = lax.broadcasted_iota(jnp.int32, (block, block), 0)
    cols = lax.broadcasted_iota(jnp.int32, (block, block), 1)
    return (rows <= cols).astype(F32)


def ssd_forward_kernel(block, heads, head_dim, *refs):
    ssd_forward_body(block, heads, head_dim, pl.program_id(0) == 0, lambda values: values, *refs)


def ssd_forward_body(
    block, heads, head_dim, is_first, pick,
    z_ref, x_ref, xp_ref, b_ref, bp_ref, step_ref, run_ref, runc_ref, tapx_ref, tapb_ref, head_ref, skip_ref,
    gated_ref, entry_ref,
    state, xdt,
):
    @pl.when(is_first)
    def _():
        state[...] = jnp.zeros_like(state)

    run_row = run_ref[0:1, :]
    everything = slice(0, b_ref.shape[0])
    vec = conv_rows(conv_inputs(bp_ref, b_ref, everything, run_row, is_first), tapb_ref[...])
    vec = vec * jax.nn.sigmoid(vec)
    size = vec.shape[0] // 2
    in_low = vec[:size].astype(BF16)
    out_low = vec[size:].astype(BF16)
    _, step = step_rows(step_ref, head_ref)
    step = pick(step)
    rate = pick(head_ref[:, 1:2])
    cum = mm_exact(step * rate, upper_ones(block))
    cum_col = jnp.transpose(cum)
    place = lax.broadcasted_iota(jnp.int32, (1, block), 1).astype(F32)
    carried = (run_row >= place + 1.0).astype(F32)
    last_run = run_row[:, block - 1 :]
    tail = (float(block - 1) - place <= last_run).astype(F32)
    last = cum[:, block - 1 :]
    entry = jnp.exp(cum) * carried
    to_end = jnp.exp(last - cum) * tail
    keep = jnp.exp(last) * carried[:, block - 1 :]
    allowed = masks_of(runc_ref[:, 0:1], block)
    cross = jnp.where(allowed, mm(out_low, in_low, 0, 0), 0.0)
    old = state[...]
    old_low = old.astype(BF16)
    entry_ref[0] = old_low
    for h in range(heads):
        rows = slice(h * head_dim, (h + 1) * head_dim)
        act = conv_rows(conv_inputs(xp_ref, x_ref, rows, run_row, is_first), tapx_ref[rows])
        act = act * jax.nn.sigmoid(act)
        part = act * step[h : h + 1]
        part_low = part.astype(BF16)
        decay = jnp.exp(jnp.minimum(cum_col[:, h : h + 1] - cum[h : h + 1], 0.0))
        weight = (cross * decay).astype(BF16)
        y_in = mm(part_low, weight, 1, 1)
        y_off = mm(old_low[rows], out_low, 1, 0)
        y_all = y_in + y_off * entry[h : h + 1] + skip_ref[rows, 0:1] * act
        gate = z_ref[rows].astype(F32)
        gated_ref[rows] = (y_all * gate * jax.nn.sigmoid(gate)).astype(gated_ref.dtype)
        xdt[rows] = (part * to_end[h : h + 1]).astype(BF16)
        state[rows] = old[rows] * keep[h : h + 1]
    state[...] += mm(xdt[...], in_low, 1, 1)


def ssd_backward_kernel(block, heads, head_dim, *refs):
    grad_ref = refs[13]
    ssd_backward_body(
        block, heads, head_dim, pl.program_id(0), pl.num_programs(0), lambda h: None,
        lambda chunk, low, high: grad_ref[low:high], *refs[:13], *refs[14:],
    )


def ssd_backward_body(
    block, heads, head_dim, index, count, hook, grad_of,
    z_ref, x_ref, xp_ref, b_ref, bp_ref, step_ref, run_ref, runc_ref, tapx_ref, tapb_ref, head_ref, skip_ref,
    entry_ref, runn_ref,
    dm_ref, db_ref, dstep_ref, drate_ref, dtapx_ref, dtapb_ref, dskip_ref,
    dstate, nextx, nextb, accx, accb, accs, xdt, dye, rowterm, colin, colst, direct, ystat,
):
    is_first = index == count - 1

    @pl.when(index == 0)
    def _():
        dstate[...] = jnp.zeros_like(dstate)
        nextx[...] = jnp.zeros_like(nextx)
        nextb[...] = jnp.zeros_like(nextb)
        accx[...] = jnp.zeros_like(accx)
        accb[...] = jnp.zeros_like(accb)
        accs[...] = jnp.zeros_like(accs)
        rowterm[...] = jnp.zeros_like(rowterm)
        colin[...] = jnp.zeros_like(colin)
        colst[...] = jnp.zeros_like(colst)
        direct[...] = jnp.zeros_like(direct)
        ystat[...] = jnp.zeros_like(ystat)

    run_row = run_ref[0:1, :]
    everything = slice(0, b_ref.shape[0])
    items_b = conv_inputs(bp_ref, b_ref, everything, run_row, is_first)
    convb = conv_rows(items_b, tapb_ref[...])
    sigb = jax.nn.sigmoid(convb)
    vec = convb * sigb
    size = vec.shape[0] // 2
    in_low = vec[:size].astype(BF16)
    out_low = vec[size:].astype(BF16)
    raw, step = step_rows(step_ref, head_ref)
    rate = head_ref[:, 1:2]
    upper = upper_ones(block)
    cum = mm_exact(step * rate, upper)
    cum_col = jnp.transpose(cum)
    place = lax.broadcasted_iota(jnp.int32, (1, block), 1).astype(F32)
    carried = (run_row >= place + 1.0).astype(F32)
    last_run = run_row[:, block - 1 :]
    tail = (float(block - 1) - place <= last_run).astype(F32)
    last = cum[:, block - 1 :]
    entry = jnp.exp(cum) * carried
    to_end = jnp.exp(last - cum) * tail
    keep = jnp.exp(last) * carried[:, block - 1 :]
    allowed = masks_of(runc_ref[:, 0:1], block)
    cross = jnp.where(allowed, mm(out_low, in_low, 0, 0), 0.0)
    old_low = entry_ref[0]
    dnew_low = dstate[...].astype(BF16)
    inner = xdt.shape[0]
    y_off = mm(old_low, out_low, 1, 0)
    u_off = mm(dnew_low, in_low, 1, 0)

    def conv_back(dvals, conv, sigm, items, taps, rows, after, acc, out_ref, out_rows):
        dconv = dvals * sigm * (1.0 + conv * (1.0 - sigm))

        def add(place, values):
            acc[place, rows] += sum(values[:, c : c + 128] for c in range(0, block, 128))

        add(4, dconv)
        for place in range(4):
            add(place, dconv * items[place])
        result = taps[:, 3:4] * dconv
        following = after[rows]
        for offset in range(1, 4):
            keep_cur = (run_row >= float(offset)).astype(F32)
            keep_next = (runn_ref[0:1, :] >= float(offset)).astype(F32)
            result = result + taps[:, 3 - offset : 4 - offset] * shift_left(
                dconv * keep_cur, following * keep_next, offset
            )
        after[rows] = dconv[:, :128]
        out_ref[out_rows] = result.astype(out_ref.dtype)

    dcross = jnp.zeros((block, block), F32)
    for h in range(heads):
        rows = slice(h * head_dim, (h + 1) * head_dim)
        one = slice(h, h + 1)
        items = conv_inputs(xp_ref, x_ref, rows, run_row, is_first)
        taps = tapx_ref[rows]
        conv = conv_rows(items, taps)
        sigm = jax.nn.sigmoid(conv)
        xh = conv * sigm
        gate = z_ref[rows].astype(F32)
        sig = jax.nn.sigmoid(gate)
        upstream = grad_of(count - 1 - index, h * head_dim, (h + 1) * head_dim).astype(F32)
        dyh = upstream * gate * sig
        dnew = dstate[rows]
        part = xh * step[one]
        part_low = part.astype(BF16)
        dy_low = dyh.astype(BF16)
        decay = jnp.exp(jnp.minimum(cum_col[:, one] - cum[one], 0.0))
        weight = (cross * decay).astype(BF16)
        y_in = mm(part_low, weight, 1, 1)
        y_scan = y_in + y_off[rows] * entry[one]
        u_in = mm(dy_low, weight, 1, 0)
        u_st = u_off[rows] * to_end[one]
        dcross = dcross + mm(dy_low, part_low, 0, 0) * decay
        part_f = part_low.astype(F32)
        u_all = u_in + u_st
        rowterm[one] = jnp.sum(dy_low.astype(F32) * y_scan, axis=0, keepdims=True)
        colin[one] = jnp.sum(part_f * u_in, axis=0, keepdims=True)
        colst[one] = jnp.sum(part_f * u_st, axis=0, keepdims=True)
        direct[one] = jnp.sum(xh * u_all, axis=0, keepdims=True)
        skip = skip_ref[rows, 0:1]
        y_all = y_scan + skip * xh
        dm_ref[rows] = (upstream * y_all * sig * (1.0 + gate * (1.0 - sig))).astype(dm_ref.dtype)
        prod = dyh * xh
        accs[rows] += sum(prod[:, c : c + 128] for c in range(0, block, 128))
        dact = step[one] * u_all + skip * dyh
        below = slice(inner + h * head_dim, inner + (h + 1) * head_dim)
        conv_back(dact, conv, sigm, items, taps, rows, nextx, accx, dm_ref, below)
        xdt[rows] = (part * to_end[one]).astype(BF16)
        dye[rows] = (dyh * entry[one]).astype(BF16)
        old = old_low[rows].astype(F32)
        ystat[one] = jnp.sum(dnew * old * keep[one], axis=0, keepdims=True)
        dstate[rows] = dnew * keep[one]
        hook(h)
    dcross_low = jnp.where(allowed, dcross, 0.0).astype(BF16)
    dout = mm(in_low, dcross_low, 1, 1) + mm(old_low, dye[...], 0, 0)
    din = mm(out_low, dcross_low, 1, 0) + mm(dnew_low, xdt[...], 0, 0)
    dstate[...] += mm(dye[...], out_low, 1, 1)
    lower = jnp.transpose(upper)
    kept_total = jnp.sum(ystat[...], axis=1, keepdims=True)
    dlog = (
        mm_exact(rowterm[...] - colin[...], lower)
        + mm_exact(colst[...], upper)
        - colst[...]
        + kept_total
    )
    dstep = direct[...] + rate * dlog
    dstep_ref[...] = dstep * jax.nn.sigmoid(raw)
    drate_ref[...] = dlog * step

    conv_back(
        jnp.concatenate([din, dout], axis=0), convb, sigb, items_b, tapb_ref[...], everything, nextb, accb,
        db_ref, everything,
    )

    @pl.when(is_first)
    def _():
        def spread(acc, out_ref):
            lanes = lax.broadcasted_iota(jnp.int32, out_ref.shape, 1)
            result = jnp.zeros(out_ref.shape, F32)
            for item in range(5):
                total = jnp.sum(acc[item], axis=1, keepdims=True)
                result = jnp.where(lanes == item, total, result)
            out_ref[...] = result

        spread(accx, dtapx_ref)
        spread(accb, dtapb_ref)
        dskip_ref[...] = jnp.broadcast_to(
            jnp.sum(accs[...], axis=1, keepdims=True), dskip_ref.shape
        )


def ssd_specs(block, inner, vec, rows16, chunk_of):
    wide = lambda i: (0, chunk_of(i))
    per = block // 128
    before = lambda i: (0, jnp.maximum(chunk_of(i) * per - 1, 0))
    whole = lambda i: (0, 0)
    return [
        pl.BlockSpec((inner, block), wide),
        pl.BlockSpec((inner, block), lambda i: (1, chunk_of(i))),
        pl.BlockSpec((inner, 128), lambda i: (1, before(i)[1])),
        pl.BlockSpec((vec, block), wide),
        pl.BlockSpec((vec, 128), before),
        pl.BlockSpec((rows16, block), wide),
        pl.BlockSpec((8, block), wide),
        pl.BlockSpec((block, 128), lambda i: (chunk_of(i), 0)),
        pl.BlockSpec((inner, 128), whole),
        pl.BlockSpec((vec, 128), whole),
        pl.BlockSpec((rows16, 128), whole),
        pl.BlockSpec((inner, 128), whole),
    ]


def ssd_forward(mixer_t, vec_t, step_t, run8, run_col, tap_x, tap_b, head_cols, skip_col, heads, head_dim, block):
    inner = mixer_t.shape[0] // 2
    seq = mixer_t.shape[1]
    vec = vec_t.shape[0]
    rows16 = step_t.shape[0]
    chunks = seq // block
    state_dim = vec // 2
    return pl.pallas_call(
        functools.partial(ssd_forward_kernel, block, heads, head_dim),
        grid=(chunks,),
        in_specs=ssd_specs(block, inner, vec, rows16, lambda i: i),
        out_specs=[
            pl.BlockSpec((inner, block), lambda i: (0, i)),
            pl.BlockSpec((1, inner, state_dim), lambda i: (i, 0, 0)),
        ],
        out_shape=[
            jax.ShapeDtypeStruct((inner, seq), BF16),
            jax.ShapeDtypeStruct((chunks, inner, state_dim), BF16),
        ],
        scratch_shapes=[
            pltpu.VMEM((inner, state_dim), F32),
            pltpu.VMEM((inner, block), BF16),
        ],
        compiler_params=pltpu.CompilerParams(vmem_limit_bytes=48 << 20),
        cost_estimate=pl.CostEstimate(flops=10**9, bytes_accessed=10**7, transcendentals=10**7),
        name="ssd_forward",
    )(mixer_t, mixer_t, mixer_t, vec_t, vec_t, step_t, run8, run_col, tap_x, tap_b, head_cols, skip_col)


def ssd_backward(mixer_t, vec_t, step_t, run8, run_col, tap_x, tap_b, head_cols, skip_col, entry, grad_t, heads, head_dim, block):
    inner = mixer_t.shape[0] // 2
    seq = mixer_t.shape[1]
    vec = vec_t.shape[0]
    rows16 = step_t.shape[0]
    chunks = seq // block
    state_dim = vec // 2
    per = block // 128
    chunk_of = lambda i: chunks - 1 - i
    wide = lambda i: (0, chunk_of(i))
    whole = lambda i: (0, 0)
    return pl.pallas_call(
        functools.partial(ssd_backward_kernel, block, heads, head_dim),
        grid=(chunks,),
        in_specs=ssd_specs(block, inner, vec, rows16, chunk_of)
        + [
            pl.BlockSpec((1, inner, state_dim), lambda i: (chunk_of(i), 0, 0)),
            pl.BlockSpec((inner, block), wide),
            pl.BlockSpec((8, 128), lambda i: (0, jnp.minimum(chunk_of(i) * per + per, chunks * per - 1))),
        ],
        out_specs=[
            pl.BlockSpec((2 * inner, block), wide),
            pl.BlockSpec((vec, block), wide),
            pl.BlockSpec((rows16, block), wide),
            pl.BlockSpec((rows16, block), wide),
            pl.BlockSpec((inner, 128), whole),
            pl.BlockSpec((vec, 128), whole),
            pl.BlockSpec((inner, 128), whole),
        ],
        out_shape=[
            jax.ShapeDtypeStruct((2 * inner, seq), BF16),
            jax.ShapeDtypeStruct((vec, seq), BF16),
            jax.ShapeDtypeStruct((rows16, seq), F32),
            jax.ShapeDtypeStruct((rows16, seq), F32),
            jax.ShapeDtypeStruct((inner, 128), F32),
            jax.ShapeDtypeStruct((vec, 128), F32),
            jax.ShapeDtypeStruct((inner, 128), F32),
        ],
        scratch_shapes=[
            pltpu.VMEM((inner, state_dim), F32),
            pltpu.VMEM((inner, 128), F32),
            pltpu.VMEM((vec, 128), F32),
            pltpu.VMEM((5, inner, 128), F32),
            pltpu.VMEM((5, vec, 128), F32),
            pltpu.VMEM((inner, 128), F32),
            pltpu.VMEM((inner, block), BF16),
            pltpu.VMEM((inner, block), BF16),
            pltpu.VMEM((rows16, block), F32),
            pltpu.VMEM((rows16, block), F32),
            pltpu.VMEM((rows16, block), F32),
            pltpu.VMEM((rows16, block), F32),
            pltpu.VMEM((rows16, state_dim), F32),
        ],
        compiler_params=pltpu.CompilerParams(vmem_limit_bytes=48 << 20),
        cost_estimate=pl.CostEstimate(flops=3 * 10**9, bytes_accessed=2 * 10**7, transcendentals=3 * 10**7),
        name="ssd_backward",
    )(
        mixer_t, mixer_t, mixer_t, vec_t, vec_t, step_t, run8, run_col, tap_x, tap_b, head_cols, skip_col,
        entry, grad_t, run8,
    )


def rotate_rows(values, cosine, sine):
    half = values.shape[0] // 2
    first, second = values[:half], values[half:]
    return jnp.concatenate(
        [first * cosine - second * sine, second * cosine + first * sine], axis=0
    )


def window_of(block_index, block, reach):
    low = max(0, (block_index * block - (reach - 1)) // block)
    return low * block, (block_index + 1) * block


def allowed_of(run_ref, begin, stop, block):
    start, end = stop
    keys = lax.broadcasted_iota(jnp.int32, (end - start, block), 0) + start
    queries = lax.broadcasted_iota(jnp.int32, (end - start, block), 1) + begin
    gap = (queries - keys).astype(F32)
    return (gap >= 0.0) & (gap <= run_ref[0:1, begin : begin + block])


def attention_forward_kernel(heads, groups, head_dim, block, reach, scale, proj_ref, cos_ref, sin_ref, run_ref, out_ref, *refs):
    def place(rows, index):
        return out_ref.at[rows, index * block : (index + 1) * block]

    attention_forward_body(
        heads, groups, head_dim, block, reach, scale, range(proj_ref.shape[1] // block), place, lambda index: None,
        proj_ref, cos_ref, sin_ref, run_ref, *refs
    )


def attention_forward_body(
    heads, groups, head_dim, block, reach, scale, order, place, hook,
    proj_ref, cos_ref, sin_ref, run_ref, rot_ref, lse_ref,
):
    seq = proj_ref.shape[1]
    cosine, sine = cos_ref[...], sin_ref[...]
    total = heads + groups
    for item in range(total):
        rows = slice(item * head_dim, (item + 1) * head_dim)
        rot_ref[rows] = rotate_rows(proj_ref[rows].astype(F32), cosine, sine).astype(BF16)
    for index in order:
        begin = index * block
        span = window_of(index, block, reach)
        allowed = allowed_of(run_ref, begin, span, block)
        for h in range(heads):
            group = h * groups // heads
            rows = slice(h * head_dim, (h + 1) * head_dim)
            krows = slice((heads + group) * head_dim, (heads + group + 1) * head_dim)
            vrows = slice((heads + groups + group) * head_dim, (heads + groups + group + 1) * head_dim)
            query = rot_ref[rows, begin : begin + block]
            key = rot_ref[krows, span[0] : span[1]]
            value = proj_ref[vrows, span[0] : span[1]].astype(BF16)
            logits = jnp.where(allowed, mm(key, query, 0, 0) * scale, -1e30)
            peak = jnp.max(logits, axis=0, keepdims=True)
            powered = jnp.exp(logits - peak)
            mass = jnp.sum(powered, axis=0, keepdims=True)
            probs = (powered * (1.0 / mass)).astype(BF16)
            place(rows, index)[...] = mm(value, probs, 1, 0).astype(BF16)
            lse_ref[h : h + 1, begin : begin + block] = peak + jnp.log(mass)
        hook(index)


def attention_backward_kernel(
    heads, groups, head_dim, block, reach, scale, grad_of, hook,
    proj_ref, rot_ref, cos_ref, sin_ref, run_ref, lse_ref, back_ref,
    acc_key, acc_value,
):
    seq = proj_ref.shape[1]
    acc_key[...] = jnp.zeros_like(acc_key)
    acc_value[...] = jnp.zeros_like(acc_value)
    for index in range(seq // block):
        begin = index * block
        span = window_of(index, block, reach)
        allowed = allowed_of(run_ref, begin, span, block)
        cosine, sine = cos_ref[:, begin : begin + block], sin_ref[:, begin : begin + block]
        for h in range(heads):
            group = h * groups // heads
            rows = slice(h * head_dim, (h + 1) * head_dim)
            krows = slice((heads + group) * head_dim, (heads + group + 1) * head_dim)
            vrows = slice((heads + groups + group) * head_dim, (heads + groups + group + 1) * head_dim)
            grows = slice(group * head_dim, (group + 1) * head_dim)
            query = rot_ref[rows, begin : begin + block]
            key = rot_ref[krows, span[0] : span[1]]
            value = proj_ref[vrows, span[0] : span[1]].astype(BF16)
            grad = grad_of(h * head_dim, (h + 1) * head_dim, begin)
            logits = jnp.where(allowed, mm(key, query, 0, 0) * scale, -1e30)
            probs = jnp.exp(logits - lse_ref[h : h + 1, begin : begin + block])
            dprobs = mm(value, grad, 0, 0)
            centre = jnp.sum(probs * dprobs, axis=0, keepdims=True)
            dscore = (probs * (dprobs - centre) * scale).astype(BF16)
            dquery = mm(key, dscore, 1, 0)
            back_ref[rows, begin : begin + block] = rotate_rows(dquery, cosine, -sine).astype(BF16)
            acc_key[grows, span[0] : span[1]] += mm(query, dscore, 1, 1)
            acc_value[grows, span[0] : span[1]] += mm(grad, probs.astype(BF16), 1, 1)
        hook(index)
    for group in range(groups):
        grows = slice(group * head_dim, (group + 1) * head_dim)
        krows = slice((heads + group) * head_dim, (heads + group + 1) * head_dim)
        vrows = slice((heads + groups + group) * head_dim, (heads + groups + group + 1) * head_dim)
        back_ref[krows] = rotate_rows(acc_key[grows], cos_ref[...], -sin_ref[...]).astype(BF16)
        back_ref[vrows] = acc_value[grows].astype(BF16)


def attention_forward(proj_t, cosine, sine, run8, heads, groups, head_dim, block, reach):
    seq = proj_t.shape[1]
    return pl.pallas_call(
        functools.partial(attention_forward_kernel, heads, groups, head_dim, block, reach, head_dim**-0.5),
        out_shape=[
            jax.ShapeDtypeStruct((heads * head_dim, seq), BF16),
            jax.ShapeDtypeStruct(((heads + groups) * head_dim, seq), BF16),
            jax.ShapeDtypeStruct((max(heads, 8), seq), F32),
        ],
        compiler_params=pltpu.CompilerParams(vmem_limit_bytes=48 << 20),
        cost_estimate=pl.CostEstimate(flops=2 * 10**9, bytes_accessed=10**7, transcendentals=4 * 10**6),
        name="attention_forward",
    )(proj_t, cosine, sine, run8)


def attention_backward_call(
    heads, groups, head_dim, block, reach, proj_ref, rot_ref, cos_ref, sin_ref, run_ref, lse_ref, grad_ref, *refs
):
    attention_backward_kernel(
        heads, groups, head_dim, block, reach, head_dim**-0.5,
        lambda low, high, begin: grad_ref[low:high, begin : begin + block], lambda index: None,
        proj_ref, rot_ref, cos_ref, sin_ref, run_ref, lse_ref, *refs,
    )


def attention_backward(proj_t, rot_t, cosine, sine, run8, lse, grad_t, heads, groups, head_dim, block, reach):
    seq = proj_t.shape[1]
    return pl.pallas_call(
        functools.partial(attention_backward_call, heads, groups, head_dim, block, reach),
        out_shape=jax.ShapeDtypeStruct(proj_t.shape, BF16),
        scratch_shapes=[
            pltpu.VMEM((groups * head_dim, seq), F32),
            pltpu.VMEM((groups * head_dim, seq), F32),
        ],
        compiler_params=pltpu.CompilerParams(vmem_limit_bytes=48 << 20),
        cost_estimate=pl.CostEstimate(flops=5 * 10**9, bytes_accessed=10**7, transcendentals=4 * 10**6),
        name="attention_backward",
    )(proj_t, rot_t, cosine, sine, run8, lse, grad_t)


def digit_of(digit):
    axis_name, bit, size = digit
    return (lax.axis_index(axis_name) // (1 << bit)) % 2


def partner_of(flipped):
    places = {}
    for digit in flipped:
        axis_name, bit, size = digit
        place = places.get(axis_name, lax.axis_index(axis_name))
        places[axis_name] = place + (1 - 2 * digit_of(digit)) * (1 << bit)
    return places


def send_to(flipped, source, target, send_sem, recv_sem):
    return pltpu.make_async_remote_copy(
        src_ref=source,
        dst_ref=target,
        send_sem=send_sem,
        recv_sem=recv_sem,
        device_id=partner_of(flipped),
        device_id_type=pl.DeviceIdType.MESH,
    )


def greet(partners):
    barrier = pltpu.get_barrier_semaphore()
    for flipped in partners:
        pl.semaphore_signal(
            barrier, inc=1, device_id=partner_of(flipped), device_id_type=pl.DeviceIdType.MESH
        )
    pl.semaphore_wait(barrier, len(partners))


def flips_of(group):
    return [
        tuple(digit for digit, bit in zip(group, bits) if bit)
        for bits in itertools.product((0, 1), repeat=len(group))
        if any(bits)
    ]


class Summer:
    def __init__(self, pieces):
        self.pieces = pieces
        self.count = len(pieces)
        for rows, cols, dtype, digits, order, gather in pieces:
            flat = [digit for group in order for digit in group]
            assert sorted(digits) == sorted(flat) and (not gather or list(digits) == flat)

    def turns(self, item):
        return len(self.pieces[item][4]) * (2 if self.pieces[item][5] else 1)

    def scratch(self):
        shapes = []
        for item, (rows, cols, dtype, digits, order, gather) in enumerate(self.pieces):
            shapes.append(pltpu.VMEM((2,) * len(digits) + (rows, cols), dtype))
            left = len(digits)
            for group in order:
                left -= len(group)
                shapes.append(pltpu.VMEM(((1 << len(group)) - 1,) + (2,) * left + (rows, cols), dtype))
            if gather:
                shapes.append(pltpu.VMEM((1 << len(digits), rows, cols), dtype))
        most = max(self.turns(item) for item in range(self.count))
        wide = max((1 << len(group)) - 1 for piece in self.pieces for group in piece[4])
        return shapes + [pltpu.SemaphoreType.DMA((self.count, most, wide))] * 2

    def bind(self, emits, refs):
        self.emits, self.full, self.gots, self.alls = emits, [], [], []
        for rows, cols, dtype, digits, order, gather in self.pieces:
            self.full.append(refs[0])
            self.gots.append(refs[1 : 1 + len(order)])
            refs = refs[1 + len(order) :]
            if gather:
                self.alls.append(refs[0])
                refs = refs[1:]
            else:
                self.alls.append(None)
        self.send_sem, self.recv_sem = refs

    def copies(self, item, turn):
        rows, cols, dtype, digits, order, gather = self.pieces[item]
        result = []
        if turn < len(order):
            done = [digit for group in order[:turn] for digit in group]
            group = order[turn]
        else:
            group = order[2 * len(order) - 1 - turn]
            ahead = [digit for group in order[: 2 * len(order) - 1 - turn] for digit in group]
            size = 1 << (len(digits) - len(ahead) - len(group))
            region = self.alls[item].at[pl.ds(self.place_of(ahead + list(group)) * size, size)]
        for slot, flipped in enumerate(flips_of(group)):
            if turn < len(order):
                index = tuple(
                    1 - digit_of(digit) if digit in flipped
                    else digit_of(digit) if digit in done or digit in group
                    else slice(None)
                    for digit in digits
                )
                source, target = self.full[item].at[index], self.gots[item][turn].at[slot]
            else:
                source = target = region
            result.append(
                send_to(
                    flipped, source, target, self.send_sem.at[item, turn, slot], self.recv_sem.at[item, turn, slot]
                )
            )
        return result

    def place_of(self, digits):
        place = 0
        for digit in digits:
            place = place * 2 + digit_of(digit)
        return place

    def start(self, item, turn=0):
        for copy in self.copies(item, turn):
            copy.start()

    def advance(self, item, turn):
        rows, cols, dtype, digits, order, gather = self.pieces[item]
        for copy in self.copies(item, turn):
            copy.wait()
        if turn >= len(order):
            if turn + 1 < 2 * len(order):
                self.start(item, turn + 1)
            else:
                self.emits[item](self.alls[item])
            return
        done = [digit for group in order[: turn + 1] for digit in group]
        left = [digit for digit in digits if digit not in done]
        for bits in itertools.product((0, 1), repeat=len(left)):
            index = tuple(
                digit_of(digit) if digit in done else bits[left.index(digit)] for digit in digits
            )
            value = self.full[item][index].astype(F32)
            for slot in range((1 << len(order[turn])) - 1):
                value = value + self.gots[item][turn][(slot,) + bits].astype(F32)
            if left:
                self.full[item][index] = value.astype(dtype)
            elif gather:
                self.alls[item][self.place_of(digits)] = value.astype(dtype)
            else:
                self.emits[item](value)
        if turn + 1 < self.turns(item):
            self.start(item, turn + 1)


def ffn_tile(eps, hidden_ref, valid_ref, gain_ref, cot_ref, gate_ref, up_ref, down_ref, act_ref, out_acc, back_acc, normed_ref):
    @pl.when(pl.program_id(0) == 0)
    def _():
        out_acc[...] = jnp.zeros_like(out_acc)
        back_acc[...] = jnp.zeros_like(back_acc)

        @pl.loop(0, normed_ref.shape[0] // 64)
        def _(t):
            at = pl.ds(pl.multiple_of(t * 64, 64), 64)
            values = hidden_ref[at]
            scale = lax.rsqrt(jnp.mean(values * values, axis=1, keepdims=True) + eps)
            normed_ref[at] = (values * scale * gain_ref[...]).astype(BF16)

    normed, cot = normed_ref[...], cot_ref[...]
    gate_w, up_w, down_w = gate_ref[...], up_ref[...], down_ref[...]
    gate = mm(normed, gate_w, 1, 0)
    up = mm(normed, up_w, 1, 0)
    grad_act = mm(cot, down_w, 1, 1)
    sig = jax.nn.sigmoid(gate)
    silu = gate * sig
    act = (silu * up).astype(BF16)
    dgate = (grad_act * up * sig * (1.0 + gate * (1.0 - sig))).astype(BF16)
    dup = (grad_act * silu).astype(BF16)
    act_ref[...] = act
    out_acc[...] += mm(act, down_w, 1, 0)
    back_acc[...] += mm(dgate, gate_w, 1, 1) + mm(dup, up_w, 1, 1)
    return normed, dgate, dup


def ffn_end(eps, hidden_ref, valid_ref, gain_ref, cot_ref, outs, out_acc, back_acc):
    block_ref, grad_ref, mixer_ref, gain_grad_ref = outs
    gain = gain_ref[...]
    gain_grad_ref[...] = jnp.zeros_like(gain_grad_ref)

    @pl.loop(0, out_acc.shape[0] // 64)
    def _(t):
        at = pl.ds(pl.multiple_of(t * 64, 64), 64)
        values = hidden_ref[at]
        scale = lax.rsqrt(jnp.mean(values * values, axis=1, keepdims=True) + eps)
        upstream = back_acc[at]
        weighted = upstream * gain
        centre = jnp.mean(weighted * values, axis=1, keepdims=True)
        grad = cot_ref[at].astype(F32) + scale * weighted - values * (scale * scale * scale * centre)
        block_ref[at] = (values + out_acc[at]).astype(BF16)
        grad_ref[at] = grad
        mixer_ref[at] = (valid_ref[at, 0:1] * grad).astype(BF16)
        gain_grad_ref[...] += jnp.sum(upstream * values * scale, axis=0, keepdims=True)


def ffn_plain_kernel(tiles, eps, *refs):
    ins, outs, accs = refs[:7], refs[7:14], refs[14:]
    normed, dgate, dup = ffn_tile(eps, *ins, outs[4], *accs)
    for wgrad_ref, grads in zip(outs[5:], (dgate, dup)):
        wgrad_ref[...] = mm(grads, normed, 0, 0).astype(BF16)

    @pl.when(pl.program_id(0) == tiles - 1)
    def _():
        ffn_end(eps, *ins[:4], outs[:4], *accs[:2])


def ffn_sum_kernel(digits, tiles, eps, *refs):
    core, near, far = digits
    ins, outs, accs = refs[:7], refs[7:14], refs[14:17]
    gate_out, up_out = outs[5:]
    full_gate, full_up, got_gate, got_up, far_gate, far_up, sems = refs[17:]
    fulls, gots = (full_gate, full_up), (got_gate, got_up)
    step = pl.program_id(0)
    mine, near_bit, far_bit = digit_of(core), digit_of(near), digit_of(far)

    def core_copy(item, tile):
        return send_to(
            (core,), fulls[item].at[tile, :, 1 - mine], gots[item].at[tile], sems.at[0, item, tile], sems.at[1, item, tile]
        )

    def near_copy(tile):
        return send_to(
            (near,), full_gate.at[tile, 1 - near_bit, mine], far_gate.at[tile], sems.at[2, 0, tile], sems.at[3, 0, tile]
        )

    def far_copy(pair):
        return send_to(
            (far,), full_up.at[2 * pair + 1 - far_bit, :, mine], far_up.at[pair], sems.at[2, 1, pair], sems.at[3, 1, pair]
        )

    def finish(tile):
        for item in range(2):
            core_copy(item, tile).wait()
            total = fulls[item][tile, :, mine].astype(F32) + gots[item][tile].astype(F32)
            fulls[item][tile, :, mine] = total.astype(BF16)
        near_copy(tile).start()

        @pl.when(tile % 2 == 1 - far_bit)
        def _():
            far_copy(tile // 2).start()

    @pl.when(step == 0)
    def _():
        greet([(item,) for item in digits])

    normed, dgate, dup = ffn_tile(eps, *ins, outs[4], *accs)
    for item, grads in enumerate((dgate, dup)):
        value = mm(grads, normed, 0, 0).astype(BF16)
        fulls[item][step] = value.reshape(fulls[item].shape[1:])
        core_copy(item, step).start()

    @pl.when(step > 0)
    def _():
        finish(step - 1)

    @pl.when(step == tiles - 1)
    def _():
        finish(step)
        ffn_end(eps, *ins[:4], outs[:4], *accs[:2])
        for tile in range(tiles):
            near_copy(tile).wait()
            total = full_gate[tile, near_bit, mine].astype(F32) + far_gate[tile].astype(F32)
            gate_out[tile] = total.astype(BF16)
        for pair in range(tiles // 2):
            far_copy(pair).wait()
            for other in range(2):
                total = full_up[2 * pair + far_bit, other, mine].astype(F32) + far_up[pair, other].astype(F32)
                up_out[2 * pair + other] = total.astype(BF16)


def feed_forward(hidden, valid, gain, cot, gate_w, up_w, down_w, tile, eps, digits, collective_id):
    rows, width = hidden.shape
    inner = gate_w.shape[1]
    tiles = inner // tile
    whole = lambda i: (0, 0)
    once = pl.Buffered(1)
    scratch = [pltpu.VMEM((rows, width), F32)] * 2 + [pltpu.VMEM((rows, width), BF16)]
    if digits is None:
        kernel = functools.partial(ffn_plain_kernel, tiles, eps)
        wgrads = [jax.ShapeDtypeStruct((inner, width), BF16)] * 2
        wgrad_specs = [pl.BlockSpec((tile, width), lambda i: (i, 0))] * 2
        params = pltpu.CompilerParams(vmem_limit_bytes=56 << 20)
    else:
        kernel = functools.partial(ffn_sum_kernel, digits, tiles, eps)
        part = tile // 4
        wgrads = [jax.ShapeDtypeStruct((tiles, part, width), BF16)] * 2
        wgrad_specs = [pl.BlockSpec((tiles, part, width), lambda i: (0, 0, 0))] * 2
        scratch += [pltpu.VMEM((tiles, 2, 2, part, width), BF16)] * 2
        scratch += [pltpu.VMEM((tiles, 2, part, width), BF16)] * 2
        scratch += [
            pltpu.VMEM((tiles, part, width), BF16),
            pltpu.VMEM((tiles // 2, 2, part, width), BF16),
            pltpu.SemaphoreType.DMA((4, 2, tiles)),
        ]
        params = pltpu.CompilerParams(
            vmem_limit_bytes=60 << 20, collective_id=collective_id, has_side_effects=True
        )
    return pl.pallas_call(
        kernel,
        grid=(tiles,),
        in_specs=[
            pl.BlockSpec((rows, width), whole, pipeline_mode=once),
            pl.BlockSpec((rows, 128), whole, pipeline_mode=once),
            pl.BlockSpec((1, width), whole, pipeline_mode=once),
            pl.BlockSpec((rows, width), whole, pipeline_mode=once),
            pl.BlockSpec((width, tile), lambda i: (0, i)),
            pl.BlockSpec((width, tile), lambda i: (0, i)),
            pl.BlockSpec((tile, width), lambda i: (i, 0)),
        ],
        out_specs=[
            pl.BlockSpec((rows, width), whole),
            pl.BlockSpec((rows, width), whole),
            pl.BlockSpec((rows, width), whole),
            pl.BlockSpec((1, width), whole),
            pl.BlockSpec((rows, tile), lambda i: (0, i)),
        ]
        + wgrad_specs,
        out_shape=[
            jax.ShapeDtypeStruct((rows, width), BF16),
            jax.ShapeDtypeStruct((rows, width), F32),
            jax.ShapeDtypeStruct((rows, width), BF16),
            jax.ShapeDtypeStruct((1, width), F32),
            jax.ShapeDtypeStruct((rows, inner), BF16),
        ]
        + wgrads,
        scratch_shapes=scratch,
        compiler_params=params,
        cost_estimate=pl.CostEstimate(
            flops=8 * 2 * rows * width * inner, bytes_accessed=3 * 10**7, transcendentals=rows * inner
        ),
        name="feed_forward",
    )(hidden, valid, gain.reshape(1, width), cot, gate_w, up_w, down_w)


def mixer_forward_kernel(across, sizes, splits, ssd_count, *refs):
    query_heads, groups, head_dim, heads, ssd_dim, block, reach = sizes
    ssd_in, refs = refs[:ssd_count], refs[ssd_count:]
    (proj_ref, cos_ref, sin_ref, run_ref), refs = refs[:4], refs[4:]
    (entry_ref, rot_ref, lse_ref, raw_out), refs = refs[:4], refs[4:]
    state, xdt, stage, attn_stage, raw, sems, out_sem = refs
    step = pl.program_id(0)
    steps = pl.num_programs(0)
    chunks = (steps - 1) // splits
    branch_pos = digit_of(across)
    attn_rows = query_heads * head_dim
    part_rows = stage.shape[2]
    own_chunks = raw.shape[2] // block
    part, chunk = step // chunks, step % chunks
    total_chunks = attn_stage.shape[0]

    def region(branch, begin, size, at_chunk):
        first = pl.multiple_of((at_chunk % own_chunks) * block, block)
        return raw.at[branch, pl.ds(begin, size), pl.ds(first, block)]

    def remote_copy(slot, source, target):
        return send_to((across,), source, target, sems.at[0, slot], sems.at[1, slot])

    def move(slot, source, begin, size, at_chunk):
        target = region(branch_pos, begin, size, at_chunk)

        @pl.when(at_chunk // own_chunks == branch_pos)
        def _():
            target[...] = source[...]

        @pl.when(at_chunk // own_chunks != branch_pos)
        def _():
            remote_copy(slot, source, target).start()

    def arrive(slot, source, begin, size, at_chunk):
        @pl.when(at_chunk // own_chunks == branch_pos)
        def _():
            remote_copy(slot, source, region(1 - branch_pos, begin, size, at_chunk)).wait_recv()

        @pl.when(at_chunk // own_chunks != branch_pos)
        def _():
            remote_copy(slot, source, region(branch_pos, begin, size, at_chunk)).wait_send()

    @pl.when(step == 0)
    def _():
        greet([(across,)])

    @pl.when(step < steps - 1)
    def _():
        count = heads // splits

        def pick(values):
            result = values[:count]
            for item in range(1, splits):
                result = jnp.where(part == item, values[item * count : (item + 1) * count], result)
            return result

        ssd_forward_body(
            block, count, ssd_dim, chunk == 0, pick, *ssd_in, stage.at[part, chunk], entry_ref, state, xdt
        )
        move(step, stage.at[part, chunk], attn_rows + part * part_rows, part_rows, chunk)

    @pl.when(step == steps - 1)
    def _():
        base = splits * total_chunks
        for branch in range(2):
            @pl.when(branch_pos == branch)
            def _():
                own = range(branch * own_chunks, (branch + 1) * own_chunks)
                others = [index for index in range(total_chunks) if index not in own]
                attention_forward_body(
                    query_heads, groups, head_dim, block, reach, head_dim**-0.5, others + list(own),
                    lambda rows, index: attn_stage.at[index, rows],
                    lambda index: move(base + index, attn_stage.at[index], 0, attn_rows, index),
                    proj_ref, cos_ref, sin_ref, run_ref, rot_ref, lse_ref,
                )

        for item in range(splits):
            for at_chunk in range(total_chunks):
                arrive(
                    item * total_chunks + at_chunk, stage.at[item, at_chunk], attn_rows + item * part_rows, part_rows, at_chunk
                )
        for at_chunk in range(total_chunks):
            arrive(base + at_chunk, attn_stage.at[at_chunk], 0, attn_rows, at_chunk)
        result = pltpu.make_async_copy(raw, raw_out, out_sem.at[0])
        result.start()
        result.wait()


def mixer_forward(ssd_args, attention_args, across, sizes, splits, collective_id):
    query_heads, groups, head_dim, heads, ssd_dim, block, reach = sizes
    mixer_t, vec_t, step_t, run8, run_col, tap_x, tap_b, head_cols, skip_col = ssd_args
    inner, seq = mixer_t.shape[0] // 2, mixer_t.shape[1]
    vec, rows16 = vec_t.shape[0], step_t.shape[0]
    chunks, per, size = seq // block, block // 128, inner // splits
    last = splits * chunks - 1
    part_of = lambda i: jnp.minimum(i, last) // chunks
    chunk_of = lambda i: jnp.minimum(i, last) % chunks
    before = lambda i: jnp.maximum(chunk_of(i) * per - 1, 0)
    whole = lambda i: (0, 0)
    once = pl.Buffered(1)
    attn_rows = query_heads * head_dim
    rot_rows = (query_heads + groups) * head_dim
    in_specs = [
        pl.BlockSpec((size, block), lambda i: (part_of(i), chunk_of(i))),
        pl.BlockSpec((size, block), lambda i: (splits + part_of(i), chunk_of(i))),
        pl.BlockSpec((size, 128), lambda i: (splits + part_of(i), before(i))),
        pl.BlockSpec((vec, block), lambda i: (0, chunk_of(i))),
        pl.BlockSpec((vec, 128), lambda i: (0, before(i))),
        pl.BlockSpec((rows16, block), lambda i: (0, chunk_of(i))),
        pl.BlockSpec((8, block), lambda i: (0, chunk_of(i))),
        pl.BlockSpec((block, 128), lambda i: (chunk_of(i), 0)),
        pl.BlockSpec((size, 128), lambda i: (part_of(i), 0)),
        pl.BlockSpec((vec, 128), whole),
        pl.BlockSpec((rows16, 128), whole),
        pl.BlockSpec((size, 128), lambda i: (part_of(i), 0)),
    ] + [pl.BlockSpec(item.shape, whole, pipeline_mode=once) for item in attention_args]
    moves = (splits + 1) * chunks
    return pl.pallas_call(
        functools.partial(mixer_forward_kernel, across, sizes, splits, 12),
        grid=(splits * chunks + 1,),
        in_specs=in_specs,
        out_specs=[
            pl.BlockSpec((1, size, vec // 2), lambda i: (chunk_of(i), part_of(i), 0)),
            pl.BlockSpec((rot_rows, seq), whole),
            pl.BlockSpec((max(query_heads, 8), seq), whole),
            pl.BlockSpec(memory_space=pl.ANY),
        ],
        out_shape=[
            jax.ShapeDtypeStruct((chunks, inner, vec // 2), BF16),
            jax.ShapeDtypeStruct((rot_rows, seq), BF16),
            jax.ShapeDtypeStruct((max(query_heads, 8), seq), F32),
            jax.ShapeDtypeStruct((2, attn_rows + inner, seq // 2), BF16),
        ],
        scratch_shapes=[
            pltpu.VMEM((size, vec // 2), F32),
            pltpu.VMEM((size, block), BF16),
            pltpu.VMEM((splits, chunks, size, block), BF16),
            pltpu.VMEM((chunks, attn_rows, block), BF16),
            pltpu.VMEM((2, attn_rows + inner, seq // 2), BF16),
            pltpu.SemaphoreType.DMA((2, moves)),
            pltpu.SemaphoreType.DMA((1,)),
        ],
        compiler_params=pltpu.CompilerParams(
            vmem_limit_bytes=48 << 20, collective_id=collective_id, has_side_effects=True
        ),
        cost_estimate=pl.CostEstimate(flops=2 * 10**10, bytes_accessed=2 * 10**7, transcendentals=2 * 10**7),
        name="mixer_forward",
    )(
        mixer_t, mixer_t, mixer_t, vec_t, vec_t, step_t, run8, run_col, tap_x, tap_b, head_cols, skip_col,
        *attention_args,
    )

def backward_kernel(plan, sizes, attention_count, ssd_count, ssd_outs, scratch_counts, *refs):
    query_heads, groups, head_dim, heads, ssd_dim, block, reach = sizes
    summer, partners, across, hooks = plan
    step = pl.program_id(0)
    steps = pl.num_programs(0)
    (act_ref, rows_ref, mixer_ref, feature_ref, pair_ref, gate_part, up_part), refs = refs[:7], refs[7:]
    attention_in, refs = refs[:attention_count], refs[attention_count:]
    ssd_in, refs = refs[:ssd_count], refs[ssd_count:]
    attention_out, refs = refs[:1], refs[1:]
    ssd_out, refs = refs[:ssd_outs], refs[ssd_outs:]
    part_out, refs = refs[:5], refs[5:]
    attention_scratch, refs = refs[: scratch_counts[0]], refs[scratch_counts[0] :]
    ssd_scratch, refs = refs[: scratch_counts[1]], refs[scratch_counts[1] :]
    (head_grad, pair_sem), refs = refs[:2], refs[2:]
    branch_pos = digit_of(across)
    attn_rows = query_heads * head_dim
    gate_out, up_out, down_out, attn_out, ssd_w_out = part_out

    def to_rows(out_ref, begin):
        def emit(value):
            out_ref[:, begin : begin + value.shape[1]] = value

        return emit

    def to_outputs(value):
        attn_out[...] = value[:, :attn_rows]
        ssd_w_out[:, : value.shape[1] - attn_rows] = value[:, attn_rows:]

    width = rows_ref.shape[1] // 2
    summer.bind(
        [
            to_rows(gate_out, 0), to_rows(up_out, 0), to_rows(down_out, 0), to_rows(down_out, width),
            to_outputs, to_rows(ssd_w_out, width - attn_rows),
        ],
        refs,
    )

    def exchange(part):
        low, high = ((0, attn_rows), (attn_rows, head_grad.shape[1]))[part]
        return send_to(
            (across,),
            pair_ref.at[1 - branch_pos, low:high],
            head_grad.at[branch_pos, low:high],
            pair_sem.at[2 * part],
            pair_sem.at[2 * part + 1],
        )

    def own_pair():
        return pltpu.make_async_copy(
            pair_ref.at[branch_pos], head_grad.at[branch_pos], pair_sem.at[4]
        )

    def run(events):
        for item, turn in events:
            summer.advance(item, turn)

    def load_of(item):
        return pltpu.make_async_copy((gate_part, up_part)[item], summer.full[item], pair_sem.at[5 + item])

    tile = 256

    @pl.when(step == 0)
    def _():
        load_of(0).start()
        load_of(1).start()
        own_pair().start()
        greet(partners)
        exchange(0).start()
        exchange(1).start()
        for item in range(2):
            load_of(item).wait()
            summer.start(item)
        right = rows_ref[...]

        @pl.loop(0, act_ref.shape[1] // tile, unroll=2)
        def _(t):
            left = act_ref[:, pl.ds(pl.multiple_of(t * tile, tile), tile)]
            value = mm(left, right, 0, 0).astype(BF16)
            for part in range(2):
                full = summer.full[2 + part]
                columns = value[:, part * width : (part + 1) * width]
                full[t // 4, (t // 2) % 2, t % 2] = columns.reshape(full.shape[3:])

        summer.start(2)
        summer.start(3)

    @pl.when(step == 1)
    def _():
        run(hooks.get((1, "begin"), ()))
        half = feature_ref.shape[0] // 2

        @pl.loop(0, mixer_ref.shape[1] // tile)
        def _(t):
            left = mixer_ref[:, pl.ds(pl.multiple_of(t * tile, tile), tile)]
            for part in range(2):
                value = mm(left, feature_ref[part * half : (part + 1) * half], 0, 1).astype(BF16)
                for piece in range(2):
                    full = summer.full[4 + piece]
                    columns = value[:, piece * width : (piece + 1) * width]
                    full[part, t // 2, t % 2] = columns.reshape(full.shape[3:])

        summer.start(4)
        summer.start(5)

    @pl.when(step == 2)
    def _():
        exchange(0).wait()
        own_pair().wait()
        run(hooks.get((2, "begin"), ()))

        def grad_of(low, high, begin):
            width = head_grad.shape[2]
            return head_grad[begin // width, low:high, begin % width : begin % width + block]

        attention_backward_kernel(
            query_heads, groups, head_dim, block, reach, head_dim**-0.5,
            grad_of, lambda index: run(hooks.get((2, index), ())), *attention_in, *attention_out, *attention_scratch,
        )

    timed = [item for item in hooks.items() if item[0] != "late"]

    @pl.when(step == 3)
    def _():
        exchange(1).wait()

    @pl.when(step > 2)
    def _():
        def hook(h):
            for (at_step, at_head), events in timed:
                if at_head == h and at_step > 2:
                    @pl.when(step == at_step)
                    def _():
                        run(events)

        def grad_of(chunk, low, high):
            per = head_grad.shape[2] // block
            begin = pl.multiple_of((chunk % per) * block, block)
            return head_grad[chunk // per, attn_rows + low : attn_rows + high, pl.ds(begin, block)]

        ssd_backward_body(block, heads, ssd_dim, step - 3, steps - 3, hook, grad_of, *ssd_in, *ssd_out, *ssd_scratch)

    late = hooks.get("late", ())

    @pl.when(step == steps - 1)
    def _():
        run(late)


def mixer_backward(act, rows, grad_mixer, features, grad_pair, gate_part, up_part, attention_args, ssd_args, entry, plan, sizes, collective_id):
    query_heads, groups, head_dim, heads, ssd_dim, block, reach = sizes
    summer = plan[0]
    mixer_t, vec_t, step_t, run8, run_col, tap_x, tap_b, head_cols, skip_col = ssd_args
    inner = mixer_t.shape[0] // 2
    seq = mixer_t.shape[1]
    vec = vec_t.shape[0]
    rows16 = step_t.shape[0]
    chunks = seq // block
    state_dim = vec // 2
    per = block // 128
    before = 3
    chunk_of = lambda i: jnp.minimum(chunks - 1 + before - i, chunks - 1)
    wide = lambda i: (0, chunk_of(i))
    whole = lambda i: (0, 0)
    proj_t = attention_args[0]
    once = pl.Buffered(1)
    ssd_in = [mixer_t, mixer_t, mixer_t, vec_t, vec_t, step_t, run8, run_col, tap_x, tap_b, head_cols, skip_col]
    ssd_in += [entry, run8]
    in_specs = [
        pl.BlockSpec(act.shape, whole, pipeline_mode=once),
        pl.BlockSpec(rows.shape, whole, pipeline_mode=once),
        pl.BlockSpec(grad_mixer.shape, whole, pipeline_mode=once),
        pl.BlockSpec(features.shape, whole, pipeline_mode=once),
        pl.BlockSpec(memory_space=pl.ANY),
        pl.BlockSpec(memory_space=pl.ANY),
        pl.BlockSpec(memory_space=pl.ANY),
    ]
    in_specs += [pl.BlockSpec(item.shape, whole, pipeline_mode=once) for item in attention_args]
    in_specs += ssd_specs(block, inner, vec, rows16, chunk_of)
    in_specs += [
        pl.BlockSpec((1, inner, state_dim), lambda i: (chunk_of(i), 0, 0)),
        pl.BlockSpec((8, 128), lambda i: (0, jnp.minimum(chunk_of(i) * per + per, chunks * per - 1))),
    ]
    ssd_out = [
        (2 * inner, seq, block, BF16),
        (vec, seq, block, BF16),
        (rows16, seq, block, F32),
        (rows16, seq, block, F32),
        (inner, 128, 128, F32),
        (vec, 128, 128, F32),
        (inner, 128, 128, F32),
    ]
    out_specs = [pl.BlockSpec(proj_t.shape, whole)]
    out_specs += [
        pl.BlockSpec((height, width), wide if full == seq else whole) for height, full, width, _ in ssd_out
    ]
    part_row = summer.pieces[0][0]
    model_dim = rows.shape[1]
    part_shapes = [
        jax.ShapeDtypeStruct(shape, F32)
        for shape in (
            (part_row, model_dim),
            (part_row, model_dim),
            (part_row, model_dim),
            (part_row, query_heads * head_dim),
            (part_row, inner),
        )
    ]
    out_specs += [pl.BlockSpec(item.shape, whole) for item in part_shapes]
    attention_scratch = [pltpu.VMEM((groups * head_dim, seq), F32)] * 2
    ssd_scratch = [
        pltpu.VMEM((inner, state_dim), F32),
        pltpu.VMEM((inner, 128), F32),
        pltpu.VMEM((vec, 128), F32),
        pltpu.VMEM((5, inner, 128), F32),
        pltpu.VMEM((5, vec, 128), F32),
        pltpu.VMEM((inner, 128), F32),
        pltpu.VMEM((inner, block), BF16),
        pltpu.VMEM((inner, block), BF16),
        pltpu.VMEM((rows16, block), F32),
        pltpu.VMEM((rows16, block), F32),
        pltpu.VMEM((rows16, block), F32),
        pltpu.VMEM((rows16, block), F32),
        pltpu.VMEM((rows16, state_dim), F32),
    ]
    results = pl.pallas_call(
        functools.partial(
            backward_kernel, plan, sizes, len(attention_args), len(ssd_in), len(ssd_out),
            (len(attention_scratch), len(ssd_scratch)),
        ),
        grid=(chunks + before,),
        in_specs=in_specs,
        out_specs=out_specs,
        out_shape=[jax.ShapeDtypeStruct(proj_t.shape, BF16)]
        + [jax.ShapeDtypeStruct((height, full), dtype) for height, full, _, dtype in ssd_out]
        + part_shapes,
        scratch_shapes=attention_scratch
        + ssd_scratch
        + [pltpu.VMEM(grad_pair.shape, BF16), pltpu.SemaphoreType.DMA((7,))]
        + summer.scratch(),
        compiler_params=pltpu.CompilerParams(
            vmem_limit_bytes=63 << 20, collective_id=collective_id, has_side_effects=True
        ),
        cost_estimate=pl.CostEstimate(flops=7 * 10**10, bytes_accessed=5 * 10**7, transcendentals=3 * 10**7),
        name="mixer_backward",
    )(act, rows, grad_mixer, features, grad_pair, gate_part, up_part, *attention_args, *ssd_in)
    return results[0], results[1:8], results[8:]

def final_kernel(plan, eps, sizes, *refs):
    summer, partners, across, order = plan
    heads, head_dim = sizes
    names = ("normed", "dvec", "dmixer", "mixer_w", "state_w", "dqkv", "qkv_w", "dstep", "step_w", "rows", "hidden")
    hbm = dict(zip(names, refs[: len(names)]))
    refs = refs[len(names) :]
    (gain_ref, tapx_ref, tapb_ref, skip_ref, rate_ref, head_ref, ffn_gain_ref, ssd_gain_ref), refs = refs[:8], refs[8:]
    (
        input_out, query_out, keyval_out, mixer_out, state_out, step_out, taps_out, bias_out, gain_out, ffn_gain_out,
        state_taps_out, state_bias_out, bias_sum_out, rate_sum_out, skip_sum_out, ssd_gain_out,
    ), refs = refs[:16], refs[16:]
    vmem = dict(zip(names, refs[: len(names)]))
    refs = refs[len(names) :]
    partial, sent, got, load_sem, swap_sem = refs[:5]
    branch_pos = digit_of(across)
    half, width = partial.shape
    inner = vmem["dmixer"].shape[0] // 2
    query_cols = query_out.shape[1]
    key_cols = keyval_out.shape[2]
    gain_rows = width // 128
    state_rows = tapb_ref.shape[0] // 128

    def emit_mixer(part):
        def emit(value):
            mixer_out[:, part, :] = value

        return emit

    def emit_qkvs(value):
        query_out[...] = value[:, :query_cols]
        for part in range(2):
            keyval_out[:, part, :] = value[:, query_cols + part * key_cols : query_cols + (part + 1) * key_cols]
        begin = query_cols + 2 * key_cols
        steps = value[:, begin:]
        steps = jnp.concatenate([steps, jnp.zeros((steps.shape[0], 128 - steps.shape[1]), F32)], axis=1)
        step_out[...] = jnp.transpose(steps)[:heads]

    def emit_state(parts):
        values = parts[...].astype(F32)
        columns = values.shape[2] // 2
        for part in range(2):
            piece = values[:, :, part * columns : (part + 1) * columns]
            state_out[:, part, :] = piece.reshape(-1, columns)

    def emit_own(value):
        turned = jnp.transpose(value)
        taps_out[...] = turned[:4]
        bias_out[...] = turned[4:5]

    def emit_shared(parts):
        per = parts.shape[1]
        row = lambda place: parts[place // per, place % per : place % per + 1]
        for place in range(gain_rows):
            gain_out[place : place + 1] = row(place)
            ffn_gain_out[place : place + 1] = row(gain_rows + place)
        begin = 2 * gain_rows
        for tap in range(4):
            for part in range(state_rows):
                state_taps_out[tap, part : part + 1] = row(begin + tap * state_rows + part)
        begin += 4 * state_rows
        for part in range(state_rows):
            state_bias_out[part : part + 1] = row(begin + part)
        begin += state_rows
        for place, out_ref in enumerate((bias_sum_out, rate_sum_out, skip_sum_out)):
            out_ref[...] = row(begin + place)[:, : out_ref.shape[1]]
        begin += 3
        for place in range(ssd_gain_out.shape[0]):
            ssd_gain_out[place : place + 1] = row(begin + place)

    summer.bind(
        [emit_mixer(0), emit_mixer(1), emit_qkvs, emit_state, emit_own, emit_shared], refs[5:]
    )

    def load(name):
        return pltpu.make_async_copy(hbm[name], vmem[name], load_sem.at[names.index(name)])

    for name in names:
        load(name).start()
    greet(partners)
    gain = gain_ref[...]

    def index_of(full, owner):
        digits = len(full.shape) - 2
        return tuple((owner >> (digits - 1 - place)) & 1 for place in range(digits))

    own = summer.full[4]
    own_rows = own.shape[-2]
    for owner in range(tapx_ref.shape[0] // own_rows):
        own[index_of(own, owner)] = tapx_ref[owner * own_rows : (owner + 1) * own_rows]
    summer.start(4)

    shared = summer.full[5]
    per = shared.shape[-2]

    def put(place, row):
        shared[index_of(shared, place // per) + (slice(place % per, place % per + 1),)] = row

    for place in range(gain_rows):
        put(gain_rows + place, ffn_gain_ref[place : place + 1])
    begin = 2 * gain_rows
    turned = jnp.transpose(tapb_ref[...])
    for tap in range(5):
        for part in range(state_rows):
            put(begin + tap * state_rows + part, turned[tap : tap + 1, part * 128 : (part + 1) * 128])
    begin += 5 * state_rows

    def head_row(column):
        row = jnp.transpose(jnp.broadcast_to(column, (column.shape[0], 128)))[0:1]
        row = jnp.concatenate([row, jnp.zeros((1, 128 - row.shape[1]), F32)], axis=1)
        lanes = lax.broadcasted_iota(jnp.int32, row.shape, 1)
        row = jnp.where(lanes < heads, row, 0.0)
        return jnp.where(branch_pos == 0, row, pltpu.roll(row, heads, 1))

    rate_column = jnp.sum(rate_ref[...], axis=1, keepdims=True) * head_ref[:, 1:2]
    put(begin + 1, head_row(rate_column))
    skips = jnp.sum(skip_ref[...].reshape(heads, head_dim, 128), axis=1)[:, 0:1]
    pad = rate_ref.shape[0] - heads
    put(begin + 2, head_row(jnp.concatenate([skips, jnp.zeros((pad, 1), F32)], axis=0)))
    for place in range(ssd_gain_ref.shape[0]):
        put(begin + 3 + place, ssd_gain_ref[place : place + 1])
    for place in range(begin + 3 + ssd_gain_ref.shape[0], per << (len(shared.shape) - 2)):
        put(place, jnp.zeros((1, 128), F32))

    def partial_of(begin):
        at = pl.ds(pl.multiple_of(begin, 256), 256)
        return (
            mm(vmem["dmixer"][:, at], vmem["mixer_w"][...], 0, 1)
            + mm(vmem["dvec"][:, at], vmem["state_w"][...], 0, 1)
            + mm(vmem["dqkv"][:, at], vmem["qkv_w"][...], 0, 1)
            + mm(vmem["dstep"][:, at].astype(BF16), vmem["step_w"][...], 0, 1)
        )

    chunks = half // 256

    def swap(part):
        rows = slice(part * 256, (part + 1) * 256)
        return send_to((across,), sent.at[rows], got.at[rows], swap_sem.at[0, part], swap_sem.at[1, part])

    tile = 256
    tiles = width // tile

    def left_tile(t):
        return vmem["normed"][:, pl.ds(pl.multiple_of(t * tile, tile), tile)]

    def gain_sum(tokens, begin):
        return jnp.sum(
            tokens * vmem["normed"][pl.ds(pl.multiple_of(begin, 256), 256)].astype(F32), axis=0, keepdims=True
        )

    load("normed").wait()
    load("dvec").wait()

    @pl.loop(0, tiles)
    def _(t):
        value = mm(left_tile(t), vmem["dvec"][...], 0, 1).astype(BF16)
        summer.full[3][t // 2, t % 2] = value.reshape(summer.full[3].shape[2:])

    summer.start(3)
    summer.advance(4, 0)
    load("dmixer").wait()
    for item, begin_row in ((1, inner), (0, 0)):
        @pl.loop(0, tiles)
        def _(t):
            value = mm(left_tile(t), vmem["dmixer"][begin_row : begin_row + inner], 0, 1).astype(BF16)
            summer.full[item][t // 2, t % 2] = value.reshape(summer.full[item].shape[2:])

        summer.start(item)
        summer.advance(*((3, 0) if item == 1 else (1, 0)))

    for name in ("mixer_w", "state_w", "dqkv", "qkv_w", "dstep", "step_w"):
        load(name).wait()
    total = jnp.zeros((1, width), F32)
    for t in range(chunks):
        rows = slice(t * 256, (t + 1) * 256)
        begin_other = (1 - branch_pos) * half + t * 256
        value = partial_of(begin_other)
        sent[rows] = value.astype(BF16)
        if t == 0:
            swap(0).start()
            summer.advance(0, 0)
            summer.advance(4, 1)
        total = total + gain_sum(value, begin_other)
    summer.advance(3, 1)
    for t in range(chunks):
        rows = slice(t * 256, (t + 1) * 256)
        begin_own = branch_pos * half + t * 256
        value = partial_of(begin_own)
        partial[rows] = value
        total = total + gain_sum(value, begin_own)
        if t == 0:
            summer.advance(4, 2)
    total = total / gain
    for place in range(gain_rows):
        put(place, total[:, place * 128 : (place + 1) * 128])
    put(begin, head_row(jnp.sum(vmem["dstep"][...], axis=1, keepdims=True)))
    summer.start(5)

    @pl.loop(0, tiles)
    def _(t):
        columns = vmem["dqkv"].shape[0]
        shape = summer.full[2].shape[2:5]
        value = mm(left_tile(t), vmem["dqkv"][...], 0, 1).astype(BF16)
        summer.full[2][t // 2, t % 2, :, :, :, :columns] = value.reshape(shape + (columns,))
        value = mm(left_tile(t), vmem["dstep"][...].astype(BF16), 0, 1).astype(BF16)
        summer.full[2][t // 2, t % 2, :, :, :, columns:] = value.reshape(shape + (value.shape[1],))

    summer.advance(5, 0)
    for part in range(1, chunks):
        swap(part).start()
    summer.start(2)

    for event in order:
        if event != "input":
            summer.advance(*event)
            continue
        load("rows").wait()
        load("hidden").wait()
        for part in range(chunks):
            swap(part).wait()

        @pl.loop(0, half // 64)
        def _(t):
            rows = pl.ds(pl.multiple_of(t * 64, 64), 64)
            values = vmem["rows"][rows].astype(F32)
            scale = lax.rsqrt(jnp.mean(values * values, axis=1, keepdims=True) + eps)
            weighted = (partial[rows].astype(BF16).astype(F32) + got[rows].astype(F32)) * gain
            centre = jnp.mean(weighted * values, axis=1, keepdims=True)
            result = vmem["hidden"][rows] + scale * weighted - values * (scale * scale * scale * centre)
            input_out[rows] = result.astype(BF16)


def final_gradients(arrays, smalls, outs, plan, eps, sizes, collective_id):
    summer = plan[0]
    half, width = arrays[9].shape
    vmem = pl.BlockSpec(memory_space=pltpu.VMEM)
    return pl.pallas_call(
        functools.partial(final_kernel, plan, eps, sizes),
        in_specs=[pl.BlockSpec(memory_space=pl.ANY)] * len(arrays) + [vmem] * len(smalls),
        out_specs=[vmem] * len(outs),
        out_shape=[jax.ShapeDtypeStruct(shape, dtype) for shape, dtype in outs],
        scratch_shapes=[pltpu.VMEM(item.shape, item.dtype) for item in arrays]
        + [
            pltpu.VMEM((half, width), F32),
            pltpu.VMEM((half, width), BF16),
            pltpu.VMEM((half, width), BF16),
            pltpu.SemaphoreType.DMA((len(arrays),)),
            pltpu.SemaphoreType.DMA((2, half // 256)),
        ]
        + summer.scratch(),
        compiler_params=pltpu.CompilerParams(
            vmem_limit_bytes=60 << 20, collective_id=collective_id, has_side_effects=True
        ),
        cost_estimate=pl.CostEstimate(flops=3 * 10**10, bytes_accessed=5 * 10**7, transcendentals=0),
        name="final_gradients",
    )(*arrays, *smalls)


def bits_of(count):
    return count.bit_length() - 1


def swap_halves(values, axis_name, bit, size):
    pairs = [(item, item ^ (1 << bit)) for item in range(size)]
    return lax.ppermute(values, axis_name, pairs)


def halve(values, place, my_bit, axis_name, bit, size):
    owners = values.shape[0]
    high = 1 << place
    parts = values.reshape((high, 2, owners // (2 * high)) + values.shape[1:])
    sent = lax.dynamic_index_in_dim(parts, 1 - my_bit, 1, keepdims=False)
    kept = lax.dynamic_index_in_dim(parts, my_bit, 1, keepdims=False)
    got = swap_halves(sent, axis_name, bit, size)
    total = (kept.astype(jnp.float32) + got.astype(jnp.float32)).astype(values.dtype)
    return total.reshape((owners // 2,) + values.shape[1:])


def scatter_sum(values, digits, order):
    left = list(digits)
    for digit in order:
        axis_name, bit, size = digit
        my_bit = (lax.axis_index(axis_name) >> bit) & 1
        values = halve(values, left.index(digit), my_bit, axis_name, bit, size)
        left.remove(digit)
    return values[0]


def gather_all(values, digits, order):
    values = values[None]
    left = []
    for digit in order:
        axis_name, bit, size = digit
        my_bit = (lax.axis_index(axis_name) >> bit) & 1
        got = swap_halves(values, axis_name, bit, size)
        place = sum(1 for item in left if digits.index(item) < digits.index(digit))
        high = 1 << place
        owners = values.shape[0]
        mine = values.reshape((high, 1, owners // high) + values.shape[1:])
        other = got.reshape(mine.shape)
        first = jnp.where(my_bit == 0, mine, other)
        second = jnp.where(my_bit == 0, other, mine)
        values = jnp.concatenate([first, second], axis=1).reshape((owners * 2,) + values.shape[1:])
        left.append(digit)
    return values


def other_branch(values):
    return lax.ppermute(values, "branch", [(0, 1), (1, 0)])


def rms_scale(values):
    return lax.rsqrt(jnp.mean(values * values, axis=-1, keepdims=True) + EPSILON)


def rms_back(upstream, values, scales, gain):
    weighted = upstream * gain
    return scales * weighted - values * scales**3 * jnp.mean(
        weighted * values, axis=-1, keepdims=True
    )


def token_runs(length_row, seq_len, doc_count):
    order = jnp.arange(doc_count, dtype=jnp.int32)
    ends = jnp.sum(jnp.where(order[:, None] >= order[None, :], length_row[None, :], 0), axis=1)
    places = jnp.arange(seq_len, dtype=jnp.int32)
    passed = places[:, None] >= ends[None, :]
    starts = jnp.sum(jnp.where(passed, length_row[None, :], 0), axis=1)
    return (places - starts).astype(F32), jnp.sum(length_row)


def join(mine, other, branch_pos, axis):
    return jnp.concatenate(
        [jnp.where(branch_pos == 0, mine, other), jnp.where(branch_pos == 0, other, mine)], axis=axis
    )


def fetch_weights(weight, near):
    quarter = weight.shape[0] // 4
    my_core, my_near = lax.axis_index("rows") & 1, (lax.axis_index("rows") >> near[1]) & 1
    return other_branch(lax.dynamic_slice_in_dim(weight, (2 * my_core + my_near) * quarter, quarter, 0))


def swap_weights(first, near):
    my_near = (lax.axis_index("rows") >> near[1]) & 1
    second = swap_halves(first, *near)
    return jnp.concatenate(
        [jnp.where(my_near == 0, first, second), jnp.where(my_near == 0, second, first)], axis=0
    )


def both_weights(weight, got, core, branch_pos):
    my_core = lax.axis_index("rows") & 1
    rest = swap_halves(got, *core)
    other = jnp.concatenate(
        [jnp.where(my_core == 0, got, rest), jnp.where(my_core == 0, rest, got)], axis=0
    )
    return join(weight, other, branch_pos, 0)


def hand_over_kernel(count, *refs):
    ins, outs, bufs, sems = refs[:count], refs[count : 2 * count], refs[2 * count : 3 * count], refs[3 * count]
    loads = [pltpu.make_async_copy(ins[item], bufs[item], sems.at[0, item]) for item in range(count)]
    stores = [pltpu.make_async_copy(bufs[item], outs[item], sems.at[1, item]) for item in range(count)]
    for copy in loads:
        copy.start()
    for load, store in zip(loads, stores):
        load.wait()
        store.start()
    for copy in stores:
        copy.wait()


def hand_over(arrays):
    anywhere = pl.BlockSpec(memory_space=pl.ANY)
    return pl.pallas_call(
        functools.partial(hand_over_kernel, len(arrays)),
        in_specs=[anywhere] * len(arrays),
        out_specs=[anywhere] * len(arrays),
        out_shape=[jax.ShapeDtypeStruct(item.shape, item.dtype) for item in arrays],
        scratch_shapes=[pltpu.VMEM(item.shape, item.dtype) for item in arrays]
        + [pltpu.SemaphoreType.DMA((2, len(arrays)))],
        compiler_params=pltpu.CompilerParams(vmem_limit_bytes=63 << 20),
        cost_estimate=pl.CostEstimate(flops=0, bytes_accessed=10**7, transcendentals=0),
        name="hand_over",
    )(*arrays)


def columns_of(items, rows):
    stacked = jnp.stack(items, axis=1)
    return jnp.pad(stacked, ((0, rows - stacked.shape[0]), (0, 128 - stacked.shape[1])))


def per_device(
    inputs,
    lengths,
    norm_gain,
    query_weight,
    keyval_weight,
    mixer_weight,
    state_weight,
    step_weight,
    conv_mixer,
    conv_state,
    bias_mixer,
    bias_state,
    step_bias,
    decay_log,
    skip_gain,
    ssd_gain,
    attn_output,
    ssd_output,
    ffn_gain,
    gate_weight,
    up_weight,
    down_weight,
    cotangent,
):
    branch_pos = lax.axis_index("branch")
    row_pos = lax.axis_index("rows")
    row_count = lax.axis_size("rows")
    row_bits = bits_of(row_count)
    row_digits = [("rows", bit, row_count) for bit in range(row_bits - 1, -1, -1)]
    across = ("branch", 0, 2)
    core = row_digits[-1]
    chip_digits = row_digits[:-1]
    near, others = chip_digits[-1], chip_digits[:-1][::-1]
    fast = row_bits == 4

    own_rows = inputs[0].astype(F32)
    upstream = cotangent[0]
    half_len, model_dim = own_rows.shape
    seq_len = 2 * half_len
    local_query = query_weight.shape[1] // HD
    local_keyval = keyval_weight.shape[2] // HD
    local_heads = step_bias.shape[0]
    local_inner = bias_mixer.shape[0]
    inner_dim = 2 * local_inner
    head_rows = -(-local_heads // 8) * 8
    own_begin = branch_pos * half_len

    run, used = token_runs(lengths[0], seq_len, lengths.shape[1])
    run8 = jnp.broadcast_to(run[None, :], (8, seq_len))
    run_col = jnp.broadcast_to(run[:, None], (seq_len, 128))
    frequency = ROPE_BASE ** (-(jnp.arange(HD // 2, dtype=F32) * 2.0) / HD)
    angles = frequency[:, None] * run[None, :]
    cosine, sine = jnp.cos(angles), jnp.sin(angles)
    own_valid = (own_begin + jnp.arange(half_len, dtype=jnp.int32) < used).astype(F32)[:, None]

    own_scale = rms_scale(own_rows)
    own_hat = own_rows * own_scale
    normed = (own_hat * norm_gain).astype(BF16)
    other_normed = other_branch(normed)
    full_normed = join(normed, other_normed, branch_pos, 0)

    out_weight = jnp.concatenate([attn_output, ssd_output], axis=0)
    held_weight, _ = lax.optimization_barrier((out_weight, normed))
    fetched = fetch_weights(held_weight, near)
    gain_full = join(ssd_gain, other_branch(ssd_gain), branch_pos, 0)

    qkv_flat = jnp.concatenate([query_weight, keyval_weight.reshape(model_dim, -1)], axis=1)
    mixer_flat = mixer_weight.reshape(model_dim, -1)
    state_flat = state_weight.reshape(model_dim, -1)
    step_flat = jnp.pad(step_weight, ((0, 0), (0, head_rows - local_heads)))

    mixer_t = mm(mixer_flat, full_normed, 0, 1).astype(BF16)
    vec_t = mm(state_flat, full_normed, 0, 1).astype(BF16)
    qkv_t = mm(qkv_flat, full_normed, 0, 1).astype(BF16)
    step_t = mm(step_flat, full_normed, 0, 1)

    fetched, mixer_t = lax.optimization_barrier((fetched, mixer_t))
    fetched = swap_weights(fetched, near)

    taps = [conv_mixer[item] for item in range(4)] + [bias_mixer]
    tap_x = columns_of(taps, local_inner)
    state_taps = [conv_state[item].reshape(-1) for item in range(4)] + [bias_state.reshape(-1)]
    tap_b = columns_of(state_taps, state_flat.shape[1])
    rates = -jnp.exp(decay_log)
    head_cols = columns_of([step_bias, rates], head_rows)
    skip_col = jnp.broadcast_to(jnp.repeat(skip_gain, SP)[:, None], (local_inner, 128))
    ssd_args = (mixer_t, vec_t, step_t, run8, run_col, tap_x, tap_b, head_cols, skip_col)

    def own_tokens(values, pos):
        return lax.dynamic_slice_in_dim(values, pos * half_len, half_len, 1)

    def to_owner(values):
        got = other_branch(own_tokens(values, 1 - branch_pos))
        mine = own_tokens(values, branch_pos)
        return jnp.where(branch_pos == 0, mine, got), jnp.where(branch_pos == 0, got, mine)

    def to_heads(first, second):
        got = other_branch(jnp.where(branch_pos == 0, second, first))
        return join(jnp.where(branch_pos == 0, first, second), got, branch_pos, 1)

    sizes = (local_query, local_keyval, HD, local_heads, SP, BLOCK, REACH)
    attn_rows = local_query * HD
    part_rows = attn_rows + local_inner
    if fast:
        entry, rot_t, log_sums, raw = mixer_forward(
            ssd_args, (qkv_t, cosine, sine, run8), across, sizes, 2, 4
        )
    else:
        gated_t, entry = ssd_forward(*ssd_args, local_heads, SP, BLOCK)
        attn_t, rot_t, log_sums = attention_forward(
            qkv_t, cosine, sine, run8, local_query, local_keyval, HD, BLOCK, REACH
        )
        raw = jnp.stack(
            [
                jnp.concatenate([first, second], axis=0)
                for first, second in zip(to_owner(attn_t), to_owner(gated_t))
            ]
        )
    fetched, raw = lax.optimization_barrier((fetched, raw))
    out_full = both_weights(out_weight, fetched, core, branch_pos)
    scanned_rows = (jnp.arange(part_rows) >= attn_rows)[None, :, None]
    gains = jnp.pad(gain_full.reshape(2, local_inner), ((0, 0), (attn_rows, 0)))[:, :, None]
    raw_values = raw.astype(F32)
    square_sum = jnp.sum(jnp.where(scanned_rows, raw_values * raw_values, 0.0), axis=(0, 1))
    gated_scale = lax.rsqrt(square_sum / inner_dim + EPSILON)[None, None, :]
    features = jnp.where(scanned_rows, (raw_values * gated_scale * gains).astype(BF16), raw)
    features = features.reshape(2 * part_rows, half_len)
    mixer_sum = mm(features, out_full, 0, 0)
    hidden = own_rows + own_valid * mixer_sum
    block_out, grad_hidden, grad_mixer, ffn_gain_grad, act_low, gate_part, up_part = feed_forward(
        hidden, jnp.broadcast_to(own_valid, (half_len, 128)), ffn_gain, upstream, gate_weight, up_weight, down_weight,
        256, EPSILON, (core, near, others[0]) if fast else None, 3,
    )
    block_out = block_out[None]

    grad_features = mm(out_full, grad_mixer, 1, 1).reshape(2, part_rows, half_len)
    ssd_gain_wgrad = jnp.sum(grad_features * raw_values * gated_scale, axis=2)[:, attn_rows:].reshape(-1)
    weighted = grad_features * gains
    row_inner = jnp.sum(weighted * raw_values, axis=(0, 1), keepdims=True) / inner_dim
    grad_pair = jnp.where(
        scanned_rows,
        gated_scale * weighted - raw_values * (gated_scale**3 * row_inner),
        grad_features,
    ).astype(BF16)

    all_digits = [across] + row_digits
    attention_args = (qkv_t, rot_t, cosine, sine, run8, log_sums)
    qkv_cols = qkv_t.shape[0]
    query_cols = local_query * HD
    if fast:
        x, y, z0, z1 = across, near, others[0], others[1]
        partners = [(item,) for item in all_digits] + [(x, y), (z0, z1)]
        orders = [
            [(z0,), (z1,), (x,)],
            [(y,), (x,), (z1,)],
            [(core,), (y,), (z1,), (x,), (z0,)],
            [(core,), (x,), (z0,), (y,), (z1,)],
            [(core,), (z0,), (y,), (z1,), (x,)],
            [(core,), (y,), (x,), (z0,), (z1,)],
        ]
        part_row = gate_weight.shape[1] // (2 * row_count)
        piece_digits = [[x, z1, z0], [x, z1, y]] + [all_digits] * 4
        piece_cols = [model_dim] * 2 + [model_dim // 2] * 4
        summer = Summer(
            [
                (part_row, cols, BF16, digits, order, False)
                for cols, digits, order in zip(piece_cols, piece_digits, orders)
            ]
        )
        hooks = {
            (2, 0): [(2, 0), (3, 0), (0, 0), (1, 0)],
            (2, 1): [(4, 0)],
            (2, 2): [(5, 0)],
            (3, 6): [(2, 1)],
            (3, 7): [(0, 1)],
            (4, 2): [(4, 1)],
            (4, 3): [(3, 1)],
            (4, 10): [(5, 1)],
            (4, 11): [(1, 1)],
            (5, 3): [(0, 2)],
            (5, 6): [(3, 2), (4, 2)],
            (5, 7): [(2, 2)],
            (6, 0): [(5, 2)],
            (6, 3): [(1, 2)],
            (6, 4): [(3, 3)],
            (6, 5): [(2, 3)],
            (6, 10): [(5, 3)],
            (6, 11): [(4, 3)],
            "late": [(2, 4), (3, 4), (4, 4), (5, 4)],
        }
        dqkv_t, ssd_grads, ffn_sums = mixer_backward(
            act_low,
            upstream,
            grad_mixer,
            features,
            grad_pair,
            gate_part.reshape((2, 2, 2) + gate_part.shape[1:]),
            up_part.reshape((2, 2, 2) + up_part.shape[1:]),
            attention_args,
            ssd_args,
            entry,
            (summer, partners[:-2], across, hooks),
            sizes,
            1,
        )
        gate_grad, up_grad, down_grad, attn_out_grad, ssd_out_grad = ffn_sums
    else:
        got = other_branch(grad_pair[1 - branch_pos])
        head_grad = join(grad_pair[branch_pos], got, branch_pos, 1)
        ssd_grads = ssd_backward(*ssd_args, entry, head_grad[attn_rows:], local_heads, SP, BLOCK)
        dqkv_t = attention_backward(
            *attention_args, head_grad[:attn_rows], local_query, local_keyval, HD, BLOCK, REACH
        )
        down_part = mm(act_low, upstream, 0, 0).astype(BF16)
        gate_sum, up_sum, down_sum = [
            scatter_sum(item.reshape(2 * row_count, -1, model_dim), all_digits, all_digits[::-1]).astype(F32)
            for item in (gate_part, up_part, down_part)
        ]
        out_part = mm(grad_mixer, features, 0, 1).astype(BF16).reshape(row_count, -1, 2, part_rows)
        out_part = jnp.moveaxis(out_part, 2, 0).reshape(2 * row_count, -1, part_rows)
        out_sum = scatter_sum(out_part, all_digits, all_digits[::-1]).astype(F32)
        gate_grad, up_grad, down_grad = gate_sum.T, up_sum.T, down_sum
        attn_out_grad, ssd_out_grad = out_sum[:, :attn_rows].T, out_sum[:, attn_rows:].T
    dmixer_t, dvec_t, dstep_t, dlog_t, dtap_x, dtap_b, dskip = ssd_grads

    qkv_step_cols = qkv_cols + head_rows
    gather_digits = [core, across, near] + others
    own_width = local_inner // row_count
    gain_rows = model_dim // 128
    tap_rows = 4 * state_flat.shape[1] // 128
    bias_rows = state_flat.shape[1] // 128
    inner_rows = inner_dim // 128
    if fast:
        row_part = model_dim // row_count
        rows_total = 2 * gain_rows + tap_rows + bias_rows + 3 + inner_rows
        shared_rows = -(-rows_total // (2 * row_count))
        first = [(core,), (y,), (z0,), (z1,)]
        second = [(core,), (z0,), (y,), (z1,)]
        gathered = [(core,), (x, y), (z0, z1)]
        gather_digits = [core, x, y, z0, z1]
        summer = Summer(
            [
                (row_part, local_inner, BF16, row_digits, first, False),
                (row_part, local_inner, BF16, row_digits, second, False),
                (row_part, qkv_step_cols, BF16, row_digits, first, False),
                (row_part // 2, state_flat.shape[1], BF16, gather_digits, gathered, True),
                (own_width, 128, F32, row_digits, [(core,), (y,), (z0, z1)], False),
                (shared_rows, 128, F32, gather_digits, gathered, True),
            ]
        )
        arrays = [
            full_normed, dvec_t, dmixer_t, mixer_flat, state_flat, dqkv_t, qkv_flat, dstep_t, step_flat,
            inputs[0], grad_hidden,
        ]
        smalls = [
            norm_gain.reshape(1, model_dim), dtap_x, dtap_b, dskip, dlog_t, head_cols,
            ffn_gain_grad.reshape(gain_rows, 128), ssd_gain_wgrad.reshape(inner_rows, 128),
        ]
        outs = [
            ((half_len, model_dim), BF16),
            ((row_part, query_cols), F32),
            ((row_part,) + keyval_weight.shape[1:], F32),
            ((row_part,) + mixer_weight.shape[1:], F32),
            (state_weight.shape, F32),
            ((local_heads, row_part), F32),
            ((4, own_width), F32),
            ((1, own_width), F32),
            ((gain_rows, 128), F32),
            ((gain_rows, 128), F32),
            (conv_state.shape, F32),
            (bias_state.shape, F32),
            ((1, 2 * local_heads), F32),
            ((1, 2 * local_heads), F32),
            ((1, 2 * local_heads), F32),
            ((inner_rows, 128), F32),
        ]
        order = [
            (1, 1), (0, 1), (3, 2), (2, 0), (5, 1), (0, 2), (1, 2), (3, 3), (5, 2), (2, 1), (0, 3), "input", (3, 4),
            (1, 3), (5, 3), (3, 5), (2, 2), (5, 4), (5, 5), (2, 3),
        ]
        (
            input_grad, query_grad, keyval_grad, mixer_grad, state_grad, step_grad, taps_grad, bias_grad, gain_grad,
            ffn_gain_sum, state_taps_grad, state_bias_grad, step_bias_grad, decay_grad, skip_grad, ssd_gain_rows,
        ) = final_gradients(
            arrays, smalls, outs, (summer, partners, across, order), EPSILON, (local_heads, SP), 2
        )
        (
            block_out, gate_grad, up_grad, down_grad, attn_out_grad, ssd_out_grad,
            input_grad, query_grad, keyval_grad, mixer_grad, state_grad, step_grad, taps_grad, bias_grad, gain_grad,
            ffn_gain_sum, state_taps_grad, state_bias_grad, step_bias_grad, decay_grad, skip_grad,
        ) = hand_over(
            [
                block_out, gate_grad, up_grad, down_grad, attn_out_grad, ssd_out_grad,
                input_grad, query_grad, keyval_grad, mixer_grad, state_grad, step_grad, taps_grad, bias_grad, gain_grad,
                ffn_gain_sum, state_taps_grad, state_bias_grad, step_bias_grad, decay_grad, skip_grad,
            ]
        )
        gate_grad, up_grad, step_grad = gate_grad.T, up_grad.T, step_grad.T
        attn_out_grad, ssd_out_grad = attn_out_grad.T, ssd_out_grad.T
        ssd_gain_sum = ssd_gain_rows.reshape(-1)
        ffn_gain_sum = ffn_gain_sum.reshape(-1)
        gain_grad, bias_grad = gain_grad.reshape(-1), bias_grad.reshape(-1)
        step_bias_grad, decay_grad, skip_grad = [
            item.reshape(-1) for item in (step_bias_grad, decay_grad, skip_grad)
        ]
    else:
        dstep_low = dstep_t.astype(BF16)
        partial_normed = (
            mm(dmixer_t, mixer_flat, 0, 1)
            + mm(dvec_t, state_flat, 0, 1)
            + mm(dqkv_t, qkv_flat, 0, 1)
            + mm(dstep_low, step_flat, 0, 1)
        ).astype(BF16)
        sent = lax.dynamic_slice_in_dim(partial_normed, (1 - branch_pos) * half_len, half_len, 0)
        kept = lax.dynamic_slice_in_dim(partial_normed, own_begin, half_len, 0)
        own_grad_normed = kept.astype(F32) + other_branch(sent).astype(F32)
        input_grad = grad_hidden + rms_back(own_grad_normed, own_rows, own_scale, norm_gain)
        input_grad = input_grad.astype(BF16)
        norm_gain_part = jnp.sum(partial_normed.astype(F32) * full_normed.astype(F32), axis=0) / norm_gain

        def row_sum(grads_t):
            value = mm(full_normed, grads_t, 0, 1).astype(BF16)
            value = value.reshape((row_count, -1) + value.shape[1:])
            return scatter_sum(value, row_digits, row_digits[::-1]).astype(F32)

        def everywhere(value):
            value = scatter_sum(value, gather_digits, gather_digits)
            return gather_all(value, gather_digits, gather_digits[::-1])

        mixer_grad = row_sum(dmixer_t).reshape((-1,) + mixer_weight.shape[1:])
        qkvs_sum = row_sum(jnp.concatenate([dqkv_t, dstep_low], axis=0))
        query_grad = qkvs_sum[:, :query_cols]
        keyval_grad = qkvs_sum[:, query_cols:qkv_cols].reshape((-1,) + keyval_weight.shape[1:])
        step_grad = qkvs_sum[:, qkv_cols : qkv_cols + local_heads]
        own_part = jnp.swapaxes(dtap_x[:, :5].T.reshape(5, row_count, own_width), 0, 1)
        own_sum = scatter_sum(own_part, row_digits, row_digits[::-1])
        taps_grad, bias_grad = own_sum[:4], own_sum[4]
        state_part = mm(full_normed, dvec_t, 0, 1).astype(BF16)
        state_part = everywhere(state_part.reshape(2 * row_count, -1, state_part.shape[1]))
        state_grad = state_part.astype(F32).reshape(state_weight.shape)

        def widen(values):
            full = jnp.zeros((2 * local_heads,), F32)
            return lax.dynamic_update_slice_in_dim(full, values, branch_pos * local_heads, 0)

        heads = slice(0, local_heads)
        small = [
            norm_gain_part,
            ffn_gain_grad,
            dtap_b[:, :4].T,
            dtap_b[:, 4],
            widen(jnp.sum(dstep_t[heads], axis=1)),
            widen(jnp.sum(dlog_t[heads], axis=1) * rates),
            widen(jnp.sum(dskip[:, 0].reshape(local_heads, SP), axis=1)),
            ssd_gain_wgrad,
        ]
        flat = jnp.concatenate([item.reshape(-1) for item in small])
        unit = 2 * row_count * 128
        flat = jnp.pad(flat, (0, -flat.shape[0] % unit)).reshape(2 * row_count, -1, 128)
        flat = everywhere(flat).reshape(-1)
        sums, begin = [], 0
        for item in small:
            sums.append(flat[begin : begin + item.size])
            begin += item.size
        gain_grad, ffn_gain_sum, state_taps_grad, state_bias_grad = sums[:4]
        step_bias_grad, decay_grad, skip_grad, ssd_gain_sum = sums[4:]
    own_gain_grad = lax.dynamic_slice_in_dim(
        ssd_gain_sum, branch_pos * local_inner + row_pos * own_width, own_width, 0
    )
    return (
        block_out,
        input_grad[None],
        gain_grad,
        query_grad,
        keyval_grad,
        mixer_grad,
        state_grad,
        step_grad,
        taps_grad,
        state_taps_grad.reshape(conv_state.shape),
        bias_grad,
        state_bias_grad.reshape(bias_state.shape),
        step_bias_grad,
        decay_grad,
        skip_grad,
        own_gain_grad,
        attn_out_grad,
        ssd_out_grad,
        ffn_gain_sum,
        gate_grad,
        up_grad,
        down_grad,
    )


def solution(mesh):
    in_specs = (
        P("rows", "branch", None),
        P("rows", None),
        P(),
        P(None, "branch"),
        P(None, None, "branch"),
        P(None, None, "branch"),
        P(),
        P(None, "branch"),
        P(None, "branch"),
        P(),
        P("branch"),
        P(),
        P("branch"),
        P("branch"),
        P("branch"),
        P("branch"),
        P("branch", None),
        P("branch", None),
        P(),
        P(),
        P(),
        P(),
        P("rows", "branch", None),
    )
    out_specs = (
        P("rows", "branch", None),
        P("rows", "branch", None),
        P(),
        P("rows", "branch"),
        P("rows", None, "branch"),
        P("rows", None, "branch"),
        P(),
        P("rows", "branch"),
        P(None, ("branch", "rows")),
        P(),
        P(("branch", "rows")),
        P(),
        P(),
        P(),
        P(),
        P(("branch", "rows")),
        P("branch", "rows"),
        P("branch", "rows"),
        P(),
        P(None, ("branch", "rows")),
        P(None, ("branch", "rows")),
        P(("branch", "rows"), None),
    )
    return jax.shard_map(
        per_device, mesh=mesh, in_specs=in_specs, out_specs=out_specs, check_vma=False
    )
```
